32 devices in a mesh: dp: 8 (over z, x), expert: 4 (over y, core).
Axes of the slice: x: 2, y: 2, z: 4, core: 2. Of those that a mesh axis runs over, the one named last changes fastest.
Arguments:
- patches: bfloat16 [2, 16, 1024, 768], P(None, 'dp', 'expert'), may hold values from -6 to 6
- routes: int32 [2, 16, 1024, 2, 2, 4], P(None, 'dp', 'expert'), may hold values from 0 to 7, all different within a row
- masks: int32 [2, 16, 1024, 256], P(None, 'dp', 'expert'), may hold values from 0 to 1
- targets: bfloat16 [2, 16, 1024, 1024], P(None, 'dp', 'expert'), may hold values from -6 to 6
- task_ids: int32 [2, 16], P(None, 'dp'), may hold values from 0 to 1, as said below
- step_count: int32 [1], replicated, may hold values from 2 to 20
- patch_weight: float32 [768, 384], replicated, may hold values from -0.21875 to 0.21875
- patch_moment: float32 [768, 384], replicated, may hold values from -2.0861626e-07 to 2.0861626e-07
- patch_square: float32 [768, 384], replicated, may hold values from 9e-17 to 3.6e-16
- keyval_weight: float32 [384, 128], replicated, may hold values from -0.3125 to 0.3125
- keyval_moment: float32 [384, 128], replicated, may hold values from -2.0861626e-07 to 2.0861626e-07
- keyval_square: float32 [384, 128], replicated, may hold values from 9e-17 to 3.6e-16
- router_weight: float32 [384, 32], replicated, may hold values from -0.15625 to 0.15625
- router_moment: float32 [384, 32], replicated, may hold values from -2.0861626e-07 to 2.0861626e-07
- router_square: float32 [384, 32], replicated, may hold values from 9e-17 to 3.6e-16
- norm_weight: float32 [6, 384], replicated
- norm_moment: float32 [6, 384], replicated, may hold values from -2.0861626e-07 to 2.0861626e-07
- norm_square: float32 [6, 384], replicated, may hold values from 3.30696e-14 to 1.322784e-13
- head_weight: float32 [384, 1024], replicated, may hold values from -0.3125 to 0.3125
- head_moment: float32 [384, 1024], replicated, may hold values from -2.0861626e-07 to 2.0861626e-07
- head_square: float32 [384, 1024], replicated, may hold values from 9e-17 to 3.6e-16
- attention_weight: float32 [2, 384, 512], P(None, None, 'expert')
- attention_moment: float32 [2, 384, 512], P(None, None, 'expert'), may hold values from -2.0861626e-07 to 2.0861626e-07
- attention_square: float32 [2, 384, 512], P(None, None, 'expert'), may hold values from 9e-17 to 3.6e-16
- expert_weight: float32 [8, 2, 384, 1536], P('expert'), may hold values from -0.3125 to 0.3125
- expert_moment: float32 [8, 2, 384, 1536], P('expert'), may hold values from -2.0861626e-07 to 2.0861626e-07
- expert_square: float32 [8, 2, 384, 1536], P('expert'), may hold values from 1.8e-17 to 7.2e-17
Outputs:
- loss: float32 [], replicated
- grad_norm: float32 [], replicated
- expert_norm: float32 [], replicated
- updated_patch: float32 [768, 384], replicated
- moment_patch: float32 [768, 384], replicated
- square_patch: float32 [768, 384], replicated
- updated_keyval: float32 [384, 128], replicated
- moment_keyval: float32 [384, 128], replicated
- square_keyval: float32 [384, 128], replicated
- updated_router: float32 [384, 32], replicated
- moment_router: float32 [384, 32], replicated
- square_router: float32 [384, 32], replicated
- updated_norm: float32 [6, 384], replicated
- moment_norm: float32 [6, 384], replicated
- square_norm: float32 [6, 384], replicated
- updated_head: float32 [384, 1024], replicated
- moment_head: float32 [384, 1024], replicated
- square_head: float32 [384, 1024], replicated
- updated_attention: float32 [2, 384, 512], P(None, None, 'expert')
- moment_attention: float32 [2, 384, 512], P(None, None, 'expert')
- square_attention: float32 [2, 384, 512], P(None, None, 'expert')
- updated_expert: float32 [8, 2, 384, 1536], P('expert')
- moment_expert: float32 [8, 2, 384, 1536], P('expert')
- square_expert: float32 [8, 2, 384, 1536], P('expert')
The draws below stay inside these ranges and needn't reach their ends.
Inputs may be any that keep to these rules, and one draw needn't show every extreme that they name: `routes`: each row names 4 different experts. `task_ids`: in each microstep every task has 8 or more images.
All inputs are finite; a program needn't handle non-finite values.
Results may differ from the reference program's by a relative error of at most 0.014.
Values may be sent and summed in bfloat16 or wider, within the bound.
No kernel may reach another device: no remote copies, remote signals or barrier semaphores. Data moves between devices by JAX's collectives and lax.ppermute only.
A program may use at most 320 MiB of HBM per device.

```python
import math
import jax
import jax.numpy as jnp
from jax import lax

D = 384
FF = 1536
HEAD = 64
PIX = 256
PATCH_IN = 768
PATCHES = 1024
TASKS = 2
TOP = 4
MICRO = 2
EXPERTS = 8
IMG_ROW = 2
IMAGES = 16
PATCH_DEV = 256
TOK_DEV = 512
CAP = 256
N_DP = 8
N_EXPERT = 4
DEVICES = 32


def draw_masks(key, part):
    rate_key, pixel_key = jax.random.split(jax.random.fold_in(key, 11))
    image_rates = jax.random.randint(rate_key, (MICRO, IMAGES, 1, 1), 1, 9)
    pixels = jax.random.randint(pixel_key, (MICRO, IMAGES, PATCHES, PIX), 0, 8)
    return (pixels < image_rates).astype(jnp.int32)


def draw_task_ids(key, part):
    key_list = jax.random.split(jax.random.fold_in(key, 17), MICRO)
    shuffled = jax.vmap(lambda single: jax.random.permutation(single, IMAGES))(key_list)
    return (shuffled % TASKS).astype(jnp.int32)


def draw_norm_weight(key, part):
    gain_key, shift_key = jax.random.split(jax.random.fold_in(key, 23))
    gains = 1.0 + 0.3 * jax.random.uniform(gain_key, (3, 1, D), jnp.float32, -1.0, 1.0)
    shifts = 0.1 * jax.random.normal(shift_key, (3, 1, D), jnp.float32)
    return jnp.concatenate([gains, shifts], axis=1).reshape(6, D)


def draw_attention_weight(key, part):
    normal_noise = jax.random.normal(jax.random.fold_in(key, 29), (2, D, EXPERTS * HEAD), jnp.float32)
    scales = jnp.array([D ** (-0.5), PATCHES ** 0.5 / (0.4 * (TOP * HEAD) ** 0.5)], jnp.float32)
    return normal_noise * scales[:, None, None]


def steps_of(own_key, shape, shards, smallest, high):
    level, own = 1.0, jax.random.fold_in(own_key, 6)
    for axis_at, parts in shards:
        draws = jnp.exp(jax.random.uniform(jax.random.fold_in(own, axis_at), (parts,), jnp.float32, smallest / len(shards), high / len(shards)))
        level = level * jnp.repeat(draws, shape[axis_at] // parts).reshape([-1 if axis == axis_at else 1 for axis in range(len(shape))])
    return level


def choose_distinct(rng, rows, number_of, top, lift):
    order = jax.random.permutation(jax.random.fold_in(rng, 1), number_of)
    pull = order
    for power in range(3):
        pull = pull * pull // number_of
    pull = pull * lift // number_of
    tickets = jax.random.randint(jax.random.fold_in(rng, 2), (rows, number_of), 0, 4096) + pull
    sure = jax.random.permutation(jax.random.fold_in(rng, 3), rows)[jnp.arange(number_of) % rows]
    tickets = jnp.where(jnp.arange(rows)[:, None] == sure[None, :], 1 << 14, tickets)
    merit = tickets * number_of + jnp.arange(number_of)
    return lax.top_k(merit.astype(jnp.int32), top)[1].astype(jnp.int32)


def gaussian(own_key, extent, width, most, cuts=(), kind=jnp.bfloat16):
    result = width * jax.random.normal(own_key, extent, jnp.float32)
    if cuts:
        result = result * steps_of(own_key, extent, cuts, -0.22, 0.18)
    return jnp.clip(result, -most, most).astype(kind)


def setup_inputs(seed: int = 0) -> dict:
    seeds = jax.random.split(jax.random.key(seed), 28)
    return {
        "patches": gaussian(seeds[0], (MICRO, IMAGES, PATCHES, PATCH_IN), 1.0, 6.0, ((1, 8), (2, 4))),
        "routes": choose_distinct(seeds[1], MICRO * IMAGES * PATCHES * 2 * TASKS, EXPERTS, TOP, 8192).reshape((MICRO, IMAGES, PATCHES, 2, TASKS, TOP)),
        "masks": draw_masks(jax.random.fold_in(seeds[27], 71), 0),
        "targets": gaussian(seeds[3], (MICRO, IMAGES, PATCHES, 4 * PIX), 1.0, 6.0, ((1, 8), (2, 4))),
        "task_ids": draw_task_ids(jax.random.fold_in(seeds[27], 71), 0),
        "step_count": jax.random.randint(seeds[5], (1,), 2, 21).astype(jnp.int32),
        "patch_weight": gaussian(seeds[6], (PATCH_IN, D), PATCH_IN ** -0.5, 0.21875, (), jnp.float32),
        "patch_moment": gaussian(seeds[7], (PATCH_IN, D), (3.3e-8), 2.086162567138672e-07, (), jnp.float32),
        "patch_square": jnp.clip(jax.random.uniform(seeds[8], (PATCH_IN, D), jnp.float32, 8.999999688540309e-17, 3.5999998754161235e-16), 8.999999688540309e-17, 3.5999998754161235e-16),
        "keyval_weight": gaussian(seeds[9], (D, 2 * HEAD), D ** -0.5, 0.3125, (), jnp.float32),
        "keyval_moment": gaussian(seeds[10], (D, 2 * HEAD), (3.3e-8), 2.086162567138672e-07, (), jnp.float32),
        "keyval_square": jnp.clip(jax.random.uniform(seeds[11], (D, 2 * HEAD), jnp.float32, 8.999999688540309e-17, 3.5999998754161235e-16), 8.999999688540309e-17, 3.5999998754161235e-16),
        "router_weight": gaussian(seeds[12], (D, 2 * TASKS * EXPERTS), (4 * D) ** -0.5, 0.15625, (), jnp.float32),
        "router_moment": gaussian(seeds[13], (D, 2 * TASKS * EXPERTS), (3.3e-8), 2.086162567138672e-07, (), jnp.float32),
        "router_square": jnp.clip(jax.random.uniform(seeds[14], (D, 2 * TASKS * EXPERTS), jnp.float32, 8.999999688540309e-17, 3.5999998754161235e-16), 8.999999688540309e-17, 3.5999998754161235e-16),
        "norm_weight": draw_norm_weight(jax.random.fold_in(seeds[27], 71), 0),
        "norm_moment": gaussian(seeds[16], (6, D), (3.3e-8), 2.086162567138672e-07, (), jnp.float32),
        "norm_square": jnp.clip(jax.random.uniform(seeds[17], (6, D), jnp.float32, 3.306959944055464e-14, 1.3227839776221856e-13), 3.306959944055464e-14, 1.3227839776221856e-13),
        "head_weight": gaussian(seeds[18], (D, 4 * PIX), D ** -0.5, 0.3125, (), jnp.float32),
        "head_moment": gaussian(seeds[19], (D, 4 * PIX), (3.3e-8), 2.086162567138672e-07, (), jnp.float32),
        "head_square": jnp.clip(jax.random.uniform(seeds[20], (D, 4 * PIX), jnp.float32, 8.999999688540309e-17, 3.5999998754161235e-16), 8.999999688540309e-17, 3.5999998754161235e-16),
        "attention_weight": draw_attention_weight(jax.random.fold_in(seeds[27], 71), 0),
        "attention_moment": gaussian(seeds[22], (2, D, EXPERTS * HEAD), (3.3e-8), 2.086162567138672e-07, ((2, 4),), jnp.float32),
        "attention_square": jnp.clip(8.999999688540309e-17 + 2.6999999065620926e-16 * jax.random.uniform(seeds[23], (2, D, EXPERTS * HEAD), jnp.float32) ** steps_of(seeds[23], (2, D, EXPERTS * HEAD), ((2, 4),), -0.2, 0.2), 8.999999688540309e-17, 3.5999998754161235e-16),
        "expert_weight": gaussian(seeds[24], (EXPERTS, 2, D, FF), D ** -0.5, 0.3125, ((0, 4),), jnp.float32),
        "expert_moment": gaussian(seeds[25], (EXPERTS, 2, D, FF), (3.3e-8), 2.086162567138672e-07, ((0, 4),), jnp.float32),
        "expert_square": jnp.clip(1.7999999377080617e-17 + 5.399999813124185e-17 * jax.random.uniform(seeds[26], (EXPERTS, 2, D, FF), jnp.float32) ** steps_of(seeds[26], (EXPERTS, 2, D, FF), ((0, 4),), -0.2, 0.2), 1.7999999377080617e-17, 7.199999750832247e-17),
    }


MI_WEIGHT = 0.5
CLIP_UNIT = 3e-07
BETA_ONE = 0.9
BETA_TWO = 0.999
EPSILON = 1e-08
RATES = (0.02, 0.02, 0.02, 0.3, 0.02, 1.2, 0.02)
DECAY = 0.05

@jax.custom_vjp
def low(v):
    return lax.optimization_barrier(v.astype(jnp.bfloat16)).astype(jnp.float32)

@jax.custom_vjp
def low_back(v):
    return v

def low_keep(v):
    return (low(v), None)

def low_pass(kept, grad):
    return (grad,)

def back_keep(v):
    return (v, None)

def back_low(kept, grad):
    return (low(grad),)
low.defvjp(low_keep, low_pass)
low_back.defvjp(back_keep, back_low)

def rounded(values):
    return low_back(low(values))

def matmul_exact(left, right):
    return jnp.dot(left, right, precision=lax.Precision.HIGHEST)

def layer_norm(values, gain_row, shift_row):
    average = lax.optimization_barrier(jnp.mean(values, axis=-1, keepdims=True))
    centred = values - average
    variance = lax.optimization_barrier(jnp.mean(centred * centred, axis=-1, keepdims=True))
    return centred * lax.rsqrt(variance + 1e-06) * gain_row + shift_row

def route_gates(inner_layer_values, weight, row_hot, chosen):
    logits_all = matmul_exact(inner_layer_values, weight).reshape(inner_layer_values.shape[0], row_hot.shape[1], -1)
    logits = lax.optimization_barrier(jnp.sum(logits_all * row_hot[:, :, None], axis=1))
    prob_rows = jax.nn.softmax(logits, axis=-1)
    picked = prob_rows * chosen
    gate_rows = picked / lax.optimization_barrier(jnp.sum(picked, axis=-1, keepdims=True))
    return (gate_rows, matmul_exact(row_hot.T, prob_rows))

def select_routes(route_rows, row_task):
    task_hot = (row_task[:, None] == jnp.arange(route_rows.shape[1])[None, :]).astype(jnp.int32)
    return lax.optimization_barrier(jnp.sum(route_rows * task_hot[:, :, None], axis=1, dtype=jnp.int32))

def expert_hot(picked, experts):
    return lax.optimization_barrier(jnp.sum((picked[:, :, None] == jnp.arange(experts)[None, None, :]).astype(jnp.float32), axis=1))

def mutual(tables):
    grand_total = lax.optimization_barrier(jnp.sum(tables, axis=(1, 2), keepdims=True))
    joint_share = tables / grand_total
    task_share = lax.optimization_barrier(jnp.sum(joint_share, axis=2, keepdims=True))
    expert_share = lax.optimization_barrier(jnp.sum(joint_share, axis=1, keepdims=True))
    return jnp.sum(joint_share * (jnp.log(joint_share) - jnp.log(task_share) - jnp.log(expert_share)))

def pixel_sums(pred, target_rows, mask_rows, row_hot):
    row_count = pred.shape[0]
    pixels = mask_rows.shape[1]
    residue = pred - target_rows
    depth_sum = lax.optimization_barrier(jnp.sum(residue[:, :pixels] ** 2 * mask_rows, axis=1))
    normal = lax.optimization_barrier(jnp.sum(residue[:, pixels:].reshape(row_count, 3, pixels) ** 2 * mask_rows[:, None, :], axis=(1, 2)))
    return lax.optimization_barrier(jnp.sum(jnp.stack([depth_sum, normal], axis=1) * row_hot, axis=0))

def attend_image(args):
    queries, keyval, gate_rows = args
    query_three = queries.reshape(PATCHES, EXPERTS, HEAD)
    key_rows = keyval[:, :HEAD]
    value_rows = keyval[:, HEAD:]
    scores = low_back(jnp.einsum('peh,kh->epk', query_three, key_rows, precision=lax.Precision.HIGHEST)) * HEAD ** (-0.5)
    prob_rows = jax.nn.softmax(scores, axis=-1)
    weighted = low(prob_rows * gate_rows.T[:, :, None])
    mixture = rounded(jnp.einsum('epk,kh->peh', weighted, value_rows, precision=lax.Precision.HIGHEST))
    return mixture.reshape(PATCHES, EXPERTS * HEAD)

def expert_apply(args):
    rows_in, weight = args
    preactivation = low_back(matmul_exact(rows_in, low(weight[0])))
    inner_layer_values = low(jax.nn.gelu(preactivation, approximate=True))
    return rounded(matmul_exact(inner_layer_values, low(weight[1]).T))

def to_devices(values):
    return values.reshape(N_DP, IMG_ROW, N_EXPERT, PATCH_DEV, -1).transpose(0, 2, 1, 3, 4).reshape(DEVICES * TOK_DEV, -1)

def from_devices(values):
    return values.reshape(N_DP, N_EXPERT, IMG_ROW, PATCH_DEV, -1).transpose(0, 2, 1, 3, 4).reshape(IMAGES * PATCHES, -1)

def micro_parts(weights, patches, routes, masks, targets, task_ids):
    patch_w, keyval_w, router_w, norms, head_w, attention_w, expert_w = weights
    row_count = IMAGES * PATCHES
    row_task = jnp.repeat(task_ids, PATCHES)
    row_hot = (row_task[:, None] == jnp.arange(TASKS)[None, :]).astype(jnp.float32)
    route_rows = routes.reshape(row_count, 2, TASKS, TOP)
    picked_att = select_routes(route_rows[:, 0], row_task)
    picked_mlp = select_routes(route_rows[:, 1], row_task)
    router_width = TASKS * EXPERTS
    embedded = low_back(matmul_exact(low(patches.reshape(row_count, PATCH_IN)), low(patch_w)))
    normed_one = layer_norm(embedded, norms[0], norms[1])
    gates_att, table_att = route_gates(normed_one, router_w[:, :router_width], row_hot, expert_hot(picked_att, EXPERTS))
    normed_low = low(normed_one)
    queries = rounded(matmul_exact(normed_low, low(attention_w[0])))
    keyval = rounded(matmul_exact(normed_low, low(keyval_w)))
    mixture = lax.map(jax.checkpoint(attend_image), (queries.reshape(IMAGES, PATCHES, -1), keyval.reshape(IMAGES, PATCHES, -1), gates_att.reshape(IMAGES, PATCHES, EXPERTS)))
    branch = low_back(matmul_exact(mixture.reshape(row_count, -1), low(attention_w[1]).T))
    resid_one = embedded + branch
    normed_two = layer_norm(resid_one, norms[2], norms[3])
    gates_mlp, table_mlp = route_gates(normed_two, router_w[:, router_width:], row_hot, expert_hot(picked_mlp, EXPERTS))
    sent_rows = low(normed_two)
    sent_dev = to_devices(sent_rows)
    picked_dev = to_devices(picked_mlp).reshape(DEVICES, TOK_DEV * TOP)
    one_hot = (picked_dev[:, :, None] == jnp.arange(EXPERTS)[None, None, :]).astype(jnp.int32)
    before = jnp.cumsum(one_hot, axis=1, dtype=jnp.int32) - one_hot
    slot_index = lax.optimization_barrier(jnp.sum(before * one_hot, axis=2, dtype=jnp.int32))
    kept_pair = slot_index < CAP
    owner_index = jnp.arange(DEVICES, dtype=jnp.int32)[:, None]
    total_slots = EXPERTS * DEVICES * CAP
    target_slot = jnp.where(kept_pair, (picked_dev * DEVICES + owner_index) * CAP + slot_index, total_slots).reshape(-1).astype(jnp.int32)
    buffer = jnp.zeros((total_slots, D), jnp.float32).at[target_slot].set(jnp.repeat(sent_dev, TOP, axis=0), mode='drop')
    outputs = lax.map(jax.checkpoint(expert_apply), (buffer.reshape(EXPERTS, DEVICES * CAP, D), expert_w)).reshape(total_slots, D)
    gathered = outputs[jnp.minimum(target_slot, total_slots - 1)] * kept_pair.reshape(-1, 1).astype(jnp.float32)
    gathered = from_devices(gathered.reshape(DEVICES * TOK_DEV, TOP * D)).reshape(row_count, TOP, D)
    pair_gate = lax.optimization_barrier(jnp.sum(gates_mlp[:, None, :] * (picked_mlp[:, :, None] == jnp.arange(EXPERTS)[None, None, :]).astype(jnp.float32), axis=2))
    resid_two = resid_one + lax.optimization_barrier(jnp.sum(pair_gate[:, :, None] * gathered, axis=1))
    normed_three = layer_norm(resid_two, norms[4], norms[5])
    pred = low_back(matmul_exact(low(normed_three), low(head_w)))
    square_sums = pixel_sums(pred, targets.reshape(row_count, -1), masks.reshape(row_count, -1), row_hot)
    return (square_sums, jnp.stack([table_att, table_mlp]))

def total_loss(weights, patches, routes, masks, targets, task_ids, counts):
    square_sums = jnp.zeros((TASKS,), jnp.float32)
    tables = jnp.zeros((2, TASKS, EXPERTS), jnp.float32)
    for microstep in range(MICRO):
        part_sums, part_table = micro_parts(weights, patches[microstep], routes[microstep], masks[microstep], targets[microstep], task_ids[microstep])
        square_sums = square_sums + part_sums
        tables = tables + part_table
    return jnp.sum(square_sums / counts) - MI_WEIGHT * mutual(tables)

def adam_update(weight, first_moment, second, gradient, factor, step_value, rate):
    gradient = gradient * factor
    first_moment = BETA_ONE * first_moment + (1.0 - BETA_ONE) * gradient
    second = BETA_TWO * second + (1.0 - BETA_TWO) * gradient * gradient
    first_hat = first_moment / (1.0 - jnp.power(BETA_ONE, step_value))
    second_hat = second / (1.0 - jnp.power(BETA_TWO, step_value))
    weight = weight - rate * (first_hat / (jnp.sqrt(second_hat) + EPSILON) + DECAY * weight)
    return (weight, first_moment, second)

def reference(patches, routes, masks, targets, task_ids, step_count, patch_weight, patch_moment, patch_square, keyval_weight, keyval_moment, keyval_square, router_weight, router_moment, router_square, norm_weight, norm_moment, norm_square, head_weight, head_moment, head_square, attention_weight, attention_moment, attention_square, expert_weight, expert_moment, expert_square):
    weights = (patch_weight, keyval_weight, router_weight, norm_weight, head_weight, attention_weight, expert_weight)
    moments = (patch_moment, keyval_moment, router_moment, norm_moment, head_moment, attention_moment, expert_moment)
    squares = (patch_square, keyval_square, router_square, norm_square, head_square, attention_square, expert_square)
    patch_data = patches.astype(jnp.float32)
    target_data = targets.astype(jnp.float32)
    mask_data = masks.astype(jnp.float32)
    image_hot = (task_ids[:, :, None] == jnp.arange(TASKS)[None, None, :]).astype(jnp.float32)
    counts = lax.optimization_barrier(jnp.sum(image_hot * lax.optimization_barrier(jnp.sum(mask_data, axis=(2, 3)))[:, :, None], axis=(0, 1)))

    def loss_of(*model_parameters):
        return total_loss(model_parameters, patch_data, routes, mask_data, target_data, task_ids, counts)
    loss, pullback = jax.vjp(loss_of, *weights)
    grads = pullback(jnp.float32(1.0))
    norm_sq = jnp.float32(0.0)
    for gradient in grads:
        norm_sq = norm_sq + jnp.sum(gradient * gradient)
    grad_norm = jnp.sqrt(norm_sq)
    expert_norm = jnp.sqrt(jnp.sum(grads[5] * grads[5]) + jnp.sum(grads[6] * grads[6]))
    total_params = sum((weight.size for weight in weights))
    factor = jnp.minimum(1.0, CLIP_UNIT * math.sqrt(total_params) / grad_norm)
    step_value = step_count[0].astype(jnp.float32)
    results = [loss, grad_norm, expert_norm]
    for index in range(len(weights)):
        results.extend(adam_update(weights[index], moments[index], squares[index], grads[index], factor, step_value, RATES[index]))
    return tuple(results)
```

```python
from functools import partial
import math

import jax
import jax.numpy as jnp
from jax import lax
from jax.experimental import pallas as pl
from jax.experimental.pallas import tpu as pltpu
from jax.sharding import PartitionSpec as P

HEAD = 64
NORM_EPS = 1e-06
MI_WEIGHT = 0.5
CLIP_UNIT = 3e-07
BETA_ONE = 0.9
BETA_TWO = 0.999
EPSILON = 1e-08
RATES = (0.02, 0.02, 0.02, 0.3, 0.02, 1.2, 0.02)
DECAY = 0.05
F32 = jnp.float32
BF16 = jnp.bfloat16
EXACT = lax.Precision.HIGHEST
NOWHERE = 1 << 20
GELU_A = 0.044715
GELU_C = math.sqrt(2.0 / math.pi)


def mm(left, right, precision=None):
    return lax.dot_general(
        left, right, (((1,), (0,)), ((), ())), precision=precision, preferred_element_type=F32
    )


def mm_nt(left, right, precision=None):
    return lax.dot_general(
        left, right, (((1,), (1,)), ((), ())), precision=precision, preferred_element_type=F32
    )


def mm_tn(left, right, precision=None):
    return lax.dot_general(
        left, right, (((0,), (0,)), ((), ())), precision=precision, preferred_element_type=F32
    )


def norm_forward(values, gain, shift):
    centred = values - jnp.mean(values, axis=-1, keepdims=True)
    inverse = lax.rsqrt(jnp.mean(centred * centred, axis=-1, keepdims=True) + NORM_EPS)
    scaled = centred * inverse
    return scaled, inverse, scaled * gain + shift


def norm_backward(slope, scaled, inverse, gain):
    inner = slope * gain
    grad = inverse * (
        inner
        - jnp.mean(inner, axis=-1, keepdims=True)
        - scaled * jnp.mean(inner * scaled, axis=-1, keepdims=True)
    )
    return grad, jnp.sum(slope * scaled, axis=0, keepdims=True), jnp.sum(slope, axis=0, keepdims=True)


def expert_rows(experts, tokens):
    return lax.broadcasted_iota(jnp.int32, (experts, tokens), 0)


def by_task(rows, task, experts):
    out = rows[:experts]
    for other in range(1, rows.shape[0] // experts):
        out = jnp.where(task == other, rows[other * experts : (other + 1) * experts], out)
    return out


def to_tasks(rows, task, tasks):
    return jnp.concatenate([jnp.where(task == t, rows, 0.0) for t in range(tasks)], axis=0)


def router_forward(router_rows, normed, task, experts):
    logits = by_task(mm_nt(router_rows, normed, EXACT), task, experts)
    powers = jnp.exp(logits - jnp.max(logits, axis=0, keepdims=True))
    return powers / jnp.sum(powers, axis=0, keepdims=True)


def gate_forward(probs, chosen):
    picked = probs * chosen
    return picked / jnp.sum(picked, axis=0, keepdims=True)


def gate_backward(probs, chosen, grad_gates, grad_probs):
    total = jnp.sum(probs * chosen, axis=0, keepdims=True)
    gates = probs * chosen / total
    inner = chosen / total * (grad_gates - jnp.sum(grad_gates * gates, axis=0, keepdims=True))
    inner = inner + grad_probs
    return probs * (inner - jnp.sum(probs * inner, axis=0, keepdims=True))


def picked_hot(picks, experts):
    rows = expert_rows(experts, picks.shape[1])
    out = jnp.zeros(rows.shape, F32)
    for k in range(picks.shape[0]):
        out = out + (picks[k : k + 1, :] == rows).astype(F32)
    return out


def add_to(ref, index, value, first):
    @pl.when(first)
    def _():
        ref[index] = value

    @pl.when(jnp.logical_not(first))
    def _():
        ref[index] = ref[index] + value


def route_kernel(tid, routes, masks, picks, slots, counts):
    micro = pl.program_id(0)
    _, images, _, tasks, _, patch_count = routes.shape
    experts = slots.shape[1]
    tokens = images * patch_count
    chosen = []
    pixel_rows = [jnp.zeros((1, masks.shape[3]), F32) for _ in range(tasks)]
    for image in range(images):
        task = tid[micro * images + image]
        att, mlp = routes[0, image, 0, 0], routes[0, image, 1, 0]
        for t in range(1, tasks):
            att = jnp.where(task == t, routes[0, image, 0, t], att)
            mlp = jnp.where(task == t, routes[0, image, 1, t], mlp)
        picks[0, :, image * patch_count : (image + 1) * patch_count] = att
        chosen.append(picked_hot(mlp, experts))
        column = jnp.sum(masks[0, image].astype(F32), axis=0, keepdims=True)
        for t in range(tasks):
            pixel_rows[t] = pixel_rows[t] + jnp.where(task == t, column, 0.0)
    chosen = jnp.concatenate(chosen, axis=1)
    earlier = lax.broadcasted_iota(jnp.int32, (tokens, tokens), 0) < lax.broadcasted_iota(
        jnp.int32, (tokens, tokens), 1
    )
    before = mm(chosen.astype(BF16), earlier.astype(F32).astype(BF16))
    slots[0] = jnp.where(chosen > 0.0, before.astype(jnp.int32), NOWHERE)
    counts[0] = jnp.concatenate(pixel_rows, axis=0)


def embed_kernel(micro, tid, patches, patch_w, keyval_w, norms, router, picks, emb, kv, gates, probs):
    experts = gates.shape[0]
    images = pl.num_programs(0)
    task = tid[micro * images + pl.program_id(0)]
    width = router.shape[0] // 2
    embedded = mm(patches[0, 0], patch_w[...])
    emb[...] = embedded
    _, _, normed = norm_forward(embedded, norms[0:1], norms[1:2])
    kv[0] = mm(normed.astype(BF16), keyval_w[...]).astype(BF16)
    prob = router_forward(router[0:width], normed, task, experts)
    probs[...] = prob
    gates[...] = gate_forward(prob, picked_hot(picks[0], experts))


def fill_keys(pieces, kvs, kv_t):
    rows = pieces[0].shape[1]
    for r, piece in enumerate(pieces):
        block = piece[0]
        kvs[r * rows : (r + 1) * rows, :] = block
        kv_t[:, r * rows : (r + 1) * rows] = block.astype(F32).T.astype(BF16)


def attend_kernel(micro, peers, tid, dev, *refs):
    emb = refs[0]
    kv_in = refs[1 : 1 + peers]
    picks, gates_in, slots = refs[1 + peers : 4 + peers]
    weights = refs[4 + peers : 4 + 2 * peers]
    norms, router = refs[4 + 2 * peers : 6 + 2 * peers]
    res_out, sent, mix_out, lse, gates_out, probs_out = refs[6 + 2 * peers : 12 + 2 * peers]
    kvs, kv_t, q_t, mix = refs[12 + 2 * peers :]
    experts, tokens = gates_in.shape
    owned = weights[0].shape[1] // HEAD
    images = pl.num_programs(0)
    task = tid[micro * images + pl.program_id(0)]
    width = router.shape[0] // 2
    mine = dev[0]
    embedded = emb[...]
    _, _, normed = norm_forward(embedded, norms[0:1], norms[1:2])
    low = normed.astype(BF16)
    span = owned * HEAD
    for r in range(peers):
        q_t[r * span : (r + 1) * span, :] = mm_nt(weights[r][0], low).astype(BF16).astype(F32)
    fill_keys(kv_in, kvs, kv_t)
    mix[...] = jnp.zeros(mix.shape, F32)
    blocks = [(r, e, (r * owned + e) * HEAD) for r in range(peers) for e in range(owned)]
    rows = expert_rows(experts, tokens)
    blank = jnp.zeros((HEAD, tokens), BF16)

    def one_pick(k, carry):
        pick = picks[0, pl.ds(k, 1), :]
        query = jnp.zeros((HEAD, tokens), F32)
        for r, e, at in blocks:
            here = pick == (mine ^ r) * owned + e
            query = query + jnp.where(here, q_t[at : at + HEAD, :], 0.0)
        gate = jnp.sum(jnp.where(rows == pick, gates_in[...], 0.0), axis=0, keepdims=True)
        scores = mm(kvs[...], jnp.concatenate([(query * HEAD ** (-0.5)).astype(BF16), blank], axis=0))
        top = jnp.max(scores, axis=0, keepdims=True)
        powers = jnp.exp(scores - top)
        total = jnp.sum(powers, axis=0, keepdims=True)
        lse[pl.ds(k, 1), :] = top + jnp.log(total)
        weighted = (powers * (gate / total)).astype(BF16)
        out = mm(kv_t[HEAD:, :], weighted)
        for r, e, at in blocks:
            here = pick == (mine ^ r) * owned + e
            mix[at : at + HEAD, :] = mix[at : at + HEAD, :] + jnp.where(here, out, 0.0)
        return carry

    lax.fori_loop(0, picks.shape[1], one_pick, 0)
    resid = embedded
    for r in range(peers):
        block = mix[r * span : (r + 1) * span, :].astype(BF16)
        mix_out[0, r * span : (r + 1) * span, :] = block
        resid = resid + mm_tn(block, weights[r][1])
    res_out[...] = resid
    _, _, normed_two = norm_forward(resid, norms[2:3], norms[3:4])
    sent[...] = normed_two.astype(BF16)
    prob = router_forward(router[width:], normed_two, task, experts)
    probs_out[...] = prob
    gates_out[...] = gate_forward(prob, (slots[0] < NOWHERE).astype(F32))


def pick_source(refs, scratch):
    for r, ref in enumerate(refs):

        @pl.when(pl.program_id(0) == r)
        def _(ref=ref):
            scratch[...] = ref[...].reshape(scratch.shape)


def moe_forward_kernel(peers, owned, dev, *refs):
    tokens_in = refs[:peers]
    slots_in = refs[peers : 2 * peers]
    gates_in = refs[2 * peers : 3 * peers]
    weights = refs[3 * peers]
    outs = refs[3 * peers + 1 : 4 * peers + 1]
    kept, tok, slot, gate = refs[4 * peers + 1 :]
    pick_source(tokens_in, tok)
    pick_source(slots_in, slot)
    pick_source(gates_in, gate)
    capacity = kept.shape[2]
    count = tok.shape[0]
    places = lax.broadcasted_iota(jnp.int32, (capacity, count), 0)
    total = jnp.zeros(tok.shape, F32)
    for e in range(owned):
        at = dev[0] * owned + e
        here = slot[pl.ds(at, 1), :] == places
        hot = here.astype(F32).astype(BF16)
        slot_gate = jnp.sum(jnp.where(here, gate[pl.ds(at, 1), :], 0.0), axis=1, keepdims=True)
        arrived = mm(hot, tok[...]).astype(BF16)
        kept[0, e] = arrived
        before = mm(arrived, weights[e, 0])
        bent = jnp.tanh(GELU_C * (before + GELU_A * before * before * before))
        inner = (0.5 * before * (1.0 + bent)).astype(BF16)
        out = (mm_nt(inner, weights[e, 1]) * slot_gate).astype(BF16)
        total = total + mm_tn(hot, out)
    for r, ref in enumerate(outs):

        @pl.when(pl.program_id(0) == r)
        def _(ref=ref):
            ref[...] = total.astype(BF16)


def head_kernel(micro, parts, tid, counts, *refs):
    res = refs[0]
    moe = refs[1 : 1 + parts]
    targets, masks, norms, head_w = refs[1 + parts : 5 + parts]
    slope_out, slope_low, grad_head, grad_norm, squares = refs[5 + parts :]
    images = pl.num_programs(0)
    image = pl.program_id(0)
    task = tid[micro * images + image]
    resid = res[...]
    for part in moe:
        resid = resid + part[...].astype(F32)
    scaled, inverse, normed = norm_forward(resid, norms[4:5], norms[5:6])
    low = normed.astype(BF16)
    pred = mm(low, head_w[...])
    mask = masks[0, 0].astype(F32)
    pixels = mask.shape[1]
    count = jnp.where(task == 0, counts[0], counts[1])
    depth_on = jnp.where(task == 0, 1.0, 0.0)
    normal_on = jnp.where(task == 0, 0.0, 1.0)
    slopes = []
    total = jnp.zeros((1, pixels), F32)
    for group in range(4):
        on = depth_on if group == 0 else normal_on
        at = group * pixels
        gap = pred[:, at : at + pixels] - targets[0, 0, :, at : at + pixels].astype(F32)
        masked = mask * gap
        total = total + on * jnp.sum(masked * gap, axis=0, keepdims=True)
        slopes.append((masked * (2.0 * on / count)).astype(BF16))
    slope = jnp.concatenate(slopes, axis=1)
    squares[0] = jnp.broadcast_to(total, squares.shape[1:])
    first = image == 0
    add_to(grad_head, ..., mm_tn(low, slope), first)
    grad, gain, shift = norm_backward(mm_nt(slope, head_w[...]), scaled, inverse, norms[4:5])
    add_to(grad_norm, slice(0, 1), gain, first)
    add_to(grad_norm, slice(1, 2), shift, first)
    slope_out[...] = grad
    slope_low[...] = grad.astype(BF16)


def moe_backward_kernel(peers, owned, has_prior, dev, *refs):
    tokens_in = refs[:peers]
    slots_in = refs[peers : 2 * peers]
    gates_in = refs[2 * peers : 3 * peers]
    kept, weights = refs[3 * peers : 3 * peers + 2]
    at = 3 * peers + 2
    if has_prior:
        prior = refs[at]
        at += 1
    outs = refs[at : at + peers]
    gate_outs = refs[at + peers : at + 2 * peers]
    grads_out = refs[at + 2 * peers]
    tok, slot, gate = refs[at + 2 * peers + 1 : at + 2 * peers + 4]
    total_grad = refs[at + 2 * peers + 4] if has_prior else grads_out
    source = pl.program_id(0)

    @pl.when(source == 0)
    def _():
        if has_prior:
            total_grad[...] = prior[...]
        else:
            total_grad[...] = jnp.zeros(total_grad.shape, F32)

    pick_source(tokens_in, tok)
    pick_source(slots_in, slot)
    pick_source(gates_in, gate)
    capacity = kept.shape[2]
    count = tok.shape[0]
    places = lax.broadcasted_iota(jnp.int32, (capacity, count), 0)
    total = jnp.zeros(tok.shape, F32)
    gate_rows = []
    for e in range(owned):
        row = dev[0] * owned + e
        here = slot[pl.ds(row, 1), :] == places
        hot = here.astype(F32).astype(BF16)
        slot_gate = jnp.sum(jnp.where(here, gate[pl.ds(row, 1), :], 0.0), axis=1, keepdims=True)
        plain = mm(hot, tok[...])
        arrived = kept[0, e]
        before = mm(arrived, weights[e, 0])
        square = before * before
        bent = jnp.tanh(GELU_C * (before + GELU_A * square * before))
        half = 0.5 * (1.0 + bent)
        bend = half + 0.5 * before * (1.0 - bent * bent) * (GELU_C + 3.0 * GELU_C * GELU_A * square)
        inner = (before * half).astype(BF16)
        hidden = mm(plain.astype(BF16), weights[e, 1])
        gate_slope = jnp.sum(hidden * inner.astype(F32), axis=1, keepdims=True)
        gate_rows.append(jnp.sum(jnp.where(here, gate_slope, 0.0), axis=0, keepdims=True))
        slope = (hidden * bend * slot_gate).astype(BF16)
        total_grad[e, 0] = total_grad[e, 0] + mm_tn(arrived, slope)
        total_grad[e, 1] = total_grad[e, 1] + mm_tn((plain * slot_gate).astype(BF16), inner)
        back = mm_nt(slope, weights[e, 0]).astype(BF16)
        total = total + mm_tn(hot, back)
    gate_block = jnp.concatenate(gate_rows, axis=0)
    for r in range(peers):

        @pl.when(source == r)
        def _(r=r):
            outs[r][...] = total.astype(BF16)
            gate_outs[r][...] = gate_block

    if has_prior:

        @pl.when(source == peers - 1)
        def _():
            grads_out[...] = total_grad[...].astype(grads_out.dtype)


def back_kernel(micro, peers, parts, tid, dev, *refs):
    slope_in = refs[0]
    sent_parts = refs[1 : 1 + parts]
    at = 1 + parts
    res, emb, probs_mlp, slots = refs[at : at + 4]
    gate_parts = refs[at + 4 : at + 4 + peers]
    at += 4 + peers
    grad_tables = refs[at]
    kv_in = refs[at + 1 : at + 1 + peers]
    at += 1 + peers
    picks, gates_in, probs_att, lse = refs[at : at + 4]
    weights = refs[at + 4 : at + 4 + peers]
    at += 4 + peers
    mix_in, norms, router = refs[at : at + 3]
    slope_one, normed_slope = refs[at + 3 : at + 5]
    kv_outs = refs[at + 5 : at + 5 + peers]
    at += 5 + peers
    grad_att, grad_router, grad_norm = refs[at : at + 3]
    kvs, kv_t, q_t, d_t, dkv, dq_t, dgate = refs[at + 3 :]
    experts, tokens = gates_in.shape
    owned = weights[0].shape[1] // HEAD
    images = pl.num_programs(0)
    image = pl.program_id(0)
    first = image == 0
    task = tid[micro * images + image]
    width = router.shape[0] // 2
    tasks = width // experts
    span = owned * HEAD
    mine = dev[0]
    rows = expert_rows(experts, tokens)

    grad_sent = jnp.zeros(slope_in.shape, F32)
    for part in sent_parts:
        grad_sent = grad_sent + part[...].astype(F32)
    grad_gates = jnp.zeros((experts, tokens), F32)
    for r in range(peers):
        for e in range(owned):
            grad_gates = grad_gates + jnp.where(
                rows == (mine ^ r) * owned + e, gate_parts[r][e : e + 1, :], 0.0
            )
    scaled_two, inverse_two, normed_two = norm_forward(res[...], norms[2:3], norms[3:4])
    chosen = (slots[0] < NOWHERE).astype(F32)
    table = grad_tables[1, :, 0:1]
    for t in range(1, tasks):
        table = jnp.where(task == t, grad_tables[1, :, t : t + 1], table)
    logits = to_tasks(gate_backward(probs_mlp[...], chosen, grad_gates, table), task, tasks)
    grad_two = grad_sent + mm_tn(logits, router[width:], EXACT)
    add_to(grad_router, slice(width, 2 * width), mm(logits, normed_two, EXACT), first)
    grad, gain, shift = norm_backward(grad_two, scaled_two, inverse_two, norms[2:3])
    add_to(grad_norm, slice(2, 3), gain, first)
    add_to(grad_norm, slice(3, 4), shift, first)
    resid_slope = slope_in[...] + grad
    slope_one[...] = resid_slope
    branch = resid_slope.astype(BF16)

    _, _, normed = norm_forward(emb[...], norms[0:1], norms[1:2])
    low = normed.astype(BF16)
    for r in range(peers):
        at_r = slice(r * span, (r + 1) * span)
        q_t[at_r, :] = mm_nt(weights[r][0], low).astype(BF16).astype(F32)
        d_t[at_r, :] = mm_nt(weights[r][1], branch).astype(BF16).astype(F32)
        add_to(grad_att, (r, 1), mm(mix_in[0, at_r, :], branch), first)
    fill_keys(kv_in, kvs, kv_t)
    dkv[...] = jnp.zeros(dkv.shape, F32)
    dq_t[...] = jnp.zeros(dq_t.shape, F32)
    dgate[...] = jnp.zeros(dgate.shape, F32)
    blocks = [(r, e, (r * owned + e) * HEAD) for r in range(peers) for e in range(owned)]
    blank = jnp.zeros((HEAD, tokens), BF16)

    def one_pick(k, carry):
        pick = picks[0, pl.ds(k, 1), :]
        query = jnp.zeros((HEAD, tokens), F32)
        down = jnp.zeros((HEAD, tokens), F32)
        for r, e, at in blocks:
            here = pick == (mine ^ r) * owned + e
            query = query + jnp.where(here, q_t[at : at + HEAD, :], 0.0)
            down = down + jnp.where(here, d_t[at : at + HEAD, :], 0.0)
        gate = jnp.sum(jnp.where(rows == pick, gates_in[...], 0.0), axis=0, keepdims=True)
        query_low, down_low = query.astype(BF16), down.astype(BF16)
        scores = mm(kvs[...], jnp.concatenate([(query * HEAD ** (-0.5)).astype(BF16), blank], axis=0))
        probs = jnp.exp(scores - lse[pl.ds(k, 1), :])
        slope = mm(kvs[...], jnp.concatenate([blank, down_low], axis=0))
        delta = jnp.sum(probs * slope, axis=0, keepdims=True)
        gated = probs * gate
        weighted = gated.astype(BF16)
        grad_scores = (gated * (slope - delta) * HEAD ** (-0.5)).astype(BF16)
        joint = jnp.concatenate([grad_scores, weighted], axis=1)
        other = jnp.concatenate(
            [
                jnp.concatenate([query_low, blank], axis=0),
                jnp.concatenate([blank, down_low], axis=0),
            ],
            axis=1,
        )
        dkv[...] = dkv[...] + mm_nt(joint, other)
        dq = mm(kv_t[:HEAD, :], grad_scores)
        for r, e, at in blocks:
            here = pick == (mine ^ r) * owned + e
            dq_t[at : at + HEAD, :] = dq_t[at : at + HEAD, :] + jnp.where(here, dq, 0.0)
        dgate[...] = dgate[...] + jnp.where(rows == pick, delta, 0.0)
        return carry

    lax.fori_loop(0, picks.shape[1], one_pick, 0)
    piece = kv_outs[0].shape[1]
    for r in range(peers):
        kv_outs[r][0] = dkv[r * piece : (r + 1) * piece, :].astype(BF16)

    table = grad_tables[0, :, 0:1]
    for t in range(1, tasks):
        table = jnp.where(task == t, grad_tables[0, :, t : t + 1], table)
    chosen = picked_hot(picks[0], experts)
    logits = to_tasks(gate_backward(probs_att[...], chosen, dgate[...], table), task, tasks)
    grad_one = mm_tn(logits, router[0:width], EXACT)
    add_to(grad_router, slice(0, width), mm(logits, normed, EXACT), first)
    for r in range(peers):
        block = dq_t[r * span : (r + 1) * span, :].astype(BF16)
        grad_one = grad_one + mm_tn(block, weights[r][0])
        add_to(grad_att, (r, 0), mm(block, low), first)
    normed_slope[...] = grad_one


def last_kernel(parts, *refs):
    patches, emb, slope_one, normed_slope = refs[:4]
    kv_parts = refs[4 : 4 + parts]
    keyval_w, norms = refs[4 + parts : 6 + parts]
    grad_patch, grad_keyval, grad_norm = refs[6 + parts :]
    first = pl.program_id(0) == 0
    scaled, inverse, normed = norm_forward(emb[...], norms[0:1], norms[1:2])
    grad_kv = jnp.zeros(kv_parts[0].shape[1:], F32)
    for part in kv_parts:
        grad_kv = grad_kv + part[0].astype(F32)
    grad_kv = grad_kv.astype(BF16)
    add_to(grad_keyval, ..., mm_tn(normed.astype(BF16), grad_kv), first)
    slope = normed_slope[...] + mm_nt(grad_kv, keyval_w[...])
    grad, gain, shift = norm_backward(slope, scaled, inverse, norms[0:1])
    add_to(grad_norm, slice(0, 1), gain, first)
    add_to(grad_norm, slice(1, 2), shift, first)
    add_to(grad_patch, ..., mm_tn(patches[0, 0], (slope_one[...] + grad).astype(BF16)), first)


def whole(array):
    rank = len(array.shape)
    return pl.BlockSpec(array.shape, lambda *_: (0,) * rank, pipeline_mode=pl.Buffered(1))


def kept_out(shape):
    rank = len(shape)
    return pl.BlockSpec(shape, lambda *_: (0,) * rank)


def shape_of(shape, dtype):
    return jax.ShapeDtypeStruct(shape, dtype)


def call(kernel, grid, scalars, inputs, outputs, scratch, cost, name):
    spec = pltpu.PrefetchScalarGridSpec(
        num_scalar_prefetch=len(scalars),
        grid=grid,
        in_specs=[s for _, s in inputs],
        out_specs=[s for _, s in outputs],
        scratch_shapes=scratch,
    )
    return pl.pallas_call(
        kernel,
        grid_spec=spec,
        out_shape=[o for o, _ in outputs],
        cost_estimate=pl.CostEstimate(flops=int(cost[0]), bytes_accessed=int(cost[1]), transcendentals=0),
        name=name,
    )(*scalars, *[a for a, _ in inputs])


def swap(value, axis, mask):
    size = lax.axis_size(axis)
    return lax.ppermute(value, axis, [(i, i ^ mask) for i in range(size)])


def bits_of(axis):
    return [1 << b for b in range(lax.axis_size(axis).bit_length() - 1)]


def gather_pieces(value):
    peers = lax.axis_size("expert")
    base = [value] + [swap(value, "expert", r) for r in range(2, peers, 2)]
    out = []
    for block in base:
        out += [block, swap(block, "expert", 1)]
    return out


def scatter_pieces(pieces):
    peers = len(pieces)
    crossed = [swap(pieces[r], "expert", 1) for r in range(1, peers, 2)]
    parts = [pieces[0], crossed[0]]
    for r in range(2, peers, 2):
        pair = (pieces[r].astype(F32) + crossed[r // 2].astype(F32)).astype(BF16)
        parts.append(swap(pair, "expert", r))
    return parts


def sum_small(value, axes):
    for axis in axes:
        for bit in bits_of(axis):
            value = value + swap(value, axis, bit)
    return value


def pair_sum(left, right):
    return (left.astype(F32) + right.astype(F32)).astype(left.dtype)


def sum_rows(value, axes):
    steps = []
    for axis in axes:
        for bit in bits_of(axis):
            rows = value.shape[0]
            if rows % 32 == 0:
                half = rows // 2
                high = (lax.axis_index(axis) & bit) != 0
                low_half, high_half = value[:half], value[half:]
                keep = jnp.where(high, high_half, low_half)
                send = jnp.where(high, low_half, high_half)
                value = pair_sum(keep, swap(send, axis, bit))
                steps.append((axis, bit, high))
            else:
                value = pair_sum(value, swap(value, axis, bit))
    for axis, bit, high in reversed(steps):
        other = swap(value, axis, bit)
        value = jnp.concatenate(
            [jnp.where(high, other, value), jnp.where(high, value, other)], axis=0
        )
    return value


def mutual(tables):
    grand_total = jnp.sum(tables, axis=(1, 2), keepdims=True)
    joint_share = tables / grand_total
    task_share = jnp.sum(joint_share, axis=2, keepdims=True)
    expert_share = jnp.sum(joint_share, axis=1, keepdims=True)
    return jnp.sum(
        joint_share * (jnp.log(joint_share) - jnp.log(task_share) - jnp.log(expert_share))
    )


def adam_update(weight, first_moment, second, gradient, factor, step_value, rate):
    gradient = gradient * factor
    first_moment = BETA_ONE * first_moment + (1.0 - BETA_ONE) * gradient
    second = BETA_TWO * second + (1.0 - BETA_TWO) * gradient * gradient
    first_hat = first_moment / (1.0 - jnp.power(BETA_ONE, step_value))
    second_hat = second / (1.0 - jnp.power(BETA_TWO, step_value))
    weight = weight - rate * (first_hat / (jnp.sqrt(second_hat) + EPSILON) + DECAY * weight)
    return (weight, first_moment, second)


def local(
    patches,
    routes,
    masks,
    targets,
    task_ids,
    step_count,
    patch_weight,
    patch_moment,
    patch_square,
    keyval_weight,
    keyval_moment,
    keyval_square,
    router_weight,
    router_moment,
    router_square,
    norm_weight,
    norm_moment,
    norm_square,
    head_weight,
    head_moment,
    head_square,
    attention_weight,
    attention_moment,
    attention_square,
    expert_weight,
    expert_moment,
    expert_square,
):
    peers = lax.axis_size("expert")
    micros, images, patch_count, patch_in = patches.shape
    _, _, _, _, tasks, top = routes.shape
    owned = expert_weight.shape[0]
    experts = owned * peers
    model, hidden = expert_weight.shape[2:]
    tokens = images * patch_count
    capacity = max(2, tokens * top // experts)
    pixels = masks.shape[3]
    outputs = targets.shape[3]
    pair_width = 2 * HEAD
    span = owned * HEAD
    keys = peers * patch_count
    head_rows = peers * span
    task_list = task_ids.reshape(-1)
    dev = lax.axis_index("expert").astype(jnp.int32).reshape(1)
    patch_low = patch_weight.astype(BF16)
    keyval_low = keyval_weight.astype(BF16)
    head_low = head_weight.astype(BF16)
    expert_low = expert_weight.astype(BF16)
    router_rows = router_weight.T
    router_count = router_rows.shape[0]
    routes_lanes = jnp.transpose(routes, (0, 1, 3, 4, 5, 2))
    attention_own = jnp.transpose(attention_weight, (0, 2, 1)).astype(BF16)
    attention = gather_pieces(attention_own)

    picks, slots, count_rows = call(
        route_kernel,
        (micros,),
        (task_list,),
        [
            (
                routes_lanes,
                pl.BlockSpec((1,) + routes_lanes.shape[1:], lambda m, *_: (m, 0, 0, 0, 0, 0)),
            ),
            (masks, pl.BlockSpec((1,) + masks.shape[1:], lambda m, *_: (m, 0, 0, 0))),
        ],
        [
            (
                shape_of((micros, top, tokens), jnp.int32),
                pl.BlockSpec((1, top, tokens), lambda m, *_: (m, 0, 0)),
            ),
            (
                shape_of((micros, experts, tokens), jnp.int32),
                pl.BlockSpec((1, experts, tokens), lambda m, *_: (m, 0, 0)),
            ),
            (
                shape_of((micros, tasks, pixels), F32),
                pl.BlockSpec((1, tasks, pixels), lambda m, *_: (m, 0, 0)),
            ),
        ],
        [],
        (micros * tokens * tokens * 32, masks.size * 4),
        "routing",
    )
    slot_pieces = gather_pieces(slots)
    counts = sum_small(jnp.sum(count_rows, axis=(0, 2)), ("expert", "dp"))

    token_block = pl.BlockSpec((patch_count, model), lambda i, *_: (i, 0))
    expert_block = pl.BlockSpec((experts, patch_count), lambda i, *_: (0, i))
    kv_block = pl.BlockSpec((1, patch_count, pair_width), lambda i, *_: (i, 0, 0))

    def micro_block(shape, micro):
        return pl.BlockSpec((1,) + shape, lambda i, *_, m=micro: (m,) + (0,) * (len(shape) - 1) + (i,))

    def image_block(array, micro):
        return pl.BlockSpec((1, 1) + array.shape[2:], lambda i, *_, m=micro: (m, i, 0, 0))

    def micro_whole(array, micro):
        return pl.BlockSpec(
            (1,) + array.shape[1:],
            lambda *_, m=micro: (m,) + (0,) * (len(array.shape) - 1),
            pipeline_mode=pl.Buffered(1),
        )

    state = [dict() for _ in range(micros)]
    for micro, s in enumerate(state):
        s["emb"], kv, s["gates_att"], s["probs_att"] = call(
            partial(embed_kernel, micro),
            (images,),
            (task_list,),
            [
                (patches, image_block(patches, micro)),
                (patch_low, whole(patch_low)),
                (keyval_low, whole(keyval_low)),
                (norm_weight, whole(norm_weight)),
                (router_rows, whole(router_rows)),
                (picks, micro_block((top, patch_count), micro)),
            ],
            [
                (shape_of((tokens, model), F32), token_block),
                (shape_of((images, patch_count, pair_width), BF16), kv_block),
                (shape_of((experts, tokens), F32), expert_block),
                (shape_of((experts, tokens), F32), expert_block),
            ],
            [],
            (2 * tokens * model * (patch_in + pair_width), tokens * (2 * patch_in + 4 * model) + patch_low.size * 2),
            "embedding",
        )
        s["kv"] = gather_pieces(kv)

    attention_flops = 2 * top * tokens * keys * HEAD * 8
    for micro, s in enumerate(state):
        s["res"], s["sent"], s["mix"], s["lse"], s["gates_mlp"], s["probs_mlp"] = call(
            partial(attend_kernel, micro, peers),
            (images,),
            (task_list, dev),
            [(s["emb"], token_block)]
            + [(piece, kv_block) for piece in s["kv"]]
            + [
                (picks, micro_block((top, patch_count), micro)),
                (s["gates_att"], expert_block),
                (slots, micro_block((experts, patch_count), micro)),
            ]
            + [(piece, whole(piece)) for piece in attention]
            + [(norm_weight, whole(norm_weight)), (router_rows, whole(router_rows))],
            [
                (shape_of((tokens, model), F32), token_block),
                (shape_of((tokens, model), BF16), token_block),
                (
                    shape_of((images, head_rows, patch_count), BF16),
                    pl.BlockSpec((1, head_rows, patch_count), lambda i, *_: (i, 0, 0)),
                ),
                (shape_of((top, tokens), F32), pl.BlockSpec((top, patch_count), lambda i, *_: (0, i))),
                (shape_of((experts, tokens), F32), expert_block),
                (shape_of((experts, tokens), F32), expert_block),
            ],
            [
                pltpu.VMEM((keys, pair_width), BF16),
                pltpu.VMEM((pair_width, keys), BF16),
                pltpu.VMEM((head_rows, patch_count), F32),
                pltpu.VMEM((head_rows, patch_count), F32),
            ],
            (attention_flops, tokens * model * 12),
            "attention",
        )
        s["tokens"] = gather_pieces(s["sent"])
        s["gates"] = gather_pieces(s["gates_mlp"])

    tables = jnp.zeros((2, tasks, experts), F32)
    for micro, s in enumerate(state):
        hot = (task_ids[micro][:, None] == jnp.arange(tasks)[None, :]).astype(F32)
        for mixture, probs in enumerate((s["probs_att"], s["probs_mlp"])):
            per_image = jnp.sum(probs.reshape(experts, images, patch_count), axis=2)
            add = jnp.sum(hot[:, :, None] * per_image.T[:, None, :], axis=0)
            tables = tables.at[mixture].add(add)
    tables = sum_small(tables, ("expert", "dp"))
    mutual_value, mutual_pull = jax.vjp(mutual, tables)
    grad_tables = jnp.transpose(mutual_pull(jnp.float32(-MI_WEIGHT))[0], (0, 2, 1))

    moe_flops = 2 * owned * peers * capacity * model * (2 * hidden + 2 * tokens)
    expert_bytes = expert_low.size * 2
    scratch_sources = [
        pltpu.VMEM((tokens, model), BF16),
        pltpu.VMEM((experts, tokens), jnp.int32),
        pltpu.VMEM((experts, tokens), F32),
    ]
    kept_block = pl.BlockSpec((1, owned, capacity, model), lambda r, *_: (r, 0, 0, 0))
    for micro, s in enumerate(state):
        results = call(
            partial(moe_forward_kernel, peers, owned),
            (peers,),
            (dev,),
            [(piece, whole(piece)) for piece in s["tokens"]]
            + [(piece, micro_whole(piece, micro)) for piece in slot_pieces]
            + [(piece, whole(piece)) for piece in s["gates"]]
            + [(expert_low, whole(expert_low))],
            [(shape_of((tokens, model), BF16), kept_out((tokens, model))) for _ in range(peers)]
            + [(shape_of((peers, owned, capacity, model), BF16), kept_block)],
            scratch_sources,
            (moe_flops, expert_bytes + 4 * peers * tokens * model),
            "experts",
        )
        s["kept"] = results[peers]
        s["moe"] = scatter_pieces(results[:peers])

    for micro, s in enumerate(state):
        s["slope"], slope_low, s["grad_head"], s["norm_three"], s["squares"] = call(
            partial(head_kernel, micro, len(s["moe"])),
            (images,),
            (task_list, counts),
            [(s["res"], token_block)]
            + [(part, token_block) for part in s["moe"]]
            + [
                (targets, image_block(targets, micro)),
                (masks, image_block(masks, micro)),
                (norm_weight, whole(norm_weight)),
                (head_low, whole(head_low)),
            ],
            [
                (shape_of((tokens, model), F32), token_block),
                (shape_of((tokens, model), BF16), token_block),
                (shape_of((model, outputs), F32), kept_out((model, outputs))),
                (shape_of((8, model), F32), kept_out((8, model))),
                (
                    shape_of((images, 8, pixels), F32),
                    pl.BlockSpec((1, 8, pixels), lambda i, *_: (i, 0, 0)),
                ),
            ],
            [],
            (6 * tokens * model * outputs, tokens * (outputs * 2 + pixels * 4 + 12 * model)),
            "head",
        )
        s["slopes"] = gather_pieces(slope_low)

    prior = None
    for micro, s in enumerate(state):
        last = micro == micros - 1
        has_prior = prior is not None
        grad_type = BF16 if last and has_prior else F32
        results = call(
            partial(moe_backward_kernel, peers, owned, has_prior),
            (peers,),
            (dev,),
            [(piece, whole(piece)) for piece in s["slopes"]]
            + [(piece, micro_whole(piece, micro)) for piece in slot_pieces]
            + [(piece, whole(piece)) for piece in s["gates"]]
            + [(s["kept"], kept_block), (expert_low, whole(expert_low))]
            + ([(prior, whole(prior))] if has_prior else []),
            [(shape_of((tokens, model), BF16), kept_out((tokens, model))) for _ in range(peers)]
            + [(shape_of((owned, tokens), F32), kept_out((owned, tokens))) for _ in range(peers)]
            + [(shape_of(expert_low.shape, grad_type), kept_out(expert_low.shape))],
            scratch_sources + ([pltpu.VMEM(expert_low.shape, F32)] if has_prior else []),
            (3 * moe_flops, expert_bytes * 5 + 4 * peers * tokens * model),
            "experts_back",
        )
        prior = results[2 * peers]
        s["sent_parts"] = scatter_pieces(results[:peers])
        gate_rows = results[peers : 2 * peers]
        s["gate_parts"] = [gate_rows[0]] + [swap(gate_rows[r], "expert", r) for r in range(1, peers)]
    expert_grad = prior.astype(BF16)

    gate_block = pl.BlockSpec((owned, patch_count), lambda i, *_: (0, i))
    top_block = pl.BlockSpec((top, patch_count), lambda i, *_: (0, i))
    for micro, s in enumerate(state):
        results = call(
            partial(back_kernel, micro, peers, len(s["sent_parts"])),
            (images,),
            (task_list, dev),
            [(s["slope"], token_block)]
            + [(part, token_block) for part in s["sent_parts"]]
            + [
                (s["res"], token_block),
                (s["emb"], token_block),
                (s["probs_mlp"], expert_block),
                (slots, micro_block((experts, patch_count), micro)),
            ]
            + [(part, gate_block) for part in s["gate_parts"]]
            + [(grad_tables, whole(grad_tables))]
            + [(piece, kv_block) for piece in s["kv"]]
            + [
                (picks, micro_block((top, patch_count), micro)),
                (s["gates_att"], expert_block),
                (s["probs_att"], expert_block),
                (s["lse"], top_block),
            ]
            + [(piece, whole(piece)) for piece in attention]
            + [
                (s["mix"], pl.BlockSpec((1, head_rows, patch_count), lambda i, *_: (i, 0, 0))),
                (norm_weight, whole(norm_weight)),
                (router_rows, whole(router_rows)),
            ],
            [
                (shape_of((tokens, model), F32), token_block),
                (shape_of((tokens, model), F32), token_block),
            ]
            + [(shape_of((images, patch_count, pair_width), BF16), kv_block) for _ in range(peers)]
            + [
                (shape_of((peers, 2, span, model), F32), kept_out((peers, 2, span, model))),
                (shape_of((router_count, model), F32), kept_out((router_count, model))),
                (shape_of((8, model), F32), kept_out((8, model))),
            ],
            [
                pltpu.VMEM((keys, pair_width), BF16),
                pltpu.VMEM((pair_width, keys), BF16),
                pltpu.VMEM((head_rows, patch_count), F32),
                pltpu.VMEM((head_rows, patch_count), F32),
                pltpu.VMEM((keys, pair_width), F32),
                pltpu.VMEM((head_rows, patch_count), F32),
                pltpu.VMEM((experts, patch_count), F32),
            ],
            (attention_flops * 3, tokens * model * 30),
            "attention_back",
        )
        s["slope_one"], s["normed_slope"] = results[:2]
        s["kv_parts"] = scatter_pieces(results[2 : 2 + peers])
        s["grad_att"], s["grad_router"], s["norm_two"] = results[2 + peers :]

    for micro, s in enumerate(state):
        s["grad_patch"], s["grad_keyval"], s["norm_one"] = call(
            partial(last_kernel, len(s["kv_parts"])),
            (images,),
            (),
            [
                (patches, image_block(patches, micro)),
                (s["emb"], token_block),
                (s["slope_one"], token_block),
                (s["normed_slope"], token_block),
            ]
            + [(part, kv_block) for part in s["kv_parts"]]
            + [(keyval_low, whole(keyval_low)), (norm_weight, whole(norm_weight))],
            [
                (shape_of((patch_in, model), F32), kept_out((patch_in, model))),
                (shape_of((model, pair_width), F32), kept_out((model, pair_width))),
                (shape_of((8, model), F32), kept_out((8, model))),
            ],
            [],
            (2 * tokens * model * (patch_in + 2 * pair_width), tokens * model * 20),
            "embedding_back",
        )

    def over_micros(name):
        out = state[0][name]
        for s in state[1:]:
            out = out + s[name]
        return out

    both = ("expert", "dp")
    grad_head = sum_rows(over_micros("grad_head").astype(BF16), both).astype(F32)
    grad_keyval = sum_rows(over_micros("grad_keyval").astype(BF16), both).astype(F32)
    grad_patch = sum_rows(over_micros("grad_patch").astype(BF16), both).astype(F32)
    norm_rows = jnp.concatenate(
        [
            over_micros("norm_one")[0:2],
            over_micros("norm_two")[2:4],
            over_micros("norm_three")[0:2],
        ],
        axis=0,
    )
    small = jnp.concatenate([over_micros("grad_router"), norm_rows], axis=0)
    small = sum_small(small, both)
    grad_router = small[:router_count].T
    grad_norms = small[router_count:]
    attention_sum = over_micros("grad_att").astype(BF16).reshape(peers, 2 * span, model)
    attention_parts = scatter_pieces([attention_sum[r] for r in range(peers)])
    attention_part = sum(part.astype(F32) for part in attention_parts).astype(BF16)
    attention_part = sum_rows(attention_part, ("dp",)).astype(F32).reshape(2, span, model)
    grad_attention = jnp.transpose(attention_part, (0, 2, 1))
    grad_expert = jnp.stack(
        [
            jnp.stack([sum_rows(expert_grad[e, w], ("dp",)) for w in range(2)], axis=0)
            for e in range(owned)
        ],
        axis=0,
    ).astype(F32)

    image_squares = jnp.stack([jnp.sum(s["squares"][:, 0, :], axis=1) for s in state], axis=0)
    image_hot = (task_ids[:, :, None] == jnp.arange(tasks)[None, None, :]).astype(F32)
    square_all = sum_small(jnp.sum(image_hot * image_squares[:, :, None], axis=(0, 1)), both)
    loss = jnp.sum(square_all / counts) - MI_WEIGHT * mutual_value

    dense_list = (grad_patch, grad_keyval, grad_router, grad_norms, grad_head)
    dense_sq = jnp.float32(0.0)
    for gradient in dense_list:
        dense_sq = dense_sq + jnp.sum(gradient * gradient)
    shard_sq = sum_small(
        (jnp.sum(grad_attention * grad_attention) + jnp.sum(grad_expert * grad_expert)).reshape(1),
        ("expert",),
    )[0]
    grad_norm = jnp.sqrt(dense_sq + shard_sq)
    expert_norm = jnp.sqrt(shard_sq)
    total_params = (
        patch_weight.size
        + keyval_weight.size
        + router_weight.size
        + norm_weight.size
        + head_weight.size
        + (attention_weight.size + expert_weight.size) * peers
    )
    factor = jnp.minimum(1.0, CLIP_UNIT * math.sqrt(total_params) / grad_norm)
    step_value = step_count[0].astype(F32)
    weights = (
        patch_weight,
        keyval_weight,
        router_weight,
        norm_weight,
        head_weight,
        attention_weight,
        expert_weight,
    )
    moments = (
        patch_moment,
        keyval_moment,
        router_moment,
        norm_moment,
        head_moment,
        attention_moment,
        expert_moment,
    )
    squares = (
        patch_square,
        keyval_square,
        router_square,
        norm_square,
        head_square,
        attention_square,
        expert_square,
    )
    all_grads = dense_list + (grad_attention, grad_expert)
    results = [loss, grad_norm, expert_norm]
    for index in range(len(weights)):
        results.extend(
            adam_update(
                weights[index],
                moments[index],
                squares[index],
                all_grads[index],
                factor,
                step_value,
                RATES[index],
            )
        )
    return tuple(results)


def solution(mesh):
    tokens = P(None, "dp", "expert", None)
    by_columns = P(None, None, "expert")
    by_expert = P("expert", None, None, None)
    same = P()
    placed = (
        (tokens, P(None, "dp", "expert", None, None, None), tokens, tokens, P(None, "dp"), same)
        + (same,) * 15
        + (by_columns,) * 3
        + (by_expert,) * 3
    )
    return jax.shard_map(
        local,
        mesh=mesh,
        in_specs=placed,
        out_specs=(same,) * 18 + (by_columns,) * 3 + (by_expert,) * 3,
        check_vma=False,
    )
```

```python
from functools import partial
import math

import jax
import jax.numpy as jnp
from jax import lax
from jax.experimental import pallas as pl
from jax.experimental.pallas import tpu as pltpu
from jax.sharding import PartitionSpec as P

HEAD = 64
NORM_EPS = 1e-06
MI_WEIGHT = 0.5
CLIP_UNIT = 3e-07
BETA_ONE = 0.9
BETA_TWO = 0.999
EPSILON = 1e-08
RATES = (0.02, 0.02, 0.02, 0.3, 0.02, 1.2, 0.02)
DECAY = 0.05
F32 = jnp.float32
BF16 = jnp.bfloat16
EXACT = lax.Precision.HIGHEST
NOWHERE = 1 << 20
LANES = 128
GELU_A = 0.044715
GELU_C = math.sqrt(2.0 / math.pi)


def mm(left, right, precision=None):
    return lax.dot_general(
        left, right, (((1,), (0,)), ((), ())), precision=precision, preferred_element_type=F32
    )


def mm_nt(left, right, precision=None):
    return lax.dot_general(
        left, right, (((1,), (1,)), ((), ())), precision=precision, preferred_element_type=F32
    )


def mm_tn(left, right, precision=None):
    return lax.dot_general(
        left, right, (((0,), (0,)), ((), ())), precision=precision, preferred_element_type=F32
    )


def norm_forward(values, gain, shift):
    centred = values - jnp.mean(values, axis=-1, keepdims=True)
    inverse = lax.rsqrt(jnp.mean(centred * centred, axis=-1, keepdims=True) + NORM_EPS)
    scaled = centred * inverse
    return scaled, inverse, scaled * gain + shift


def norm_backward(slope, scaled, inverse, gain):
    inner = slope * gain
    grad = inverse * (
        inner
        - jnp.mean(inner, axis=-1, keepdims=True)
        - scaled * jnp.mean(inner * scaled, axis=-1, keepdims=True)
    )
    return grad, jnp.sum(slope * scaled, axis=0, keepdims=True), jnp.sum(slope, axis=0, keepdims=True)


def expert_rows(experts, tokens):
    return lax.broadcasted_iota(jnp.int32, (experts, tokens), 0)


def by_task(rows, task, experts):
    out = rows[:experts]
    for other in range(1, rows.shape[0] // experts):
        out = jnp.where(task == other, rows[other * experts : (other + 1) * experts], out)
    return out


def to_tasks(rows, task, tasks):
    return jnp.concatenate([jnp.where(task == t, rows, 0.0) for t in range(tasks)], axis=0)


def router_forward(router_rows, normed, task, experts):
    logits = by_task(mm_nt(router_rows, normed, EXACT), task, experts)
    powers = jnp.exp(logits - jnp.max(logits, axis=0, keepdims=True))
    return powers / jnp.sum(powers, axis=0, keepdims=True)


def gate_forward(probs, chosen):
    picked = probs * chosen
    return picked / jnp.sum(picked, axis=0, keepdims=True)


def gate_backward(probs, chosen, grad_gates, grad_probs):
    total = jnp.sum(probs * chosen, axis=0, keepdims=True)
    gates = probs * chosen / total
    inner = chosen / total * (grad_gates - jnp.sum(grad_gates * gates, axis=0, keepdims=True))
    inner = inner + grad_probs
    return probs * (inner - jnp.sum(probs * inner, axis=0, keepdims=True))


def picked_hot(picks, experts):
    rows = expert_rows(experts, picks.shape[1])
    out = jnp.zeros(rows.shape, F32)
    for k in range(picks.shape[0]):
        out = out + (picks[k : k + 1, :] == rows).astype(F32)
    return out


def add_to(ref, index, value, first):
    @pl.when(first)
    def _():
        ref[index] = value

    @pl.when(jnp.logical_not(first))
    def _():
        ref[index] = ref[index] + value


def route_kernel(tid, routes, masks, picks, slots, counts):
    micro = pl.program_id(0)
    _, images, _, tasks, _, patch_count = routes.shape
    experts = slots.shape[1]
    tokens = images * patch_count
    chosen = []
    pixel_rows = [jnp.zeros((1, masks.shape[3]), F32) for _ in range(tasks)]
    for image in range(images):
        task = tid[micro, image]
        att, mlp = routes[0, image, 0, 0], routes[0, image, 1, 0]
        for t in range(1, tasks):
            att = jnp.where(task == t, routes[0, image, 0, t], att)
            mlp = jnp.where(task == t, routes[0, image, 1, t], mlp)
        picks[0, :, image * patch_count : (image + 1) * patch_count] = att
        chosen.append(picked_hot(mlp, experts))
        column = jnp.sum(masks[0, image].astype(F32), axis=0, keepdims=True)
        for t in range(tasks):
            pixel_rows[t] = pixel_rows[t] + jnp.where(task == t, column, 0.0)
    chosen = jnp.concatenate(chosen, axis=1)
    earlier = lax.broadcasted_iota(jnp.int32, (tokens, tokens), 0) < lax.broadcasted_iota(
        jnp.int32, (tokens, tokens), 1
    )
    before = mm(chosen.astype(BF16), earlier.astype(F32).astype(BF16))
    slots[0] = jnp.where(chosen > 0.0, before.astype(jnp.int32), NOWHERE)
    counts[0] = jnp.concatenate(pixel_rows, axis=0)


def embed_kernel(micro, tid, patches, patch_w, keyval_w, norms, router, picks, emb, kv, gates, probs):
    experts = gates.shape[0]
    task = tid[micro, pl.program_id(0)]
    width = router.shape[0] // 2
    embedded = mm(patches[0, 0], patch_w[...].astype(BF16))
    emb[...] = embedded
    _, _, normed = norm_forward(embedded, norms[0:1], norms[1:2])
    kv[...] = mm(normed.astype(BF16), keyval_w[...].astype(BF16)).astype(BF16)
    prob = router_forward(router[0:width], normed, task, experts)
    probs[...] = prob
    gates[...] = gate_forward(prob, picked_hot(picks[0], experts))


def split_planes(values):
    high = values.astype(BF16).astype(F32)
    middle = (values - high).astype(BF16).astype(F32)
    return [high, middle, (values - high - middle).astype(BF16).astype(F32)]


def put_planes(ref, planes, image, token_rows, images):
    patch_count, model = token_rows.shape
    block = jnp.concatenate(planes, axis=0).astype(BF16)
    height = block.shape[0]
    columns, chunks = model // LANES, patch_count // LANES
    rows, base = ref.shape[0], images * patch_count
    for i in range(images):

        @pl.when(image == i)
        def _(i=i):
            ref[i * patch_count : (i + 1) * patch_count, :] = token_rows
            if i == 0:
                ref[base:, :] = jnp.zeros((rows - base, model), BF16)
            for j in range(chunks):
                c = i * chunks + j
                top, left = base + c // columns * height, c % columns * LANES
                ref[top : top + height, left : left + LANES] = block[:, j * LANES : (j + 1) * LANES]


def lanes_of(shape):
    return lax.broadcasted_iota(jnp.int32, shape, 1)


def put_statistics(ref, images, patch_count, values):
    high, middle, rest = split_planes(values)
    block = high + pltpu.roll(middle, 8, 1) + pltpu.roll(rest, 16, 1)
    ref[ref.shape[0] - values.shape[0] :, ref.shape[1] - LANES :] = block.astype(BF16)


def get_statistics(block):
    block = block.astype(F32)
    total = block + pltpu.roll(block, LANES - 8, 1) + pltpu.roll(block, LANES - 16, 1)
    return jnp.where(lanes_of(block.shape) < 8, total, 0.0)


def extra_rows(count, experts, model):
    return -(-(count // LANES) // (model // LANES)) * 4 * experts


def get_planes(block, count, experts, columns):
    height = 4 * experts
    out = []
    for c in range(count // LANES):
        top, left = c // columns * height, c % columns * LANES
        out.append(block[top : top + height, left : left + LANES].astype(F32))
    return out


def three_sum(planes, experts):
    return planes[:experts] + planes[experts : 2 * experts] + planes[2 * experts : 3 * experts]


def fill_keys(pieces, kvs, kv_t):
    rows = pieces[0].shape[0]
    for r, piece in enumerate(pieces):
        block = piece[...]
        kvs[r * rows : (r + 1) * rows, :] = block
        kv_t[:, r * rows : (r + 1) * rows] = block.astype(F32).T.astype(BF16)


def attend_kernel(micro, peers, capacity, images, tid, dev, *refs):
    emb = refs[0]
    kv_in = refs[1 : 1 + peers]
    picks, gates_in, slots = refs[1 + peers : 4 + peers]
    weights = refs[4 + peers : 4 + 2 * peers]
    norms, router = refs[4 + 2 * peers : 6 + 2 * peers]
    probs_att, counts = refs[6 + 2 * peers : 8 + 2 * peers]
    res_out, sent, mix_out, lse, probs_out = refs[8 + 2 * peers : 13 + 2 * peers]
    table, kvs, kv_t, q_t, mix = refs[13 + 2 * peers :]
    experts, tokens = gates_in.shape
    owned = weights[0].shape[1] // HEAD
    task = tid[micro, pl.program_id(0)]
    width = router.shape[0] // 2
    mine = dev[0]
    embedded = emb[...]
    _, _, normed = norm_forward(embedded, norms[0:1], norms[1:2])
    low = normed.astype(BF16)
    span = owned * HEAD
    for r in range(peers):
        q_t[r * span : (r + 1) * span, :] = mm_nt(weights[r][0], low).astype(BF16).astype(F32)
    fill_keys(kv_in, kvs, kv_t)
    mix[...] = jnp.zeros(mix.shape, F32)
    blocks = [(r, e, (r * owned + e) * HEAD) for r in range(peers) for e in range(owned)]
    rows = expert_rows(experts, tokens)
    blank = jnp.zeros((HEAD, tokens), BF16)

    def one_pick(k, carry):
        pick = picks[0, pl.ds(k, 1), :]
        query = jnp.zeros((HEAD, tokens), F32)
        for r, e, at in blocks:
            here = pick == (mine ^ r) * owned + e
            query = query + jnp.where(here, q_t[at : at + HEAD, :], 0.0)
        gate = jnp.sum(jnp.where(rows == pick, gates_in[...], 0.0), axis=0, keepdims=True)
        scores = mm(kvs[...], jnp.concatenate([(query * HEAD ** (-0.5)).astype(BF16), blank], axis=0))
        top = jnp.max(scores, axis=0, keepdims=True)
        powers = jnp.exp(scores - top)
        total = jnp.sum(powers, axis=0, keepdims=True)
        lse[pl.ds(k, 1), :] = top + jnp.log(total)
        weighted = (powers * (gate / total)).astype(BF16)
        out = mm(kv_t[HEAD:, :], weighted)
        for r, e, at in blocks:
            here = pick == (mine ^ r) * owned + e
            mix[at : at + HEAD, :] = mix[at : at + HEAD, :] + jnp.where(here, out, 0.0)
        return carry

    lax.fori_loop(0, picks.shape[1], one_pick, 0)
    resid = embedded
    for r in range(peers):
        block = mix[r * span : (r + 1) * span, :].astype(BF16)
        mix_out[0, r * span : (r + 1) * span, :] = block
        resid = resid + mm_tn(block, weights[r][1])
    res_out[...] = resid
    _, _, normed_two = norm_forward(resid, norms[2:3], norms[3:4])
    prob = router_forward(router[width:], normed_two, task, experts)
    probs_out[...] = prob
    both = jnp.concatenate([probs_att[...], prob], axis=0)
    lane = lanes_of((2 * experts, LANES))
    per_task = jnp.where(lane == task, jnp.sum(both, axis=1, keepdims=True), 0.0)
    add_to(table, ..., per_task, pl.program_id(0) == 0)
    slot = slots[0]
    gates = gate_forward(prob, (slot < NOWHERE).astype(F32))
    places = jnp.minimum(slot, capacity).astype(F32)
    low_two = normed_two.astype(BF16)
    put_planes(sent, split_planes(gates) + [places], pl.program_id(0), low_two, images)

    @pl.when(pl.program_id(0) == images - 1)
    def _():
        rest = jnp.zeros((2 * experts - 8, LANES), F32)
        block = jnp.concatenate([table[...], counts[...], rest], axis=0)
        put_statistics(sent, images, tokens, block)


def pick_source(blocks, scratch):
    for r, read in enumerate(blocks):

        @pl.when(pl.program_id(0) == r)
        def _(read=read):
            scratch[...] = read()


def read_planes(block, slot, gate):
    experts, count = slot.shape
    for c, planes in enumerate(get_planes(block, count, experts, block.shape[1] // LANES)):
        at = slice(c * LANES, (c + 1) * LANES)
        gate[:, at] = three_sum(planes, experts)
        slot[:, at] = planes[3 * experts :]


def put_piece(outs, value):
    for r, out in enumerate(outs):

        @pl.when(pl.program_id(0) == r)
        def _(out=out):
            out[...] = value


def put_halves(odd, evens, value):
    for r in range(2 * len(evens)):

        @pl.when(pl.program_id(0) == r)
        def _(r=r):
            if r % 2:
                odd[r // 2] = value
            else:
                evens[r // 2][...] = value


def moe_forward_kernel(peers, owned, dev, *refs):
    arrays = refs[:peers]
    weights = refs[peers]
    half = peers // 2
    odd = refs[peers + 1]
    evens = refs[peers + 2 : peers + 2 + half]
    kept, statistics, tok, slot, gate = refs[peers + 2 + half :]
    pick_source([lambda a=a: a[...] for a in arrays], tok)
    count = slot.shape[1]
    read_planes(tok[count:, :], slot, gate)
    rows = statistics.shape[0]
    block = get_statistics(tok[tok.shape[0] - rows :, tok.shape[1] - LANES :])
    add_to(statistics, ..., block, pl.program_id(0) == 0)
    capacity = kept.shape[2]
    places = lax.broadcasted_iota(jnp.int32, (capacity, count), 0).astype(F32)
    total = jnp.zeros((count, tok.shape[1]), F32)
    for e in range(owned):
        at = dev[0] * owned + e
        here = slot[pl.ds(at, 1), :] == places
        hot = here.astype(F32).astype(BF16)
        slot_gate = jnp.sum(jnp.where(here, gate[pl.ds(at, 1), :], 0.0), axis=1, keepdims=True)
        arrived = mm(hot, tok[:count, :]).astype(BF16)
        kept[0, e] = arrived
        before = mm(arrived, weights[e, 0])
        bent = jnp.tanh(GELU_C * (before + GELU_A * before * before * before))
        inner = (0.5 * before * (1.0 + bent)).astype(BF16)
        out = (mm_nt(inner, weights[e, 1]) * slot_gate).astype(BF16)
        total = total + mm_tn(hot, out)
    put_halves(odd, evens, total.astype(BF16))


def head_kernel(micro, parts, count_row, tid, *refs):
    res = refs[0]
    moe = refs[1 : 1 + parts]
    targets, masks, norms, head_w, counts = refs[1 + parts : 6 + parts]
    slope_out, slope_low, grad_head, grad_norm, squares = refs[6 + parts :]
    image = pl.program_id(0)
    task = tid[micro, image]
    resid = res[...]
    for part in moe:
        resid = resid + part[...].astype(F32)
    scaled, inverse, normed = norm_forward(resid, norms[4:5], norms[5:6])
    low = normed.astype(BF16)
    head_low = head_w[...].astype(BF16)
    pred = mm(low, head_low)
    mask = masks[0, 0].astype(F32)
    pixels = mask.shape[1]
    count_rows = counts[count_row : count_row + 1, :]
    count = jnp.sum(jnp.where(lanes_of((1, LANES)) == task, count_rows, 0.0), axis=1, keepdims=True)
    depth_on = jnp.where(task == 0, 1.0, 0.0)
    normal_on = jnp.where(task == 0, 0.0, 1.0)
    slopes = []
    total = jnp.zeros((1, pixels), F32)
    for group in range(4):
        on = depth_on if group == 0 else normal_on
        at = group * pixels
        gap = pred[:, at : at + pixels] - targets[0, 0, :, at : at + pixels].astype(F32)
        masked = mask * gap
        total = total + on * jnp.sum(masked * gap, axis=0, keepdims=True)
        slopes.append((masked * (2.0 * on / count)).astype(BF16))
    slope = jnp.concatenate(slopes, axis=1)
    first = image == 0
    spots = lax.broadcasted_iota(jnp.int32, (8, LANES), 0) * LANES + lanes_of((8, LANES))
    add_to(squares, ..., jnp.where(spots == task, jnp.sum(total, axis=1, keepdims=True), 0.0), first)
    add_to(grad_head, ..., mm_tn(slope, low), first)
    grad, gain, shift = norm_backward(mm_nt(slope, head_low), scaled, inverse, norms[4:5])
    add_to(grad_norm, slice(0, 1), gain, first)
    add_to(grad_norm, slice(1, 2), shift, first)
    slope_out[...] = grad
    slope_low[...] = grad.astype(BF16)


def moe_backward_kernel(peers, local_expert, owned, more_grads, more_tokens, split, dev, place, *refs):
    refs = list(refs)

    def take(count):
        out = refs[:count]
        del refs[:count]
        return out

    slopes, extras = take(peers), take(peers)
    kept, weights = take(2)
    if more_grads:
        (prior_grads,) = take(1)
    if more_tokens:
        prior_pieces = take(peers)
    outs = take(peers)
    grads_out = take(2 if split else 1)
    tok, extra, slot, gate, prior = take(5)
    grads = take(1)[0] if split else grads_out[0]
    source = pl.program_id(0)

    @pl.when(source == 0)
    def _():
        if more_grads:
            grads[...] = prior_grads[...]
        else:
            grads[...] = jnp.zeros(grads.shape, F32)

    pick_source([lambda a=a: a[...] for a in slopes], tok)
    pick_source([lambda a=a: a[...] for a in extras], extra)
    if more_tokens:
        pick_source([lambda a=a: a[...] for a in prior_pieces], prior)
    read_planes(extra[...], slot, gate)
    experts, count = slot.shape
    model = tok.shape[1]
    capacity = kept.shape[2]
    places = lax.broadcasted_iota(jnp.int32, (capacity, count), 0).astype(F32)
    row = dev[0] * owned + local_expert
    here = slot[pl.ds(row, 1), :] == places
    hot = here.astype(F32).astype(BF16)
    slot_gate = jnp.sum(jnp.where(here, gate[pl.ds(row, 1), :], 0.0), axis=1, keepdims=True)
    plain = mm(hot, tok[...])
    arrived = kept[0, 0]
    before = mm(arrived, weights[0, 0])
    square = before * before
    bent = jnp.tanh(GELU_C * (before + GELU_A * square * before))
    middle = 0.5 * (1.0 + bent)
    bend = middle + 0.5 * before * (1.0 - bent * bent) * (GELU_C + 3.0 * GELU_C * GELU_A * square)
    inner = (before * middle).astype(BF16)
    hidden = mm(plain.astype(BF16), weights[0, 1])
    gate_slope = jnp.sum(hidden * inner.astype(F32), axis=1, keepdims=True)
    gate_row = jnp.sum(jnp.where(here, gate_slope, 0.0), axis=0, keepdims=True)
    slope = (hidden * bend * slot_gate).astype(BF16)
    grads[0] = grads[0] + mm_tn(arrived, slope)
    grads[1] = grads[1] + mm_tn((plain * slot_gate).astype(BF16), inner)
    back = mm_nt(slope, weights[0, 0]).astype(BF16)
    tokens_back = mm_tn(hot, back)
    rows = expert_rows(experts, count)
    gate_planes = split_planes(jnp.where(rows == row, gate_row, 0.0))
    block = jnp.concatenate(gate_planes + [jnp.zeros((experts, count), F32)], axis=0)
    columns = model // LANES
    height = 4 * experts
    chunks = count // LANES
    lines = []
    for line in range(-(-chunks // columns)):
        cells = [
            block[:, c * LANES : (c + 1) * LANES] if c < chunks else jnp.zeros((height, LANES), F32)
            for c in range(line * columns, (line + 1) * columns)
        ]
        lines.append(jnp.concatenate(cells, axis=1))
    whole_piece = jnp.concatenate([tokens_back] + lines, axis=0)
    if more_tokens:
        whole_piece = whole_piece + prior[...].astype(F32)
    put_piece(outs, whole_piece.astype(BF16))

    if split:

        @pl.when(source == peers - 1)
        def _():
            grads_out[0][...] = grads[place[0]].astype(BF16)
            grads_out[1][...] = grads[1 - place[0]].astype(BF16)


def table_slope(table, task, tasks):
    lane = lanes_of(table.shape)
    valid = lane < tasks
    table = jnp.where(valid, table, 0.0)
    total = jnp.sum(jnp.sum(table, axis=1, keepdims=True), axis=0, keepdims=True)
    share = table / total
    by_expert = jnp.sum(share, axis=1, keepdims=True)
    by_task_sum = jnp.sum(share, axis=0, keepdims=True)
    safe = jnp.where(valid, share, 1.0)
    gain = jnp.log(safe) - jnp.log(jnp.where(valid, by_task_sum, 1.0)) - jnp.log(by_expert)
    gain = jnp.where(valid, gain, 0.0)
    mean = jnp.sum(jnp.sum(gain * share, axis=1, keepdims=True), axis=0, keepdims=True)
    slope = -MI_WEIGHT * (gain - mean) / total
    return jnp.sum(jnp.where(lane == task, slope, 0.0), axis=1, keepdims=True), mean


def back_kernel(micro, peers, parts, image_count, tid, dev, *refs):
    slope_in = refs[0]
    sent_parts = refs[1 : 1 + parts]
    gate_parts = refs[1 + parts : 1 + 2 * parts]
    at = 1 + 2 * parts
    res, emb, probs_mlp, slots = refs[at : at + 4]
    at += 4
    tables = refs[at]
    kv_in = refs[at + 1 : at + 1 + peers]
    at += 1 + peers
    picks, gates_in, probs_att, lse = refs[at : at + 4]
    weights = refs[at + 4 : at + 4 + peers]
    at += 4 + peers
    mix_in, norms, router = refs[at : at + 3]
    slope_one, normed_slope = refs[at + 3 : at + 5]
    kv_outs = refs[at + 5 : at + 5 + peers]
    at += 5 + peers
    grad_att, grad_router, grad_norm, mutual = refs[at : at + 4]
    kvs, kv_t, q_t, d_t, dkv, dq_t, dgate = refs[at + 4 :]
    experts, tokens = gates_in.shape
    owned = weights[0].shape[1] // HEAD
    image = pl.program_id(0)
    first = image == 0
    task = tid[micro, image]
    width = router.shape[0] // 2
    tasks = width // experts
    span = owned * HEAD
    mine = dev[0]
    rows = expert_rows(experts, tokens)

    grad_sent = jnp.zeros(slope_in.shape, F32)
    for part in sent_parts:
        grad_sent = grad_sent + part[...].astype(F32)
    planes = gate_parts[0][...].astype(F32)
    for part in gate_parts[1:]:
        planes = planes + part[...].astype(F32)
    columns = planes.shape[1] // LANES
    chunks = get_planes(planes, image_count * tokens, experts, columns)
    per = tokens // LANES
    grad_gates = jnp.zeros((experts, tokens), F32)
    for i in range(image_count):
        cells = [three_sum(c, experts) for c in chunks[i * per : (i + 1) * per]]
        grad_gates = jnp.where(image == i, jnp.concatenate(cells, axis=1), grad_gates)
    scaled_two, inverse_two, normed_two = norm_forward(res[...], norms[2:3], norms[3:4])
    chosen = (slots[0] < NOWHERE).astype(F32)
    table, gain_mlp = table_slope(tables[experts : 2 * experts, :], task, tasks)
    logits = to_tasks(gate_backward(probs_mlp[...], chosen, grad_gates, table), task, tasks)
    grad_two = grad_sent + mm_tn(logits, router[width:], EXACT)
    add_to(grad_router, slice(width, 2 * width), mm(logits, normed_two, EXACT), first)
    grad, gain, shift = norm_backward(grad_two, scaled_two, inverse_two, norms[2:3])
    add_to(grad_norm, slice(2, 3), gain, first)
    add_to(grad_norm, slice(3, 4), shift, first)
    resid_slope = slope_in[...] + grad
    slope_one[...] = resid_slope
    branch = resid_slope.astype(BF16)

    _, _, normed = norm_forward(emb[...], norms[0:1], norms[1:2])
    low = normed.astype(BF16)
    for r in range(peers):
        at_r = slice(r * span, (r + 1) * span)
        q_t[at_r, :] = mm_nt(weights[r][0], low).astype(BF16).astype(F32)
        d_t[at_r, :] = mm_nt(weights[r][1], branch).astype(BF16).astype(F32)
        add_to(grad_att, (r, 1), mm(mix_in[0, at_r, :], branch), first)
    fill_keys(kv_in, kvs, kv_t)
    dkv[...] = jnp.zeros(dkv.shape, F32)
    dq_t[...] = jnp.zeros(dq_t.shape, F32)
    dgate[...] = jnp.zeros(dgate.shape, F32)
    blocks = [(r, e, (r * owned + e) * HEAD) for r in range(peers) for e in range(owned)]
    blank = jnp.zeros((HEAD, tokens), BF16)

    def one_pick(k, carry):
        pick = picks[0, pl.ds(k, 1), :]
        query = jnp.zeros((HEAD, tokens), F32)
        down = jnp.zeros((HEAD, tokens), F32)
        for r, e, at in blocks:
            here = pick == (mine ^ r) * owned + e
            query = query + jnp.where(here, q_t[at : at + HEAD, :], 0.0)
            down = down + jnp.where(here, d_t[at : at + HEAD, :], 0.0)
        gate = jnp.sum(jnp.where(rows == pick, gates_in[...], 0.0), axis=0, keepdims=True)
        query_low, down_low = query.astype(BF16), down.astype(BF16)
        scores = mm(kvs[...], jnp.concatenate([(query * HEAD ** (-0.5)).astype(BF16), blank], axis=0))
        probs = jnp.exp(scores - lse[pl.ds(k, 1), :])
        slope = mm(kvs[...], jnp.concatenate([blank, down_low], axis=0))
        delta = jnp.sum(probs * slope, axis=0, keepdims=True)
        gated = probs * gate
        weighted = gated.astype(BF16)
        grad_scores = (gated * (slope - delta) * HEAD ** (-0.5)).astype(BF16)
        joint = jnp.concatenate([grad_scores, weighted], axis=1)
        other = jnp.concatenate(
            [
                jnp.concatenate([query_low, blank], axis=0),
                jnp.concatenate([blank, down_low], axis=0),
            ],
            axis=1,
        )
        dkv[...] = dkv[...] + mm_nt(joint, other)
        dq = mm(kv_t[:HEAD, :], grad_scores)
        for r, e, at in blocks:
            here = pick == (mine ^ r) * owned + e
            dq_t[at : at + HEAD, :] = dq_t[at : at + HEAD, :] + jnp.where(here, dq, 0.0)
        dgate[...] = dgate[...] + jnp.where(rows == pick, delta, 0.0)
        return carry

    lax.fori_loop(0, picks.shape[1], one_pick, 0)
    for r in range(peers):
        block = dkv[r * tokens : (r + 1) * tokens, :].astype(BF16)
        kv_outs[r][...] = block

    table, gain_att = table_slope(tables[:experts, :], task, tasks)
    mutual[...] = jnp.broadcast_to(gain_att + gain_mlp, mutual.shape)
    chosen = picked_hot(picks[0], experts)
    logits = to_tasks(gate_backward(probs_att[...], chosen, dgate[...], table), task, tasks)
    grad_one = mm_tn(logits, router[0:width], EXACT)
    add_to(grad_router, slice(0, width), mm(logits, normed, EXACT), first)
    for r in range(peers):
        block = dq_t[r * span : (r + 1) * span, :].astype(BF16)
        grad_one = grad_one + mm_tn(block, weights[r][0])
        add_to(grad_att, (r, 0), mm(block, low), first)
    normed_slope[...] = grad_one


def last_kernel(parts, *refs):
    patches, emb, slope_one, normed_slope = refs[:4]
    kv_parts = refs[4 : 4 + parts]
    keyval_w, norms = refs[4 + parts : 6 + parts]
    grad_patch, grad_keyval, grad_norm = refs[6 + parts :]
    first = pl.program_id(0) == 0
    scaled, inverse, normed = norm_forward(emb[...], norms[0:1], norms[1:2])
    grad_kv = jnp.zeros(kv_parts[0].shape, F32)
    for part in kv_parts:
        grad_kv = grad_kv + part[...].astype(F32)
    grad_kv = grad_kv.astype(BF16)
    add_to(grad_keyval, ..., mm_tn(grad_kv, normed.astype(BF16)), first)
    slope = normed_slope[...] + mm_nt(grad_kv, keyval_w[...].astype(BF16))
    grad, gain, shift = norm_backward(slope, scaled, inverse, norms[0:1])
    add_to(grad_norm, slice(0, 1), gain, first)
    add_to(grad_norm, slice(1, 2), shift, first)
    add_to(grad_patch, ..., mm_tn(patches[0, 0], (slope_one[...] + grad).astype(BF16)), first)


def pack_kernel(peers, micros, dense_rows, dev, *refs):
    names = 8
    values = []
    for n in range(names):
        value = refs[n][...]
        for m in range(1, micros):
            value = value + refs[m * names + n][...]
        values.append(value)
    head, patch, keyval, router, one, two, three, attention = values
    odd = refs[micros * names]
    evens = refs[micros * names + 1 : -1]
    dense = refs[-1]
    at = 0
    for value in (head, patch, keyval):
        dense[at : at + value.shape[0], :] = value.astype(BF16)
        at += value.shape[0]
    rest = [router, one[0:2], two[2:4], three[0:2]]
    pad = dense_rows - at - router.shape[0] - 6
    if pad:
        rest.append(jnp.zeros((pad, dense.shape[1]), F32))
    dense[at:, :] = jnp.concatenate(rest, axis=0).astype(BF16)
    share = dense_rows // peers
    model = dense.shape[1]
    for r in range(peers):
        start = pl.multiple_of((dev[0] ^ r) * share, 16)
        rows = dense[pl.ds(start, share), :]
        owned_rows = attention[r].reshape(-1, model).astype(BF16)
        if r % 2:
            odd[r // 2, :share] = rows
            odd[r // 2, share:] = owned_rows
        else:
            evens[r // 2][0, :share] = rows
            evens[r // 2][0, share:] = owned_rows


def halves_kernel(parts, place, *refs):
    keep, send, total = refs[parts:]
    value = refs[0][0].astype(F32)
    for part in refs[1:parts]:
        value = value + part[0].astype(F32)
    total[...] = value.astype(BF16)
    rows = keep.shape[0]
    keep[...] = total[pl.ds(pl.multiple_of(place[0] * rows, 16), rows), :]
    send[...] = total[pl.ds(pl.multiple_of((1 - place[0]) * rows, 16), rows), :]


def share_sum_kernel(dense_rows, place, shares, outs, squares):
    count, rows, width = shares.shape
    value = shares[0].astype(F32)
    for r in range(1, count):
        value = value + shares[r].astype(F32)
    low = value.astype(BF16)
    for r in range(count):
        outs[r] = low
    value = low.astype(F32)
    value = value * value
    both = jnp.sum(value, axis=0, keepdims=True)
    if dense_rows:
        start = (place[0] * count + place[1]) * rows
        row = lax.broadcasted_iota(jnp.int32, (rows, width), 0) + start
        dense = jnp.sum(jnp.where(row < dense_rows, value, 0.0), axis=0, keepdims=True)
    else:
        dense = jnp.zeros((1, width), F32)
    spots = lax.broadcasted_iota(jnp.int32, (8, LANES), 0) * LANES + lanes_of((8, LANES))
    own = jnp.sum(both - dense, axis=1, keepdims=True)
    dense = jnp.sum(dense, axis=1, keepdims=True)
    squares[...] = jnp.where(spots == 2, own, 0.0) + jnp.where(spots == 3, dense, 0.0)


def join_halves_kernel(dense_rows, place, own, other, dense, rest, total):
    rows = own.shape[0]
    total[pl.ds(pl.multiple_of(place[0] * rows, 16), rows), :] = own[...]
    total[pl.ds(pl.multiple_of((1 - place[0]) * rows, 16), rows), :] = other[...]
    dense[...] = total[:dense_rows, :]
    rest[...] = total[dense_rows:, :]


def clip_factor(sums, other_sums, limit):
    total = sums[0:1, :] + other_sums[0:1, :]
    own, dense = total[:, 2:3], total[:, 3:4]
    norm = jnp.sqrt(own + dense)
    return jnp.minimum(1.0, limit / norm), norm, jnp.sqrt(own), total


def adam_step(weight, first, second, gradient, rate, factor, scales):
    gradient = gradient * factor
    moment = BETA_ONE * first + (1.0 - BETA_ONE) * gradient
    square = BETA_TWO * second + (1.0 - BETA_TWO) * gradient * gradient
    step = moment * scales[0] / (jnp.sqrt(square * scales[1]) + EPSILON) + DECAY * weight
    return weight - rate * step, moment, square


def adam_kernel(rate, limit, place, scales, *refs):
    own, other, sums, other_sums, weight, first, second = refs[:7]
    mine = (pl.program_id(0) == place[0]).astype(F32)
    factor = clip_factor(sums, other_sums, limit)[0]
    gradient = own[...].astype(F32) * mine + other[...].astype(F32) * (1.0 - mine)
    news = adam_step(weight[0, 0], first[0, 0], second[0, 0], gradient, rate, factor, scales)
    for ref, new in zip(refs[-3:], news):
        ref[0, 0] = new


def adam_dense_kernel(peers, rates, limit, tasks, count_row, dev, scales, *refs):
    pieces, attention = refs[:peers], refs[peers]
    sums, other_sums, counts, mutual = refs[peers + 1 : peers + 5]
    states = [refs[peers + 5 + 3 * n : peers + 8 + 3 * n] for n in range(6)]
    outs = [refs[peers + 23 + 3 * n : peers + 26 + 3 * n] for n in range(6)]
    scalars, dense = refs[-2:]
    factor, norm, own_norm, total = clip_factor(sums, other_sums, limit)
    lane = lanes_of((1, LANES))
    ratio = total / jnp.where(lane < tasks, counts[count_row : count_row + 1, :], 1.0)
    loss = jnp.sum(jnp.where(lane < tasks, ratio, 0.0), axis=1, keepdims=True)
    loss = loss - MI_WEIGHT * mutual[0:1, 0:1]
    lane = lanes_of(scalars.shape)
    scalars[...] = jnp.where(lane == 0, loss, jnp.where(lane == 1, norm, own_norm))
    share = pieces[0].shape[0]
    for r in range(peers):
        dense[pl.ds(pl.multiple_of((dev[0] ^ r) * share, 16), share), :] = pieces[r][...]

    def update(n, index, gradient):
        olds = [ref[index] for ref in states[n]]
        news = adam_step(*olds, gradient, rates[n], factor, scales)
        for ref, new in zip(outs[n], news):
            ref[index] = new

    outputs = states[0][0].shape[1]
    step = 2 * LANES
    for left in range(0, outputs, step):
        block = dense[left : left + step, :].astype(F32).T
        update(0, (slice(None), slice(left, left + step)), block)
    at = outputs
    rows = states[1][0].shape[0]
    update(1, ..., dense[at : at + rows, :].astype(F32))
    at += rows
    width = states[2][0].shape[1]
    update(2, ..., dense[at : at + width, :].astype(F32).T)
    at += width
    rest = dense[at:, :].astype(F32)
    rows = states[3][0].shape[0]
    update(3, ..., rest[:rows])
    update(4, ..., rest[rows : rows + states[4][0].shape[0]])
    width = states[5][0].shape[2]
    for n in range(2):
        update(5, n, attention[n * width : (n + 1) * width, :].astype(F32).T)


def whole(array):
    rank = len(array.shape)
    return pl.BlockSpec(array.shape, lambda *_: (0,) * rank, pipeline_mode=pl.Buffered(1))


def kept_out(shape):
    rank = len(shape)
    return pl.BlockSpec(shape, lambda *_: (0,) * rank)


def shape_of(shape, dtype):
    return jax.ShapeDtypeStruct(shape, dtype)


def call(kernel, grid, scalars, inputs, outputs, scratch, cost, name):
    spec = pltpu.PrefetchScalarGridSpec(
        num_scalar_prefetch=len(scalars),
        grid=grid,
        in_specs=[s for _, s in inputs],
        out_specs=[s for _, s in outputs],
        scratch_shapes=scratch,
    )
    return pl.pallas_call(
        kernel,
        grid_spec=spec,
        out_shape=[o for o, _ in outputs],
        cost_estimate=pl.CostEstimate(
            flops=int(cost[0]), bytes_accessed=int(cost[1]), transcendentals=0
        ),
        name=name,
    )(*scalars, *[a for a, _ in inputs])


def swap(value, axis, mask):
    size = lax.axis_size(axis)
    return lax.ppermute(value, axis, [(i, i ^ mask) for i in range(size)])


def bits_of(axis):
    return [1 << b for b in range(lax.axis_size(axis).bit_length() - 1)]


def gather_direct(value):
    return [value] + [swap(value, "expert", r) for r in range(1, lax.axis_size("expert"))]


def scatter_direct(pieces):
    return [pieces[0]] + [swap(pieces[r], "expert", r) for r in range(1, len(pieces))]


def across(value):
    rest = [swap(value, "expert", r) for r in range(2, lax.axis_size("expert"), 2)]
    return rest + [swap(value, "expert", 1)]


def beside(value, came):
    rest = came[:-1]
    return [swap(block, "expert", 1) for block in rest]


def ordered(value, came, more):
    out = [value, came[-1]]
    for block, other in zip(came[:-1], more):
        out += [block, other]
    return out


def gather_pieces(value):
    came = across(value)
    return ordered(value, came, beside(value, came))


def after(value, *anchors):
    return lax.optimization_barrier((value,) + anchors)[0]


class Hops:
    def __init__(self, value, axes):
        self.value = value
        self.steps = [(axis, bit) for axis in axes for bit in bits_of(axis)]
        self.came = []

    def start(self):
        if self.steps:
            self.came = [swap(self.value, *self.steps.pop(0))]

    def land(self, came):
        if self.came:
            self.value = self.value + came[-1]
            self.came = []
        self.start()

    def finish(self):
        while self.came or self.steps:
            self.land(self.came)
        return self.value


def along_z(value):
    size = lax.axis_size("dp")
    groups = [[i for i in range(size) if i % 2 == low] for low in range(2)]
    return lax.all_to_all(
        value, "dp", split_axis=0, concat_axis=0, axis_index_groups=groups, tiled=True
    )


def local(
    patches,
    routes,
    masks,
    targets,
    task_ids,
    step_count,
    patch_weight,
    patch_moment,
    patch_square,
    keyval_weight,
    keyval_moment,
    keyval_square,
    router_weight,
    router_moment,
    router_square,
    norm_weight,
    norm_moment,
    norm_square,
    head_weight,
    head_moment,
    head_square,
    attention_weight,
    attention_moment,
    attention_square,
    expert_weight,
    expert_moment,
    expert_square,
):
    peers = lax.axis_size("expert")
    half_peers = peers // 2
    micros, images, patch_count, patch_in = patches.shape
    _, _, _, _, tasks, top = routes.shape
    owned = expert_weight.shape[0]
    experts = owned * peers
    model, hidden = expert_weight.shape[2:]
    tokens = images * patch_count
    capacity = max(2, tokens * top // experts)
    pixels = masks.shape[3]
    outputs = targets.shape[3]
    pair_width = 2 * HEAD
    span = owned * HEAD
    keys = peers * patch_count
    head_rows = peers * span
    extra = extra_rows(tokens, experts, model)
    long = tokens + extra
    far = lax.axis_size("dp") // 2
    dev = lax.axis_index("expert").astype(jnp.int32).reshape(1)
    spot = lax.axis_index("dp").astype(jnp.int32)
    place = jnp.stack([spot & 1, spot >> 1])
    router_rows = router_weight.T
    router_count = router_rows.shape[0]
    routes_lanes = jnp.transpose(routes, (0, 1, 3, 4, 5, 2))
    attention_own = jnp.transpose(attention_weight, (0, 2, 1)).astype(BF16)
    attention = gather_direct(attention_own)

    order = [task_ids, dev]

    def settle(*values):
        out = lax.optimization_barrier((order[0], order[1]) + values)
        order[:] = out[:2]
        return list(out[2:])

    def settle_groups(*groups):
        out = settle(*[value for group in groups for value in group])
        back = []
        for group in groups:
            back.append(out[: len(group)])
            out = out[len(group) :]
        return back

    token_block = pl.BlockSpec((patch_count, model), lambda i, *_: (i, 0))
    expert_block = pl.BlockSpec((experts, patch_count), lambda i, *_: (0, i))
    kv_block = pl.BlockSpec((patch_count, pair_width), lambda i, *_: (i, 0))
    top_block = pl.BlockSpec((top, patch_count), lambda i, *_: (0, i))

    def micro_block(shape, micro):
        return pl.BlockSpec((1,) + shape, lambda i, *_, m=micro: (m,) + (0,) * (len(shape) - 1) + (i,))

    def image_block(array, micro):
        return pl.BlockSpec((1, 1) + array.shape[2:], lambda i, *_, m=micro: (m, i, 0, 0))

    def pieces_out(rows, width):
        return [(shape_of((rows, width), BF16), kept_out((rows, width)))] * peers


    def one_whole(array, lead):
        return pl.BlockSpec(
            (pl.Squeezed(), patch_count, array.shape[2]), lambda i, *_: (lead, i, 0)
        )

    state = [dict() for _ in range(micros)]

    def run_routing():
        return call(
            route_kernel,
            (micros,),
            (order[0],),
            [
                (
                    routes_lanes,
                    pl.BlockSpec((1,) + routes_lanes.shape[1:], lambda m, *_: (m, 0, 0, 0, 0, 0)),
                ),
                (masks, pl.BlockSpec((1,) + masks.shape[1:], lambda m, *_: (m, 0, 0, 0))),
            ],
            [
                (
                    shape_of((micros, top, tokens), jnp.int32),
                    pl.BlockSpec((1, top, tokens), lambda m, *_: (m, 0, 0)),
                ),
                (
                    shape_of((micros, experts, tokens), jnp.int32),
                    pl.BlockSpec((1, experts, tokens), lambda m, *_: (m, 0, 0)),
                ),
                (
                    shape_of((micros, tasks, pixels), F32),
                    pl.BlockSpec((1, tasks, pixels), lambda m, *_: (m, 0, 0)),
                ),
            ],
            [],
            (micros * tokens * tokens * 32, masks.size * 4),
            "routing",
        )

    def run_embed(micro):
        s = state[micro]
        s["emb"], kv, s["gates_att"], s["probs_att"] = call(
            partial(embed_kernel, micro),
            (images,),
            (order[0],),
            [
                (patches, image_block(patches, micro)),
                (patch_weight, whole(patch_weight)),
                (keyval_weight, whole(keyval_weight)),
                (norm_weight, whole(norm_weight)),
                (router_rows, whole(router_rows)),
                (picks, micro_block((top, patch_count), micro)),
            ],
            [
                (shape_of((tokens, model), F32), token_block),
                (shape_of((tokens, pair_width), BF16), kv_block),
                (shape_of((experts, tokens), F32), expert_block),
                (shape_of((experts, tokens), F32), expert_block),
            ],
            [],
            (2 * tokens * model * (patch_in + pair_width), tokens * (2 * patch_in + 4 * model) + patch_weight.size * 4),
            "embedding",
        )
        return kv

    attention_flops = 2 * top * tokens * keys * HEAD * 8

    def run_attend(micro):
        s = state[micro]
        s["res"], s["sent"], s["mix"], s["lse"], s["probs_mlp"] = call(
            partial(attend_kernel, micro, peers, capacity, images),
            (images,),
            (order[0], order[1]),
            [(s["emb"], token_block)]
            + [(piece, kv_block) for piece in s["kv"]]
            + [
                (picks, micro_block((top, patch_count), micro)),
                (s["gates_att"], expert_block),
                (slots, micro_block((experts, patch_count), micro)),
            ]
            + [(piece, whole(piece)) for piece in attention]
            + [
                (norm_weight, whole(norm_weight)),
                (router_rows, whole(router_rows)),
                (s["probs_att"], expert_block),
                (counts, whole(counts)),
            ],
            [
                (shape_of((tokens, model), F32), token_block),
                (shape_of((long, model), BF16), kept_out((long, model))),
                (
                    shape_of((images, head_rows, patch_count), BF16),
                    pl.BlockSpec((1, head_rows, patch_count), lambda i, *_: (i, 0, 0)),
                ),
                (shape_of((top, tokens), F32), top_block),
                (shape_of((experts, tokens), F32), expert_block),
            ],
            [
                pltpu.VMEM((2 * experts, LANES), F32),
                pltpu.VMEM((keys, pair_width), BF16),
                pltpu.VMEM((pair_width, keys), BF16),
                pltpu.VMEM((head_rows, patch_count), F32),
                pltpu.VMEM((head_rows, patch_count), F32),
            ],
            (attention_flops, tokens * model * 12),
            "attention",
        )

    moe_flops = 2 * owned * peers * capacity * model * (2 * hidden + 2 * tokens)
    expert_bytes = expert_weight.size * 2
    planes_scratch = [pltpu.VMEM((experts, tokens), F32), pltpu.VMEM((experts, tokens), F32)]
    odd_shape = (half_peers, tokens, model)

    def run_experts(micro):
        s = state[micro]
        results = call(
            partial(moe_forward_kernel, peers, owned),
            (peers,),
            (order[1],),
            [(piece, whole(piece)) for piece in s["tokens"]] + [(expert_low, whole(expert_low))],
            [(shape_of(odd_shape, BF16), kept_out(odd_shape))]
            + [(shape_of((tokens, model), BF16), kept_out((tokens, model)))] * half_peers
            + [
                (
                    shape_of((peers, owned, capacity, model), BF16),
                    pl.BlockSpec((1, owned, capacity, model), lambda r, *_: (r, 0, 0, 0)),
                ),
                (shape_of((4 * experts, LANES), F32), kept_out((4 * experts, LANES))),
            ],
            [pltpu.VMEM((long, model), BF16)] + planes_scratch,
            (moe_flops, expert_bytes + 4 * peers * tokens * model),
            "experts",
        )
        s["kept"], s["statistics"] = results[-2:]
        return results[0], list(results[1 : 1 + half_peers])

    count_row = 2 * experts

    def run_head(micro):
        s = state[micro]
        s["slope"], slope_low, s["grad_head"], s["norm_three"], s["squares"] = call(
            partial(head_kernel, micro, len(s["moe"]), count_row),
            (images,),
            (order[0],),
            [(s["res"], token_block)]
            + [
                (part, token_block if lead is None else one_whole(part, lead))
                for part, lead in s["moe"]
            ]
            + [
                (targets, image_block(targets, micro)),
                (masks, image_block(masks, micro)),
                (norm_weight, whole(norm_weight)),
                (head_weight, whole(head_weight)),
                (statistics, whole(statistics)),
            ],
            [
                (shape_of((tokens, model), F32), token_block),
                (shape_of((tokens, model), BF16), token_block),
                (shape_of((outputs, model), F32), kept_out((outputs, model))),
                (shape_of((8, model), F32), kept_out((8, model))),
                (shape_of((8, LANES), F32), kept_out((8, LANES))),
            ],
            [],
            (6 * tokens * model * outputs, tokens * (outputs * 2 + pixels * 4 + 12 * model)),
            "head",
        )
        return slope_low

    extra_block = pl.BlockSpec(
        (extra, model), lambda *_: (tokens // extra, 0), pipeline_mode=pl.Buffered(1)
    )

    def run_experts_back(micro, e, prior):
        s = state[micro]
        more_grads, more_tokens = prior is not None, e > 0
        split = micro == micros - 1
        weight_block = pl.BlockSpec(
            (1, 2, model, hidden), lambda *_, e=e: (e, 0, 0, 0), pipeline_mode=pl.Buffered(1)
        )
        kept_block = pl.BlockSpec((1, 1, capacity, model), lambda r, *_, e=e: (r, e, 0, 0))
        inputs = (
            [(piece, whole(piece)) for piece in s["slopes"]]
            + [(piece, extra_block) for piece in s["tokens"]]
            + [(s["kept"], kept_block), (expert_low, weight_block)]
        )
        if more_grads:
            inputs.append((prior, whole(prior)))
        if more_tokens:
            inputs += [(piece, whole(piece)) for piece in s["pieces"]]
        grad_shape = (2, model, hidden)
        grads_out = (
            [(shape_of(grad_shape[1:], BF16), kept_out(grad_shape[1:]))] * 2
            if split
            else [(shape_of(grad_shape, F32), kept_out(grad_shape))]
        )
        results = call(
            partial(moe_backward_kernel, peers, e, owned, more_grads, more_tokens, split),
            (peers,),
            (order[1], place),
            inputs,
            pieces_out(long, model) + grads_out,
            [pltpu.VMEM((tokens, model), BF16), pltpu.VMEM((extra, model), BF16)]
            + planes_scratch
            + [pltpu.VMEM((long, model), BF16)]
            + ([pltpu.VMEM(grad_shape, F32)] if split else []),
            (3 * moe_flops // owned, expert_bytes * 5 // owned + 4 * peers * tokens * model),
            "experts_back",
        )
        s["pieces"] = list(results[:peers])
        return list(results[peers:])

    def run_attend_back(micro):
        s = state[micro]
        parts = s["sent_parts"]
        results = call(
            partial(back_kernel, micro, peers, peers, images),
            (images,),
            (order[0], order[1]),
            [(s["slope"], token_block)]
            + [(part, token_block) for part in parts]
            + [
                (part, pl.BlockSpec((extra, model), lambda *_: (tokens // extra, 0)))
                for part in parts
            ]
            + [
                (s["res"], token_block),
                (s["emb"], token_block),
                (s["probs_mlp"], expert_block),
                (slots, micro_block((experts, patch_count), micro)),
                (tables, whole(tables)),
            ]
            + [(piece, kv_block) for piece in s["kv"]]
            + [
                (picks, micro_block((top, patch_count), micro)),
                (s["gates_att"], expert_block),
                (s["probs_att"], expert_block),
                (s["lse"], top_block),
            ]
            + [(piece, whole(piece)) for piece in attention]
            + [
                (s["mix"], pl.BlockSpec((1, head_rows, patch_count), lambda i, *_: (i, 0, 0))),
                (norm_weight, whole(norm_weight)),
                (router_rows, whole(router_rows)),
            ],
            [
                (shape_of((tokens, model), F32), token_block),
                (shape_of((tokens, model), F32), token_block),
            ]
            + [(shape_of((tokens, pair_width), BF16), kv_block)] * peers
            + [
                (shape_of((peers, 2, span, model), F32), kept_out((peers, 2, span, model))),
                (shape_of((router_count, model), F32), kept_out((router_count, model))),
                (shape_of((8, model), F32), kept_out((8, model))),
                (shape_of((8, LANES), F32), kept_out((8, LANES))),
            ],
            [
                pltpu.VMEM((keys, pair_width), BF16),
                pltpu.VMEM((pair_width, keys), BF16),
                pltpu.VMEM((head_rows, patch_count), F32),
                pltpu.VMEM((head_rows, patch_count), F32),
                pltpu.VMEM((keys, pair_width), F32),
                pltpu.VMEM((head_rows, patch_count), F32),
                pltpu.VMEM((experts, patch_count), F32),
            ],
            (attention_flops * 3, tokens * model * 30),
            "attention_back",
        )
        s["slope_one"], s["normed_slope"] = results[:2]
        s["grad_att"], s["grad_router"], s["norm_two"], s["mutual"] = results[2 + peers :]
        return list(results[2 : 2 + peers])

    def run_last(micro):
        s = state[micro]
        s["grad_patch"], s["grad_keyval"], s["norm_one"] = call(
            partial(last_kernel, peers),
            (images,),
            (),
            [
                (patches, image_block(patches, micro)),
                (s["emb"], token_block),
                (s["slope_one"], token_block),
                (s["normed_slope"], token_block),
            ]
            + [(part, kv_block) for part in s["kv_parts"]]
            + [(keyval_weight, whole(keyval_weight)), (norm_weight, whole(norm_weight))],
            [
                (shape_of((patch_in, model), F32), kept_out((patch_in, model))),
                (shape_of((pair_width, model), F32), kept_out((pair_width, model))),
                (shape_of((8, model), F32), kept_out((8, model))),
            ],
            [],
            (2 * tokens * model * (patch_in + 2 * pair_width), tokens * model * 20),
            "embedding_back",
        )

    first, second = state
    came_w = across(attention_own)
    picks, slots, count_rows = run_routing()
    (picks,) = settle(picks)
    counts = jnp.zeros((8, LANES), F32).at[0, :tasks].set(jnp.sum(count_rows, axis=(0, 2)))
    hops = Hops(counts, ("dp",))
    hops.start()
    kv = run_embed(0)
    (first["emb"], kv), came_w, came = settle_groups([first["emb"], kv], came_w, hops.came)
    more_w = beside(attention_own, came_w)
    first["kv"] = gather_direct(kv)
    hops.land(came)
    kv = run_embed(1)
    (second["emb"], kv), more_w, first["kv"], came = settle_groups(
        [second["emb"], kv], more_w, first["kv"], hops.came
    )
    attention = ordered(attention_own, came_w, more_w)
    second["kv"] = gather_direct(kv)
    hops.land(came)

    counts = hops.value
    run_attend(0)
    (first["res"], first["sent"]), second["kv"], came = settle_groups(
        [first["res"], first["sent"]], second["kv"], hops.came
    )
    hops.land(came)
    counts = hops.finish()
    came_first = across(first["sent"])
    run_attend(1)
    (second["res"], second["sent"]), came_first = settle_groups(
        [second["res"], second["sent"]], came_first
    )
    more_first = beside(first["sent"], came_first)
    came_second = across(second["sent"])
    expert_low = after(expert_weight, order[1]).astype(BF16)
    (expert_low,), more_first = settle_groups([expert_low], more_first)
    first["tokens"] = ordered(first["sent"], came_first, more_first)

    first_odd, first_evens = run_experts(0)
    (first["kept"], first_odd), came_second = settle_groups([first["kept"], first_odd], came_second)
    more_second = beside(second["sent"], came_second)
    first_crossed = swap(first_odd, "expert", 1)
    (more_second,) = settle_groups(more_second)
    second["tokens"] = ordered(second["sent"], came_second, more_second)
    second_odd, second_evens = run_experts(1)
    second["kept"], second_odd, first_crossed = settle(second["kept"], second_odd, first_crossed)

    def onward(evens, crossed):
        out = []
        for n in range(1, half_peers):
            pair = (evens[n].astype(F32) + crossed[n].astype(F32)).astype(BF16)
            out.append(swap(pair, "expert", 2 * n))
        return out

    def arrived(evens, crossed, rest):
        return [(evens[0], None), (crossed, 0)] + [(part, None) for part in rest]

    first_rest = onward(first_evens, first_crossed)
    second_crossed = swap(second_odd, "expert", 1)
    statistics = second["statistics"]
    hops = Hops(first["statistics"] + statistics, ("dp",))
    (second_crossed,) = settle(second_crossed)
    second_rest = onward(second_evens, second_crossed)
    hops.start()
    (first_rest,) = settle_groups(first_rest)
    first["moe"] = arrived(first_evens, first_crossed, first_rest)

    first_low = run_head(0)
    (first["slope"], first_low), second_rest, came = settle_groups(
        [first["slope"], first_low], second_rest, hops.came
    )
    second["moe"] = arrived(second_evens, second_crossed, second_rest)
    came_first = across(first_low)
    hops.land(came)
    second_low = run_head(1)
    (second["slope"], second_low), came_first, came = settle_groups(
        [second["slope"], second_low], came_first, hops.came
    )
    more_first = beside(first_low, came_first)
    second["slopes"] = gather_direct(second_low)
    hops.land(came)
    (more_first,) = settle_groups(more_first)
    first["slopes"] = ordered(first_low, came_first, more_first)

    def small_call(kernel, scalars, inputs, shapes, scratch, name):
        return call(
            kernel,
            (1,),
            scalars,
            [(a, whole(a)) for a in inputs],
            [(s, kept_out(s.shape)) for s in shapes],
            scratch,
            (0, 1000),
            name,
        )

    exchanged = [dev]

    def exchange(value):
        value = along_z(after(value, exchanged[0], order[1]))
        exchanged[0] = value
        return value

    def cut_shares(keep, came):
        rows, width = keep.shape
        total = (keep.astype(F32) + came.astype(F32)).astype(BF16)
        return exchange(total.reshape(far, rows // far, width))

    def sum_shares(moved, dense_rows):
        return small_call(
            partial(share_sum_kernel, dense_rows),
            (place,),
            [moved],
            [shape_of(moved.shape, BF16), shape_of((8, LANES), F32)],
            [],
            "share_sum",
        )

    prior = run_experts_back(0, 0, None)
    first["pieces"], second["slopes"], prior, came = settle_groups(
        first["pieces"], second["slopes"], prior, hops.came
    )
    hops.land(came)
    keep_first, send_first = run_experts_back(1, 0, prior[0])
    second["pieces"], (keep_first, send_first), came = settle_groups(
        second["pieces"], [keep_first, send_first], hops.came
    )
    hops.land(came)
    tables = hops.finish()
    came_x_first = swap(send_first, "dp", 1)
    prior = run_experts_back(0, 1, None)
    first["pieces"], prior = settle_groups(first["pieces"], prior)
    first["sent_parts"] = scatter_direct(first["pieces"])
    keep_second, send_second = run_experts_back(1, 1, prior[0])
    (keep_second, send_second), second["pieces"], first["sent_parts"], (came_x_first, tables) = (
        settle_groups(
            [keep_second, send_second],
            second["pieces"],
            first["sent_parts"],
            [came_x_first, tables],
        )
    )
    came_x_second = swap(send_second, "dp", 1)
    second["sent_parts"] = scatter_direct(second["pieces"])
    square_parts = [s["squares"] for s in state]
    shares_first = cut_shares(keep_first, came_x_first)

    kv_parts = run_attend_back(0)
    kv_parts, second["sent_parts"], (came_x_second, shares_first) = settle_groups(
        kv_parts, second["sent_parts"], [came_x_second, shares_first]
    )
    first["kv_parts"] = scatter_direct(kv_parts)
    summed_first, squares = sum_shares(shares_first, 0)
    square_parts.append(squares)
    shares_second = cut_shares(keep_second, came_x_second)
    (summed_first,) = settle(summed_first)
    kv_parts = run_attend_back(1)
    kv_parts, first["kv_parts"], (shares_second,) = settle_groups(
        kv_parts, first["kv_parts"], [shares_second]
    )
    second["kv_parts"] = scatter_direct(kv_parts)
    own_first = exchange(summed_first).reshape(model, hidden)
    summed_second, squares = sum_shares(shares_second, 0)
    square_parts.append(squares)
    (summed_second,) = settle(summed_second)
    run_last(0)
    (first["norm_one"],), second["kv_parts"] = settle_groups([first["norm_one"]], second["kv_parts"])
    run_last(1)
    (second["norm_one"],) = settle(second["norm_one"])

    names = ("grad_head", "grad_patch", "grad_keyval", "grad_router", "norm_one", "norm_two", "norm_three", "grad_att")
    used_rows = outputs + patch_in + pair_width + router_count + 6
    dense_rows = -(-used_rows // 256) * 256
    dense_share = dense_rows // peers
    all_rows = dense_share + 2 * span
    packed = small_call(
        partial(pack_kernel, peers, micros, dense_rows),
        (order[1],),
        [s[name] for s in state for name in names],
        [shape_of((half_peers, all_rows, model), BF16)]
        + [shape_of((1, all_rows, model), BF16)] * half_peers,
        [pltpu.VMEM((dense_rows, model), BF16)],
        "pack",
    )
    packed = settle(*packed)
    odd, evens = packed[0], packed[1:]
    crossed = swap(odd, "expert", 1)
    (crossed,) = settle(crossed)
    parts = [(evens[0], 0), (crossed, 0)]
    for n in range(1, half_peers):
        pair = (evens[n].astype(F32) + crossed[n : n + 1].astype(F32)).astype(BF16)
        parts.append((swap(pair, "expert", 2 * n), 0))
    (own_first,) = settle(own_first)
    other_first = swap(own_first, "dp", 1)
    own_second = exchange(summed_second).reshape(model, hidden)
    lead_parts = settle(*[part for part, _ in parts])
    parts = [(part, lead) for part, (_, lead) in zip(lead_parts, parts)]
    half_shape = shape_of((all_rows // 2, model), BF16)
    keep, send = call(
        partial(halves_kernel, len(parts)),
        (1,),
        (place,),
        [(part, pl.BlockSpec((1, all_rows, model), lambda *_, lead=lead: (lead, 0, 0))) for part, lead in parts],
        [(half_shape, kept_out(half_shape.shape))] * 2,
        [pltpu.VMEM((all_rows, model), BF16)],
        (0, 8 * all_rows * model),
        "halves",
    )
    keep, send = settle(keep, send)
    came = swap(send, "dp", 1)
    came, other_first, own_second = settle(came, other_first, own_second)
    shares, squares = sum_shares(cut_shares(keep, came), dense_share)
    sums = squares
    for part in square_parts:
        sums = sums + part
    sums, shares = settle(sums, shares)
    hops = Hops(sums, ("expert", "dp"))
    hops.start()
    own = exchange(shares).reshape(all_rows // 2, model)
    (own,), came = settle_groups([own], hops.came)
    other = swap(own, "dp", 1)
    hops.land(came)
    (other,), came = settle_groups([other], hops.came)
    other_second = swap(after(own_second, order[1]), "dp", 1)
    dense_part, attention_part = small_call(
        partial(join_halves_kernel, dense_share),
        (place,),
        [own, other],
        [shape_of((dense_share, model), BF16), shape_of((2 * span, model), BF16)],
        [pltpu.VMEM((all_rows, model), BF16)],
        "join_halves",
    )
    came_quarters = across(dense_part)
    hops.land(came)
    came_quarters, came = settle_groups(came_quarters, hops.came)
    quarters = ordered(dense_part, came_quarters, beside(dense_part, came_quarters))
    hops.land(came)
    while len(hops.steps):
        hops.land(hops.came)
    sums, last_came = hops.value, hops.came[0]

    total_params = (
        patch_weight.size
        + keyval_weight.size
        + router_weight.size
        + norm_weight.size
        + head_weight.size
        + (attention_weight.size + expert_weight.size) * peers
    )
    limit = CLIP_UNIT * math.sqrt(total_params)
    step_value = step_count[0].astype(F32)
    scales = jnp.stack(
        [1.0 / (1.0 - jnp.power(BETA_ONE, step_value)), 1.0 / (1.0 - jnp.power(BETA_TWO, step_value))]
    )
    block_rows = model // 4
    expert_results = None
    for e, (own, other) in enumerate([(own_first, other_first), (own_second, other_second)]):
        block = pl.BlockSpec((1, 1, block_rows, hidden), lambda w, b, *_, e=e: (e, w, b, 0))
        grad_block = pl.BlockSpec((block_rows, hidden), lambda w, b, *_: (b, 0))
        inputs = [own, other, sums, last_came, expert_weight, expert_moment, expert_square]
        specs = [grad_block, grad_block, whole(sums), whole(last_came), block, block, block]
        aliases = {}
        if expert_results is not None:
            aliases = {2 + len(inputs) + n: n for n in range(3)}
            inputs += list(expert_results)
            specs += [pl.BlockSpec(memory_space=pl.ANY)] * 3
        expert_results = pl.pallas_call(
            partial(adam_kernel, RATES[6], limit),
            grid_spec=pltpu.PrefetchScalarGridSpec(
                num_scalar_prefetch=2,
                grid=(2, model // block_rows),
                in_specs=specs,
                out_specs=[block] * 3,
            ),
            out_shape=[shape_of(expert_weight.shape, F32)] * 3,
            input_output_aliases=aliases,
            cost_estimate=pl.CostEstimate(
                flops=expert_weight.size * 20 // owned,
                bytes_accessed=expert_weight.size * 26 // owned,
                transcendentals=0,
            ),
            name="adam",
        )(place, scales, *inputs)
    dense_states = [
        head_weight,
        head_moment,
        head_square,
        patch_weight,
        patch_moment,
        patch_square,
        keyval_weight,
        keyval_moment,
        keyval_square,
        router_rows,
        router_moment.T,
        router_square.T,
        norm_weight,
        norm_moment,
        norm_square,
        attention_weight,
        attention_moment,
        attention_square,
    ]
    dense_results = small_call(
        partial(
            adam_dense_kernel,
            peers,
            (RATES[4], RATES[0], RATES[1], RATES[2], RATES[3], RATES[5]),
            limit,
            tasks,
            count_row,
        ),
        (order[1], scales),
        quarters
        + [attention_part, sums, last_came, statistics, state[0]["mutual"]]
        + dense_states,
        [shape_of(a.shape, F32) for a in dense_states] + [shape_of((8, LANES), F32)],
        [pltpu.VMEM((dense_rows, model), BF16)],
        "adam_dense",
    )
    new_head, new_patch, new_keyval, new_router, new_norm, new_attention = [
        list(dense_results[3 * n : 3 * n + 3]) for n in range(6)
    ]
    new_router = [a.T for a in new_router]
    return tuple(
        [dense_results[18][0, n] for n in range(3)]
        + new_patch
        + new_keyval
        + new_router
        + new_norm
        + new_head
        + new_attention
        + list(expert_results)
    )


def solution(mesh):
    tokens = P(None, "dp", "expert", None)
    by_columns = P(None, None, "expert")
    by_expert = P("expert", None, None, None)
    same = P()
    placed = (
        (tokens, P(None, "dp", "expert", None, None, None), tokens, tokens, P(None, "dp"), same)
        + (same,) * 15
        + (by_columns,) * 3
        + (by_expert,) * 3
    )
    return jax.shard_map(
        local,
        mesh=mesh,
        in_specs=placed,
        out_specs=(same,) * 18 + (by_columns,) * 3 + (by_expert,) * 3,
        check_vma=False,
    )
```

```python
from functools import partial
import math
from types import SimpleNamespace

import jax
import jax.numpy as jnp
from jax import lax
from jax.experimental import pallas as pl
from jax.experimental.pallas import tpu as pltpu
from jax.sharding import PartitionSpec as P

HEAD = 64
NORM_EPS = 1e-06
MI_WEIGHT = 0.5
CLIP_UNIT = 3e-07
BETA_ONE = 0.9
BETA_TWO = 0.999
EPSILON = 1e-08
RATES = (0.02, 0.02, 0.02, 0.3, 0.02, 1.2, 0.02)
DECAY = 0.05
F32 = jnp.float32
BF16 = jnp.bfloat16
EXACT = lax.Precision.HIGHEST
NOWHERE = 1 << 20
LANES = 128
GELU_A = 0.044715
GELU_C = math.sqrt(2.0 / math.pi)


def mm(left, right, precision=None):
    return lax.dot_general(
        left, right, (((1,), (0,)), ((), ())), precision=precision, preferred_element_type=F32
    )


def mm_nt(left, right, precision=None):
    return lax.dot_general(
        left, right, (((1,), (1,)), ((), ())), precision=precision, preferred_element_type=F32
    )


def mm_tn(left, right, precision=None):
    return lax.dot_general(
        left, right, (((0,), (0,)), ((), ())), precision=precision, preferred_element_type=F32
    )


def norm_forward(values, gain, shift):
    centred = values - jnp.mean(values, axis=-1, keepdims=True)
    inverse = lax.rsqrt(jnp.mean(centred * centred, axis=-1, keepdims=True) + NORM_EPS)
    scaled = centred * inverse
    return scaled, inverse, scaled * gain + shift


def norm_backward(slope, scaled, inverse, gain):
    inner = slope * gain
    grad = inverse * (
        inner
        - jnp.mean(inner, axis=-1, keepdims=True)
        - scaled * jnp.mean(inner * scaled, axis=-1, keepdims=True)
    )
    return grad, jnp.sum(slope * scaled, axis=0, keepdims=True), jnp.sum(slope, axis=0, keepdims=True)


def expert_rows(experts, tokens):
    return lax.broadcasted_iota(jnp.int32, (experts, tokens), 0)


def by_task(rows, task, experts):
    out = rows[:experts]
    for other in range(1, rows.shape[0] // experts):
        out = jnp.where(task == other, rows[other * experts : (other + 1) * experts], out)
    return out


def to_tasks(rows, task, tasks):
    return jnp.concatenate([jnp.where(task == t, rows, 0.0) for t in range(tasks)], axis=0)


def router_forward(router_rows, normed, task, experts):
    logits = by_task(mm_nt(router_rows, normed, EXACT), task, experts)
    powers = jnp.exp(logits - jnp.max(logits, axis=0, keepdims=True))
    return powers / jnp.sum(powers, axis=0, keepdims=True)


def gate_forward(probs, chosen):
    picked = probs * chosen
    return picked / jnp.sum(picked, axis=0, keepdims=True)


def gate_backward(probs, chosen, grad_gates, grad_probs):
    total = jnp.sum(probs * chosen, axis=0, keepdims=True)
    gates = probs * chosen / total
    inner = chosen / total * (grad_gates - jnp.sum(grad_gates * gates, axis=0, keepdims=True))
    inner = inner + grad_probs
    return probs * (inner - jnp.sum(probs * inner, axis=0, keepdims=True))


def picked_hot(picks, experts):
    rows = expert_rows(experts, picks.shape[1])
    out = jnp.zeros(rows.shape, F32)
    for k in range(picks.shape[0]):
        out = out + (picks[k : k + 1, :] == rows).astype(F32)
    return out


def add_to(ref, index, value, first):
    @pl.when(first)
    def _():
        ref[index] = value

    @pl.when(jnp.logical_not(first))
    def _():
        ref[index] = ref[index] + value


def route_kernel(tid, routes, masks, picks, slots, counts):
    micro = pl.program_id(0)
    _, images, _, tasks, _, patch_count = routes.shape
    experts = slots.shape[1]
    tokens = images * patch_count
    chosen = []
    pixel_rows = [jnp.zeros((1, masks.shape[3]), F32) for _ in range(tasks)]
    for image in range(images):
        task = tid[micro, image]
        att, mlp = routes[0, image, 0, 0], routes[0, image, 1, 0]
        for t in range(1, tasks):
            att = jnp.where(task == t, routes[0, image, 0, t], att)
            mlp = jnp.where(task == t, routes[0, image, 1, t], mlp)
        picks[0, :, image * patch_count : (image + 1) * patch_count] = att
        chosen.append(picked_hot(mlp, experts))
        column = jnp.sum(masks[0, image].astype(F32), axis=0, keepdims=True)
        for t in range(tasks):
            pixel_rows[t] = pixel_rows[t] + jnp.where(task == t, column, 0.0)
    chosen = jnp.concatenate(chosen, axis=1)
    earlier = lax.broadcasted_iota(jnp.int32, (tokens, tokens), 0) < lax.broadcasted_iota(
        jnp.int32, (tokens, tokens), 1
    )
    before = mm(chosen.astype(BF16), earlier.astype(F32).astype(BF16))
    slots[0] = jnp.where(chosen > 0.0, before.astype(jnp.int32), NOWHERE)
    counts[0] = jnp.concatenate(pixel_rows, axis=0)


def embed_kernel(micro, tid, patches, patch_w, keyval_w, norms, router, picks, emb, kv, gates, probs):
    experts = gates.shape[0]
    task = tid[micro, pl.program_id(0)]
    width = router.shape[0] // 2
    embedded = mm(patches[0, 0], patch_w[...].astype(BF16))
    emb[...] = embedded
    _, _, normed = norm_forward(embedded, norms[0:1], norms[1:2])
    kv[...] = mm(normed.astype(BF16), keyval_w[...].astype(BF16)).astype(BF16)
    prob = router_forward(router[0:width], normed, task, experts)
    probs[...] = prob
    gates[...] = gate_forward(prob, picked_hot(picks[0], experts))


def split_planes(values):
    high = values.astype(BF16).astype(F32)
    middle = (values - high).astype(BF16).astype(F32)
    return [high, middle, (values - high - middle).astype(BF16).astype(F32)]


def put_planes(ref, planes, image, token_rows, images):
    patch_count, model = token_rows.shape
    block = jnp.concatenate(planes, axis=0).astype(BF16)
    height = block.shape[0]
    columns, chunks = model // LANES, patch_count // LANES
    rows, base = ref.shape[0], images * patch_count
    for i in range(images):

        @pl.when(image == i)
        def _(i=i):
            ref[i * patch_count : (i + 1) * patch_count, :] = token_rows
            if i == 0:
                ref[base:, :] = jnp.zeros((rows - base, model), BF16)
            for j in range(chunks):
                c = i * chunks + j
                top, left = base + c // columns * height, c % columns * LANES
                ref[top : top + height, left : left + LANES] = block[:, j * LANES : (j + 1) * LANES]


def lanes_of(shape):
    return lax.broadcasted_iota(jnp.int32, shape, 1)


def put_statistics(ref, images, patch_count, values):
    high, middle, rest = split_planes(values)
    block = high + pltpu.roll(middle, 8, 1) + pltpu.roll(rest, 16, 1)
    ref[ref.shape[0] - values.shape[0] :, ref.shape[1] - LANES :] = block.astype(BF16)


def get_statistics(block):
    block = block.astype(F32)
    total = block + pltpu.roll(block, LANES - 8, 1) + pltpu.roll(block, LANES - 16, 1)
    return jnp.where(lanes_of(block.shape) < 8, total, 0.0)


def extra_rows(count, experts, model):
    return -(-(count // LANES) // (model // LANES)) * 4 * experts


def get_planes(block, count, experts, columns):
    height = 4 * experts
    out = []
    for c in range(count // LANES):
        top, left = c // columns * height, c % columns * LANES
        out.append(block[top : top + height, left : left + LANES].astype(F32))
    return out


def three_sum(planes, experts):
    return planes[:experts] + planes[experts : 2 * experts] + planes[2 * experts : 3 * experts]


def fill_keys(pieces, kvs, kv_t):
    rows = pieces[0].shape[0]
    for r, piece in enumerate(pieces):
        block = piece[...]
        kvs[r * rows : (r + 1) * rows, :] = block
        kv_t[:, r * rows : (r + 1) * rows] = block.astype(F32).T.astype(BF16)


def attend_kernel(micro, peers, capacity, images, tid, dev, *refs):
    emb = refs[0]
    kv_in = refs[1 : 1 + peers]
    picks, gates_in, slots = refs[1 + peers : 4 + peers]
    weights = refs[4 + peers : 4 + 2 * peers]
    norms, router = refs[4 + 2 * peers : 6 + 2 * peers]
    probs_att, counts = refs[6 + 2 * peers : 8 + 2 * peers]
    res_out, sent, mix_out, lse, probs_out = refs[8 + 2 * peers : 13 + 2 * peers]
    table, kvs, kv_t, q_t, mix = refs[13 + 2 * peers :]
    experts, tokens = gates_in.shape
    owned = weights[0].shape[1] // HEAD
    task = tid[micro, pl.program_id(0)]
    width = router.shape[0] // 2
    mine = dev[0]
    embedded = emb[...]
    _, _, normed = norm_forward(embedded, norms[0:1], norms[1:2])
    low = normed.astype(BF16)
    span = owned * HEAD
    for r in range(peers):
        q_t[r * span : (r + 1) * span, :] = mm_nt(weights[r][0], low).astype(BF16).astype(F32)
    fill_keys(kv_in, kvs, kv_t)
    mix[...] = jnp.zeros(mix.shape, F32)
    blocks = [(r, e, (r * owned + e) * HEAD) for r in range(peers) for e in range(owned)]
    rows = expert_rows(experts, tokens)
    blank = jnp.zeros((HEAD, tokens), BF16)

    def one_pick(k, carry):
        pick = picks[0, pl.ds(k, 1), :]
        query = jnp.zeros((HEAD, tokens), F32)
        for r, e, at in blocks:
            here = pick == (mine ^ r) * owned + e
            query = query + jnp.where(here, q_t[at : at + HEAD, :], 0.0)
        gate = jnp.sum(jnp.where(rows == pick, gates_in[...], 0.0), axis=0, keepdims=True)
        scores = mm(kvs[...], jnp.concatenate([(query * HEAD ** (-0.5)).astype(BF16), blank], axis=0))
        top = jnp.max(scores, axis=0, keepdims=True)
        powers = jnp.exp(scores - top)
        total = jnp.sum(powers, axis=0, keepdims=True)
        lse[pl.ds(k, 1), :] = top + jnp.log(total)
        weighted = (powers * (gate / total)).astype(BF16)
        out = mm(kv_t[HEAD:, :], weighted)
        for r, e, at in blocks:
            here = pick == (mine ^ r) * owned + e
            mix[at : at + HEAD, :] = mix[at : at + HEAD, :] + jnp.where(here, out, 0.0)
        return carry

    lax.fori_loop(0, picks.shape[1], one_pick, 0)
    resid = embedded
    for r in range(peers):
        block = mix[r * span : (r + 1) * span, :].astype(BF16)
        mix_out[0, r * span : (r + 1) * span, :] = block
        resid = resid + mm_tn(block, weights[r][1])
    res_out[...] = resid
    _, _, normed_two = norm_forward(resid, norms[2:3], norms[3:4])
    prob = router_forward(router[width:], normed_two, task, experts)
    probs_out[...] = prob
    both = jnp.concatenate([probs_att[...], prob], axis=0)
    lane = lanes_of((2 * experts, LANES))
    per_task = jnp.where(lane == task, jnp.sum(both, axis=1, keepdims=True), 0.0)
    add_to(table, ..., per_task, pl.program_id(0) == 0)
    slot = slots[0]
    gates = gate_forward(prob, (slot < NOWHERE).astype(F32))
    places = jnp.minimum(slot, capacity).astype(F32)
    low_two = normed_two.astype(BF16)
    put_planes(sent, split_planes(gates) + [places], pl.program_id(0), low_two, images)

    @pl.when(pl.program_id(0) == images - 1)
    def _():
        rest = jnp.zeros((2 * experts - 8, LANES), F32)
        block = jnp.concatenate([table[...], counts[...], rest], axis=0)
        put_statistics(sent, images, tokens, block)


def read_planes(block, experts, count):
    chunks = get_planes(block, count, experts, block.shape[1] // LANES)
    gates = jnp.concatenate([three_sum(chunk, experts) for chunk in chunks], axis=1)
    return jnp.concatenate([chunk[3 * experts :] for chunk in chunks], axis=1), gates


def one_row(rows, at):
    index = expert_rows(rows.shape[0], rows.shape[1])
    return jnp.sum(jnp.where(index == at, rows, 0.0), axis=0, keepdims=True)


def dispatch(blocks, at, experts, count, hot, gate):
    capacity = hot.shape[0] // len(blocks)
    places = lax.broadcasted_iota(jnp.int32, (capacity, count), 0).astype(F32)
    for r, block in enumerate(blocks):
        slots, gates = read_planes(block, experts, count)
        here = one_row(slots, at) == places
        rows = slice(r * capacity, (r + 1) * capacity)
        hot[rows, :] = here.astype(F32).astype(BF16)
        gate[rows, :] = jnp.sum(jnp.where(here, one_row(gates, at), 0.0), axis=1, keepdims=True)


def moe_forward_kernel(peers, owned, experts, dev, *refs):
    half = peers // 2
    arrays = refs[:peers]
    weights, odd = refs[peers], refs[peers + 1]
    evens = refs[peers + 2 : peers + 2 + half]
    kept, made, statistics, hot, gate, back = refs[peers + 2 + half :]
    e = pl.program_id(0)
    count = hot.shape[1]
    capacity = hot.shape[0] // peers
    dispatch([a[count:, :] for a in arrays], dev[0] * owned + e, experts, count, hot, gate)
    for r in range(peers):
        rows = slice(r * capacity, (r + 1) * capacity)
        kept[0, rows, :] = mm(hot[rows, :], arrays[r][:count, :]).astype(BF16)
    before = mm(kept[0], weights[0, 0])
    bent = jnp.tanh(before * (GELU_C + GELU_C * GELU_A * (before * before)))
    halved = 0.5 * before
    out = mm_nt((halved + halved * bent).astype(BF16), weights[0, 1])
    made[0] = out.astype(BF16)
    weighted = (out * gate[...]).astype(BF16)
    for r in range(peers):
        rows = slice(r * capacity, (r + 1) * capacity)
        value = mm_tn(hot[rows, :], weighted[rows, :])
        if owned > 1:
            add_to(back, r, value, e == 0)

    @pl.when(e == owned - 1)
    def _():
        for r in range(peers):
            piece = back[r].astype(BF16) if owned > 1 else value.astype(BF16)
            if r % 2:
                odd[r // 2] = piece
            else:
                evens[r // 2][...] = piece
        rows = statistics.shape[0]
        block = jnp.zeros(statistics.shape, F32)
        for a in arrays:
            block = block + get_statistics(a[a.shape[0] - rows :, a.shape[1] - LANES :])
        statistics[...] = block


def head_kernel(micro, parts, count_row, tid, *refs):
    res = refs[0]
    moe = refs[1 : 1 + parts]
    targets, masks, norms, head_w, counts = refs[1 + parts : 6 + parts]
    slope_out, slope_low, grad_head, grad_norm, squares = refs[6 + parts :]
    image = pl.program_id(0)
    task = tid[micro, image]
    resid = res[...]
    for part in moe:
        resid = resid + part[...].astype(F32)
    scaled, inverse, normed = norm_forward(resid, norms[4:5], norms[5:6])
    low = normed.astype(BF16)
    head_low = head_w[...].astype(BF16)
    pred = mm(low, head_low)
    mask = masks[0, 0].astype(F32)
    pixels = mask.shape[1]
    count_rows = counts[count_row : count_row + 1, :]
    count = jnp.sum(jnp.where(lanes_of((1, LANES)) == task, count_rows, 0.0), axis=1, keepdims=True)
    depth_on = jnp.where(task == 0, 1.0, 0.0)
    normal_on = jnp.where(task == 0, 0.0, 1.0)
    slopes = []
    total = jnp.zeros((1, pixels), F32)
    for group in range(4):
        on = depth_on if group == 0 else normal_on
        at = group * pixels
        gap = pred[:, at : at + pixels] - targets[0, 0, :, at : at + pixels].astype(F32)
        masked = mask * gap
        total = total + on * jnp.sum(masked * gap, axis=0, keepdims=True)
        slopes.append((masked * (2.0 * on / count)).astype(BF16))
    slope = jnp.concatenate(slopes, axis=1)
    first = image == 0
    spots = lax.broadcasted_iota(jnp.int32, (8, LANES), 0) * LANES + lanes_of((8, LANES))
    add_to(squares, ..., jnp.where(spots == task, jnp.sum(total, axis=1, keepdims=True), 0.0), first)
    add_to(grad_head, ..., mm_tn(slope, low), first)
    grad, gain, shift = norm_backward(mm_nt(slope, head_low), scaled, inverse, norms[4:5])
    add_to(grad_norm, slice(0, 1), gain, first)
    add_to(grad_norm, slice(1, 2), shift, first)
    slope_out[...] = grad
    slope_low[...] = grad.astype(BF16)


def moe_backward_kernel(peers, local_expert, owned, experts, more_grads, more_tokens, split, dev, place, *refs):
    refs = list(refs)

    def take(count):
        out = refs[:count]
        del refs[:count]
        return out

    slopes, extras = take(peers), take(peers)
    kept, made, weights = take(3)
    if more_grads:
        (prior_grads,) = take(1)
    if more_tokens:
        prior_pieces = take(peers)
    outs = take(peers)
    grads_out = take(2 if split else 1)
    hot, gate, plain = take(3)
    count, model = slopes[0].shape
    capacity = hot.shape[0] // peers
    at = dev[0] * owned + local_expert
    dispatch([extra[...] for extra in extras], at, experts, count, hot, gate)
    gate_slopes = []
    for r in range(peers):
        rows = slice(r * capacity, (r + 1) * capacity)
        value = mm(hot[rows, :], slopes[r][...])
        gate_slopes.append(jnp.sum(value * made[0, rows, :].astype(F32), axis=1, keepdims=True))
        plain[rows, :] = (value * gate[rows, :]).astype(BF16)
    before = mm(kept[0], weights[0, 0])
    hidden = mm(plain[...], weights[0, 1])
    cubic = GELU_C * GELU_A * (before * before)
    bent = jnp.tanh(before * (GELU_C + cubic))
    middle = 0.5 + 0.5 * bent
    inner = (before * middle).astype(BF16)
    bend = middle + (middle - middle * bent) * (before * (GELU_C + 3.0 * cubic))
    slope = (hidden * bend).astype(BF16)
    entry = mm_tn(kept[0], slope)
    leave = mm_tn(plain[...], inner)
    if more_grads:
        entry = entry + prior_grads[0].astype(F32)
        leave = leave + prior_grads[1].astype(F32)
    if split:
        flip = place[0] == 0
        grads_out[0][...] = jnp.where(flip, entry, leave).astype(BF16)
        grads_out[1][...] = jnp.where(flip, leave, entry).astype(BF16)
    else:
        grads_out[0][0] = entry.astype(BF16)
        grads_out[0][1] = leave.astype(BF16)
    received = mm_nt(slope, weights[0, 0]).astype(BF16)
    columns, chunks, height = model // LANES, count // LANES, 4 * experts
    rows_of = expert_rows(experts, count)
    lane = lanes_of((capacity, LANES))
    for r in range(peers):
        rows = slice(r * capacity, (r + 1) * capacity)
        tokens_back = mm_tn(hot[rows, :], received[rows, :])
        terms = split_planes(gate_slopes[r])
        terms = jnp.where(lane == 0, terms[0], jnp.where(lane == 1, terms[1], terms[2]))
        terms = jnp.where(lane < 3, terms, 0.0).astype(BF16)
        gate_row = jnp.sum(mm_tn(terms, hot[rows, :])[:8, :], axis=0, keepdims=True)
        planes = split_planes(jnp.where(rows_of == at, gate_row, 0.0))
        block = jnp.concatenate(planes + [jnp.zeros((experts, count), F32)], axis=0)
        lines = []
        for line in range(-(-chunks // columns)):
            cells = [
                block[:, c * LANES : (c + 1) * LANES]
                if c < chunks
                else jnp.zeros((height, LANES), F32)
                for c in range(line * columns, (line + 1) * columns)
            ]
            lines.append(jnp.concatenate(cells, axis=1))
        piece = jnp.concatenate([tokens_back] + lines, axis=0)
        if more_tokens:
            piece = piece + prior_pieces[r][...].astype(F32)
        outs[r][...] = piece.astype(BF16)


def table_slope(table, task, tasks):
    lane = lanes_of(table.shape)
    valid = lane < tasks
    table = jnp.where(valid, table, 0.0)
    total = jnp.sum(jnp.sum(table, axis=1, keepdims=True), axis=0, keepdims=True)
    share = table / total
    by_expert = jnp.sum(share, axis=1, keepdims=True)
    by_task_sum = jnp.sum(share, axis=0, keepdims=True)
    safe = jnp.where(valid, share, 1.0)
    gain = jnp.log(safe) - jnp.log(jnp.where(valid, by_task_sum, 1.0)) - jnp.log(by_expert)
    gain = jnp.where(valid, gain, 0.0)
    mean = jnp.sum(jnp.sum(gain * share, axis=1, keepdims=True), axis=0, keepdims=True)
    slope = -MI_WEIGHT * (gain - mean) / total
    return jnp.sum(jnp.where(lane == task, slope, 0.0), axis=1, keepdims=True), mean


def back_kernel(micro, peers, parts, image_count, tid, dev, *refs):
    slope_in = refs[0]
    sent_parts = refs[1 : 1 + parts]
    gate_parts = refs[1 + parts : 1 + 2 * parts]
    at = 1 + 2 * parts
    res, emb, probs_mlp, slots = refs[at : at + 4]
    at += 4
    tables = refs[at]
    kv_in = refs[at + 1 : at + 1 + peers]
    at += 1 + peers
    picks, gates_in, probs_att, lse = refs[at : at + 4]
    weights = refs[at + 4 : at + 4 + peers]
    at += 4 + peers
    mix_in, norms, router = refs[at : at + 3]
    slope_one, normed_slope = refs[at + 3 : at + 5]
    kv_outs = refs[at + 5 : at + 5 + peers]
    at += 5 + peers
    grad_att, grad_router, grad_norm, mutual = refs[at : at + 4]
    kvs, kv_t, q_t, d_t, dkv, dq_t, dgate = refs[at + 4 :]
    experts, tokens = gates_in.shape
    owned = weights[0].shape[1] // HEAD
    image = pl.program_id(0)
    first = image == 0
    task = tid[micro, image]
    width = router.shape[0] // 2
    tasks = width // experts
    span = owned * HEAD
    mine = dev[0]
    rows = expert_rows(experts, tokens)

    grad_sent = jnp.zeros(slope_in.shape, F32)
    for part in sent_parts:
        grad_sent = grad_sent + part[...].astype(F32)
    planes = gate_parts[0][...].astype(F32)
    for part in gate_parts[1:]:
        planes = planes + part[...].astype(F32)
    columns = planes.shape[1] // LANES
    chunks = get_planes(planes, image_count * tokens, experts, columns)
    per = tokens // LANES
    grad_gates = jnp.zeros((experts, tokens), F32)
    for i in range(image_count):
        cells = [three_sum(c, experts) for c in chunks[i * per : (i + 1) * per]]
        grad_gates = jnp.where(image == i, jnp.concatenate(cells, axis=1), grad_gates)
    scaled_two, inverse_two, normed_two = norm_forward(res[...], norms[2:3], norms[3:4])
    chosen = (slots[0] < NOWHERE).astype(F32)
    table, gain_mlp = table_slope(tables[experts : 2 * experts, :], task, tasks)
    logits = to_tasks(gate_backward(probs_mlp[...], chosen, grad_gates, table), task, tasks)
    grad_two = grad_sent + mm_tn(logits, router[width:], EXACT)
    add_to(grad_router, slice(width, 2 * width), mm(logits, normed_two, EXACT), first)
    grad, gain, shift = norm_backward(grad_two, scaled_two, inverse_two, norms[2:3])
    add_to(grad_norm, slice(2, 3), gain, first)
    add_to(grad_norm, slice(3, 4), shift, first)
    resid_slope = slope_in[...] + grad
    slope_one[...] = resid_slope
    branch = resid_slope.astype(BF16)

    _, _, normed = norm_forward(emb[...], norms[0:1], norms[1:2])
    low = normed.astype(BF16)
    for r in range(peers):
        at_r = slice(r * span, (r + 1) * span)
        q_t[at_r, :] = mm_nt(weights[r][0], low).astype(BF16).astype(F32)
        d_t[at_r, :] = mm_nt(weights[r][1], branch).astype(BF16).astype(F32)
        add_to(grad_att, (r, 1), mm(mix_in[0, at_r, :], branch), first)
    fill_keys(kv_in, kvs, kv_t)
    dkv[...] = jnp.zeros(dkv.shape, F32)
    dq_t[...] = jnp.zeros(dq_t.shape, F32)
    dgate[...] = jnp.zeros(dgate.shape, F32)
    blocks = [(r, e, (r * owned + e) * HEAD) for r in range(peers) for e in range(owned)]
    blank = jnp.zeros((HEAD, tokens), BF16)

    def one_pick(k, carry):
        pick = picks[0, pl.ds(k, 1), :]
        query = jnp.zeros((HEAD, tokens), F32)
        down = jnp.zeros((HEAD, tokens), F32)
        for r, e, at in blocks:
            here = pick == (mine ^ r) * owned + e
            query = query + jnp.where(here, q_t[at : at + HEAD, :], 0.0)
            down = down + jnp.where(here, d_t[at : at + HEAD, :], 0.0)
        gate = jnp.sum(jnp.where(rows == pick, gates_in[...], 0.0), axis=0, keepdims=True)
        query_low, down_low = query.astype(BF16), down.astype(BF16)
        scores = mm(kvs[...], jnp.concatenate([(query * HEAD ** (-0.5)).astype(BF16), blank], axis=0))
        probs = jnp.exp(scores - lse[pl.ds(k, 1), :])
        slope = mm(kvs[...], jnp.concatenate([blank, down_low], axis=0))
        delta = jnp.sum(probs * slope, axis=0, keepdims=True)
        gated = probs * gate
        weighted = gated.astype(BF16)
        grad_scores = (gated * (slope - delta) * HEAD ** (-0.5)).astype(BF16)
        joint = jnp.concatenate([grad_scores, weighted], axis=1)
        other = jnp.concatenate(
            [
                jnp.concatenate([query_low, blank], axis=0),
                jnp.concatenate([blank, down_low], axis=0),
            ],
            axis=1,
        )
        dkv[...] = dkv[...] + mm_nt(joint, other)
        dq = mm(kv_t[:HEAD, :], grad_scores)
        for r, e, at in blocks:
            here = pick == (mine ^ r) * owned + e
            dq_t[at : at + HEAD, :] = dq_t[at : at + HEAD, :] + jnp.where(here, dq, 0.0)
        dgate[...] = dgate[...] + jnp.where(rows == pick, delta, 0.0)
        return carry

    lax.fori_loop(0, picks.shape[1], one_pick, 0)
    for r in range(peers):
        block = dkv[r * tokens : (r + 1) * tokens, :].astype(BF16)
        kv_outs[r][...] = block

    table, gain_att = table_slope(tables[:experts, :], task, tasks)
    mutual[...] = jnp.broadcast_to(gain_att + gain_mlp, mutual.shape)
    chosen = picked_hot(picks[0], experts)
    logits = to_tasks(gate_backward(probs_att[...], chosen, dgate[...], table), task, tasks)
    grad_one = mm_tn(logits, router[0:width], EXACT)
    add_to(grad_router, slice(0, width), mm(logits, normed, EXACT), first)
    for r in range(peers):
        block = dq_t[r * span : (r + 1) * span, :].astype(BF16)
        grad_one = grad_one + mm_tn(block, weights[r][0])
        add_to(grad_att, (r, 0), mm(block, low), first)
    normed_slope[...] = grad_one


def last_kernel(parts, *refs):
    patches, emb, slope_one, normed_slope = refs[:4]
    kv_parts = refs[4 : 4 + parts]
    keyval_w, norms = refs[4 + parts : 6 + parts]
    grad_patch, grad_keyval, grad_norm = refs[6 + parts :]
    first = pl.program_id(0) == 0
    scaled, inverse, normed = norm_forward(emb[...], norms[0:1], norms[1:2])
    grad_kv = jnp.zeros(kv_parts[0].shape, F32)
    for part in kv_parts:
        grad_kv = grad_kv + part[...].astype(F32)
    grad_kv = grad_kv.astype(BF16)
    add_to(grad_keyval, ..., mm_tn(grad_kv, normed.astype(BF16)), first)
    slope = normed_slope[...] + mm_nt(grad_kv, keyval_w[...].astype(BF16))
    grad, gain, shift = norm_backward(slope, scaled, inverse, norms[0:1])
    add_to(grad_norm, slice(0, 1), gain, first)
    add_to(grad_norm, slice(1, 2), shift, first)
    add_to(grad_patch, ..., mm_tn(patches[0, 0], (slope_one[...] + grad).astype(BF16)), first)


def pack_kernel(peers, micros, dense_rows, dev, *refs):
    names = 8
    values = []
    for n in range(names):
        value = refs[n][...]
        for m in range(1, micros):
            value = value + refs[m * names + n][...]
        values.append(value)
    head, patch, keyval, router, one, two, three, attention = values
    odd = refs[micros * names]
    evens = refs[micros * names + 1 : -1]
    dense = refs[-1]
    at = 0
    for value in (head, patch, keyval):
        dense[at : at + value.shape[0], :] = value.astype(BF16)
        at += value.shape[0]
    rest = [router, one[0:2], two[2:4], three[0:2]]
    pad = dense_rows - at - router.shape[0] - 6
    if pad:
        rest.append(jnp.zeros((pad, dense.shape[1]), F32))
    dense[at:, :] = jnp.concatenate(rest, axis=0).astype(BF16)
    share = dense_rows // peers
    model = dense.shape[1]
    for r in range(peers):
        start = pl.multiple_of((dev[0] ^ r) * share, 16)
        rows = dense[pl.ds(start, share), :]
        owned_rows = attention[r].reshape(-1, model).astype(BF16)
        if r % 2:
            odd[r // 2, :share] = rows
            odd[r // 2, share:] = owned_rows
        else:
            evens[r // 2][0, :share] = rows
            evens[r // 2][0, share:] = owned_rows


def halves_kernel(parts, place, *refs):
    keep, send, total = refs[parts:]
    value = refs[0][0].astype(F32)
    for part in refs[1:parts]:
        value = value + part[0].astype(F32)
    total[...] = value.astype(BF16)
    rows = keep.shape[0]
    keep[...] = total[pl.ds(pl.multiple_of(place[0] * rows, 16), rows), :]
    send[...] = total[pl.ds(pl.multiple_of((1 - place[0]) * rows, 16), rows), :]


def share_sum_kernel(dense_rows, place, shares, outs, squares):
    count, rows, width = shares.shape
    value = shares[0].astype(F32)
    for r in range(1, count):
        value = value + shares[r].astype(F32)
    low = value.astype(BF16)
    for r in range(count):
        outs[r] = low
    value = low.astype(F32)
    value = value * value
    both = jnp.sum(value, axis=0, keepdims=True)
    if dense_rows:
        start = (place[0] * count + place[1]) * rows
        row = lax.broadcasted_iota(jnp.int32, (rows, width), 0) + start
        dense = jnp.sum(jnp.where(row < dense_rows, value, 0.0), axis=0, keepdims=True)
    else:
        dense = jnp.zeros((1, width), F32)
    spots = lax.broadcasted_iota(jnp.int32, (8, LANES), 0) * LANES + lanes_of((8, LANES))
    own = jnp.sum(both - dense, axis=1, keepdims=True)
    dense = jnp.sum(dense, axis=1, keepdims=True)
    squares[...] = jnp.where(spots == 2, own, 0.0) + jnp.where(spots == 3, dense, 0.0)


def join_halves_kernel(dense_rows, place, own, other, dense, rest, total):
    rows = own.shape[0]
    total[pl.ds(pl.multiple_of(place[0] * rows, 16), rows), :] = own[...]
    total[pl.ds(pl.multiple_of((1 - place[0]) * rows, 16), rows), :] = other[...]
    dense[...] = total[:dense_rows, :]
    rest[...] = total[dense_rows:, :]


def clip_factor(sums, other_sums, limit):
    total = sums[0:1, :] + other_sums[0:1, :]
    own, dense = total[:, 2:3], total[:, 3:4]
    norm = jnp.sqrt(own + dense)
    return jnp.minimum(1.0, limit / norm), norm, jnp.sqrt(own), total


def adam_step(weight, first, second, gradient, rate, factor, scales):
    gradient = gradient * factor
    moment = BETA_ONE * first + (1.0 - BETA_ONE) * gradient
    square = BETA_TWO * second + ((1.0 - BETA_TWO) * gradient) * gradient
    step = (moment * (rate * scales[0])) / (jnp.sqrt(square * scales[1]) + EPSILON)
    return weight * (1.0 - rate * DECAY) - step, moment, square


def adam_kernel(rate, limit, place, scales, *refs):
    own, other, sums, other_sums, weight, first, second = refs[:7]
    factor = clip_factor(sums, other_sums, limit)[0]
    gradient = jnp.where(pl.program_id(0) == place[0], own[...], other[...]).astype(F32)
    news = adam_step(weight[0, 0], first[0, 0], second[0, 0], gradient, rate, factor, scales)
    for ref, new in zip(refs[-3:], news):
        ref[0, 0] = new


def adam_dense_kernel(peers, rates, limit, tasks, count_row, dev, scales, *refs):
    pieces, attention = refs[:peers], refs[peers]
    sums, other_sums, counts, mutual = refs[peers + 1 : peers + 5]
    states = [refs[peers + 5 + 3 * n : peers + 8 + 3 * n] for n in range(6)]
    outs = [refs[peers + 23 + 3 * n : peers + 26 + 3 * n] for n in range(6)]
    scalars, dense = refs[-2:]
    factor, norm, own_norm, total = clip_factor(sums, other_sums, limit)
    lane = lanes_of((1, LANES))
    ratio = total / jnp.where(lane < tasks, counts[count_row : count_row + 1, :], 1.0)
    loss = jnp.sum(jnp.where(lane < tasks, ratio, 0.0), axis=1, keepdims=True)
    loss = loss - MI_WEIGHT * mutual[0:1, 0:1]
    lane = lanes_of(scalars.shape)
    scalars[...] = jnp.where(lane == 0, loss, jnp.where(lane == 1, norm, own_norm))
    share = pieces[0].shape[0]
    for r in range(peers):
        dense[pl.ds(pl.multiple_of((dev[0] ^ r) * share, 16), share), :] = pieces[r][...]

    def update(n, index, gradient):
        olds = [ref[index] for ref in states[n]]
        news = adam_step(*olds, gradient, rates[n], factor, scales)
        for ref, new in zip(outs[n], news):
            ref[index] = new

    outputs = states[0][0].shape[1]
    step = 2 * LANES
    for left in range(0, outputs, step):
        block = dense[left : left + step, :].astype(F32).T
        update(0, (slice(None), slice(left, left + step)), block)
    at = outputs
    rows = states[1][0].shape[0]
    update(1, ..., dense[at : at + rows, :].astype(F32))
    at += rows
    width = states[2][0].shape[1]
    update(2, ..., dense[at : at + width, :].astype(F32).T)
    at += width
    rest = dense[at:, :].astype(F32)
    rows = states[3][0].shape[0]
    update(3, ..., rest[:rows])
    update(4, ..., rest[rows : rows + states[4][0].shape[0]])
    width = states[5][0].shape[2]
    for n in range(2):
        update(5, n, attention[n * width : (n + 1) * width, :].astype(F32).T)


def whole(array):
    rank = len(array.shape)
    return pl.BlockSpec(array.shape, lambda *_: (0,) * rank, pipeline_mode=pl.Buffered(1))


def kept_out(shape):
    rank = len(shape)
    return pl.BlockSpec(shape, lambda *_: (0,) * rank)


def shape_of(shape, dtype):
    return jax.ShapeDtypeStruct(shape, dtype)


def call(kernel, grid, scalars, inputs, outputs, scratch, cost, name):
    spec = pltpu.PrefetchScalarGridSpec(
        num_scalar_prefetch=len(scalars),
        grid=grid,
        in_specs=[s for _, s in inputs],
        out_specs=[s for _, s in outputs],
        scratch_shapes=scratch,
    )
    return pl.pallas_call(
        kernel,
        grid_spec=spec,
        out_shape=[o for o, _ in outputs],
        cost_estimate=pl.CostEstimate(
            flops=int(cost[0]), bytes_accessed=int(cost[1]), transcendentals=0
        ),
        name=name,
    )(*scalars, *[a for a, _ in inputs])


def swap(value, axis, mask):
    size = lax.axis_size(axis)
    return lax.ppermute(value, axis, [(i, i ^ mask) for i in range(size)])


def bits_of(axis):
    return [1 << b for b in range(lax.axis_size(axis).bit_length() - 1)]


def gather_direct(value):
    return [value] + [swap(value, "expert", r) for r in range(1, lax.axis_size("expert"))]


def scatter_direct(pieces):
    return [pieces[0]] + [swap(pieces[r], "expert", r) for r in range(1, len(pieces))]


def across(value):
    rest = [swap(value, "expert", r) for r in range(2, lax.axis_size("expert"), 2)]
    return rest + [swap(value, "expert", 1)]


def beside(value, came):
    rest = came[:-1]
    return [swap(block, "expert", 1) for block in rest]


def ordered(value, came, more):
    out = [value, came[-1]]
    for block, other in zip(came[:-1], more):
        out += [block, other]
    return out


def gather_pieces(value):
    came = across(value)
    return ordered(value, came, beside(value, came))


def after(value, *anchors):
    return lax.optimization_barrier((value,) + anchors)[0]


class Hops:
    def __init__(self, value, axes):
        self.value = value
        self.steps = [(axis, bit) for axis in axes for bit in bits_of(axis)]
        self.came = []

    def start(self):
        if self.steps:
            self.came = [swap(self.value, *self.steps.pop(0))]

    def land(self, came):
        if self.came:
            self.value = self.value + came[-1]
            self.came = []
        self.start()

    def finish(self):
        while self.came or self.steps:
            self.land(self.came)
        return self.value


def along_z(value):
    size = lax.axis_size("dp")
    groups = [[i for i in range(size) if i % 2 == low] for low in range(2)]
    return lax.all_to_all(
        value, "dp", split_axis=0, concat_axis=0, axis_index_groups=groups, tiled=True
    )


def local(
    patches,
    routes,
    masks,
    targets,
    task_ids,
    step_count,
    patch_weight,
    patch_moment,
    patch_square,
    keyval_weight,
    keyval_moment,
    keyval_square,
    router_weight,
    router_moment,
    router_square,
    norm_weight,
    norm_moment,
    norm_square,
    head_weight,
    head_moment,
    head_square,
    attention_weight,
    attention_moment,
    attention_square,
    expert_weight,
    expert_moment,
    expert_square,
):
    peers = lax.axis_size("expert")
    half_peers = peers // 2
    micros, images, patch_count, patch_in = patches.shape
    _, _, _, _, tasks, top = routes.shape
    owned = expert_weight.shape[0]
    experts = owned * peers
    model, hidden = expert_weight.shape[2:]
    tokens = images * patch_count
    capacity = max(2, tokens * top // experts)
    pixels = masks.shape[3]
    outputs = targets.shape[3]
    pair_width = 2 * HEAD
    span = owned * HEAD
    keys = peers * patch_count
    head_rows = peers * span
    extra = extra_rows(tokens, experts, model)
    long = tokens + extra
    far = lax.axis_size("dp") // 2
    dev = lax.axis_index("expert").astype(jnp.int32).reshape(1)
    spot = lax.axis_index("dp").astype(jnp.int32)
    place = jnp.stack([spot & 1, spot >> 1])
    router_rows = router_weight.T
    router_count = router_rows.shape[0]
    routes_lanes = jnp.transpose(routes, (0, 1, 3, 4, 5, 2))
    attention_own = jnp.transpose(attention_weight, (0, 2, 1)).astype(BF16)
    attention = gather_direct(attention_own)

    order = [task_ids, dev]

    def settle(*values):
        out = lax.optimization_barrier((order[0], order[1]) + values)
        order[:] = out[:2]
        return list(out[2:])

    def settle_groups(*groups):
        out = settle(*[value for group in groups for value in group])
        back = []
        for group in groups:
            back.append(out[: len(group)])
            out = out[len(group) :]
        return back

    token_block = pl.BlockSpec((patch_count, model), lambda i, *_: (i, 0))
    expert_block = pl.BlockSpec((experts, patch_count), lambda i, *_: (0, i))
    kv_block = pl.BlockSpec((patch_count, pair_width), lambda i, *_: (i, 0))
    top_block = pl.BlockSpec((top, patch_count), lambda i, *_: (0, i))

    def micro_block(shape, micro):
        return pl.BlockSpec((1,) + shape, lambda i, *_, m=micro: (m,) + (0,) * (len(shape) - 1) + (i,))

    def image_block(array, micro):
        return pl.BlockSpec((1, 1) + array.shape[2:], lambda i, *_, m=micro: (m, i, 0, 0))

    def pieces_out(rows, width):
        return [(shape_of((rows, width), BF16), kept_out((rows, width)))] * peers


    def one_whole(array, lead):
        return pl.BlockSpec(
            (pl.Squeezed(), patch_count, array.shape[2]), lambda i, *_: (lead, i, 0)
        )

    state = [SimpleNamespace() for _ in range(micros)]

    def run_routing():
        return call(
            route_kernel,
            (micros,),
            (order[0],),
            [
                (
                    routes_lanes,
                    pl.BlockSpec((1,) + routes_lanes.shape[1:], lambda m, *_: (m, 0, 0, 0, 0, 0)),
                ),
                (masks, pl.BlockSpec((1,) + masks.shape[1:], lambda m, *_: (m, 0, 0, 0))),
            ],
            [
                (
                    shape_of((micros, top, tokens), jnp.int32),
                    pl.BlockSpec((1, top, tokens), lambda m, *_: (m, 0, 0)),
                ),
                (
                    shape_of((micros, experts, tokens), jnp.int32),
                    pl.BlockSpec((1, experts, tokens), lambda m, *_: (m, 0, 0)),
                ),
                (
                    shape_of((micros, tasks, pixels), F32),
                    pl.BlockSpec((1, tasks, pixels), lambda m, *_: (m, 0, 0)),
                ),
            ],
            [],
            (micros * tokens * tokens * 32, masks.size * 4),
            "routing",
        )

    def run_embed(micro):
        s = state[micro]
        s.emb, kv, s.gates_att, s.probs_att = call(
            partial(embed_kernel, micro),
            (images,),
            (order[0],),
            [
                (patches, image_block(patches, micro)),
                (patch_weight, whole(patch_weight)),
                (keyval_weight, whole(keyval_weight)),
                (norm_weight, whole(norm_weight)),
                (router_rows, whole(router_rows)),
                (picks, micro_block((top, patch_count), micro)),
            ],
            [
                (shape_of((tokens, model), F32), token_block),
                (shape_of((tokens, pair_width), BF16), kv_block),
                (shape_of((experts, tokens), F32), expert_block),
                (shape_of((experts, tokens), F32), expert_block),
            ],
            [],
            (2 * tokens * model * (patch_in + pair_width), tokens * (2 * patch_in + 4 * model) + patch_weight.size * 4),
            "embedding",
        )
        return kv

    attention_flops = 2 * top * tokens * keys * HEAD * 8

    def run_attend(micro):
        s = state[micro]
        s.res, s.sent, s.mix, s.lse, s.probs_mlp = call(
            partial(attend_kernel, micro, peers, capacity, images),
            (images,),
            (order[0], order[1]),
            [(s.emb, token_block)]
            + [(piece, kv_block) for piece in s.kv]
            + [
                (picks, micro_block((top, patch_count), micro)),
                (s.gates_att, expert_block),
                (slots, micro_block((experts, patch_count), micro)),
            ]
            + [(piece, whole(piece)) for piece in attention]
            + [
                (norm_weight, whole(norm_weight)),
                (router_rows, whole(router_rows)),
                (s.probs_att, expert_block),
                (counts, whole(counts)),
            ],
            [
                (shape_of((tokens, model), F32), token_block),
                (shape_of((long, model), BF16), kept_out((long, model))),
                (
                    shape_of((images, head_rows, patch_count), BF16),
                    pl.BlockSpec((1, head_rows, patch_count), lambda i, *_: (i, 0, 0)),
                ),
                (shape_of((top, tokens), F32), top_block),
                (shape_of((experts, tokens), F32), expert_block),
            ],
            [
                pltpu.VMEM((2 * experts, LANES), F32),
                pltpu.VMEM((keys, pair_width), BF16),
                pltpu.VMEM((pair_width, keys), BF16),
                pltpu.VMEM((head_rows, patch_count), F32),
                pltpu.VMEM((head_rows, patch_count), F32),
            ],
            (attention_flops, tokens * model * 12),
            "attention",
        )

    moe_flops = 2 * owned * peers * capacity * model * (2 * hidden + 2 * tokens)
    expert_bytes = expert_weight.size * 2
    odd_shape = (half_peers, tokens, model)

    slots_total = peers * capacity
    by_slot = shape_of((owned, slots_total, model), BF16)
    slot_block = pl.BlockSpec((1, slots_total, model), lambda e, *_: (e, 0, 0))

    def run_experts(micro):
        s = state[micro]
        results = call(
            partial(moe_forward_kernel, peers, owned, experts),
            (owned,),
            (order[1],),
            [(piece, whole(piece)) for piece in s.tokens]
            + [(expert_low, pl.BlockSpec((1, 2, model, hidden), lambda e, *_: (e, 0, 0, 0)))],
            [(shape_of(odd_shape, BF16), kept_out(odd_shape))]
            + [(shape_of((tokens, model), BF16), kept_out((tokens, model)))] * half_peers
            + [
                (by_slot, slot_block),
                (by_slot, slot_block),
                (shape_of((4 * experts, LANES), F32), kept_out((4 * experts, LANES))),
            ],
            [
                pltpu.VMEM((slots_total, tokens), BF16),
                pltpu.VMEM((slots_total, 1), F32),
                pltpu.VMEM((peers, tokens, model), F32),
            ],
            (moe_flops, expert_bytes + 4 * peers * tokens * model),
            "experts",
        )
        s.kept, s.made, s.statistics = results[-3:]
        return results[0], list(results[1 : 1 + half_peers])

    count_row = 2 * experts

    def run_head(micro):
        s = state[micro]
        s.slope, slope_low, s.grad_head, s.norm_three, s.squares = call(
            partial(head_kernel, micro, len(s.moe), count_row),
            (images,),
            (order[0],),
            [(s.res, token_block)]
            + [
                (part, token_block if lead is None else one_whole(part, lead))
                for part, lead in s.moe
            ]
            + [
                (targets, image_block(targets, micro)),
                (masks, image_block(masks, micro)),
                (norm_weight, whole(norm_weight)),
                (head_weight, whole(head_weight)),
                (statistics, whole(statistics)),
            ],
            [
                (shape_of((tokens, model), F32), token_block),
                (shape_of((tokens, model), BF16), token_block),
                (shape_of((outputs, model), F32), kept_out((outputs, model))),
                (shape_of((8, model), F32), kept_out((8, model))),
                (shape_of((8, LANES), F32), kept_out((8, LANES))),
            ],
            [],
            (6 * tokens * model * outputs, tokens * (outputs * 2 + pixels * 4 + 12 * model)),
            "head",
        )
        return slope_low

    extra_block = pl.BlockSpec(
        (extra, model), lambda *_: (tokens // extra, 0), pipeline_mode=pl.Buffered(1)
    )

    def run_experts_back(micro, e, prior):
        s = state[micro]
        more_grads, more_tokens = prior is not None, e > 0
        split = micro == micros - 1
        one_block = pl.BlockSpec(
            (1, slots_total, model), lambda *_: (e, 0, 0), pipeline_mode=pl.Buffered(1)
        )
        weight_block = pl.BlockSpec(
            (1, 2, model, hidden), lambda *_: (e, 0, 0, 0), pipeline_mode=pl.Buffered(1)
        )
        inputs = (
            [(piece, whole(piece)) for piece in s.slopes]
            + [(piece, extra_block) for piece in s.tokens]
            + [(s.kept, one_block), (s.made, one_block), (expert_low, weight_block)]
        )
        if more_grads:
            inputs.append((prior, whole(prior)))
        if more_tokens:
            inputs += [(piece, whole(piece)) for piece in s.pieces]
        grad_shape = (2, model, hidden)
        grads_out = (
            [(shape_of(grad_shape[1:], BF16), kept_out(grad_shape[1:]))] * 2
            if split
            else [(shape_of(grad_shape, BF16), kept_out(grad_shape))]
        )
        results = call(
            partial(
                moe_backward_kernel,
                peers,
                e,
                owned,
                experts,
                more_grads,
                more_tokens,
                split,
            ),
            (1,),
            (order[1], place),
            inputs,
            pieces_out(long, model) + grads_out,
            [
                pltpu.VMEM((slots_total, tokens), BF16),
                pltpu.VMEM((slots_total, 1), F32),
                pltpu.VMEM((slots_total, model), BF16),
            ],
            (3 * moe_flops // owned, expert_bytes * 5 // owned + 4 * peers * tokens * model),
            "experts_back",
        )
        s.pieces = list(results[:peers])
        return list(results[peers:])

    def run_attend_back(micro):
        s = state[micro]
        parts = s.sent_parts
        results = call(
            partial(back_kernel, micro, peers, peers, images),
            (images,),
            (order[0], order[1]),
            [(s.slope, token_block)]
            + [(part, token_block) for part in parts]
            + [
                (part, pl.BlockSpec((extra, model), lambda *_: (tokens // extra, 0)))
                for part in parts
            ]
            + [
                (s.res, token_block),
                (s.emb, token_block),
                (s.probs_mlp, expert_block),
                (slots, micro_block((experts, patch_count), micro)),
                (tables, whole(tables)),
            ]
            + [(piece, kv_block) for piece in s.kv]
            + [
                (picks, micro_block((top, patch_count), micro)),
                (s.gates_att, expert_block),
                (s.probs_att, expert_block),
                (s.lse, top_block),
            ]
            + [(piece, whole(piece)) for piece in attention]
            + [
                (s.mix, pl.BlockSpec((1, head_rows, patch_count), lambda i, *_: (i, 0, 0))),
                (norm_weight, whole(norm_weight)),
                (router_rows, whole(router_rows)),
            ],
            [
                (shape_of((tokens, model), F32), token_block),
                (shape_of((tokens, model), F32), token_block),
            ]
            + [(shape_of((tokens, pair_width), BF16), kv_block)] * peers
            + [
                (shape_of((peers, 2, span, model), F32), kept_out((peers, 2, span, model))),
                (shape_of((router_count, model), F32), kept_out((router_count, model))),
                (shape_of((8, model), F32), kept_out((8, model))),
                (shape_of((8, LANES), F32), kept_out((8, LANES))),
            ],
            [
                pltpu.VMEM((keys, pair_width), BF16),
                pltpu.VMEM((pair_width, keys), BF16),
                pltpu.VMEM((head_rows, patch_count), F32),
                pltpu.VMEM((head_rows, patch_count), F32),
                pltpu.VMEM((keys, pair_width), F32),
                pltpu.VMEM((head_rows, patch_count), F32),
                pltpu.VMEM((experts, patch_count), F32),
            ],
            (attention_flops * 3, tokens * model * 30),
            "attention_back",
        )
        s.slope_one, s.normed_slope = results[:2]
        s.grad_att, s.grad_router, s.norm_two, s.mutual = results[2 + peers :]
        return list(results[2 : 2 + peers])

    def run_last(micro):
        s = state[micro]
        s.grad_patch, s.grad_keyval, s.norm_one = call(
            partial(last_kernel, peers),
            (images,),
            (),
            [
                (patches, image_block(patches, micro)),
                (s.emb, token_block),
                (s.slope_one, token_block),
                (s.normed_slope, token_block),
            ]
            + [(part, kv_block) for part in s.kv_parts]
            + [(keyval_weight, whole(keyval_weight)), (norm_weight, whole(norm_weight))],
            [
                (shape_of((patch_in, model), F32), kept_out((patch_in, model))),
                (shape_of((pair_width, model), F32), kept_out((pair_width, model))),
                (shape_of((8, model), F32), kept_out((8, model))),
            ],
            [],
            (2 * tokens * model * (patch_in + 2 * pair_width), tokens * model * 20),
            "embedding_back",
        )

    first, second = state
    came_w = across(attention_own)
    picks, slots, count_rows = run_routing()
    (picks,) = settle(picks)
    counts = jnp.zeros((8, LANES), F32).at[0, :tasks].set(jnp.sum(count_rows, axis=(0, 2)))
    hops = Hops(counts, ("dp",))
    hops.start()
    kv = run_embed(0)
    (first.emb, kv), came_w, came = settle_groups([first.emb, kv], came_w, hops.came)
    more_w = beside(attention_own, came_w)
    first.kv = gather_direct(kv)
    hops.land(came)
    kv = run_embed(1)
    (second.emb, kv), more_w, first.kv, came = settle_groups(
        [second.emb, kv], more_w, first.kv, hops.came
    )
    attention = ordered(attention_own, came_w, more_w)
    second.kv = gather_direct(kv)
    hops.land(came)

    counts = hops.value
    run_attend(0)
    (first.res, first.sent), second.kv, came = settle_groups(
        [first.res, first.sent], second.kv, hops.came
    )
    hops.land(came)
    counts = hops.finish()
    came_first = across(first.sent)
    run_attend(1)
    (second.res, second.sent), came_first = settle_groups(
        [second.res, second.sent], came_first
    )
    more_first = beside(first.sent, came_first)
    came_second = across(second.sent)
    expert_low = after(expert_weight, order[1]).astype(BF16)
    (expert_low,), more_first = settle_groups([expert_low], more_first)
    first.tokens = ordered(first.sent, came_first, more_first)

    first_odd, first_evens = run_experts(0)
    (first.kept, first_odd), came_second = settle_groups([first.kept, first_odd], came_second)
    more_second = beside(second.sent, came_second)
    first_crossed = swap(first_odd, "expert", 1)
    (more_second,) = settle_groups(more_second)
    second.tokens = ordered(second.sent, came_second, more_second)
    second_odd, second_evens = run_experts(1)
    second.kept, second_odd, first_crossed = settle(second.kept, second_odd, first_crossed)

    def onward(evens, crossed):
        out = []
        for n in range(1, half_peers):
            pair = (evens[n].astype(F32) + crossed[n].astype(F32)).astype(BF16)
            out.append(swap(pair, "expert", 2 * n))
        return out

    def arrived(evens, crossed, rest):
        return [(evens[0], None), (crossed, 0)] + [(part, None) for part in rest]

    first_rest = onward(first_evens, first_crossed)
    second_crossed = swap(second_odd, "expert", 1)
    statistics = second.statistics
    hops = Hops(first.statistics + statistics, ("dp",))
    (second_crossed,) = settle(second_crossed)
    second_rest = onward(second_evens, second_crossed)
    hops.start()
    (first_rest,) = settle_groups(first_rest)
    first.moe = arrived(first_evens, first_crossed, first_rest)

    first_low = run_head(0)
    (first.slope, first_low), second_rest, came = settle_groups(
        [first.slope, first_low], second_rest, hops.came
    )
    second.moe = arrived(second_evens, second_crossed, second_rest)
    came_first = across(first_low)
    hops.land(came)
    second_low = run_head(1)
    (second.slope, second_low), came_first, came = settle_groups(
        [second.slope, second_low], came_first, hops.came
    )
    more_first = beside(first_low, came_first)
    second.slopes = gather_direct(second_low)
    hops.land(came)
    (more_first,) = settle_groups(more_first)
    first.slopes = ordered(first_low, came_first, more_first)

    def small_call(kernel, scalars, inputs, shapes, scratch, name):
        return call(
            kernel,
            (1,),
            scalars,
            [(a, whole(a)) for a in inputs],
            [(s, kept_out(s.shape)) for s in shapes],
            scratch,
            (0, 1000),
            name,
        )

    exchanged = [dev]

    def exchange(value):
        value = along_z(after(value, exchanged[0], order[1]))
        exchanged[0] = value
        return value

    def cut_shares(keep, came):
        rows, width = keep.shape
        total = (keep.astype(F32) + came.astype(F32)).astype(BF16)
        return exchange(total.reshape(far, rows // far, width))

    def sum_shares(moved, dense_rows):
        return small_call(
            partial(share_sum_kernel, dense_rows),
            (place,),
            [moved],
            [shape_of(moved.shape, BF16), shape_of((8, LANES), F32)],
            [],
            "share_sum",
        )

    prior = run_experts_back(0, 0, None)
    first.pieces, second.slopes, prior, came = settle_groups(
        first.pieces, second.slopes, prior, hops.came
    )
    hops.land(came)
    keep_first, send_first = run_experts_back(1, 0, prior[0])
    second.pieces, (keep_first, send_first), came = settle_groups(
        second.pieces, [keep_first, send_first], hops.came
    )
    hops.land(came)
    tables = hops.finish()
    came_x_first = swap(send_first, "dp", 1)
    prior = run_experts_back(0, 1, None)
    first.pieces, prior = settle_groups(first.pieces, prior)
    first.sent_parts = scatter_direct(first.pieces)
    keep_second, send_second = run_experts_back(1, 1, prior[0])
    (keep_second, send_second), second.pieces, first.sent_parts, (came_x_first, tables) = (
        settle_groups(
            [keep_second, send_second],
            second.pieces,
            first.sent_parts,
            [came_x_first, tables],
        )
    )
    came_x_second = swap(send_second, "dp", 1)
    second.sent_parts = scatter_direct(second.pieces)
    square_parts = [s.squares for s in state]
    shares_first = cut_shares(keep_first, came_x_first)

    kv_parts = run_attend_back(0)
    kv_parts, second.sent_parts, (came_x_second, shares_first) = settle_groups(
        kv_parts, second.sent_parts, [came_x_second, shares_first]
    )
    first.kv_parts = scatter_direct(kv_parts)
    summed_first, squares = sum_shares(shares_first, 0)
    square_parts.append(squares)
    shares_second = cut_shares(keep_second, came_x_second)
    (summed_first,) = settle(summed_first)
    kv_parts = run_attend_back(1)
    kv_parts, first.kv_parts, (shares_second,) = settle_groups(
        kv_parts, first.kv_parts, [shares_second]
    )
    second.kv_parts = scatter_direct(kv_parts)
    own_first = exchange(summed_first).reshape(model, hidden)
    summed_second, squares = sum_shares(shares_second, 0)
    square_parts.append(squares)
    (summed_second,) = settle(summed_second)
    run_last(0)
    (first.norm_one,), second.kv_parts = settle_groups([first.norm_one], second.kv_parts)
    run_last(1)
    (second.norm_one,) = settle(second.norm_one)

    packed_parts = []
    for s in state:
        packed_parts += [s.grad_head, s.grad_patch, s.grad_keyval, s.grad_router]
        packed_parts += [s.norm_one, s.norm_two, s.norm_three, s.grad_att]
    used_rows = outputs + patch_in + pair_width + router_count + 6
    dense_rows = -(-used_rows // 256) * 256
    dense_share = dense_rows // peers
    all_rows = dense_share + 2 * span
    packed = small_call(
        partial(pack_kernel, peers, micros, dense_rows),
        (order[1],),
        packed_parts,
        [shape_of((half_peers, all_rows, model), BF16)]
        + [shape_of((1, all_rows, model), BF16)] * half_peers,
        [pltpu.VMEM((dense_rows, model), BF16)],
        "pack",
    )
    packed = settle(*packed)
    odd, evens = packed[0], packed[1:]
    crossed = swap(odd, "expert", 1)
    (crossed,) = settle(crossed)
    pairs = [
        (evens[n].astype(F32) + crossed[n : n + 1].astype(F32)).astype(BF16)
        for n in range(1, half_peers)
    ]
    pairs = settle(*pairs)
    lead_parts = [evens[0], crossed] + [
        swap(pair, "expert", 2 * n + 2) for n, pair in enumerate(pairs)
    ]
    own_first = after(own_first, order[1])
    other_first = swap(own_first, "dp", 1)
    own_second = exchange(summed_second).reshape(model, hidden)
    lead_parts = settle(*lead_parts)
    parts = [(part, 0) for part in lead_parts]
    half_shape = shape_of((all_rows // 2, model), BF16)
    keep, send = call(
        partial(halves_kernel, len(parts)),
        (1,),
        (place,),
        [(part, pl.BlockSpec((1, all_rows, model), lambda *_, lead=lead: (lead, 0, 0))) for part, lead in parts],
        [(half_shape, kept_out(half_shape.shape))] * 2,
        [pltpu.VMEM((all_rows, model), BF16)],
        (0, 8 * all_rows * model),
        "halves",
    )
    keep, send = settle(keep, send)
    came = swap(send, "dp", 1)
    came, other_first, own_second = settle(came, other_first, own_second)
    shares, squares = sum_shares(cut_shares(keep, came), dense_share)
    sums = squares
    for part in square_parts:
        sums = sums + part
    sums, shares = settle(sums, shares)
    hops = Hops(sums, ("dp", "expert"))
    hops.start()
    own = exchange(shares).reshape(all_rows // 2, model)
    (own,), came = settle_groups([own], hops.came)
    other = swap(own, "dp", 1)
    hops.land(came)
    (other,), came = settle_groups([other], hops.came)
    other_second = swap(after(own_second, order[1]), "dp", 1)
    dense_part, attention_part = small_call(
        partial(join_halves_kernel, dense_share),
        (place,),
        [own, other],
        [shape_of((dense_share, model), BF16), shape_of((2 * span, model), BF16)],
        [pltpu.VMEM((all_rows, model), BF16)],
        "join_halves",
    )
    came_quarters = across(dense_part)
    hops.land(came)
    came_quarters, came = settle_groups(came_quarters, hops.came)
    quarters = ordered(dense_part, came_quarters, beside(dense_part, came_quarters))
    hops.land(came)
    while len(hops.steps):
        hops.land(hops.came)
    sums, last_came = hops.value, hops.came[0]

    total_params = (
        patch_weight.size
        + keyval_weight.size
        + router_weight.size
        + norm_weight.size
        + head_weight.size
        + (attention_weight.size + expert_weight.size) * peers
    )
    limit = CLIP_UNIT * math.sqrt(total_params)
    step_value = step_count[0].astype(F32)
    scales = jnp.stack(
        [1.0 / (1.0 - jnp.power(BETA_ONE, step_value)), 1.0 / (1.0 - jnp.power(BETA_TWO, step_value))]
    )
    block_rows = model // 4
    expert_results = None
    for e, (own, other) in enumerate([(own_first, other_first), (own_second, other_second)]):
        block = pl.BlockSpec((1, 1, block_rows, hidden), lambda w, b, *_, e=e: (e, w, b, 0))
        grad_block = pl.BlockSpec((block_rows, hidden), lambda w, b, *_: (b, 0))
        inputs = [own, other, sums, last_came, expert_weight, expert_moment, expert_square]
        specs = [grad_block, grad_block, whole(sums), whole(last_came), block, block, block]
        aliases = {}
        if expert_results is not None:
            aliases = {2 + len(inputs) + n: n for n in range(3)}
            inputs += list(expert_results)
            specs += [pl.BlockSpec(memory_space=pl.ANY)] * 3
        expert_results = pl.pallas_call(
            partial(adam_kernel, RATES[6], limit),
            grid_spec=pltpu.PrefetchScalarGridSpec(
                num_scalar_prefetch=2,
                grid=(2, model // block_rows),
                in_specs=specs,
                out_specs=[block] * 3,
            ),
            out_shape=[shape_of(expert_weight.shape, F32)] * 3,
            input_output_aliases=aliases,
            cost_estimate=pl.CostEstimate(
                flops=expert_weight.size * 20 // owned,
                bytes_accessed=expert_weight.size * 26 // owned,
                transcendentals=0,
            ),
            name="adam",
        )(place, scales, *inputs)
    dense_states = [
        head_weight,
        head_moment,
        head_square,
        patch_weight,
        patch_moment,
        patch_square,
        keyval_weight,
        keyval_moment,
        keyval_square,
        router_rows,
        router_moment.T,
        router_square.T,
        norm_weight,
        norm_moment,
        norm_square,
        attention_weight,
        attention_moment,
        attention_square,
    ]
    dense_results = small_call(
        partial(
            adam_dense_kernel,
            peers,
            (RATES[4], RATES[0], RATES[1], RATES[2], RATES[3], RATES[5]),
            limit,
            tasks,
            count_row,
        ),
        (order[1], scales),
        quarters
        + [attention_part, sums, last_came, statistics, state[0].mutual]
        + dense_states,
        [shape_of(a.shape, F32) for a in dense_states] + [shape_of((8, LANES), F32)],
        [pltpu.VMEM((dense_rows, model), BF16)],
        "adam_dense",
    )
    new_head, new_patch, new_keyval, new_router, new_norm, new_attention = [
        list(dense_results[3 * n : 3 * n + 3]) for n in range(6)
    ]
    new_router = [a.T for a in new_router]
    return tuple(
        [dense_results[18][0, n] for n in range(3)]
        + new_patch
        + new_keyval
        + new_router
        + new_norm
        + new_head
        + new_attention
        + list(expert_results)
    )


def solution(mesh):
    tokens = P(None, "dp", "expert", None)
    by_columns = P(None, None, "expert")
    by_expert = P("expert", None, None, None)
    same = P()
    placed = (
        (tokens, P(None, "dp", "expert", None, None, None), tokens, tokens, P(None, "dp"), same)
        + (same,) * 15
        + (by_columns,) * 3
        + (by_expert,) * 3
    )
    return jax.shard_map(
        local,
        mesh=mesh,
        in_specs=placed,
        out_specs=(same,) * 18 + (by_columns,) * 3 + (by_expert,) * 3,
        check_vma=False,
    )
```

```python
from functools import partial
import math
from types import SimpleNamespace

import jax
import jax.numpy as jnp
from jax import lax
from jax.experimental import pallas as pl
from jax.experimental.pallas import tpu as pltpu
from jax.sharding import PartitionSpec as P

HEAD = 64
NORM_EPS = 1e-06
MI_WEIGHT = 0.5
CLIP_UNIT = 3e-07
BETA_ONE = 0.9
BETA_TWO = 0.999
EPSILON = 1e-08
RATES = (0.02, 0.02, 0.02, 0.3, 0.02, 1.2, 0.02)
DECAY = 0.05
F32 = jnp.float32
BF16 = jnp.bfloat16
NOWHERE = 1 << 20
LANES = 128
GELU_A = 0.044715
GELU_C = math.sqrt(2.0 / math.pi)


def mm(left, right, precision=None):
    return lax.dot_general(
        left, right, (((1,), (0,)), ((), ())), precision=precision, preferred_element_type=F32
    )


def mm_nt(left, right, precision=None):
    return lax.dot_general(
        left, right, (((1,), (1,)), ((), ())), precision=precision, preferred_element_type=F32
    )


def mm_tn(left, right, precision=None):
    return lax.dot_general(
        left, right, (((0,), (0,)), ((), ())), precision=precision, preferred_element_type=F32
    )


def two_terms(values):
    high = values.astype(BF16)
    return high, (values - high.astype(F32)).astype(BF16)


def fine(product, left, right, axis):
    left_high, left_low = two_terms(left)
    right_high, right_low = two_terms(right)
    both = product(jnp.concatenate([left_high, left_low], axis=axis), right_high)
    rest = product(left_high, right_low)
    rows = rest.shape[0]
    if both.shape[0] == rows:
        return both + rest
    return both[:rows] + both[rows:] + rest


def small_tn(left, right):
    left_high, left_low = two_terms(left)
    right_high, right_low = two_terms(right)
    return mm_tn(
        jnp.concatenate([left_high, left_low, left_high], axis=0),
        jnp.concatenate([right_high, right_high, right_low], axis=0),
    )


def norm_forward(values, gain, shift):
    centred = values - jnp.mean(values, axis=-1, keepdims=True)
    inverse = lax.rsqrt(jnp.mean(centred * centred, axis=-1, keepdims=True) + NORM_EPS)
    scaled = centred * inverse
    return scaled, inverse, scaled * gain + shift


def norm_backward(slope, scaled, inverse, gain):
    inner = slope * gain
    grad = inverse * (
        inner
        - jnp.mean(inner, axis=-1, keepdims=True)
        - scaled * jnp.mean(inner * scaled, axis=-1, keepdims=True)
    )
    return grad, jnp.sum(slope * scaled, axis=0, keepdims=True), jnp.sum(slope, axis=0, keepdims=True)


def expert_rows(experts, tokens):
    return lax.broadcasted_iota(jnp.int32, (experts, tokens), 0)


def by_task(rows, task, experts):
    out = rows[:experts]
    for other in range(1, rows.shape[0] // experts):
        out = jnp.where(task == other, rows[other * experts : (other + 1) * experts], out)
    return out


def to_tasks(rows, task, tasks):
    return jnp.concatenate([jnp.where(task == t, rows, 0.0) for t in range(tasks)], axis=0)


def router_forward(router_rows, normed, task, experts):
    logits = by_task(fine(mm_nt, router_rows, normed, 0), task, experts)
    powers = jnp.exp(logits - jnp.max(logits, axis=0, keepdims=True))
    return powers / jnp.sum(powers, axis=0, keepdims=True)


def gate_forward(probs, chosen):
    picked = probs * chosen
    return picked / jnp.sum(picked, axis=0, keepdims=True)


def gate_backward(probs, chosen, grad_gates, grad_probs):
    total = jnp.sum(probs * chosen, axis=0, keepdims=True)
    gates = probs * chosen / total
    inner = chosen / total * (grad_gates - jnp.sum(grad_gates * gates, axis=0, keepdims=True))
    inner = inner + grad_probs
    return probs * (inner - jnp.sum(probs * inner, axis=0, keepdims=True))


def picked_hot(picks, experts):
    rows = expert_rows(experts, picks.shape[1])
    out = jnp.zeros(rows.shape, F32)
    for k in range(picks.shape[0]):
        out = out + (picks[k : k + 1, :] == rows).astype(F32)
    return out


def add_to(ref, index, value, first):
    @pl.when(first)
    def _():
        ref[index] = value

    @pl.when(jnp.logical_not(first))
    def _():
        ref[index] = ref[index] + value


def route_kernel(tid, routes, masks, picks, slots, counts):
    micro = pl.program_id(0)
    _, images, _, tasks, _, patch_count = routes.shape
    experts = slots.shape[1]
    tokens = images * patch_count
    chosen = []
    pixel_rows = [jnp.zeros((1, masks.shape[3]), F32) for _ in range(tasks)]
    for image in range(images):
        task = tid[micro, image]
        att, mlp = routes[0, image, 0, 0], routes[0, image, 1, 0]
        for t in range(1, tasks):
            att = jnp.where(task == t, routes[0, image, 0, t], att)
            mlp = jnp.where(task == t, routes[0, image, 1, t], mlp)
        picks[0, :, image * patch_count : (image + 1) * patch_count] = att
        chosen.append(picked_hot(mlp, experts))
        column = jnp.sum(masks[0, image].astype(F32), axis=0, keepdims=True)
        for t in range(tasks):
            pixel_rows[t] = pixel_rows[t] + jnp.where(task == t, column, 0.0)
    chosen = jnp.concatenate(chosen, axis=1)
    earlier = lax.broadcasted_iota(jnp.int32, (tokens, tokens), 0) < lax.broadcasted_iota(
        jnp.int32, (tokens, tokens), 1
    )
    before = mm(chosen.astype(BF16), earlier.astype(F32).astype(BF16))
    slots[0] = jnp.where(chosen > 0.0, before.astype(jnp.int32), NOWHERE)
    counts[0] = jnp.concatenate(pixel_rows, axis=0)


def embed_kernel(micro, tid, patches, patch_w, keyval_w, norms, router, picks, emb, kv, gates, probs):
    experts = gates.shape[0]
    task = tid[micro, pl.program_id(0)]
    width = router.shape[0] // 2
    embedded = mm(patches[0, 0], patch_w[...].astype(BF16))
    emb[...] = embedded
    _, _, normed = norm_forward(embedded, norms[0:1], norms[1:2])
    kv[...] = mm(normed.astype(BF16), keyval_w[...].astype(BF16)).astype(BF16)
    prob = router_forward(router[0:width], normed, task, experts)
    probs[...] = prob
    gates[...] = gate_forward(prob, picked_hot(picks[0], experts))


def split_planes(values):
    high = values.astype(BF16).astype(F32)
    middle = (values - high).astype(BF16).astype(F32)
    return [high, middle, (values - high - middle).astype(BF16).astype(F32)]


def put_planes(ref, planes, image, token_rows, images):
    patch_count, model = token_rows.shape
    block = jnp.concatenate(planes, axis=0).astype(BF16)
    height = block.shape[0]
    columns, chunks = model // LANES, patch_count // LANES
    rows, base = ref.shape[0], images * patch_count
    for i in range(images):

        @pl.when(image == i)
        def _(i=i):
            ref[i * patch_count : (i + 1) * patch_count, :] = token_rows
            if i == 0:
                ref[base:, :] = jnp.zeros((rows - base, model), BF16)
            for j in range(chunks):
                c = i * chunks + j
                top, left = base + c // columns * height, c % columns * LANES
                ref[top : top + height, left : left + LANES] = block[:, j * LANES : (j + 1) * LANES]


def lanes_of(shape):
    return lax.broadcasted_iota(jnp.int32, shape, 1)


def put_statistics(ref, images, patch_count, values):
    high, middle, rest = split_planes(values)
    block = high + pltpu.roll(middle, 8, 1) + pltpu.roll(rest, 16, 1)
    ref[ref.shape[0] - values.shape[0] :, ref.shape[1] - LANES :] = block.astype(BF16)


def get_statistics(block):
    block = block.astype(F32)
    total = block + pltpu.roll(block, LANES - 8, 1) + pltpu.roll(block, LANES - 16, 1)
    return jnp.where(lanes_of(block.shape) < 8, total, 0.0)


def extra_rows(count, experts, model):
    return -(-(count // LANES) // (model // LANES)) * 4 * experts


def get_planes(block, count, experts, columns):
    height = 4 * experts
    out = []
    for c in range(count // LANES):
        top, left = c // columns * height, c % columns * LANES
        out.append(block[top : top + height, left : left + LANES].astype(F32))
    return out


def three_sum(planes, experts):
    return planes[:experts] + planes[experts : 2 * experts] + planes[2 * experts : 3 * experts]


def fill_keys(pieces, kvs, kv_t):
    rows = pieces[0].shape[0]
    for r, piece in enumerate(pieces):
        block = piece[...]
        kvs[r * rows : (r + 1) * rows, :] = block
        kv_t[:, r * rows : (r + 1) * rows] = block.astype(F32).T.astype(BF16)


def attend_kernel(micro, peers, capacity, images, tid, dev, *refs):
    emb = refs[0]
    kv_in = refs[1 : 1 + peers]
    picks, gates_in, slots = refs[1 + peers : 4 + peers]
    weights = refs[4 + peers : 4 + 2 * peers]
    norms, router = refs[4 + 2 * peers : 6 + 2 * peers]
    probs_att, counts = refs[6 + 2 * peers : 8 + 2 * peers]
    res_out, sent, mix_out, lse, probs_out = refs[8 + 2 * peers : 13 + 2 * peers]
    table, kvs, kv_t, q_t, mix = refs[13 + 2 * peers :]
    experts, tokens = gates_in.shape
    owned = weights[0].shape[1] // HEAD
    task = tid[micro, pl.program_id(0)]
    width = router.shape[0] // 2
    mine = dev[0]
    embedded = emb[...]
    _, _, normed = norm_forward(embedded, norms[0:1], norms[1:2])
    low = normed.astype(BF16)
    span = owned * HEAD
    for r in range(peers):
        q_t[r * span : (r + 1) * span, :] = mm_nt(weights[r][0], low).astype(BF16).astype(F32)
    fill_keys(kv_in, kvs, kv_t)
    mix[...] = jnp.zeros(mix.shape, F32)
    blocks = [(r, e, (r * owned + e) * HEAD) for r in range(peers) for e in range(owned)]
    rows = expert_rows(experts, tokens)
    blank = jnp.zeros((HEAD, tokens), BF16)

    def one_pick(k, carry):
        pick = picks[0, pl.ds(k, 1), :]
        query = jnp.zeros((HEAD, tokens), F32)
        for r, e, at in blocks:
            here = pick == (mine ^ r) * owned + e
            query = query + jnp.where(here, q_t[at : at + HEAD, :], 0.0)
        gate = jnp.sum(jnp.where(rows == pick, gates_in[...], 0.0), axis=0, keepdims=True)
        scores = mm(kvs[...], jnp.concatenate([(query * HEAD ** (-0.5)).astype(BF16), blank], axis=0))
        top = jnp.max(scores, axis=0, keepdims=True)
        powers = jnp.exp(scores - top)
        total = jnp.sum(powers, axis=0, keepdims=True)
        lse[pl.ds(k, 1), :] = top + jnp.log(total)
        weighted = (powers * (gate / total)).astype(BF16)
        out = mm(kv_t[HEAD:, :], weighted)
        for r, e, at in blocks:
            here = pick == (mine ^ r) * owned + e
            mix[at : at + HEAD, :] = mix[at : at + HEAD, :] + jnp.where(here, out, 0.0)
        return carry

    lax.fori_loop(0, picks.shape[1], one_pick, 0, unroll=True)
    resid = embedded
    for r in range(peers):
        block = mix[r * span : (r + 1) * span, :].astype(BF16)
        mix_out[0, r * span : (r + 1) * span, :] = block
        resid = resid + mm_tn(block, weights[r][1])
    res_out[...] = resid
    _, _, normed_two = norm_forward(resid, norms[2:3], norms[3:4])
    prob = router_forward(router[width:], normed_two, task, experts)
    probs_out[...] = prob
    both = jnp.concatenate([probs_att[...], prob], axis=0)
    lane = lanes_of((2 * experts, LANES))
    per_task = jnp.where(lane == task, jnp.sum(both, axis=1, keepdims=True), 0.0)
    add_to(table, ..., per_task, pl.program_id(0) == 0)
    slot = slots[0]
    gates = gate_forward(prob, (slot < NOWHERE).astype(F32))
    places = jnp.minimum(slot, capacity).astype(F32)
    low_two = normed_two.astype(BF16)
    put_planes(sent, split_planes(gates) + [places], pl.program_id(0), low_two, images)

    @pl.when(pl.program_id(0) == images - 1)
    def _():
        rest = jnp.zeros((2 * experts - 8, LANES), F32)
        block = jnp.concatenate([table[...], counts[...], rest], axis=0)
        put_statistics(sent, images, tokens, block)


def read_planes(block, experts, count):
    chunks = get_planes(block, count, experts, block.shape[1] // LANES)
    gates = jnp.concatenate([three_sum(chunk, experts) for chunk in chunks], axis=1)
    return jnp.concatenate([chunk[3 * experts :] for chunk in chunks], axis=1), gates


def one_row(rows, at):
    index = expert_rows(rows.shape[0], rows.shape[1])
    return jnp.sum(jnp.where(index == at, rows, 0.0), axis=0, keepdims=True)


def loss_scale(counts, task):
    own = jnp.where(lanes_of(counts.shape) == task, counts, 0.0)
    return 1.0 / jnp.sum(own, axis=1, keepdims=True)


def dispatch(blocks, at, experts, count, hot, gate, scale=None):
    capacity = hot.shape[0] // len(blocks)
    places = lax.broadcasted_iota(jnp.int32, (capacity, count), 0).astype(F32)
    for r, block in enumerate(blocks):
        slots, gates = read_planes(block, experts, count)
        here = one_row(slots, at) == places
        rows = slice(r * capacity, (r + 1) * capacity)
        hot[rows, :] = here.astype(F32).astype(BF16)
        own = one_row(gates, at)
        if scale is not None:
            own = own * scale
        gate[rows, :] = jnp.sum(jnp.where(here, own, 0.0), axis=1, keepdims=True)


def moe_forward_kernel(peers, owned, experts, dev, *refs):
    half = peers // 2
    arrays = refs[:peers]
    weights, odd = refs[peers], refs[peers + 1]
    evens = refs[peers + 2 : peers + 2 + half]
    kept, made, statistics, hot, gate, back = refs[peers + 2 + half :]
    e = pl.program_id(0)
    count = hot.shape[1]
    capacity = hot.shape[0] // peers
    dispatch([a[count:, :] for a in arrays], dev[0] * owned + e, experts, count, hot, gate)
    for r in range(peers):
        rows = slice(r * capacity, (r + 1) * capacity)
        kept[0, rows, :] = mm(hot[rows, :], arrays[r][:count, :]).astype(BF16)
    before = mm(kept[0], weights[0, 0])
    bent = jnp.tanh(before * (GELU_C + GELU_C * GELU_A * (before * before)))
    halved = 0.5 * before
    out = mm_nt((halved + halved * bent).astype(BF16), weights[0, 1])
    made[0] = out.astype(BF16)
    weighted = (out * gate[...]).astype(BF16)
    for r in range(peers):
        rows = slice(r * capacity, (r + 1) * capacity)
        value = mm_tn(hot[rows, :], weighted[rows, :])
        if owned > 1:
            add_to(back, r, value, e == 0)

    @pl.when(e == owned - 1)
    def _():
        for r in range(peers):
            piece = back[r].astype(BF16) if owned > 1 else value.astype(BF16)
            if r % 2:
                odd[r // 2] = piece
            else:
                evens[r // 2][...] = piece
        rows = statistics.shape[0]
        block = jnp.zeros(statistics.shape, F32)
        for a in arrays:
            block = block + get_statistics(a[a.shape[0] - rows :, a.shape[1] - LANES :])
        statistics[...] = block


def head_kernel(micro, parts, tasks, tid, *refs):
    res = refs[0]
    moe = refs[1 : 1 + parts]
    targets, masks, norms, head_w = refs[1 + parts : 5 + parts]
    slope_out, slope_low, grad_head, grad_norm, squares = refs[5 + parts :]
    image = pl.program_id(0)
    task = tid[micro, image]
    resid = res[...]
    for part in moe:
        resid = resid + part[...].astype(F32)
    scaled, inverse, normed = norm_forward(resid, norms[4:5], norms[5:6])
    low = normed.astype(BF16)
    head_low = head_w[...].astype(BF16)
    pred = mm(low, head_low)
    mask = masks[0, 0].astype(F32)
    pixels = mask.shape[1]
    depth_on = jnp.where(task == 0, 1.0, 0.0)
    normal_on = jnp.where(task == 0, 0.0, 1.0)
    slopes = []
    total = jnp.zeros((1, pixels), F32)
    for group in range(4):
        on = depth_on if group == 0 else normal_on
        at = group * pixels
        gap = pred[:, at : at + pixels] - targets[0, 0, :, at : at + pixels].astype(F32)
        masked = mask * gap
        total = total + on * jnp.sum(masked * gap, axis=0, keepdims=True)
        slopes.append((masked * (2.0 * on)).astype(BF16))
    slope = jnp.concatenate(slopes, axis=1)
    first = image == 0
    spots = lax.broadcasted_iota(jnp.int32, (8, LANES), 0) * LANES + lanes_of((8, LANES))
    add_to(squares, ..., jnp.where(spots == task, jnp.sum(total, axis=1, keepdims=True), 0.0), first)
    add_to(grad_head, ..., mm_tn(slope, low), first)
    grad, gain, shift = norm_backward(mm_nt(slope, head_low), scaled, inverse, norms[4:5])
    both = jnp.concatenate([gain, shift], axis=0)
    for t in range(tasks):
        add_to(grad_norm, slice(2 * t, 2 * t + 2), jnp.where(task == t, both, 0.0), first)
    slope_out[...] = grad
    slope_low[...] = grad.astype(BF16)


def moe_backward_kernel(shape, more_grads, more_tokens, split, tid, dev, place, *refs):
    peers, micro, images, local_expert, owned, experts = shape
    refs = list(refs)

    def take(count):
        out = refs[:count]
        del refs[:count]
        return out

    slopes, extras = take(peers), take(peers)
    kept, made, weights, tables = take(4)
    if more_grads:
        (prior_grads,) = take(1)
    if more_tokens:
        prior_pieces = take(peers)
    outs = take(peers)
    grads_out = take(2 if split else 1)
    hot, gate, plain = take(3)
    count, model = slopes[0].shape
    capacity = hot.shape[0] // peers
    at = dev[0] * owned + local_expert
    counts = tables[2 * experts : 2 * experts + 1, :]
    per_image = count // images
    scale = jnp.concatenate(
        [
            jnp.broadcast_to(loss_scale(counts, tid[micro, image]), (1, per_image))
            for image in range(images)
        ],
        axis=1,
    )
    dispatch([extra[...] for extra in extras], at, experts, count, hot, gate, scale)
    gate_slopes = []
    for r in range(peers):
        rows = slice(r * capacity, (r + 1) * capacity)
        value = mm(hot[rows, :], slopes[r][...])
        gate_slopes.append(jnp.sum(value * made[0, rows, :].astype(F32), axis=1, keepdims=True))
        plain[rows, :] = (value * gate[rows, :]).astype(BF16)
    before = mm(kept[0], weights[0, 0])
    hidden = mm(plain[...], weights[0, 1])
    cubic = GELU_C * GELU_A * (before * before)
    bent = jnp.tanh(before * (GELU_C + cubic))
    middle = 0.5 + 0.5 * bent
    inner = (before * middle).astype(BF16)
    bend = middle + (middle - middle * bent) * (before * (GELU_C + 3.0 * cubic))
    slope = (hidden * bend).astype(BF16)
    entry = mm_tn(kept[0], slope)
    leave = mm_tn(plain[...], inner)
    if more_grads:
        entry = entry + prior_grads[0].astype(F32)
        leave = leave + prior_grads[1].astype(F32)
    if split:
        flip = place[0] == 0
        grads_out[0][...] = jnp.where(flip, entry, leave).astype(BF16)
        grads_out[1][...] = jnp.where(flip, leave, entry).astype(BF16)
    else:
        grads_out[0][0] = entry.astype(BF16)
        grads_out[0][1] = leave.astype(BF16)
    received = mm_nt(slope, weights[0, 0]).astype(BF16)
    columns, chunks, height = model // LANES, count // LANES, 4 * experts
    rows_of = expert_rows(experts, count)
    lane = lanes_of((capacity, LANES))
    for r in range(peers):
        rows = slice(r * capacity, (r + 1) * capacity)
        tokens_back = mm_tn(hot[rows, :], received[rows, :])
        terms = split_planes(gate_slopes[r])
        terms = jnp.where(lane == 0, terms[0], jnp.where(lane == 1, terms[1], terms[2]))
        terms = jnp.where(lane < 3, terms, 0.0).astype(BF16)
        gate_row = jnp.sum(mm_tn(terms, hot[rows, :])[:8, :], axis=0, keepdims=True) * scale
        planes = split_planes(jnp.where(rows_of == at, gate_row, 0.0))
        block = jnp.concatenate(planes + [jnp.zeros((experts, count), F32)], axis=0)
        lines = []
        for line in range(-(-chunks // columns)):
            cells = [
                block[:, c * LANES : (c + 1) * LANES]
                if c < chunks
                else jnp.zeros((height, LANES), F32)
                for c in range(line * columns, (line + 1) * columns)
            ]
            lines.append(jnp.concatenate(cells, axis=1))
        piece = jnp.concatenate([tokens_back] + lines, axis=0)
        if more_tokens:
            piece = piece + prior_pieces[r][...].astype(F32)
        outs[r][...] = piece.astype(BF16)


def table_slope(table, task, tasks):
    lane = lanes_of(table.shape)
    valid = lane < tasks
    table = jnp.where(valid, table, 0.0)
    total = jnp.sum(jnp.sum(table, axis=1, keepdims=True), axis=0, keepdims=True)
    share = table / total
    by_expert = jnp.sum(share, axis=1, keepdims=True)
    by_task_sum = jnp.sum(share, axis=0, keepdims=True)
    safe = jnp.where(valid, share, 1.0)
    gain = jnp.log(safe) - jnp.log(jnp.where(valid, by_task_sum, 1.0)) - jnp.log(by_expert)
    gain = jnp.where(valid, gain, 0.0)
    mean = jnp.sum(jnp.sum(gain * share, axis=1, keepdims=True), axis=0, keepdims=True)
    slope = -MI_WEIGHT * (gain - mean) / total
    return jnp.sum(jnp.where(lane == task, slope, 0.0), axis=1, keepdims=True), mean


def back_kernel(micro, peers, parts, image_count, tid, dev, *refs):
    slope_in = refs[0]
    sent_parts = refs[1 : 1 + parts]
    gate_parts = refs[1 + parts : 1 + 2 * parts]
    at = 1 + 2 * parts
    res, emb, probs_mlp, slots = refs[at : at + 4]
    at += 4
    tables = refs[at]
    kv_in = refs[at + 1 : at + 1 + peers]
    at += 1 + peers
    picks, gates_in, probs_att, lse = refs[at : at + 4]
    weights = refs[at + 4 : at + 4 + peers]
    at += 4 + peers
    mix_in, norms, router = refs[at : at + 3]
    slope_one, normed_slope = refs[at + 3 : at + 5]
    kv_outs = refs[at + 5 : at + 5 + peers]
    at += 5 + peers
    grad_att, grad_router, grad_norm, mutual = refs[at : at + 4]
    kvs, kv_t, q_t, d_t, dkv, dq_t, dgate = refs[at + 4 :]
    experts, tokens = gates_in.shape
    owned = weights[0].shape[1] // HEAD
    image = pl.program_id(0)
    first = image == 0
    task = tid[micro, image]
    width = router.shape[0] // 2
    tasks = width // experts
    span = owned * HEAD
    mine = dev[0]
    rows = expert_rows(experts, tokens)

    grad_sent = jnp.zeros(slope_in.shape, F32)
    for part in sent_parts:
        grad_sent = grad_sent + part[...].astype(F32)
    planes = gate_parts[0][...].astype(F32)
    for part in gate_parts[1:]:
        planes = planes + part[...].astype(F32)
    columns = planes.shape[1] // LANES
    chunks = get_planes(planes, image_count * tokens, experts, columns)
    per = tokens // LANES
    grad_gates = jnp.zeros((experts, tokens), F32)
    for i in range(image_count):
        cells = [three_sum(c, experts) for c in chunks[i * per : (i + 1) * per]]
        grad_gates = jnp.where(image == i, jnp.concatenate(cells, axis=1), grad_gates)
    scaled_two, inverse_two, normed_two = norm_forward(res[...], norms[2:3], norms[3:4])
    chosen = (slots[0] < NOWHERE).astype(F32)
    table, gain_mlp = table_slope(tables[experts : 2 * experts, :], task, tasks)
    logits = to_tasks(gate_backward(probs_mlp[...], chosen, grad_gates, table), task, tasks)
    grad_two = grad_sent + small_tn(logits, router[width:])
    add_to(grad_router, slice(width, 2 * width), fine(mm, logits, normed_two, 0), first)
    grad, gain, shift = norm_backward(grad_two, scaled_two, inverse_two, norms[2:3])
    add_to(grad_norm, slice(2, 3), gain, first)
    add_to(grad_norm, slice(3, 4), shift, first)
    scale = loss_scale(tables[2 * experts : 2 * experts + 1, :], task)
    resid_slope = slope_in[...] * scale + grad
    slope_one[...] = resid_slope
    branch = resid_slope.astype(BF16)

    _, _, normed = norm_forward(emb[...], norms[0:1], norms[1:2])
    low = normed.astype(BF16)
    for r in range(peers):
        at_r = slice(r * span, (r + 1) * span)
        q_t[at_r, :] = mm_nt(weights[r][0], low).astype(BF16).astype(F32)
        d_t[at_r, :] = mm_nt(weights[r][1], branch).astype(BF16).astype(F32)
        add_to(grad_att, (r, 1), mm(mix_in[0, at_r, :], branch), first)
    fill_keys(kv_in, kvs, kv_t)
    dkv[...] = jnp.zeros(dkv.shape, F32)
    dq_t[...] = jnp.zeros(dq_t.shape, F32)
    dgate[...] = jnp.zeros(dgate.shape, F32)
    blocks = [(r, e, (r * owned + e) * HEAD) for r in range(peers) for e in range(owned)]
    blank = jnp.zeros((HEAD, tokens), BF16)

    def one_pick(k, carry):
        pick = picks[0, pl.ds(k, 1), :]
        query = jnp.zeros((HEAD, tokens), F32)
        down = jnp.zeros((HEAD, tokens), F32)
        for r, e, at in blocks:
            here = pick == (mine ^ r) * owned + e
            query = query + jnp.where(here, q_t[at : at + HEAD, :], 0.0)
            down = down + jnp.where(here, d_t[at : at + HEAD, :], 0.0)
        gate = jnp.sum(jnp.where(rows == pick, gates_in[...], 0.0), axis=0, keepdims=True)
        query_low, down_low = query.astype(BF16), down.astype(BF16)
        scores = mm(kvs[...], jnp.concatenate([(query * HEAD ** (-0.5)).astype(BF16), blank], axis=0))
        probs = jnp.exp(scores - lse[pl.ds(k, 1), :])
        slope = mm(kvs[...], jnp.concatenate([blank, down_low], axis=0))
        delta = jnp.sum(probs * slope, axis=0, keepdims=True)
        gated = probs * gate
        weighted = gated.astype(BF16)
        grad_scores = (gated * (slope - delta) * HEAD ** (-0.5)).astype(BF16)
        joint = jnp.concatenate([grad_scores, weighted], axis=1)
        other = jnp.concatenate(
            [
                jnp.concatenate([query_low, blank], axis=0),
                jnp.concatenate([blank, down_low], axis=0),
            ],
            axis=1,
        )
        dkv[...] = dkv[...] + mm_nt(joint, other)
        dq = mm(kv_t[:HEAD, :], grad_scores)
        for r, e, at in blocks:
            here = pick == (mine ^ r) * owned + e
            dq_t[at : at + HEAD, :] = dq_t[at : at + HEAD, :] + jnp.where(here, dq, 0.0)
        dgate[...] = dgate[...] + jnp.where(rows == pick, delta, 0.0)
        return carry

    lax.fori_loop(0, picks.shape[1], one_pick, 0, unroll=True)
    for r in range(peers):
        block = dkv[r * tokens : (r + 1) * tokens, :].astype(BF16)
        kv_outs[r][...] = block

    table, gain_att = table_slope(tables[:experts, :], task, tasks)
    mutual[...] = jnp.broadcast_to(gain_att + gain_mlp, mutual.shape)
    chosen = picked_hot(picks[0], experts)
    logits = to_tasks(gate_backward(probs_att[...], chosen, dgate[...], table), task, tasks)
    grad_one = small_tn(logits, router[0:width])
    add_to(grad_router, slice(0, width), fine(mm, logits, normed, 0), first)
    for r in range(peers):
        block = dq_t[r * span : (r + 1) * span, :].astype(BF16)
        grad_one = grad_one + mm_tn(block, weights[r][0])
        add_to(grad_att, (r, 0), mm(block, low), first)
    normed_slope[...] = grad_one


def last_kernel(parts, *refs):
    patches, emb, slope_one, normed_slope = refs[:4]
    kv_parts = refs[4 : 4 + parts]
    keyval_w, norms = refs[4 + parts : 6 + parts]
    grad_patch, grad_keyval, grad_norm = refs[6 + parts :]
    first = pl.program_id(0) == 0
    scaled, inverse, normed = norm_forward(emb[...], norms[0:1], norms[1:2])
    grad_kv = jnp.zeros(kv_parts[0].shape, F32)
    for part in kv_parts:
        grad_kv = grad_kv + part[...].astype(F32)
    grad_kv = grad_kv.astype(BF16)
    add_to(grad_keyval, ..., mm_tn(grad_kv, normed.astype(BF16)), first)
    slope = normed_slope[...] + mm_nt(grad_kv, keyval_w[...].astype(BF16))
    grad, gain, shift = norm_backward(slope, scaled, inverse, norms[0:1])
    add_to(grad_norm, slice(0, 1), gain, first)
    add_to(grad_norm, slice(1, 2), shift, first)
    add_to(grad_patch, ..., mm_tn(patches[0, 0], (slope_one[...] + grad).astype(BF16)), first)


def pack_kernel(peers, micros, dense_rows, sizes, dev, *refs):
    names = 8
    values = []
    for n in range(names):
        value = refs[n][...]
        for m in range(1, micros):
            value = value + refs[m * names + n][...]
        values.append(value)
    head, patch, keyval, router, one, two, three, attention = values
    tables, odd = refs[micros * names : micros * names + 2]
    evens = refs[micros * names + 2 : -1]
    dense = refs[-1]
    tasks, pixels, count_row = sizes
    scales = [loss_scale(tables[count_row : count_row + 1, :], t) for t in range(tasks)]
    head = jnp.concatenate([head[:pixels] * scales[0], head[pixels:] * scales[1]], axis=0)
    three = sum(three[2 * t : 2 * t + 2] * scales[t] for t in range(tasks))
    at = 0
    for value in (head, patch, keyval):
        dense[at : at + value.shape[0], :] = value.astype(BF16)
        at += value.shape[0]
    rest = [router, one[0:2], two[2:4], three]
    pad = dense_rows - at - router.shape[0] - 6
    if pad:
        rest.append(jnp.zeros((pad, dense.shape[1]), F32))
    dense[at:, :] = jnp.concatenate(rest, axis=0).astype(BF16)
    share = dense_rows // peers
    model = dense.shape[1]
    for r in range(peers):
        start = pl.multiple_of((dev[0] ^ r) * share, 16)
        rows = dense[pl.ds(start, share), :]
        owned_rows = attention[r].reshape(-1, model).astype(BF16)
        if r % 2:
            odd[r // 2, :share] = rows
            odd[r // 2, share:] = owned_rows
        else:
            evens[r // 2][0, :share] = rows
            evens[r // 2][0, share:] = owned_rows


def halves_kernel(parts, place, *refs):
    keep, send, total = refs[parts:]
    value = refs[0][0].astype(F32)
    for part in refs[1:parts]:
        value = value + part[0].astype(F32)
    total[...] = value.astype(BF16)
    rows = keep.shape[0]
    keep[...] = total[pl.ds(pl.multiple_of(place[0] * rows, 16), rows), :]
    send[...] = total[pl.ds(pl.multiple_of((1 - place[0]) * rows, 16), rows), :]


def share_sum_kernel(dense_rows, place, shares, outs, squares):
    count, rows, width = shares.shape
    value = shares[0].astype(F32)
    for r in range(1, count):
        value = value + shares[r].astype(F32)
    low = value.astype(BF16)
    for r in range(count):
        outs[r] = low
    value = low.astype(F32)
    value = value * value
    both = jnp.sum(value, axis=0, keepdims=True)
    if dense_rows:
        start = (place[0] * count + place[1]) * rows
        row = lax.broadcasted_iota(jnp.int32, (rows, width), 0) + start
        dense = jnp.sum(jnp.where(row < dense_rows, value, 0.0), axis=0, keepdims=True)
    else:
        dense = jnp.zeros((1, width), F32)
    spots = lax.broadcasted_iota(jnp.int32, (8, LANES), 0) * LANES + lanes_of((8, LANES))
    own = jnp.sum(both - dense, axis=1, keepdims=True)
    dense = jnp.sum(dense, axis=1, keepdims=True)
    squares[...] = jnp.where(spots == 2, own, 0.0) + jnp.where(spots == 3, dense, 0.0)


def join_halves_kernel(dense_rows, place, own, other, dense, rest, total):
    rows = own.shape[0]
    total[pl.ds(pl.multiple_of(place[0] * rows, 16), rows), :] = own[...]
    total[pl.ds(pl.multiple_of((1 - place[0]) * rows, 16), rows), :] = other[...]
    dense[...] = total[:dense_rows, :]
    rest[...] = total[dense_rows:, :]


def clip_factor(sums, other_sums, limit):
    total = sums[0:1, :] + other_sums[0:1, :]
    own, dense = total[:, 2:3], total[:, 3:4]
    norm = jnp.sqrt(own + dense)
    return jnp.minimum(1.0, limit / norm), norm, jnp.sqrt(own), total


def adam_step(weight, first, second, gradient, rate, factor, scales):
    gradient = gradient * factor
    moment = BETA_ONE * first + (1.0 - BETA_ONE) * gradient
    square = BETA_TWO * second + ((1.0 - BETA_TWO) * gradient) * gradient
    step = (moment * (rate * scales[0])) / (jnp.sqrt(square * scales[1]) + EPSILON)
    return weight * (1.0 - rate * DECAY) - step, moment, square


def adam_kernel(rate, limit, place, scales, *refs):
    own, other, sums, other_sums, weight, first, second = refs[:7]
    factor = clip_factor(sums, other_sums, limit)[0]
    gradient = jnp.where(pl.program_id(0) == place[0], own[...], other[...]).astype(F32)
    news = adam_step(weight[0, 0], first[0, 0], second[0, 0], gradient, rate, factor, scales)
    for ref, new in zip(refs[-3:], news):
        ref[0, 0] = new


def adam_dense_kernel(peers, rates, limit, tasks, count_row, dev, scales, *refs):
    pieces, attention = refs[:peers], refs[peers]
    sums, other_sums, counts, mutual = refs[peers + 1 : peers + 5]
    states = [refs[peers + 5 + 3 * n : peers + 8 + 3 * n] for n in range(6)]
    outs = [refs[peers + 23 + 3 * n : peers + 26 + 3 * n] for n in range(6)]
    scalars, dense = refs[-2:]
    factor, norm, own_norm, total = clip_factor(sums, other_sums, limit)
    lane = lanes_of((1, LANES))
    ratio = total / jnp.where(lane < tasks, counts[count_row : count_row + 1, :], 1.0)
    loss = jnp.sum(jnp.where(lane < tasks, ratio, 0.0), axis=1, keepdims=True)
    loss = loss - MI_WEIGHT * mutual[0:1, 0:1]
    lane = lanes_of(scalars.shape)
    scalars[...] = jnp.where(lane == 0, loss, jnp.where(lane == 1, norm, own_norm))
    share = pieces[0].shape[0]
    for r in range(peers):
        dense[pl.ds(pl.multiple_of((dev[0] ^ r) * share, 16), share), :] = pieces[r][...]

    def update(n, index, gradient):
        olds = [ref[index] for ref in states[n]]
        news = adam_step(*olds, gradient, rates[n], factor, scales)
        for ref, new in zip(outs[n], news):
            ref[index] = new

    outputs = states[0][0].shape[1]
    step = 2 * LANES
    for left in range(0, outputs, step):
        block = dense[left : left + step, :].astype(F32).T
        update(0, (slice(None), slice(left, left + step)), block)
    at = outputs
    rows = states[1][0].shape[0]
    update(1, ..., dense[at : at + rows, :].astype(F32))
    at += rows
    width = states[2][0].shape[1]
    update(2, ..., dense[at : at + width, :].astype(F32).T)
    at += width
    rest = dense[at:, :].astype(F32)
    rows = states[3][0].shape[0]
    update(3, ..., rest[:rows])
    update(4, ..., rest[rows : rows + states[4][0].shape[0]])
    width = states[5][0].shape[2]
    for n in range(2):
        update(5, n, attention[n * width : (n + 1) * width, :].astype(F32).T)


def whole(array):
    rank = len(array.shape)
    return pl.BlockSpec(array.shape, lambda *_: (0,) * rank, pipeline_mode=pl.Buffered(1))


def kept_out(shape):
    rank = len(shape)
    return pl.BlockSpec(shape, lambda *_: (0,) * rank)


def shape_of(shape, dtype):
    return jax.ShapeDtypeStruct(shape, dtype)


def call(kernel, grid, scalars, inputs, outputs, scratch, cost, name, room=None):
    spec = pltpu.PrefetchScalarGridSpec(
        num_scalar_prefetch=len(scalars),
        grid=grid,
        in_specs=[s for _, s in inputs],
        out_specs=[s for _, s in outputs],
        scratch_shapes=scratch,
    )
    return pl.pallas_call(
        kernel,
        grid_spec=spec,
        out_shape=[o for o, _ in outputs],
        cost_estimate=pl.CostEstimate(
            flops=int(cost[0]), bytes_accessed=int(cost[1]), transcendentals=0
        ),
        compiler_params=None if room is None else pltpu.CompilerParams(vmem_limit_bytes=room << 20),
        name=name,
    )(*scalars, *[a for a, _ in inputs])


def swap(value, axis, mask):
    size = lax.axis_size(axis)
    return lax.ppermute(value, axis, [(i, i ^ mask) for i in range(size)])


def bits_of(axis):
    return [1 << b for b in range(lax.axis_size(axis).bit_length() - 1)]


def gather_direct(value):
    return [value] + [swap(value, "expert", r) for r in range(1, lax.axis_size("expert"))]


def scatter_direct(pieces):
    return [pieces[0]] + [swap(pieces[r], "expert", r) for r in range(1, len(pieces))]


def across(value):
    rest = [swap(value, "expert", r) for r in range(2, lax.axis_size("expert"), 2)]
    return rest + [swap(value, "expert", 1)]


def beside(value, came):
    rest = came[:-1]
    return [swap(block, "expert", 1) for block in rest]


def ordered(value, came, more):
    out = [value, came[-1]]
    for block, other in zip(came[:-1], more):
        out += [block, other]
    return out


def gather_pieces(value):
    came = across(value)
    return ordered(value, came, beside(value, came))


def after(value, *anchors):
    return lax.optimization_barrier((value,) + anchors)[0]


class Hops:
    def __init__(self, value, axes):
        self.value = value
        self.steps = [(axis, bit) for axis in axes for bit in bits_of(axis)]
        if len(axes) > 1:
            self.steps.sort(key=lambda step: step == (axes[1], 1))
        self.came = []

    def start(self):
        if self.steps:
            self.came = [swap(self.value, *self.steps.pop(0))]

    def land(self, came):
        if self.came:
            self.value = self.value + came[-1]
            self.came = []
        self.start()

    def finish(self):
        while self.came or self.steps:
            self.land(self.came)
        return self.value


def along_z(value):
    size = lax.axis_size("dp")
    groups = [[i for i in range(size) if i % 2 == low] for low in range(2)]
    return lax.all_to_all(
        value, "dp", split_axis=0, concat_axis=0, axis_index_groups=groups, tiled=True
    )


def local(
    patches,
    routes,
    masks,
    targets,
    task_ids,
    step_count,
    patch_weight,
    patch_moment,
    patch_square,
    keyval_weight,
    keyval_moment,
    keyval_square,
    router_weight,
    router_moment,
    router_square,
    norm_weight,
    norm_moment,
    norm_square,
    head_weight,
    head_moment,
    head_square,
    attention_weight,
    attention_moment,
    attention_square,
    expert_weight,
    expert_moment,
    expert_square,
):
    peers = lax.axis_size("expert")
    half_peers = peers // 2
    micros, images, patch_count, patch_in = patches.shape
    _, _, _, _, tasks, top = routes.shape
    owned = expert_weight.shape[0]
    experts = owned * peers
    model, hidden = expert_weight.shape[2:]
    tokens = images * patch_count
    capacity = max(2, tokens * top // experts)
    pixels = masks.shape[3]
    outputs = targets.shape[3]
    pair_width = 2 * HEAD
    span = owned * HEAD
    keys = peers * patch_count
    head_rows = peers * span
    extra = extra_rows(tokens, experts, model)
    long = tokens + extra
    far = lax.axis_size("dp") // 2
    dev = lax.axis_index("expert").astype(jnp.int32).reshape(1)
    spot = lax.axis_index("dp").astype(jnp.int32)
    place = jnp.stack([spot & 1, spot >> 1])
    router_rows = router_weight.T
    router_count = router_rows.shape[0]
    routes_lanes = jnp.transpose(routes, (0, 1, 3, 4, 5, 2))
    attention_own = jnp.transpose(attention_weight, (0, 2, 1)).astype(BF16)
    attention = gather_direct(attention_own)

    order = [task_ids, dev]

    def settle(*values):
        out = lax.optimization_barrier((order[0], order[1]) + values)
        order[:] = out[:2]
        return list(out[2:])

    def settle_groups(*groups):
        out = settle(*[value for group in groups for value in group])
        back = []
        for group in groups:
            back.append(out[: len(group)])
            out = out[len(group) :]
        return back

    token_block = pl.BlockSpec((patch_count, model), lambda i, *_: (i, 0))
    expert_block = pl.BlockSpec((experts, patch_count), lambda i, *_: (0, i))
    kv_block = pl.BlockSpec((patch_count, pair_width), lambda i, *_: (i, 0))
    top_block = pl.BlockSpec((top, patch_count), lambda i, *_: (0, i))

    def micro_block(shape, micro):
        return pl.BlockSpec((1,) + shape, lambda i, *_, m=micro: (m,) + (0,) * (len(shape) - 1) + (i,))

    def image_block(array, micro):
        return pl.BlockSpec((1, 1) + array.shape[2:], lambda i, *_, m=micro: (m, i, 0, 0))

    def pieces_out(rows, width):
        return [(shape_of((rows, width), BF16), kept_out((rows, width)))] * peers


    def one_whole(array, lead):
        return pl.BlockSpec(
            (pl.Squeezed(), patch_count, array.shape[2]), lambda i, *_: (lead, i, 0)
        )

    state = [SimpleNamespace() for _ in range(micros)]

    def run_routing():
        return call(
            route_kernel,
            (micros,),
            (order[0],),
            [
                (
                    routes_lanes,
                    pl.BlockSpec((1,) + routes_lanes.shape[1:], lambda m, *_: (m, 0, 0, 0, 0, 0)),
                ),
                (masks, pl.BlockSpec((1,) + masks.shape[1:], lambda m, *_: (m, 0, 0, 0))),
            ],
            [
                (
                    shape_of((micros, top, tokens), jnp.int32),
                    pl.BlockSpec((1, top, tokens), lambda m, *_: (m, 0, 0)),
                ),
                (
                    shape_of((micros, experts, tokens), jnp.int32),
                    pl.BlockSpec((1, experts, tokens), lambda m, *_: (m, 0, 0)),
                ),
                (
                    shape_of((micros, tasks, pixels), F32),
                    pl.BlockSpec((1, tasks, pixels), lambda m, *_: (m, 0, 0)),
                ),
            ],
            [],
            (micros * tokens * tokens * 32, masks.size * 4),
            "routing",
        )

    def run_embed(micro):
        s = state[micro]
        s.emb, kv, s.gates_att, s.probs_att = call(
            partial(embed_kernel, micro),
            (images,),
            (order[0],),
            [
                (patches, image_block(patches, micro)),
                (patch_weight, whole(patch_weight)),
                (keyval_weight, whole(keyval_weight)),
                (norm_weight, whole(norm_weight)),
                (router_rows, whole(router_rows)),
                (picks, micro_block((top, patch_count), micro)),
            ],
            [
                (shape_of((tokens, model), F32), token_block),
                (shape_of((tokens, pair_width), BF16), kv_block),
                (shape_of((experts, tokens), F32), expert_block),
                (shape_of((experts, tokens), F32), expert_block),
            ],
            [],
            (2 * tokens * model * (patch_in + pair_width), tokens * (2 * patch_in + 4 * model) + patch_weight.size * 4),
            "embedding",
        )
        return kv

    attention_flops = 2 * top * tokens * keys * HEAD * 8

    def run_attend(micro):
        s = state[micro]
        s.res, s.sent, s.mix, s.lse, s.probs_mlp = call(
            partial(attend_kernel, micro, peers, capacity, images),
            (images,),
            (order[0], order[1]),
            [(s.emb, token_block)]
            + [(piece, kv_block) for piece in s.kv]
            + [
                (picks, micro_block((top, patch_count), micro)),
                (s.gates_att, expert_block),
                (slots, micro_block((experts, patch_count), micro)),
            ]
            + [(piece, whole(piece)) for piece in attention]
            + [
                (norm_weight, whole(norm_weight)),
                (router_rows, whole(router_rows)),
                (s.probs_att, expert_block),
                (counts, whole(counts)),
            ],
            [
                (shape_of((tokens, model), F32), token_block),
                (shape_of((long, model), BF16), kept_out((long, model))),
                (
                    shape_of((images, head_rows, patch_count), BF16),
                    pl.BlockSpec((1, head_rows, patch_count), lambda i, *_: (i, 0, 0)),
                ),
                (shape_of((top, tokens), F32), top_block),
                (shape_of((experts, tokens), F32), expert_block),
            ],
            [
                pltpu.VMEM((2 * experts, LANES), F32),
                pltpu.VMEM((keys, pair_width), BF16),
                pltpu.VMEM((pair_width, keys), BF16),
                pltpu.VMEM((head_rows, patch_count), F32),
                pltpu.VMEM((head_rows, patch_count), F32),
            ],
            (attention_flops, tokens * model * 12),
            "attention",
        )

    moe_flops = 2 * owned * peers * capacity * model * (2 * hidden + 2 * tokens)
    expert_bytes = expert_weight.size * 2
    odd_shape = (half_peers, tokens, model)

    slots_total = peers * capacity
    by_slot = shape_of((owned, slots_total, model), BF16)
    slot_block = pl.BlockSpec((1, slots_total, model), lambda e, *_: (e, 0, 0))

    def run_experts(micro):
        s = state[micro]
        results = call(
            partial(moe_forward_kernel, peers, owned, experts),
            (owned,),
            (order[1],),
            [(piece, whole(piece)) for piece in s.tokens]
            + [(expert_low, pl.BlockSpec((1, 2, model, hidden), lambda e, *_: (e, 0, 0, 0)))],
            [(shape_of(odd_shape, BF16), kept_out(odd_shape))]
            + [(shape_of((tokens, model), BF16), kept_out((tokens, model)))] * half_peers
            + [
                (by_slot, slot_block),
                (by_slot, slot_block),
                (shape_of((4 * experts, LANES), F32), kept_out((4 * experts, LANES))),
            ],
            [
                pltpu.VMEM((slots_total, tokens), BF16),
                pltpu.VMEM((slots_total, 1), F32),
                pltpu.VMEM((peers, tokens, model), F32),
            ],
            (moe_flops, expert_bytes + 4 * peers * tokens * model),
            "experts",
        )
        s.kept, s.made, s.statistics = results[-3:]
        return results[0], list(results[1 : 1 + half_peers])

    count_row = 2 * experts

    def run_head(micro):
        s = state[micro]
        s.slope, slope_low, s.grad_head, s.norm_three, s.squares = call(
            partial(head_kernel, micro, len(s.moe), tasks),
            (images,),
            (order[0],),
            [(s.res, token_block)]
            + [
                (part, token_block if lead is None else one_whole(part, lead))
                for part, lead in s.moe
            ]
            + [
                (targets, image_block(targets, micro)),
                (masks, image_block(masks, micro)),
                (norm_weight, whole(norm_weight)),
                (head_weight, whole(head_weight)),
            ],
            [
                (shape_of((tokens, model), F32), token_block),
                (shape_of((tokens, model), BF16), token_block),
                (shape_of((outputs, model), F32), kept_out((outputs, model))),
                (shape_of((8, model), F32), kept_out((8, model))),
                (shape_of((8, LANES), F32), kept_out((8, LANES))),
            ],
            [],
            (6 * tokens * model * outputs, tokens * (outputs * 2 + pixels * 4 + 12 * model)),
            "head",
            24,
        )
        return slope_low

    extra_block = pl.BlockSpec(
        (extra, model), lambda *_: (tokens // extra, 0), pipeline_mode=pl.Buffered(1)
    )

    def run_experts_back(micro, e, prior):
        s = state[micro]
        more_grads, more_tokens = prior is not None, e > 0
        split = micro == micros - 1
        one_block = pl.BlockSpec(
            (1, slots_total, model), lambda *_: (e, 0, 0), pipeline_mode=pl.Buffered(1)
        )
        weight_block = pl.BlockSpec(
            (1, 2, model, hidden), lambda *_: (e, 0, 0, 0), pipeline_mode=pl.Buffered(1)
        )
        inputs = (
            [(piece, whole(piece)) for piece in s.slopes]
            + [(piece, extra_block) for piece in s.tokens]
            + [(s.kept, one_block), (s.made, one_block), (expert_low, weight_block)]
            + [(tables, whole(tables))]
        )
        if more_grads:
            inputs.append((prior, whole(prior)))
        if more_tokens:
            inputs += [(piece, whole(piece)) for piece in s.pieces]
        grad_shape = (2, model, hidden)
        grads_out = (
            [(shape_of(grad_shape[1:], BF16), kept_out(grad_shape[1:]))] * 2
            if split
            else [(shape_of(grad_shape, BF16), kept_out(grad_shape))]
        )
        results = call(
            partial(
                moe_backward_kernel,
                (peers, micro, images, e, owned, experts),
                more_grads,
                more_tokens,
                split,
            ),
            (1,),
            (order[0], order[1], place),
            inputs,
            pieces_out(long, model) + grads_out,
            [
                pltpu.VMEM((slots_total, tokens), BF16),
                pltpu.VMEM((slots_total, 1), F32),
                pltpu.VMEM((slots_total, model), BF16),
            ],
            (3 * moe_flops // owned, expert_bytes * 5 // owned + 4 * peers * tokens * model),
            "experts_back",
        )
        s.pieces = list(results[:peers])
        return list(results[peers:])

    def run_attend_back(micro):
        s = state[micro]
        parts = s.sent_parts
        results = call(
            partial(back_kernel, micro, peers, peers, images),
            (images,),
            (order[0], order[1]),
            [(s.slope, token_block)]
            + [(part, token_block) for part in parts]
            + [
                (part, pl.BlockSpec((extra, model), lambda *_: (tokens // extra, 0)))
                for part in parts
            ]
            + [
                (s.res, token_block),
                (s.emb, token_block),
                (s.probs_mlp, expert_block),
                (slots, micro_block((experts, patch_count), micro)),
                (tables, whole(tables)),
            ]
            + [(piece, kv_block) for piece in s.kv]
            + [
                (picks, micro_block((top, patch_count), micro)),
                (s.gates_att, expert_block),
                (s.probs_att, expert_block),
                (s.lse, top_block),
            ]
            + [(piece, whole(piece)) for piece in attention]
            + [
                (s.mix, pl.BlockSpec((1, head_rows, patch_count), lambda i, *_: (i, 0, 0))),
                (norm_weight, whole(norm_weight)),
                (router_rows, whole(router_rows)),
            ],
            [
                (shape_of((tokens, model), F32), token_block),
                (shape_of((tokens, model), F32), token_block),
            ]
            + [(shape_of((tokens, pair_width), BF16), kv_block)] * peers
            + [
                (shape_of((peers, 2, span, model), F32), kept_out((peers, 2, span, model))),
                (shape_of((router_count, model), F32), kept_out((router_count, model))),
                (shape_of((8, model), F32), kept_out((8, model))),
                (shape_of((8, LANES), F32), kept_out((8, LANES))),
            ],
            [
                pltpu.VMEM((keys, pair_width), BF16),
                pltpu.VMEM((pair_width, keys), BF16),
                pltpu.VMEM((head_rows, patch_count), F32),
                pltpu.VMEM((head_rows, patch_count), F32),
                pltpu.VMEM((keys, pair_width), F32),
                pltpu.VMEM((head_rows, patch_count), F32),
                pltpu.VMEM((experts, patch_count), F32),
            ],
            (attention_flops * 3, tokens * model * 30),
            "attention_back",
        )
        s.slope_one, s.normed_slope = results[:2]
        s.grad_att, s.grad_router, s.norm_two, s.mutual = results[2 + peers :]
        return list(results[2 : 2 + peers])

    def run_last(micro):
        s = state[micro]
        s.grad_patch, s.grad_keyval, s.norm_one = call(
            partial(last_kernel, peers),
            (images,),
            (),
            [
                (patches, image_block(patches, micro)),
                (s.emb, token_block),
                (s.slope_one, token_block),
                (s.normed_slope, token_block),
            ]
            + [(part, kv_block) for part in s.kv_parts]
            + [(keyval_weight, whole(keyval_weight)), (norm_weight, whole(norm_weight))],
            [
                (shape_of((patch_in, model), F32), kept_out((patch_in, model))),
                (shape_of((pair_width, model), F32), kept_out((pair_width, model))),
                (shape_of((8, model), F32), kept_out((8, model))),
            ],
            [],
            (2 * tokens * model * (patch_in + 2 * pair_width), tokens * model * 20),
            "embedding_back",
            24,
        )

    step_value = step_count[0].astype(F32)
    scales = jnp.stack(
        [1.0 / (1.0 - jnp.power(BETA_ONE, step_value)), 1.0 / (1.0 - jnp.power(BETA_TWO, step_value))]
    )
    first, second = state
    came_w = across(attention_own)
    picks, slots, count_rows = run_routing()
    (picks,) = settle(picks)
    counts = jnp.zeros((8, LANES), F32).at[0, :tasks].set(jnp.sum(count_rows, axis=(0, 2)))
    kv = run_embed(0)
    (first.emb, kv), came_w = settle_groups([first.emb, kv], came_w)
    more_w = beside(attention_own, came_w)
    first.kv = gather_direct(kv)
    kv = run_embed(1)
    (second.emb, kv), more_w, first.kv = settle_groups([second.emb, kv], more_w, first.kv)
    attention = ordered(attention_own, came_w, more_w)
    second.kv = gather_direct(kv)

    run_attend(0)
    (first.res, first.sent), second.kv = settle_groups([first.res, first.sent], second.kv)
    counts = jnp.zeros((8, LANES), F32)
    came_first = across(first.sent)
    run_attend(1)
    (second.res, second.sent), came_first = settle_groups(
        [second.res, second.sent], came_first
    )
    more_first = beside(first.sent, came_first)
    came_second = across(second.sent)
    expert_low = after(expert_weight, order[1]).astype(BF16)
    (expert_low,), more_first = settle_groups([expert_low], more_first)
    first.tokens = ordered(first.sent, came_first, more_first)

    first_odd, first_evens = run_experts(0)
    (first.kept, first_odd), came_second = settle_groups([first.kept, first_odd], came_second)
    more_second = beside(second.sent, came_second)
    first_crossed = swap(first_odd, "expert", 1)
    (more_second,) = settle_groups(more_second)
    second.tokens = ordered(second.sent, came_second, more_second)
    second_odd, second_evens = run_experts(1)
    second.kept, second_odd, first_crossed = settle(second.kept, second_odd, first_crossed)

    def onward(evens, crossed):
        out = []
        for n in range(1, half_peers):
            pair = (evens[n].astype(F32) + crossed[n].astype(F32)).astype(BF16)
            out.append(swap(pair, "expert", 2 * n))
        return out

    def arrived(evens, crossed, rest):
        return [(evens[0], None), (crossed, 0)] + [(part, None) for part in rest]

    first_rest = onward(first_evens, first_crossed)
    second_crossed = swap(second_odd, "expert", 1)
    hops = Hops(first.statistics + second.statistics, ("dp",))
    hops.start()
    second_crossed, came = settle(second_crossed, *hops.came)
    hops.land([came])
    second_rest = onward(second_evens, second_crossed)
    first_rest, came = settle_groups(first_rest, hops.came)
    hops.land(came)
    first.moe = arrived(first_evens, first_crossed, first_rest)

    first_low = run_head(0)
    (first.slope, first_low), second_rest, came = settle_groups(
        [first.slope, first_low], second_rest, hops.came
    )
    second.moe = arrived(second_evens, second_crossed, second_rest)
    came_first = across(first_low)
    hops.land(came)
    second_low = run_head(1)
    (second.slope, second_low), came_first, came = settle_groups(
        [second.slope, second_low], came_first, hops.came
    )
    more_first = beside(first_low, came_first)
    second.slopes = gather_direct(second_low)
    hops.land(came)
    (more_first,) = settle_groups(more_first)
    first.slopes = ordered(first_low, came_first, more_first)
    tables = hops.finish()

    def small_call(kernel, scalars, inputs, shapes, scratch, name, room=24):
        return call(
            kernel,
            (1,),
            scalars,
            [(a, whole(a)) for a in inputs],
            [(s, kept_out(s.shape)) for s in shapes],
            scratch,
            (0, 1000),
            name,
            room,
        )

    exchanged = [dev]

    def exchange(value):
        value = along_z(after(value, exchanged[0], order[1]))
        exchanged[0] = value
        return value

    def cut_shares(keep, came):
        rows, width = keep.shape
        total = (keep.astype(F32) + came.astype(F32)).astype(BF16)
        return exchange(total.reshape(far, rows // far, width))

    def sum_shares(moved, dense_rows):
        return small_call(
            partial(share_sum_kernel, dense_rows),
            (place,),
            [moved],
            [shape_of(moved.shape, BF16), shape_of((8, LANES), F32)],
            [],
            "share_sum",
        )

    prior = run_experts_back(0, 0, None)
    first.pieces, second.slopes, prior = settle_groups(first.pieces, second.slopes, prior)
    keep_first, send_first = run_experts_back(1, 0, prior[0])
    second.pieces, (keep_first, send_first) = settle_groups(
        second.pieces, [keep_first, send_first]
    )
    came_x_first = swap(send_first, "dp", 1)
    prior = run_experts_back(0, 1, None)
    first.pieces, prior = settle_groups(first.pieces, prior)
    first.sent_parts = scatter_direct(first.pieces)
    keep_second, send_second = run_experts_back(1, 1, prior[0])
    (keep_second, send_second), second.pieces, first.sent_parts, (came_x_first,) = settle_groups(
        [keep_second, send_second], second.pieces, first.sent_parts, [came_x_first]
    )
    came_x_second = swap(send_second, "dp", 1)
    second.sent_parts = scatter_direct(second.pieces)
    square_parts = [s.squares for s in state]
    shares_first = cut_shares(keep_first, came_x_first)

    kv_parts = run_attend_back(0)
    kv_parts, second.sent_parts, (came_x_second, shares_first) = settle_groups(
        kv_parts, second.sent_parts, [came_x_second, shares_first]
    )
    first.kv_parts = scatter_direct(kv_parts)
    summed_first, squares = sum_shares(shares_first, 0)
    square_parts.append(squares)
    shares_second = cut_shares(keep_second, came_x_second)
    (summed_first,) = settle(summed_first)
    kv_parts = run_attend_back(1)
    kv_parts, first.kv_parts, (shares_second,) = settle_groups(
        kv_parts, first.kv_parts, [shares_second]
    )
    second.kv_parts = scatter_direct(kv_parts)
    own_first = exchange(summed_first).reshape(model, hidden)
    summed_second, squares = sum_shares(shares_second, 0)
    square_parts.append(squares)
    (summed_second,) = settle(summed_second)
    run_last(0)
    (first.norm_one,), second.kv_parts = settle_groups([first.norm_one], second.kv_parts)
    run_last(1)
    (second.norm_one,) = settle(second.norm_one)

    packed_parts = []
    for s in state:
        packed_parts += [s.grad_head, s.grad_patch, s.grad_keyval, s.grad_router]
        packed_parts += [s.norm_one, s.norm_two, s.norm_three, s.grad_att]
    used_rows = outputs + patch_in + pair_width + router_count + 6
    dense_rows = -(-used_rows // 256) * 256
    dense_share = dense_rows // peers
    all_rows = dense_share + 2 * span
    packed = small_call(
        partial(pack_kernel, peers, micros, dense_rows, (tasks, pixels, count_row)),
        (order[1],),
        packed_parts + [tables],
        [shape_of((half_peers, all_rows, model), BF16)]
        + [shape_of((1, all_rows, model), BF16)] * half_peers,
        [pltpu.VMEM((dense_rows, model), BF16)],
        "pack",
    )
    packed = settle(*packed)
    odd, evens = packed[0], packed[1:]
    crossed = swap(odd, "expert", 1)
    (crossed,) = settle(crossed)
    pairs = [
        (evens[n].astype(F32) + crossed[n : n + 1].astype(F32)).astype(BF16)
        for n in range(1, half_peers)
    ]
    pairs = settle(*pairs)
    lead_parts = [evens[0], crossed] + [
        swap(pair, "expert", 2 * n + 2) for n, pair in enumerate(pairs)
    ]
    own_first = after(own_first, order[1])
    own_second = exchange(summed_second).reshape(model, hidden)
    *lead_parts, scales = settle(*lead_parts, scales)
    parts = [(part, 0) for part in lead_parts]
    half_shape = shape_of((all_rows // 2, model), BF16)
    keep, send = call(
        partial(halves_kernel, len(parts)),
        (1,),
        (place,),
        [(part, pl.BlockSpec((1, all_rows, model), lambda *_, lead=lead: (lead, 0, 0))) for part, lead in parts],
        [(half_shape, kept_out(half_shape.shape))] * 2,
        [pltpu.VMEM((all_rows, model), BF16)],
        (0, 8 * all_rows * model),
        "halves",
        24,
    )
    keep, send = settle(keep, send)
    came = swap(send, "dp", 1)
    came, own_first = settle(came, own_first)
    other_first = swap(own_first, "dp", 1)
    (own_second,) = settle(own_second)
    shares, squares = sum_shares(cut_shares(keep, came), dense_share)
    sums = squares
    for part in square_parts:
        sums = sums + part
    sums, shares = settle(sums, shares)
    hops = Hops(sums, ("expert", "dp"))
    hops.start()
    own = exchange(shares).reshape(all_rows // 2, model)
    while len(hops.steps) > 2:
        hops.land(settle(*hops.came))
    (own, other_first), came = settle_groups([own, other_first], hops.came)
    other = swap(own, "dp", 1)
    hops.land(came)
    (other,), came = settle_groups([other], hops.came)
    hops.land(came)
    dense_part, attention_part = small_call(
        partial(join_halves_kernel, dense_share),
        (place,),
        [own, other],
        [shape_of((dense_share, model), BF16), shape_of((2 * span, model), BF16)],
        [pltpu.VMEM((all_rows, model), BF16)],
        "join_halves",
    )
    came_quarters = across(dense_part)
    (last_came,) = settle(*hops.came)
    sums = hops.value
    other_second = swap(after(own_second, order[1]), "dp", 1)
    total_params = (
        patch_weight.size
        + keyval_weight.size
        + router_weight.size
        + norm_weight.size
        + head_weight.size
        + (attention_weight.size + expert_weight.size) * peers
    )
    limit = CLIP_UNIT * math.sqrt(total_params)
    block_rows = model // 2
    def adam_expert(e, own, other, before):
        block = pl.BlockSpec((1, 1, block_rows, hidden), lambda w, b, *_: (e, w, b, 0))
        grad_block = pl.BlockSpec((block_rows, hidden), lambda w, b, *_: (b, 0))
        inputs = [own, other, sums, last_came, expert_weight, expert_moment, expert_square]
        specs = [grad_block, grad_block, whole(sums), whole(last_came), block, block, block]
        aliases = {}
        if before is not None:
            aliases = {2 + len(inputs) + n: n for n in range(3)}
            inputs += list(before)
            specs += [pl.BlockSpec(memory_space=pl.ANY)] * 3
        return pl.pallas_call(
            partial(adam_kernel, RATES[6], limit),
            grid_spec=pltpu.PrefetchScalarGridSpec(
                num_scalar_prefetch=2,
                grid=(2, model // block_rows),
                in_specs=specs,
                out_specs=[block] * 3,
            ),
            out_shape=[shape_of(expert_weight.shape, F32)] * 3,
            input_output_aliases=aliases,
            cost_estimate=pl.CostEstimate(
                flops=expert_weight.size * 20 // owned,
                bytes_accessed=expert_weight.size * 26 // owned,
                transcendentals=0,
            ),
            name="adam",
        )(place, scales, *inputs)

    expert_results = adam_expert(0, own_first, other_first, None)
    (expert_results, came_quarters) = settle_groups(list(expert_results), came_quarters)
    quarters = ordered(dense_part, came_quarters, beside(dense_part, came_quarters))
    expert_results = adam_expert(1, own_second, other_second, expert_results)
    dense_states = [
        head_weight,
        head_moment,
        head_square,
        patch_weight,
        patch_moment,
        patch_square,
        keyval_weight,
        keyval_moment,
        keyval_square,
        router_rows,
        router_moment.T,
        router_square.T,
        norm_weight,
        norm_moment,
        norm_square,
        attention_weight,
        attention_moment,
        attention_square,
    ]
    dense_results = small_call(
        partial(
            adam_dense_kernel,
            peers,
            (RATES[4], RATES[0], RATES[1], RATES[2], RATES[3], RATES[5]),
            limit,
            tasks,
            count_row,
        ),
        (order[1], scales),
        quarters
        + [attention_part, sums, last_came, tables, state[0].mutual]
        + dense_states,
        [shape_of(a.shape, F32) for a in dense_states] + [shape_of((8, LANES), F32)],
        [pltpu.VMEM((dense_rows, model), BF16)],
        "adam_dense",
        None,
    )
    new_head, new_patch, new_keyval, new_router, new_norm, new_attention = [
        list(dense_results[3 * n : 3 * n + 3]) for n in range(6)
    ]
    new_router = [a.T for a in new_router]
    return tuple(
        [dense_results[18][0, n] for n in range(3)]
        + new_patch
        + new_keyval
        + new_router
        + new_norm
        + new_head
        + new_attention
        + list(expert_results)
    )


def solution(mesh):
    tokens = P(None, "dp", "expert", None)
    by_columns = P(None, None, "expert")
    by_expert = P("expert", None, None, None)
    same = P()
    placed = (
        (tokens, P(None, "dp", "expert", None, None, None), tokens, tokens, P(None, "dp"), same)
        + (same,) * 15
        + (by_columns,) * 3
        + (by_expert,) * 3
    )
    return jax.shard_map(
        local,
        mesh=mesh,
        in_specs=placed,
        out_specs=(same,) * 18 + (by_columns,) * 3 + (by_expert,) * 3,
        check_vma=False,
    )
```

```python
from functools import partial
import math
from types import SimpleNamespace

import jax
import jax.numpy as jnp
from jax import lax
from jax.experimental import pallas as pl
from jax.experimental.pallas import tpu as pltpu
from jax.sharding import PartitionSpec as P

HEAD = 64
NORM_EPS = 1e-06
MI_WEIGHT = 0.5
CLIP_UNIT = 3e-07
BETA_ONE = 0.9
BETA_TWO = 0.999
EPSILON = 1e-08
RATES = (0.02, 0.02, 0.02, 0.3, 0.02, 1.2, 0.02)
DECAY = 0.05
F32 = jnp.float32
BF16 = jnp.bfloat16
NOWHERE = 1 << 20
LANES = 128
GELU_A = 0.044715
GELU_C = math.sqrt(2.0 / math.pi)


def mm(left, right, precision=None):
    return lax.dot_general(
        left, right, (((1,), (0,)), ((), ())), precision=precision, preferred_element_type=F32
    )


def mm_nt(left, right, precision=None):
    return lax.dot_general(
        left, right, (((1,), (1,)), ((), ())), precision=precision, preferred_element_type=F32
    )


def mm_tn(left, right, precision=None):
    return lax.dot_general(
        left, right, (((0,), (0,)), ((), ())), precision=precision, preferred_element_type=F32
    )


def two_terms(values):
    high = values.astype(BF16)
    return high, (values - high.astype(F32)).astype(BF16)


def fine(product, left, right, axis):
    left_high, left_low = two_terms(left)
    right_high, right_low = two_terms(right)
    both = product(jnp.concatenate([left_high, left_low], axis=axis), right_high)
    rest = product(left_high, right_low)
    rows = rest.shape[0]
    if both.shape[0] == rows:
        return both + rest
    return both[:rows] + both[rows:] + rest


def small_tn(left, right):
    left_high, left_low = two_terms(left)
    right_high, right_low = two_terms(right)
    return mm_tn(
        jnp.concatenate([left_high, left_low, left_high], axis=0),
        jnp.concatenate([right_high, right_high, right_low], axis=0),
    )


def norm_forward(values, gain, shift):
    centred = values - jnp.mean(values, axis=-1, keepdims=True)
    inverse = lax.rsqrt(jnp.mean(centred * centred, axis=-1, keepdims=True) + NORM_EPS)
    scaled = centred * inverse
    return scaled, inverse, scaled * gain + shift


def norm_backward(slope, scaled, inverse, gain):
    inner = slope * gain
    grad = inverse * (
        inner
        - jnp.mean(inner, axis=-1, keepdims=True)
        - scaled * jnp.mean(inner * scaled, axis=-1, keepdims=True)
    )
    return grad, jnp.sum(slope * scaled, axis=0, keepdims=True), jnp.sum(slope, axis=0, keepdims=True)


def expert_rows(experts, tokens):
    return lax.broadcasted_iota(jnp.int32, (experts, tokens), 0)


def by_task(rows, task, experts):
    out = rows[:experts]
    for other in range(1, rows.shape[0] // experts):
        out = jnp.where(task == other, rows[other * experts : (other + 1) * experts], out)
    return out


def to_tasks(rows, task, tasks):
    return jnp.concatenate([jnp.where(task == t, rows, 0.0) for t in range(tasks)], axis=0)


def router_forward(router_rows, normed, task, experts):
    logits = by_task(fine(mm_nt, router_rows, normed, 0), task, experts)
    powers = jnp.exp(logits - jnp.max(logits, axis=0, keepdims=True))
    return powers / jnp.sum(powers, axis=0, keepdims=True)


def gate_forward(probs, chosen):
    picked = probs * chosen
    return picked / jnp.sum(picked, axis=0, keepdims=True)


def gate_backward(probs, chosen, grad_gates, grad_probs):
    total = jnp.sum(probs * chosen, axis=0, keepdims=True)
    gates = probs * chosen / total
    inner = chosen / total * (grad_gates - jnp.sum(grad_gates * gates, axis=0, keepdims=True))
    inner = inner + grad_probs
    return probs * (inner - jnp.sum(probs * inner, axis=0, keepdims=True))


def picked_hot(picks, experts):
    rows = expert_rows(experts, picks.shape[1])
    out = jnp.zeros(rows.shape, F32)
    for k in range(picks.shape[0]):
        out = out + (picks[k : k + 1, :] == rows).astype(F32)
    return out


def add_to(ref, index, value, first):
    @pl.when(first)
    def _():
        ref[index] = value

    @pl.when(jnp.logical_not(first))
    def _():
        ref[index] = ref[index] + value


def route_kernel(tid, routes, masks, picks, slots, counts):
    micro = pl.program_id(0)
    _, images, _, tasks, _, patch_count = routes.shape
    experts = slots.shape[1]
    tokens = images * patch_count
    chosen = []
    pixel_rows = [jnp.zeros((1, masks.shape[3]), F32) for _ in range(tasks)]
    for image in range(images):
        task = tid[micro, image]
        att, mlp = routes[0, image, 0, 0], routes[0, image, 1, 0]
        for t in range(1, tasks):
            att = jnp.where(task == t, routes[0, image, 0, t], att)
            mlp = jnp.where(task == t, routes[0, image, 1, t], mlp)
        picks[0, :, image * patch_count : (image + 1) * patch_count] = att
        chosen.append(picked_hot(mlp, experts))
        column = jnp.sum(masks[0, image].astype(F32), axis=0, keepdims=True)
        for t in range(tasks):
            pixel_rows[t] = pixel_rows[t] + jnp.where(task == t, column, 0.0)
    chosen = jnp.concatenate(chosen, axis=1)
    earlier = lax.broadcasted_iota(jnp.int32, (tokens, tokens), 0) < lax.broadcasted_iota(
        jnp.int32, (tokens, tokens), 1
    )
    before = mm(chosen.astype(BF16), earlier.astype(F32).astype(BF16))
    slots[0] = jnp.where(chosen > 0.0, before.astype(jnp.int32), NOWHERE)
    counts[0] = jnp.concatenate(pixel_rows, axis=0)


def embed_kernel(micro, tid, patches, patch_w, keyval_w, norms, router, picks, emb, kv, gates, probs):
    experts = gates.shape[0]
    task = tid[micro, pl.program_id(0)]
    width = router.shape[0] // 2
    embedded = mm(patches[0, 0], patch_w[...].astype(BF16))
    emb[...] = embedded
    _, _, normed = norm_forward(embedded, norms[0:1], norms[1:2])
    kv[...] = mm(normed.astype(BF16), keyval_w[...].astype(BF16)).astype(BF16)
    prob = router_forward(router[0:width], normed, task, experts)
    probs[...] = prob
    gates[...] = gate_forward(prob, picked_hot(picks[0], experts))


def split_planes(values):
    high = values.astype(BF16).astype(F32)
    middle = (values - high).astype(BF16).astype(F32)
    return [high, middle, (values - high - middle).astype(BF16).astype(F32)]


def put_planes(ref, planes, image, token_rows, images):
    patch_count, model = token_rows.shape
    block = jnp.concatenate(planes, axis=0).astype(BF16)
    height = block.shape[0]
    columns, chunks = model // LANES, patch_count // LANES
    rows, base = ref.shape[0], images * patch_count
    for i in range(images):

        @pl.when(image == i)
        def _(i=i):
            ref[i * patch_count : (i + 1) * patch_count, :] = token_rows
            if i == 0:
                ref[base:, :] = jnp.zeros((rows - base, model), BF16)
            for j in range(chunks):
                c = i * chunks + j
                top, left = base + c // columns * height, c % columns * LANES
                ref[top : top + height, left : left + LANES] = block[:, j * LANES : (j + 1) * LANES]


def lanes_of(shape):
    return lax.broadcasted_iota(jnp.int32, shape, 1)


def put_statistics(ref, images, patch_count, values):
    high, middle, rest = split_planes(values)
    block = high + pltpu.roll(middle, 8, 1) + pltpu.roll(rest, 16, 1)
    ref[ref.shape[0] - values.shape[0] :, ref.shape[1] - LANES :] = block.astype(BF16)


def get_statistics(block):
    block = block.astype(F32)
    total = block + pltpu.roll(block, LANES - 8, 1) + pltpu.roll(block, LANES - 16, 1)
    return jnp.where(lanes_of(block.shape) < 8, total, 0.0)


def extra_rows(count, experts, model):
    return -(-(count // LANES) // (model // LANES)) * 4 * experts


def get_planes(block, count, experts, columns):
    height = 4 * experts
    out = []
    for c in range(count // LANES):
        top, left = c // columns * height, c % columns * LANES
        out.append(block[top : top + height, left : left + LANES].astype(F32))
    return out


def three_sum(planes, experts):
    return planes[:experts] + planes[experts : 2 * experts] + planes[2 * experts : 3 * experts]


def fill_keys(pieces, kvs, kv_t):
    rows = pieces[0].shape[0]
    for r, piece in enumerate(pieces):
        block = piece[...]
        kvs[r * rows : (r + 1) * rows, :] = block
        kv_t[:, r * rows : (r + 1) * rows] = block.astype(F32).T.astype(BF16)


def attend_kernel(micro, peers, capacity, images, tid, dev, *refs):
    emb = refs[0]
    kv_in = refs[1 : 1 + peers]
    picks, gates_in, slots = refs[1 + peers : 4 + peers]
    weights = refs[4 + peers : 4 + 2 * peers]
    norms, router = refs[4 + 2 * peers : 6 + 2 * peers]
    probs_att, counts = refs[6 + 2 * peers : 8 + 2 * peers]
    res_out, sent, mix_out, lse, probs_out = refs[8 + 2 * peers : 13 + 2 * peers]
    table, kvs, kv_t, q_t, mix = refs[13 + 2 * peers :]
    experts, tokens = gates_in.shape
    owned = weights[0].shape[1] // HEAD
    task = tid[micro, pl.program_id(0)]
    width = router.shape[0] // 2
    mine = dev[0]
    embedded = emb[...]
    _, _, normed = norm_forward(embedded, norms[0:1], norms[1:2])
    low = normed.astype(BF16)
    span = owned * HEAD
    for r in range(peers):
        q_t[r * span : (r + 1) * span, :] = mm_nt(weights[r][0], low).astype(BF16).astype(F32)
    fill_keys(kv_in, kvs, kv_t)
    mix[...] = jnp.zeros(mix.shape, F32)
    blocks = [(r, e, (r * owned + e) * HEAD) for r in range(peers) for e in range(owned)]
    rows = expert_rows(experts, tokens)
    blank = jnp.zeros((HEAD, tokens), BF16)

    def one_pick(k, carry):
        pick = picks[0, pl.ds(k, 1), :]
        query = jnp.zeros((HEAD, tokens), F32)
        for r, e, at in blocks:
            here = pick == (mine ^ r) * owned + e
            query = query + jnp.where(here, q_t[at : at + HEAD, :], 0.0)
        gate = jnp.sum(jnp.where(rows == pick, gates_in[...], 0.0), axis=0, keepdims=True)
        scores = mm(kvs[...], jnp.concatenate([(query * HEAD ** (-0.5)).astype(BF16), blank], axis=0))
        top = jnp.max(scores, axis=0, keepdims=True)
        powers = jnp.exp(scores - top)
        total = jnp.sum(powers, axis=0, keepdims=True)
        lse[pl.ds(k, 1), :] = top + jnp.log(total)
        weighted = (powers * (gate / total)).astype(BF16)
        out = mm(kv_t[HEAD:, :], weighted)
        for r, e, at in blocks:
            here = pick == (mine ^ r) * owned + e
            mix[at : at + HEAD, :] = mix[at : at + HEAD, :] + jnp.where(here, out, 0.0)
        return carry

    lax.fori_loop(0, picks.shape[1], one_pick, 0, unroll=True)
    resid = embedded
    for r in range(peers):
        block = mix[r * span : (r + 1) * span, :].astype(BF16)
        mix_out[0, r * span : (r + 1) * span, :] = block
        resid = resid + mm_tn(block, weights[r][1])
    res_out[...] = resid
    _, _, normed_two = norm_forward(resid, norms[2:3], norms[3:4])
    prob = router_forward(router[width:], normed_two, task, experts)
    probs_out[...] = prob
    both = jnp.concatenate([probs_att[...], prob], axis=0)
    lane = lanes_of((2 * experts, LANES))
    per_task = jnp.where(lane == task, jnp.sum(both, axis=1, keepdims=True), 0.0)
    add_to(table, ..., per_task, pl.program_id(0) == 0)
    slot = slots[0]
    gates = gate_forward(prob, (slot < NOWHERE).astype(F32))
    places = jnp.minimum(slot, capacity).astype(F32)
    low_two = normed_two.astype(BF16)
    put_planes(sent, split_planes(gates) + [places], pl.program_id(0), low_two, images)

    @pl.when(pl.program_id(0) == images - 1)
    def _():
        rest = jnp.zeros((2 * experts - 8, LANES), F32)
        block = jnp.concatenate([table[...], counts[...], rest], axis=0)
        put_statistics(sent, images, tokens, block)


def read_planes(block, experts, count):
    chunks = get_planes(block, count, experts, block.shape[1] // LANES)
    gates = jnp.concatenate([three_sum(chunk, experts) for chunk in chunks], axis=1)
    return jnp.concatenate([chunk[3 * experts :] for chunk in chunks], axis=1), gates


def one_row(rows, at):
    index = expert_rows(rows.shape[0], rows.shape[1])
    return jnp.sum(jnp.where(index == at, rows, 0.0), axis=0, keepdims=True)


def loss_scale(counts, task):
    own = jnp.where(lanes_of(counts.shape) == task, counts, 0.0)
    return 1.0 / jnp.sum(own, axis=1, keepdims=True)


def dispatch(blocks, at, experts, count, hot, gate, scale=None):
    capacity = hot.shape[0] // len(blocks)
    places = lax.broadcasted_iota(jnp.int32, (capacity, count), 0).astype(F32)
    for r, block in enumerate(blocks):
        slots, gates = read_planes(block, experts, count)
        here = one_row(slots, at) == places
        rows = slice(r * capacity, (r + 1) * capacity)
        hot[rows, :] = here.astype(F32).astype(BF16)
        own = one_row(gates, at)
        if scale is not None:
            own = own * scale
        gate[rows, :] = jnp.sum(jnp.where(here, own, 0.0), axis=1, keepdims=True)


def moe_forward_kernel(peers, owned, experts, merged, dev, *refs):
    made_outs = 1 + peers // 2 if merged else peers
    arrays = refs[:peers]
    weights = refs[peers]
    outs = refs[peers + 1 : peers + 1 + made_outs]
    kept, made, statistics, hot, gate, back = refs[peers + 1 + made_outs :]
    e = pl.program_id(0)
    count = hot.shape[1]
    capacity = hot.shape[0] // peers
    dispatch([a[count:, :] for a in arrays], dev[0] * owned + e, experts, count, hot, gate)
    for r in range(peers):
        rows = slice(r * capacity, (r + 1) * capacity)
        kept[0, rows, :] = mm(hot[rows, :], arrays[r][:count, :]).astype(BF16)
    before = mm(kept[0], weights[0, 0])
    bent = jnp.tanh(before * (GELU_C + GELU_C * GELU_A * (before * before)))
    halved = 0.5 * before
    out = mm_nt((halved + halved * bent).astype(BF16), weights[0, 1])
    made[0] = out.astype(BF16)
    weighted = (out * gate[...]).astype(BF16)
    for r in range(peers):
        rows = slice(r * capacity, (r + 1) * capacity)
        value = mm_tn(hot[rows, :], weighted[rows, :])
        if owned > 1:
            add_to(back, r, value, e == 0)

    @pl.when(e == owned - 1)
    def _():
        for r in range(peers):
            piece = back[r].astype(BF16) if owned > 1 else value.astype(BF16)
            if not merged:
                outs[r][...] = piece
            elif r % 2:
                outs[0][r // 2] = piece
            else:
                outs[1 + r // 2][...] = piece
        rows = statistics.shape[0]
        block = jnp.zeros(statistics.shape, F32)
        for a in arrays:
            block = block + get_statistics(a[a.shape[0] - rows :, a.shape[1] - LANES :])
        statistics[...] = block


def head_kernel(micro, parts, tasks, tid, *refs):
    res = refs[0]
    moe = refs[1 : 1 + parts]
    targets, masks, norms, head_w = refs[1 + parts : 5 + parts]
    slope_out, slope_low, grad_head, grad_norm, squares = refs[5 + parts :]
    image = pl.program_id(0)
    task = tid[micro, image]
    resid = res[...]
    for part in moe:
        resid = resid + part[...].astype(F32)
    scaled, inverse, normed = norm_forward(resid, norms[4:5], norms[5:6])
    low = normed.astype(BF16)
    head_low = head_w[...].astype(BF16)
    pred = mm(low, head_low)
    mask = masks[0, 0].astype(F32)
    pixels = mask.shape[1]
    depth_on = jnp.where(task == 0, 1.0, 0.0)
    normal_on = jnp.where(task == 0, 0.0, 1.0)
    slopes = []
    total = jnp.zeros((1, pixels), F32)
    for group in range(4):
        on = depth_on if group == 0 else normal_on
        at = group * pixels
        gap = pred[:, at : at + pixels] - targets[0, 0, :, at : at + pixels].astype(F32)
        masked = mask * gap
        total = total + on * jnp.sum(masked * gap, axis=0, keepdims=True)
        slopes.append((masked * (2.0 * on)).astype(BF16))
    slope = jnp.concatenate(slopes, axis=1)
    first = image == 0
    spots = lax.broadcasted_iota(jnp.int32, (8, LANES), 0) * LANES + lanes_of((8, LANES))
    add_to(squares, ..., jnp.where(spots == task, jnp.sum(total, axis=1, keepdims=True), 0.0), first)
    add_to(grad_head, ..., mm_tn(slope, low), first)
    grad, gain, shift = norm_backward(mm_nt(slope, head_low), scaled, inverse, norms[4:5])
    both = jnp.concatenate([gain, shift], axis=0)
    for t in range(tasks):
        add_to(grad_norm, slice(2 * t, 2 * t + 2), jnp.where(task == t, both, 0.0), first)
    slope_out[...] = grad
    slope_low[...] = grad.astype(BF16)


def moe_backward_kernel(shape, more_grads, more_tokens, split, tid, dev, place, *refs):
    peers, micro, images, local_expert, owned, experts = shape
    refs = list(refs)

    def take(count):
        out = refs[:count]
        del refs[:count]
        return out

    slopes, extras = take(peers), take(peers)
    kept, made, weights, tables = take(4)
    if more_grads:
        (prior_grads,) = take(1)
    if more_tokens:
        prior_pieces = take(peers)
    outs = take(peers)
    grads_out = take(2 if split else 1)
    hot, gate, plain = take(3)
    count, model = slopes[0].shape
    capacity = hot.shape[0] // peers
    at = dev[0] * owned + local_expert
    counts = tables[2 * experts : 2 * experts + 1, :]
    per_image = count // images
    scale = jnp.concatenate(
        [
            jnp.broadcast_to(loss_scale(counts, tid[micro, image]), (1, per_image))
            for image in range(images)
        ],
        axis=1,
    )
    dispatch([extra[...] for extra in extras], at, experts, count, hot, gate, scale)
    gate_slopes = []
    for r in range(peers):
        rows = slice(r * capacity, (r + 1) * capacity)
        value = mm(hot[rows, :], slopes[r][...])
        gate_slopes.append(jnp.sum(value * made[0, rows, :].astype(F32), axis=1, keepdims=True))
        plain[rows, :] = (value * gate[rows, :]).astype(BF16)
    before = mm(kept[0], weights[0, 0])
    hidden = mm(plain[...], weights[0, 1])
    cubic = GELU_C * GELU_A * (before * before)
    bent = jnp.tanh(before * (GELU_C + cubic))
    middle = 0.5 + 0.5 * bent
    inner = (before * middle).astype(BF16)
    bend = middle + (middle - middle * bent) * (before * (GELU_C + 3.0 * cubic))
    slope = (hidden * bend).astype(BF16)
    entry = mm_tn(kept[0], slope)
    leave = mm_tn(plain[...], inner)
    if more_grads:
        entry = entry + prior_grads[0].astype(F32)
        leave = leave + prior_grads[1].astype(F32)
    if split:
        flip = place[0] == 0
        grads_out[0][...] = jnp.where(flip, entry, leave).astype(BF16)
        grads_out[1][...] = jnp.where(flip, leave, entry).astype(BF16)
    else:
        grads_out[0][0] = entry.astype(BF16)
        grads_out[0][1] = leave.astype(BF16)
    received = mm_nt(slope, weights[0, 0]).astype(BF16)
    columns, chunks, height = model // LANES, count // LANES, 4 * experts
    rows_of = expert_rows(experts, count)
    lane = lanes_of((capacity, LANES))
    for r in range(peers):
        rows = slice(r * capacity, (r + 1) * capacity)
        tokens_back = mm_tn(hot[rows, :], received[rows, :])
        terms = split_planes(gate_slopes[r])
        terms = jnp.where(lane == 0, terms[0], jnp.where(lane == 1, terms[1], terms[2]))
        terms = jnp.where(lane < 3, terms, 0.0).astype(BF16)
        gate_row = jnp.sum(mm_tn(terms, hot[rows, :])[:8, :], axis=0, keepdims=True) * scale
        planes = split_planes(jnp.where(rows_of == at, gate_row, 0.0))
        block = jnp.concatenate(planes + [jnp.zeros((experts, count), F32)], axis=0)
        lines = []
        for line in range(-(-chunks // columns)):
            cells = [
                block[:, c * LANES : (c + 1) * LANES]
                if c < chunks
                else jnp.zeros((height, LANES), F32)
                for c in range(line * columns, (line + 1) * columns)
            ]
            lines.append(jnp.concatenate(cells, axis=1))
        piece = jnp.concatenate([tokens_back] + lines, axis=0)
        if more_tokens:
            piece = piece + prior_pieces[r][...].astype(F32)
        outs[r][...] = piece.astype(BF16)


def table_slope(table, task, tasks):
    lane = lanes_of(table.shape)
    valid = lane < tasks
    table = jnp.where(valid, table, 0.0)
    total = jnp.sum(jnp.sum(table, axis=1, keepdims=True), axis=0, keepdims=True)
    share = table / total
    by_expert = jnp.sum(share, axis=1, keepdims=True)
    by_task_sum = jnp.sum(share, axis=0, keepdims=True)
    safe = jnp.where(valid, share, 1.0)
    gain = jnp.log(safe) - jnp.log(jnp.where(valid, by_task_sum, 1.0)) - jnp.log(by_expert)
    gain = jnp.where(valid, gain, 0.0)
    mean = jnp.sum(jnp.sum(gain * share, axis=1, keepdims=True), axis=0, keepdims=True)
    slope = -MI_WEIGHT * (gain - mean) / total
    return jnp.sum(jnp.where(lane == task, slope, 0.0), axis=1, keepdims=True), mean


def back_kernel(micro, peers, parts, image_count, tid, dev, *refs):
    slope_in = refs[0]
    sent_parts = refs[1 : 1 + parts]
    gate_parts = refs[1 + parts : 1 + 2 * parts]
    at = 1 + 2 * parts
    res, emb, probs_mlp, slots = refs[at : at + 4]
    at += 4
    tables = refs[at]
    kv_in = refs[at + 1 : at + 1 + peers]
    at += 1 + peers
    picks, gates_in, probs_att, lse = refs[at : at + 4]
    weights = refs[at + 4 : at + 4 + peers]
    at += 4 + peers
    mix_in, norms, router = refs[at : at + 3]
    slope_one, normed_slope = refs[at + 3 : at + 5]
    kv_outs = refs[at + 5 : at + 5 + peers]
    at += 5 + peers
    grad_att, grad_router, grad_norm, mutual = refs[at : at + 4]
    kvs, kv_t, q_t, d_t, dkv, dq_t, dgate = refs[at + 4 :]
    experts, tokens = gates_in.shape
    owned = weights[0].shape[1] // HEAD
    image = pl.program_id(0)
    first = image == 0
    task = tid[micro, image]
    width = router.shape[0] // 2
    tasks = width // experts
    span = owned * HEAD
    mine = dev[0]
    rows = expert_rows(experts, tokens)

    grad_sent = jnp.zeros(slope_in.shape, F32)
    for part in sent_parts:
        grad_sent = grad_sent + part[...].astype(F32)
    planes = gate_parts[0][...].astype(F32)
    for part in gate_parts[1:]:
        planes = planes + part[...].astype(F32)
    columns = planes.shape[1] // LANES
    chunks = get_planes(planes, image_count * tokens, experts, columns)
    per = tokens // LANES
    grad_gates = jnp.zeros((experts, tokens), F32)
    for i in range(image_count):
        cells = [three_sum(c, experts) for c in chunks[i * per : (i + 1) * per]]
        grad_gates = jnp.where(image == i, jnp.concatenate(cells, axis=1), grad_gates)
    scaled_two, inverse_two, normed_two = norm_forward(res[...], norms[2:3], norms[3:4])
    chosen = (slots[0] < NOWHERE).astype(F32)
    table, gain_mlp = table_slope(tables[experts : 2 * experts, :], task, tasks)
    logits = to_tasks(gate_backward(probs_mlp[...], chosen, grad_gates, table), task, tasks)
    grad_two = grad_sent + small_tn(logits, router[width:])
    add_to(grad_router, slice(width, 2 * width), fine(mm, logits, normed_two, 0), first)
    grad, gain, shift = norm_backward(grad_two, scaled_two, inverse_two, norms[2:3])
    add_to(grad_norm, slice(2, 3), gain, first)
    add_to(grad_norm, slice(3, 4), shift, first)
    scale = loss_scale(tables[2 * experts : 2 * experts + 1, :], task)
    resid_slope = slope_in[...] * scale + grad
    slope_one[...] = resid_slope
    branch = resid_slope.astype(BF16)

    _, _, normed = norm_forward(emb[...], norms[0:1], norms[1:2])
    low = normed.astype(BF16)
    for r in range(peers):
        at_r = slice(r * span, (r + 1) * span)
        q_t[at_r, :] = mm_nt(weights[r][0], low).astype(BF16).astype(F32)
        d_t[at_r, :] = mm_nt(weights[r][1], branch).astype(BF16).astype(F32)
        add_to(grad_att, (r, 1), mm(mix_in[0, at_r, :], branch), first)
    fill_keys(kv_in, kvs, kv_t)
    dkv[...] = jnp.zeros(dkv.shape, F32)
    dq_t[...] = jnp.zeros(dq_t.shape, F32)
    dgate[...] = jnp.zeros(dgate.shape, F32)
    blocks = [(r, e, (r * owned + e) * HEAD) for r in range(peers) for e in range(owned)]
    blank = jnp.zeros((HEAD, tokens), BF16)

    def one_pick(k, carry):
        pick = picks[0, pl.ds(k, 1), :]
        query = jnp.zeros((HEAD, tokens), F32)
        down = jnp.zeros((HEAD, tokens), F32)
        for r, e, at in blocks:
            here = pick == (mine ^ r) * owned + e
            query = query + jnp.where(here, q_t[at : at + HEAD, :], 0.0)
            down = down + jnp.where(here, d_t[at : at + HEAD, :], 0.0)
        gate = jnp.sum(jnp.where(rows == pick, gates_in[...], 0.0), axis=0, keepdims=True)
        query_low, down_low = query.astype(BF16), down.astype(BF16)
        scores = mm(kvs[...], jnp.concatenate([(query * HEAD ** (-0.5)).astype(BF16), blank], axis=0))
        probs = jnp.exp(scores - lse[pl.ds(k, 1), :])
        slope = mm(kvs[...], jnp.concatenate([blank, down_low], axis=0))
        delta = jnp.sum(probs * slope, axis=0, keepdims=True)
        gated = probs * gate
        weighted = gated.astype(BF16)
        grad_scores = (gated * (slope - delta) * HEAD ** (-0.5)).astype(BF16)
        joint = jnp.concatenate([grad_scores, weighted], axis=1)
        other = jnp.concatenate(
            [
                jnp.concatenate([query_low, blank], axis=0),
                jnp.concatenate([blank, down_low], axis=0),
            ],
            axis=1,
        )
        dkv[...] = dkv[...] + mm_nt(joint, other)
        dq = mm(kv_t[:HEAD, :], grad_scores)
        for r, e, at in blocks:
            here = pick == (mine ^ r) * owned + e
            dq_t[at : at + HEAD, :] = dq_t[at : at + HEAD, :] + jnp.where(here, dq, 0.0)
        dgate[...] = dgate[...] + jnp.where(rows == pick, delta, 0.0)
        return carry

    lax.fori_loop(0, picks.shape[1], one_pick, 0, unroll=True)
    for r in range(peers):
        block = dkv[r * tokens : (r + 1) * tokens, :].astype(BF16)
        kv_outs[r][...] = block

    table, gain_att = table_slope(tables[:experts, :], task, tasks)
    mutual[...] = jnp.broadcast_to(gain_att + gain_mlp, mutual.shape)
    chosen = picked_hot(picks[0], experts)
    logits = to_tasks(gate_backward(probs_att[...], chosen, dgate[...], table), task, tasks)
    grad_one = small_tn(logits, router[0:width])
    add_to(grad_router, slice(0, width), fine(mm, logits, normed, 0), first)
    for r in range(peers):
        block = dq_t[r * span : (r + 1) * span, :].astype(BF16)
        grad_one = grad_one + mm_tn(block, weights[r][0])
        add_to(grad_att, (r, 0), mm(block, low), first)
    normed_slope[...] = grad_one


def last_kernel(parts, *refs):
    patches, emb, slope_one, normed_slope = refs[:4]
    kv_parts = refs[4 : 4 + parts]
    keyval_w, norms = refs[4 + parts : 6 + parts]
    grad_patch, grad_keyval, grad_norm = refs[6 + parts :]
    first = pl.program_id(0) == 0
    scaled, inverse, normed = norm_forward(emb[...], norms[0:1], norms[1:2])
    grad_kv = jnp.zeros(kv_parts[0].shape, F32)
    for part in kv_parts:
        grad_kv = grad_kv + part[...].astype(F32)
    grad_kv = grad_kv.astype(BF16)
    add_to(grad_keyval, ..., mm_tn(grad_kv, normed.astype(BF16)), first)
    slope = normed_slope[...] + mm_nt(grad_kv, keyval_w[...].astype(BF16))
    grad, gain, shift = norm_backward(slope, scaled, inverse, norms[0:1])
    add_to(grad_norm, slice(0, 1), gain, first)
    add_to(grad_norm, slice(1, 2), shift, first)
    add_to(grad_patch, ..., mm_tn(patches[0, 0], (slope_one[...] + grad).astype(BF16)), first)


def pack_kernel(peers, micros, dense_rows, sizes, dev, *refs):
    names = 8
    values = []
    for n in range(names):
        value = refs[n][...]
        for m in range(1, micros):
            value = value + refs[m * names + n][...]
        values.append(value)
    head, patch, keyval, router, one, two, three, attention = values
    tables, odd = refs[micros * names : micros * names + 2]
    evens = refs[micros * names + 2 : -1]
    dense = refs[-1]
    tasks, pixels, count_row = sizes
    scales = [loss_scale(tables[count_row : count_row + 1, :], t) for t in range(tasks)]
    head = jnp.concatenate([head[:pixels] * scales[0], head[pixels:] * scales[1]], axis=0)
    three = sum(three[2 * t : 2 * t + 2] * scales[t] for t in range(tasks))
    at = 0
    for value in (head, patch, keyval):
        dense[at : at + value.shape[0], :] = value.astype(BF16)
        at += value.shape[0]
    rest = [router, one[0:2], two[2:4], three]
    pad = dense_rows - at - router.shape[0] - 6
    if pad:
        rest.append(jnp.zeros((pad, dense.shape[1]), F32))
    dense[at:, :] = jnp.concatenate(rest, axis=0).astype(BF16)
    share = dense_rows // peers
    model = dense.shape[1]
    for r in range(peers):
        start = pl.multiple_of((dev[0] ^ r) * share, 16)
        rows = dense[pl.ds(start, share), :]
        owned_rows = attention[r].reshape(-1, model).astype(BF16)
        if r % 2:
            odd[r // 2, :share] = rows
            odd[r // 2, share:] = owned_rows
        else:
            evens[r // 2][0, :share] = rows
            evens[r // 2][0, share:] = owned_rows


def halves_kernel(parts, place, *refs):
    keep, send, total = refs[parts:]
    value = refs[0][0].astype(F32)
    for part in refs[1:parts]:
        value = value + part[0].astype(F32)
    total[...] = value.astype(BF16)
    rows = keep.shape[0]
    keep[...] = total[pl.ds(pl.multiple_of(place[0] * rows, 16), rows), :]
    send[...] = total[pl.ds(pl.multiple_of((1 - place[0]) * rows, 16), rows), :]


def share_sum_kernel(dense_rows, place, shares, outs, squares):
    count, rows, width = shares.shape
    value = shares[0].astype(F32)
    for r in range(1, count):
        value = value + shares[r].astype(F32)
    low = value.astype(BF16)
    for r in range(count):
        outs[r] = low
    value = low.astype(F32)
    value = value * value
    both = jnp.sum(value, axis=0, keepdims=True)
    if dense_rows:
        start = (place[0] * count + place[1]) * rows
        row = lax.broadcasted_iota(jnp.int32, (rows, width), 0) + start
        dense = jnp.sum(jnp.where(row < dense_rows, value, 0.0), axis=0, keepdims=True)
    else:
        dense = jnp.zeros((1, width), F32)
    spots = lax.broadcasted_iota(jnp.int32, (8, LANES), 0) * LANES + lanes_of((8, LANES))
    own = jnp.sum(both - dense, axis=1, keepdims=True)
    dense = jnp.sum(dense, axis=1, keepdims=True)
    squares[...] = jnp.where(spots == 2, own, 0.0) + jnp.where(spots == 3, dense, 0.0)


def join_halves_kernel(dense_rows, place, own, other, dense, rest, total):
    rows = own.shape[0]
    total[pl.ds(pl.multiple_of(place[0] * rows, 16), rows), :] = own[...]
    total[pl.ds(pl.multiple_of((1 - place[0]) * rows, 16), rows), :] = other[...]
    dense[...] = total[:dense_rows, :]
    rest[...] = total[dense_rows:, :]


def clip_factor(sums, other_sums, limit):
    total = sums[0:1, :] + other_sums[0:1, :]
    own, dense = total[:, 2:3], total[:, 3:4]
    norm = jnp.sqrt(own + dense)
    return jnp.minimum(1.0, limit / norm), norm, jnp.sqrt(own), total


def adam_step(weight, first, second, gradient, rate, factor, scales):
    gradient = gradient * factor
    moment = BETA_ONE * first + (1.0 - BETA_ONE) * gradient
    square = BETA_TWO * second + ((1.0 - BETA_TWO) * gradient) * gradient
    step = (moment * (rate * scales[0])) / (jnp.sqrt(square * scales[1]) + EPSILON)
    return weight * (1.0 - rate * DECAY) - step, moment, square


def adam_kernel(rate, limit, place, scales, *refs):
    own, other, sums, other_sums, weight, first, second = refs[:7]
    factor = clip_factor(sums, other_sums, limit)[0]
    gradient = jnp.where(pl.program_id(0) == place[0], own[...], other[...]).astype(F32)
    news = adam_step(weight[0, 0], first[0, 0], second[0, 0], gradient, rate, factor, scales)
    for ref, new in zip(refs[-3:], news):
        ref[0, 0] = new


def adam_dense_kernel(peers, rates, limit, tasks, count_row, dev, scales, *refs):
    pieces, attention = refs[:peers], refs[peers]
    sums, other_sums, counts, mutual = refs[peers + 1 : peers + 5]
    states = [refs[peers + 5 + 3 * n : peers + 8 + 3 * n] for n in range(6)]
    outs = [refs[peers + 23 + 3 * n : peers + 26 + 3 * n] for n in range(6)]
    scalars, dense = refs[-2:]
    factor, norm, own_norm, total = clip_factor(sums, other_sums, limit)
    lane = lanes_of((1, LANES))
    ratio = total / jnp.where(lane < tasks, counts[count_row : count_row + 1, :], 1.0)
    loss = jnp.sum(jnp.where(lane < tasks, ratio, 0.0), axis=1, keepdims=True)
    loss = loss - MI_WEIGHT * mutual[0:1, 0:1]
    lane = lanes_of(scalars.shape)
    scalars[...] = jnp.where(lane == 0, loss, jnp.where(lane == 1, norm, own_norm))
    share = pieces[0].shape[0]
    for r in range(peers):
        dense[pl.ds(pl.multiple_of((dev[0] ^ r) * share, 16), share), :] = pieces[r][...]

    def update(n, index, gradient):
        olds = [ref[index] for ref in states[n]]
        news = adam_step(*olds, gradient, rates[n], factor, scales)
        for ref, new in zip(outs[n], news):
            ref[index] = new

    outputs = states[0][0].shape[1]
    step = 2 * LANES
    for left in range(0, outputs, step):
        block = dense[left : left + step, :].astype(F32).T
        update(0, (slice(None), slice(left, left + step)), block)
    at = outputs
    rows = states[1][0].shape[0]
    update(1, ..., dense[at : at + rows, :].astype(F32))
    at += rows
    width = states[2][0].shape[1]
    update(2, ..., dense[at : at + width, :].astype(F32).T)
    at += width
    rest = dense[at:, :].astype(F32)
    rows = states[3][0].shape[0]
    update(3, ..., rest[:rows])
    update(4, ..., rest[rows : rows + states[4][0].shape[0]])
    width = states[5][0].shape[2]
    for n in range(2):
        update(5, n, attention[n * width : (n + 1) * width, :].astype(F32).T)


def whole(array):
    rank = len(array.shape)
    return pl.BlockSpec(array.shape, lambda *_: (0,) * rank, pipeline_mode=pl.Buffered(1))


def kept_out(shape):
    rank = len(shape)
    return pl.BlockSpec(shape, lambda *_: (0,) * rank)


def shape_of(shape, dtype):
    return jax.ShapeDtypeStruct(shape, dtype)


def call(kernel, grid, scalars, inputs, outputs, scratch, cost, name, room=None):
    spec = pltpu.PrefetchScalarGridSpec(
        num_scalar_prefetch=len(scalars),
        grid=grid,
        in_specs=[s for _, s in inputs],
        out_specs=[s for _, s in outputs],
        scratch_shapes=scratch,
    )
    return pl.pallas_call(
        kernel,
        grid_spec=spec,
        out_shape=[o for o, _ in outputs],
        cost_estimate=pl.CostEstimate(
            flops=int(cost[0]), bytes_accessed=int(cost[1]), transcendentals=0
        ),
        compiler_params=None if room is None else pltpu.CompilerParams(vmem_limit_bytes=room << 20),
        name=name,
    )(*scalars, *[a for a, _ in inputs])


def swap(value, axis, mask):
    size = lax.axis_size(axis)
    return lax.ppermute(value, axis, [(i, i ^ mask) for i in range(size)])


def bits_of(axis):
    return [1 << b for b in range(lax.axis_size(axis).bit_length() - 1)]


def gather_direct(value):
    return [value] + [swap(value, "expert", r) for r in range(1, lax.axis_size("expert"))]


def scatter_direct(pieces):
    return [pieces[0]] + [swap(pieces[r], "expert", r) for r in range(1, len(pieces))]


def across(value):
    rest = [swap(value, "expert", r) for r in range(2, lax.axis_size("expert"), 2)]
    return rest + [swap(value, "expert", 1)]


def beside(value, came):
    rest = came[:-1]
    return [swap(block, "expert", 1) for block in rest]


def ordered(value, came, more):
    out = [value, came[-1]]
    for block, other in zip(came[:-1], more):
        out += [block, other]
    return out


def gather_pieces(value):
    came = across(value)
    return ordered(value, came, beside(value, came))


def after(value, *anchors):
    return lax.optimization_barrier((value,) + anchors)[0]


class Hops:
    def __init__(self, value, axes):
        self.value = value
        self.steps = [(axis, bit) for axis in axes for bit in bits_of(axis)]
        if len(axes) > 1:
            self.steps.sort(key=lambda step: step == (axes[1], 1))
        self.came = []

    def start(self):
        if self.steps:
            self.came = [swap(self.value, *self.steps.pop(0))]

    def land(self, came):
        if self.came:
            self.value = self.value + came[-1]
            self.came = []
        self.start()

    def finish(self):
        while self.came or self.steps:
            self.land(self.came)
        return self.value


def along_z(value):
    size = lax.axis_size("dp")
    groups = [[i for i in range(size) if i % 2 == low] for low in range(2)]
    return lax.all_to_all(
        value, "dp", split_axis=0, concat_axis=0, axis_index_groups=groups, tiled=True
    )


def local(
    patches,
    routes,
    masks,
    targets,
    task_ids,
    step_count,
    patch_weight,
    patch_moment,
    patch_square,
    keyval_weight,
    keyval_moment,
    keyval_square,
    router_weight,
    router_moment,
    router_square,
    norm_weight,
    norm_moment,
    norm_square,
    head_weight,
    head_moment,
    head_square,
    attention_weight,
    attention_moment,
    attention_square,
    expert_weight,
    expert_moment,
    expert_square,
):
    peers = lax.axis_size("expert")
    half_peers = peers // 2
    micros, images, patch_count, patch_in = patches.shape
    _, _, _, _, tasks, top = routes.shape
    owned = expert_weight.shape[0]
    experts = owned * peers
    model, hidden = expert_weight.shape[2:]
    tokens = images * patch_count
    capacity = max(2, tokens * top // experts)
    pixels = masks.shape[3]
    outputs = targets.shape[3]
    pair_width = 2 * HEAD
    span = owned * HEAD
    keys = peers * patch_count
    head_rows = peers * span
    extra = extra_rows(tokens, experts, model)
    long = tokens + extra
    far = lax.axis_size("dp") // 2
    dev = lax.axis_index("expert").astype(jnp.int32).reshape(1)
    spot = lax.axis_index("dp").astype(jnp.int32)
    place = jnp.stack([spot & 1, spot >> 1])
    router_rows = router_weight.T
    router_count = router_rows.shape[0]
    routes_lanes = jnp.transpose(routes, (0, 1, 3, 4, 5, 2))
    attention_own = jnp.transpose(attention_weight, (0, 2, 1)).astype(BF16)
    attention = gather_direct(attention_own)

    order = [task_ids, dev]

    def settle(*values):
        out = lax.optimization_barrier((order[0], order[1]) + values)
        order[:] = out[:2]
        return list(out[2:])

    def settle_groups(*groups):
        out = settle(*[value for group in groups for value in group])
        back = []
        for group in groups:
            back.append(out[: len(group)])
            out = out[len(group) :]
        return back

    token_block = pl.BlockSpec((patch_count, model), lambda i, *_: (i, 0))
    expert_block = pl.BlockSpec((experts, patch_count), lambda i, *_: (0, i))
    kv_block = pl.BlockSpec((patch_count, pair_width), lambda i, *_: (i, 0))
    top_block = pl.BlockSpec((top, patch_count), lambda i, *_: (0, i))

    def micro_block(shape, micro):
        return pl.BlockSpec((1,) + shape, lambda i, *_, m=micro: (m,) + (0,) * (len(shape) - 1) + (i,))

    def image_block(array, micro):
        return pl.BlockSpec((1, 1) + array.shape[2:], lambda i, *_, m=micro: (m, i, 0, 0))

    def pieces_out(rows, width):
        return [(shape_of((rows, width), BF16), kept_out((rows, width)))] * peers


    def one_whole(array, lead):
        return pl.BlockSpec(
            (pl.Squeezed(), patch_count, array.shape[2]), lambda i, *_: (lead, i, 0)
        )

    state = [SimpleNamespace() for _ in range(micros)]

    def run_routing():
        return call(
            route_kernel,
            (micros,),
            (order[0],),
            [
                (
                    routes_lanes,
                    pl.BlockSpec((1,) + routes_lanes.shape[1:], lambda m, *_: (m, 0, 0, 0, 0, 0)),
                ),
                (masks, pl.BlockSpec((1,) + masks.shape[1:], lambda m, *_: (m, 0, 0, 0))),
            ],
            [
                (
                    shape_of((micros, top, tokens), jnp.int32),
                    pl.BlockSpec((1, top, tokens), lambda m, *_: (m, 0, 0)),
                ),
                (
                    shape_of((micros, experts, tokens), jnp.int32),
                    pl.BlockSpec((1, experts, tokens), lambda m, *_: (m, 0, 0)),
                ),
                (
                    shape_of((micros, tasks, pixels), F32),
                    pl.BlockSpec((1, tasks, pixels), lambda m, *_: (m, 0, 0)),
                ),
            ],
            [],
            (micros * tokens * tokens * 32, masks.size * 4),
            "routing",
        )

    def run_embed(micro):
        s = state[micro]
        s.emb, kv, s.gates_att, s.probs_att = call(
            partial(embed_kernel, micro),
            (images,),
            (order[0],),
            [
                (patches, image_block(patches, micro)),
                (patch_weight, whole(patch_weight)),
                (keyval_weight, whole(keyval_weight)),
                (norm_weight, whole(norm_weight)),
                (router_rows, whole(router_rows)),
                (picks, micro_block((top, patch_count), micro)),
            ],
            [
                (shape_of((tokens, model), F32), token_block),
                (shape_of((tokens, pair_width), BF16), kv_block),
                (shape_of((experts, tokens), F32), expert_block),
                (shape_of((experts, tokens), F32), expert_block),
            ],
            [],
            (2 * tokens * model * (patch_in + pair_width), tokens * (2 * patch_in + 4 * model) + patch_weight.size * 4),
            "embedding",
        )
        return kv

    attention_flops = 2 * top * tokens * keys * HEAD * 8

    def run_attend(micro):
        s = state[micro]
        s.res, s.sent, s.mix, s.lse, s.probs_mlp = call(
            partial(attend_kernel, micro, peers, capacity, images),
            (images,),
            (order[0], order[1]),
            [(s.emb, token_block)]
            + [(piece, kv_block) for piece in s.kv]
            + [
                (picks, micro_block((top, patch_count), micro)),
                (s.gates_att, expert_block),
                (slots, micro_block((experts, patch_count), micro)),
            ]
            + [(piece, whole(piece)) for piece in attention]
            + [
                (norm_weight, whole(norm_weight)),
                (router_rows, whole(router_rows)),
                (s.probs_att, expert_block),
                (counts, whole(counts)),
            ],
            [
                (shape_of((tokens, model), F32), token_block),
                (shape_of((long, model), BF16), kept_out((long, model))),
                (
                    shape_of((images, head_rows, patch_count), BF16),
                    pl.BlockSpec((1, head_rows, patch_count), lambda i, *_: (i, 0, 0)),
                ),
                (shape_of((top, tokens), F32), top_block),
                (shape_of((experts, tokens), F32), expert_block),
            ],
            [
                pltpu.VMEM((2 * experts, LANES), F32),
                pltpu.VMEM((keys, pair_width), BF16),
                pltpu.VMEM((pair_width, keys), BF16),
                pltpu.VMEM((head_rows, patch_count), F32),
                pltpu.VMEM((head_rows, patch_count), F32),
            ],
            (attention_flops, tokens * model * 12),
            "attention",
        )

    moe_flops = 2 * owned * peers * capacity * model * (2 * hidden + 2 * tokens)
    expert_bytes = expert_weight.size * 2
    odd_shape = (half_peers, tokens, model)

    slots_total = peers * capacity
    by_slot = shape_of((owned, slots_total, model), BF16)
    slot_block = pl.BlockSpec((1, slots_total, model), lambda e, *_: (e, 0, 0))

    def run_experts(micro, merged):
        s = state[micro]
        results = call(
            partial(moe_forward_kernel, peers, owned, experts, merged),
            (owned,),
            (order[1],),
            [(piece, whole(piece)) for piece in s.tokens]
            + [(expert_low, pl.BlockSpec((1, 2, model, hidden), lambda e, *_: (e, 0, 0, 0)))],
            (
                [(shape_of(odd_shape, BF16), kept_out(odd_shape))]
                + [(shape_of((tokens, model), BF16), kept_out((tokens, model)))] * half_peers
                if merged
                else pieces_out(tokens, model)
            )
            + [
                (by_slot, slot_block),
                (by_slot, slot_block),
                (shape_of((4 * experts, LANES), F32), kept_out((4 * experts, LANES))),
            ],
            [
                pltpu.VMEM((slots_total, tokens), BF16),
                pltpu.VMEM((slots_total, 1), F32),
                pltpu.VMEM((peers, tokens, model), F32),
            ],
            (moe_flops, expert_bytes + 4 * peers * tokens * model),
            "experts",
        )
        s.kept, s.made, s.statistics = results[-3:]
        return list(results[:-3])

    count_row = 2 * experts

    def run_head(micro):
        s = state[micro]
        s.slope, slope_low, s.grad_head, s.norm_three, s.squares = call(
            partial(head_kernel, micro, len(s.moe), tasks),
            (images,),
            (order[0],),
            [(s.res, token_block)]
            + [
                (part, token_block if lead is None else one_whole(part, lead))
                for part, lead in s.moe
            ]
            + [
                (targets, image_block(targets, micro)),
                (masks, image_block(masks, micro)),
                (norm_weight, whole(norm_weight)),
                (head_weight, whole(head_weight)),
            ],
            [
                (shape_of((tokens, model), F32), token_block),
                (shape_of((tokens, model), BF16), token_block),
                (shape_of((outputs, model), F32), kept_out((outputs, model))),
                (shape_of((8, model), F32), kept_out((8, model))),
                (shape_of((8, LANES), F32), kept_out((8, LANES))),
            ],
            [],
            (6 * tokens * model * outputs, tokens * (outputs * 2 + pixels * 4 + 12 * model)),
            "head",
            24,
        )
        return slope_low

    extra_block = pl.BlockSpec(
        (extra, model), lambda *_: (tokens // extra, 0), pipeline_mode=pl.Buffered(1)
    )

    def run_experts_back(micro, e, prior):
        s = state[micro]
        more_grads, more_tokens = prior is not None, e > 0
        split = micro == micros - 1
        one_block = pl.BlockSpec(
            (1, slots_total, model), lambda *_: (e, 0, 0), pipeline_mode=pl.Buffered(1)
        )
        weight_block = pl.BlockSpec(
            (1, 2, model, hidden), lambda *_: (e, 0, 0, 0), pipeline_mode=pl.Buffered(1)
        )
        inputs = (
            [(piece, whole(piece)) for piece in s.slopes]
            + [(piece, extra_block) for piece in s.tokens]
            + [(s.kept, one_block), (s.made, one_block), (expert_low, weight_block)]
            + [(tables, whole(tables))]
        )
        if more_grads:
            inputs.append((prior, whole(prior)))
        if more_tokens:
            inputs += [(piece, whole(piece)) for piece in s.pieces]
        grad_shape = (2, model, hidden)
        grads_out = (
            [(shape_of(grad_shape[1:], BF16), kept_out(grad_shape[1:]))] * 2
            if split
            else [(shape_of(grad_shape, BF16), kept_out(grad_shape))]
        )
        results = call(
            partial(
                moe_backward_kernel,
                (peers, micro, images, e, owned, experts),
                more_grads,
                more_tokens,
                split,
            ),
            (1,),
            (order[0], order[1], place),
            inputs,
            pieces_out(long, model) + grads_out,
            [
                pltpu.VMEM((slots_total, tokens), BF16),
                pltpu.VMEM((slots_total, 1), F32),
                pltpu.VMEM((slots_total, model), BF16),
            ],
            (3 * moe_flops // owned, expert_bytes * 5 // owned + 4 * peers * tokens * model),
            "experts_back",
        )
        s.pieces = list(results[:peers])
        return list(results[peers:])

    def run_attend_back(micro):
        s = state[micro]
        parts = s.sent_parts
        results = call(
            partial(back_kernel, micro, peers, peers, images),
            (images,),
            (order[0], order[1]),
            [(s.slope, token_block)]
            + [(part, token_block) for part in parts]
            + [
                (part, pl.BlockSpec((extra, model), lambda *_: (tokens // extra, 0)))
                for part in parts
            ]
            + [
                (s.res, token_block),
                (s.emb, token_block),
                (s.probs_mlp, expert_block),
                (slots, micro_block((experts, patch_count), micro)),
                (tables, whole(tables)),
            ]
            + [(piece, kv_block) for piece in s.kv]
            + [
                (picks, micro_block((top, patch_count), micro)),
                (s.gates_att, expert_block),
                (s.probs_att, expert_block),
                (s.lse, top_block),
            ]
            + [(piece, whole(piece)) for piece in attention]
            + [
                (s.mix, pl.BlockSpec((1, head_rows, patch_count), lambda i, *_: (i, 0, 0))),
                (norm_weight, whole(norm_weight)),
                (router_rows, whole(router_rows)),
            ],
            [
                (shape_of((tokens, model), F32), token_block),
                (shape_of((tokens, model), F32), token_block),
            ]
            + [(shape_of((tokens, pair_width), BF16), kv_block)] * peers
            + [
                (shape_of((peers, 2, span, model), F32), kept_out((peers, 2, span, model))),
                (shape_of((router_count, model), F32), kept_out((router_count, model))),
                (shape_of((8, model), F32), kept_out((8, model))),
                (shape_of((8, LANES), F32), kept_out((8, LANES))),
            ],
            [
                pltpu.VMEM((keys, pair_width), BF16),
                pltpu.VMEM((pair_width, keys), BF16),
                pltpu.VMEM((head_rows, patch_count), F32),
                pltpu.VMEM((head_rows, patch_count), F32),
                pltpu.VMEM((keys, pair_width), F32),
                pltpu.VMEM((head_rows, patch_count), F32),
                pltpu.VMEM((experts, patch_count), F32),
            ],
            (attention_flops * 3, tokens * model * 30),
            "attention_back",
        )
        s.slope_one, s.normed_slope = results[:2]
        s.grad_att, s.grad_router, s.norm_two, s.mutual = results[2 + peers :]
        return list(results[2 : 2 + peers])

    def run_last(micro):
        s = state[micro]
        s.grad_patch, s.grad_keyval, s.norm_one = call(
            partial(last_kernel, peers),
            (images,),
            (),
            [
                (patches, image_block(patches, micro)),
                (s.emb, token_block),
                (s.slope_one, token_block),
                (s.normed_slope, token_block),
            ]
            + [(part, kv_block) for part in s.kv_parts]
            + [(keyval_weight, whole(keyval_weight)), (norm_weight, whole(norm_weight))],
            [
                (shape_of((patch_in, model), F32), kept_out((patch_in, model))),
                (shape_of((pair_width, model), F32), kept_out((pair_width, model))),
                (shape_of((8, model), F32), kept_out((8, model))),
            ],
            [],
            (2 * tokens * model * (patch_in + 2 * pair_width), tokens * model * 20),
            "embedding_back",
            24,
        )

    step_value = step_count[0].astype(F32)
    scales = jnp.stack(
        [1.0 / (1.0 - jnp.power(BETA_ONE, step_value)), 1.0 / (1.0 - jnp.power(BETA_TWO, step_value))]
    )
    first, second = state
    came_w = across(attention_own)
    picks, slots, count_rows = run_routing()
    (picks,) = settle(picks)
    counts = jnp.zeros((8, LANES), F32).at[0, :tasks].set(jnp.sum(count_rows, axis=(0, 2)))
    kv = run_embed(0)
    (first.emb, kv), came_w = settle_groups([first.emb, kv], came_w)
    more_w = beside(attention_own, came_w)
    first.kv = gather_direct(kv)
    kv = run_embed(1)
    (second.emb, kv), more_w, first.kv = settle_groups([second.emb, kv], more_w, first.kv)
    attention = ordered(attention_own, came_w, more_w)
    second.kv = gather_direct(kv)

    run_attend(0)
    (first.res, first.sent), second.kv = settle_groups([first.res, first.sent], second.kv)
    counts = jnp.zeros((8, LANES), F32)
    came_first = across(first.sent)
    run_attend(1)
    (second.res, second.sent), came_first = settle_groups(
        [second.res, second.sent], came_first
    )
    more_first = beside(first.sent, came_first)
    came_second = across(second.sent)
    expert_low = after(expert_weight, order[1]).astype(BF16)
    (expert_low,), more_first = settle_groups([expert_low], more_first)
    first.tokens = ordered(first.sent, came_first, more_first)

    first_pieces = run_experts(0, False)
    (first.kept,), first_pieces, came_second = settle_groups(
        [first.kept], first_pieces, came_second
    )
    more_second = beside(second.sent, came_second)
    first_parts = scatter_direct(first_pieces)
    (more_second,) = settle_groups(more_second)
    second.tokens = ordered(second.sent, came_second, more_second)
    second_odd, *second_evens = run_experts(1, True)
    (second.kept, second_odd), rest = settle_groups([second.kept, second_odd], first_parts[1:])
    first.moe = [(part, None) for part in first_parts[:1] + rest]
    second_crossed = swap(second_odd, "expert", 1)
    hops = Hops(first.statistics + second.statistics, ("dp",))
    hops.start()
    (second_crossed,) = settle(second_crossed)
    second_rest = [
        swap(
            (second_evens[n].astype(F32) + second_crossed[n].astype(F32)).astype(BF16),
            "expert",
            2 * n,
        )
        for n in range(1, half_peers)
    ]

    first_low = run_head(0)
    (first.slope, first_low), came = settle_groups([first.slope, first_low], hops.came)
    came_first = across(first_low)
    hops.land(came)
    (second_rest,) = settle_groups(second_rest)
    second.moe = [(second_evens[0], None), (second_crossed, 0)]
    second.moe += [(part, None) for part in second_rest]
    second_low = run_head(1)
    (second.slope, second_low), came_first, came = settle_groups(
        [second.slope, second_low], came_first, hops.came
    )
    more_first = beside(first_low, came_first)
    second.slopes = gather_direct(second_low)
    hops.land(came)
    more_first, came = settle_groups(more_first, hops.came)
    hops.land(came)
    first.slopes = ordered(first_low, came_first, more_first)
    tables = hops.finish()

    def small_call(kernel, scalars, inputs, shapes, scratch, name, room=24):
        return call(
            kernel,
            (1,),
            scalars,
            [(a, whole(a)) for a in inputs],
            [(s, kept_out(s.shape)) for s in shapes],
            scratch,
            (0, 1000),
            name,
            room,
        )

    exchanged = [dev]

    def exchange(value):
        value = along_z(after(value, exchanged[0], order[1]))
        exchanged[0] = value
        return value

    def cut_shares(keep, came):
        rows, width = keep.shape
        total = (keep.astype(F32) + came.astype(F32)).astype(BF16)
        return exchange(total.reshape(far, rows // far, width))

    def sum_shares(moved, dense_rows):
        return small_call(
            partial(share_sum_kernel, dense_rows),
            (place,),
            [moved],
            [shape_of(moved.shape, BF16), shape_of((8, LANES), F32)],
            [],
            "share_sum",
        )

    prior = run_experts_back(0, 0, None)
    first.pieces, second.slopes, prior = settle_groups(first.pieces, second.slopes, prior)
    keep_first, send_first = run_experts_back(1, 0, prior[0])
    second.pieces, (keep_first, send_first) = settle_groups(
        second.pieces, [keep_first, send_first]
    )
    came_x_first = swap(send_first, "dp", 1)
    prior = run_experts_back(0, 1, None)
    first.pieces, prior = settle_groups(first.pieces, prior)
    first.sent_parts = scatter_direct(first.pieces)
    keep_second, send_second = run_experts_back(1, 1, prior[0])
    (keep_second, send_second), second.pieces, first.sent_parts, (came_x_first,) = settle_groups(
        [keep_second, send_second], second.pieces, first.sent_parts, [came_x_first]
    )
    came_x_second = swap(send_second, "dp", 1)
    second.sent_parts = scatter_direct(second.pieces)
    square_parts = [s.squares for s in state]
    shares_first = cut_shares(keep_first, came_x_first)

    kv_parts = run_attend_back(0)
    kv_parts, second.sent_parts, (came_x_second, shares_first) = settle_groups(
        kv_parts, second.sent_parts, [came_x_second, shares_first]
    )
    first.kv_parts = scatter_direct(kv_parts)
    summed_first, squares = sum_shares(shares_first, 0)
    square_parts.append(squares)
    shares_second = cut_shares(keep_second, came_x_second)
    (summed_first,) = settle(summed_first)
    kv_parts = run_attend_back(1)
    kv_parts, first.kv_parts, (shares_second,) = settle_groups(
        kv_parts, first.kv_parts, [shares_second]
    )
    second.kv_parts = scatter_direct(kv_parts)
    own_first = exchange(summed_first).reshape(model, hidden)
    summed_second, squares = sum_shares(shares_second, 0)
    square_parts.append(squares)
    (summed_second,) = settle(summed_second)
    run_last(0)
    (first.norm_one,), second.kv_parts = settle_groups([first.norm_one], second.kv_parts)
    run_last(1)
    (second.norm_one,) = settle(second.norm_one)

    packed_parts = []
    for s in state:
        packed_parts += [s.grad_head, s.grad_patch, s.grad_keyval, s.grad_router]
        packed_parts += [s.norm_one, s.norm_two, s.norm_three, s.grad_att]
    used_rows = outputs + patch_in + pair_width + router_count + 6
    dense_rows = -(-used_rows // 256) * 256
    dense_share = dense_rows // peers
    all_rows = dense_share + 2 * span
    packed = small_call(
        partial(pack_kernel, peers, micros, dense_rows, (tasks, pixels, count_row)),
        (order[1],),
        packed_parts + [tables],
        [shape_of((half_peers, all_rows, model), BF16)]
        + [shape_of((1, all_rows, model), BF16)] * half_peers,
        [pltpu.VMEM((dense_rows, model), BF16)],
        "pack",
    )
    packed = settle(*packed)
    odd, evens = packed[0], packed[1:]
    crossed = swap(odd, "expert", 1)
    (crossed,) = settle(crossed)
    pairs = [
        (evens[n].astype(F32) + crossed[n : n + 1].astype(F32)).astype(BF16)
        for n in range(1, half_peers)
    ]
    pairs = settle(*pairs)
    lead_parts = [evens[0], crossed] + [
        swap(pair, "expert", 2 * n + 2) for n, pair in enumerate(pairs)
    ]
    own_first = after(own_first, order[1])
    own_second = exchange(summed_second).reshape(model, hidden)
    *lead_parts, scales = settle(*lead_parts, scales)
    parts = [(part, 0) for part in lead_parts]
    half_shape = shape_of((all_rows // 2, model), BF16)
    keep, send = call(
        partial(halves_kernel, len(parts)),
        (1,),
        (place,),
        [(part, pl.BlockSpec((1, all_rows, model), lambda *_, lead=lead: (lead, 0, 0))) for part, lead in parts],
        [(half_shape, kept_out(half_shape.shape))] * 2,
        [pltpu.VMEM((all_rows, model), BF16)],
        (0, 8 * all_rows * model),
        "halves",
        24,
    )
    keep, send = settle(keep, send)
    came = swap(send, "dp", 1)
    came, own_first = settle(came, own_first)
    other_first = swap(own_first, "dp", 1)
    (own_second,) = settle(own_second)
    shares, squares = sum_shares(cut_shares(keep, came), dense_share)
    sums = squares
    for part in square_parts:
        sums = sums + part
    sums, shares = settle(sums, shares)
    hops = Hops(sums, ("expert", "dp"))
    hops.start()
    own = exchange(shares).reshape(all_rows // 2, model)
    while len(hops.steps) > 2:
        hops.land(settle(*hops.came))
    (own, other_first), came = settle_groups([own, other_first], hops.came)
    other = swap(own, "dp", 1)
    hops.land(came)
    (other,), came = settle_groups([other], hops.came)
    hops.land(came)
    dense_part, attention_part = small_call(
        partial(join_halves_kernel, dense_share),
        (place,),
        [own, other],
        [shape_of((dense_share, model), BF16), shape_of((2 * span, model), BF16)],
        [pltpu.VMEM((all_rows, model), BF16)],
        "join_halves",
    )
    came_quarters = across(dense_part)
    (last_came,) = settle(*hops.came)
    sums = hops.value
    other_second = swap(after(own_second, order[1]), "dp", 1)
    total_params = (
        patch_weight.size
        + keyval_weight.size
        + router_weight.size
        + norm_weight.size
        + head_weight.size
        + (attention_weight.size + expert_weight.size) * peers
    )
    limit = CLIP_UNIT * math.sqrt(total_params)
    block_rows = model // 2
    def adam_expert(e, own, other, before):
        block = pl.BlockSpec((1, 1, block_rows, hidden), lambda w, b, *_: (e, w, b, 0))
        grad_block = pl.BlockSpec((block_rows, hidden), lambda w, b, *_: (b, 0))
        inputs = [own, other, sums, last_came, expert_weight, expert_moment, expert_square]
        specs = [grad_block, grad_block, whole(sums), whole(last_came), block, block, block]
        aliases = {}
        if before is not None:
            aliases = {2 + len(inputs) + n: n for n in range(3)}
            inputs += list(before)
            specs += [pl.BlockSpec(memory_space=pl.ANY)] * 3
        return pl.pallas_call(
            partial(adam_kernel, RATES[6], limit),
            grid_spec=pltpu.PrefetchScalarGridSpec(
                num_scalar_prefetch=2,
                grid=(2, model // block_rows),
                in_specs=specs,
                out_specs=[block] * 3,
            ),
            out_shape=[shape_of(expert_weight.shape, F32)] * 3,
            input_output_aliases=aliases,
            cost_estimate=pl.CostEstimate(
                flops=expert_weight.size * 20 // owned,
                bytes_accessed=expert_weight.size * 26 // owned,
                transcendentals=0,
            ),
            name="adam",
        )(place, scales, *inputs)

    expert_results = adam_expert(0, own_first, other_first, None)
    (expert_results, came_quarters) = settle_groups(list(expert_results), came_quarters)
    quarters = ordered(dense_part, came_quarters, beside(dense_part, came_quarters))
    expert_results = adam_expert(1, own_second, other_second, expert_results)
    dense_states = [
        head_weight,
        head_moment,
        head_square,
        patch_weight,
        patch_moment,
        patch_square,
        keyval_weight,
        keyval_moment,
        keyval_square,
        router_rows,
        router_moment.T,
        router_square.T,
        norm_weight,
        norm_moment,
        norm_square,
        attention_weight,
        attention_moment,
        attention_square,
    ]
    dense_results = small_call(
        partial(
            adam_dense_kernel,
            peers,
            (RATES[4], RATES[0], RATES[1], RATES[2], RATES[3], RATES[5]),
            limit,
            tasks,
            count_row,
        ),
        (order[1], scales),
        quarters
        + [attention_part, sums, last_came, tables, state[0].mutual]
        + dense_states,
        [shape_of(a.shape, F32) for a in dense_states] + [shape_of((8, LANES), F32)],
        [pltpu.VMEM((dense_rows, model), BF16)],
        "adam_dense",
        None,
    )
    new_head, new_patch, new_keyval, new_router, new_norm, new_attention = [
        list(dense_results[3 * n : 3 * n + 3]) for n in range(6)
    ]
    new_router = [a.T for a in new_router]
    return tuple(
        [dense_results[18][0, n] for n in range(3)]
        + new_patch
        + new_keyval
        + new_router
        + new_norm
        + new_head
        + new_attention
        + list(expert_results)
    )


def solution(mesh):
    tokens = P(None, "dp", "expert", None)
    by_columns = P(None, None, "expert")
    by_expert = P("expert", None, None, None)
    same = P()
    placed = (
        (tokens, P(None, "dp", "expert", None, None, None), tokens, tokens, P(None, "dp"), same)
        + (same,) * 15
        + (by_columns,) * 3
        + (by_expert,) * 3
    )
    return jax.shard_map(
        local,
        mesh=mesh,
        in_specs=placed,
        out_specs=(same,) * 18 + (by_columns,) * 3 + (by_expert,) * 3,
        check_vma=False,
    )
```

```python
from functools import partial
import math
from types import SimpleNamespace

import jax
import jax.numpy as jnp
from jax import lax
from jax.experimental import pallas as pl
from jax.experimental.pallas import tpu as pltpu
from jax.sharding import PartitionSpec as P

HEAD = 64
NORM_EPS = 1e-06
MI_WEIGHT = 0.5
CLIP_UNIT = 3e-07
BETA_ONE = 0.9
BETA_TWO = 0.999
EPSILON = 1e-08
RATES = (0.02, 0.02, 0.02, 0.3, 0.02, 1.2, 0.02)
DECAY = 0.05
F32 = jnp.float32
BF16 = jnp.bfloat16
NOWHERE = 1 << 20
LANES = 128
GELU_A = 0.044715
GELU_C = math.sqrt(2.0 / math.pi)


def mm(left, right, precision=None):
    return lax.dot_general(
        left, right, (((1,), (0,)), ((), ())), precision=precision, preferred_element_type=F32
    )


def mm_nt(left, right, precision=None):
    return lax.dot_general(
        left, right, (((1,), (1,)), ((), ())), precision=precision, preferred_element_type=F32
    )


def mm_tn(left, right, precision=None):
    return lax.dot_general(
        left, right, (((0,), (0,)), ((), ())), precision=precision, preferred_element_type=F32
    )


def two_terms(values):
    high = values.astype(BF16)
    return high, (values - high.astype(F32)).astype(BF16)


def fine(product, left, right, axis):
    left_high, left_low = two_terms(left)
    right_high, right_low = two_terms(right)
    both = product(jnp.concatenate([left_high, left_low], axis=axis), right_high)
    rest = product(left_high, right_low)
    rows = rest.shape[0]
    if both.shape[0] == rows:
        return both + rest
    return both[:rows] + both[rows:] + rest


def small_tn(left, right):
    left_high, left_low = two_terms(left)
    right_high, right_low = two_terms(right)
    return mm_tn(
        jnp.concatenate([left_high, left_low, left_high], axis=0),
        jnp.concatenate([right_high, right_high, right_low], axis=0),
    )


def norm_forward(values, gain, shift):
    centred = values - jnp.mean(values, axis=-1, keepdims=True)
    inverse = lax.rsqrt(jnp.mean(centred * centred, axis=-1, keepdims=True) + NORM_EPS)
    scaled = centred * inverse
    return scaled, inverse, scaled * gain + shift


def norm_backward(slope, scaled, inverse, gain):
    inner = slope * gain
    grad = inverse * (
        inner
        - jnp.mean(inner, axis=-1, keepdims=True)
        - scaled * jnp.mean(inner * scaled, axis=-1, keepdims=True)
    )
    return grad, jnp.sum(slope * scaled, axis=0, keepdims=True), jnp.sum(slope, axis=0, keepdims=True)


def expert_rows(experts, tokens):
    return lax.broadcasted_iota(jnp.int32, (experts, tokens), 0)


def by_task(rows, task, experts):
    out = rows[:experts]
    for other in range(1, rows.shape[0] // experts):
        out = jnp.where(task == other, rows[other * experts : (other + 1) * experts], out)
    return out


def to_tasks(rows, task, tasks):
    return jnp.concatenate([jnp.where(task == t, rows, 0.0) for t in range(tasks)], axis=0)


def router_forward(router_rows, normed, task, experts):
    logits = by_task(fine(mm_nt, router_rows, normed, 0), task, experts)
    powers = jnp.exp(logits - jnp.max(logits, axis=0, keepdims=True))
    return powers / jnp.sum(powers, axis=0, keepdims=True)


def gate_forward(probs, chosen):
    picked = probs * chosen
    return picked / jnp.sum(picked, axis=0, keepdims=True)


def gate_backward(probs, chosen, grad_gates, grad_probs):
    total = jnp.sum(probs * chosen, axis=0, keepdims=True)
    gates = probs * chosen / total
    inner = chosen / total * (grad_gates - jnp.sum(grad_gates * gates, axis=0, keepdims=True))
    inner = inner + grad_probs
    return probs * (inner - jnp.sum(probs * inner, axis=0, keepdims=True))


def picked_hot(picks, experts):
    rows = expert_rows(experts, picks.shape[1])
    out = jnp.zeros(rows.shape, F32)
    for k in range(picks.shape[0]):
        out = out + (picks[k : k + 1, :] == rows).astype(F32)
    return out


def add_to(ref, index, value, first):
    @pl.when(first)
    def _():
        ref[index] = value

    @pl.when(jnp.logical_not(first))
    def _():
        ref[index] = ref[index] + value


def route_kernel(tid, routes, masks, picks, slots, counts):
    micro = pl.program_id(0)
    _, images, _, tasks, _, patch_count = routes.shape
    experts = slots.shape[1]
    tokens = images * patch_count
    chosen = []
    pixel_rows = [jnp.zeros((1, masks.shape[3]), F32) for _ in range(tasks)]
    for image in range(images):
        task = tid[micro, image]
        att, mlp = routes[0, image, 0, 0], routes[0, image, 1, 0]
        for t in range(1, tasks):
            att = jnp.where(task == t, routes[0, image, 0, t], att)
            mlp = jnp.where(task == t, routes[0, image, 1, t], mlp)
        picks[0, :, image * patch_count : (image + 1) * patch_count] = att
        chosen.append(picked_hot(mlp, experts))
        column = jnp.sum(masks[0, image].astype(F32), axis=0, keepdims=True)
        for t in range(tasks):
            pixel_rows[t] = pixel_rows[t] + jnp.where(task == t, column, 0.0)
    chosen = jnp.concatenate(chosen, axis=1)
    earlier = lax.broadcasted_iota(jnp.int32, (tokens, tokens), 0) < lax.broadcasted_iota(
        jnp.int32, (tokens, tokens), 1
    )
    before = mm(chosen.astype(BF16), earlier.astype(F32).astype(BF16))
    slots[0] = jnp.where(chosen > 0.0, before.astype(jnp.int32), NOWHERE)
    counts[0] = jnp.concatenate(pixel_rows, axis=0)


def embed_kernel(micro, tid, patches, patch_w, keyval_w, norms, router, picks, emb, kv, gates, probs):
    experts = gates.shape[0]
    task = tid[micro, pl.program_id(0)]
    width = router.shape[0] // 2
    embedded = mm(patches[0, 0], patch_w[...].astype(BF16))
    emb[...] = embedded
    _, _, normed = norm_forward(embedded, norms[0:1], norms[1:2])
    kv[...] = mm(normed.astype(BF16), keyval_w[...].astype(BF16)).astype(BF16)
    prob = router_forward(router[0:width], normed, task, experts)
    probs[...] = prob
    gates[...] = gate_forward(prob, picked_hot(picks[0], experts))


def split_planes(values):
    high = values.astype(BF16).astype(F32)
    middle = (values - high).astype(BF16).astype(F32)
    return [high, middle, (values - high - middle).astype(BF16).astype(F32)]


def put_planes(ref, planes, image, token_rows, images):
    patch_count, model = token_rows.shape
    block = jnp.concatenate(planes, axis=0).astype(BF16)
    height = block.shape[0]
    columns, chunks = model // LANES, patch_count // LANES
    rows, base = ref.shape[0], images * patch_count
    for i in range(images):

        @pl.when(image == i)
        def _(i=i):
            ref[i * patch_count : (i + 1) * patch_count, :] = token_rows
            if i == 0:
                ref[base:, :] = jnp.zeros((rows - base, model), BF16)
            for j in range(chunks):
                c = i * chunks + j
                top, left = base + c // columns * height, c % columns * LANES
                ref[top : top + height, left : left + LANES] = block[:, j * LANES : (j + 1) * LANES]


def lanes_of(shape):
    return lax.broadcasted_iota(jnp.int32, shape, 1)


def put_statistics(ref, images, patch_count, values):
    high, middle, rest = split_planes(values)
    block = high + pltpu.roll(middle, 8, 1) + pltpu.roll(rest, 16, 1)
    ref[ref.shape[0] - values.shape[0] :, ref.shape[1] - LANES :] = block.astype(BF16)


def get_statistics(block):
    block = block.astype(F32)
    total = block + pltpu.roll(block, LANES - 8, 1) + pltpu.roll(block, LANES - 16, 1)
    return jnp.where(lanes_of(block.shape) < 8, total, 0.0)


def extra_rows(count, experts, model):
    return -(-(count // LANES) // (model // LANES)) * 4 * experts


def get_planes(block, count, experts, columns):
    height = 4 * experts
    out = []
    for c in range(count // LANES):
        top, left = c // columns * height, c % columns * LANES
        out.append(block[top : top + height, left : left + LANES].astype(F32))
    return out


def three_sum(planes, experts):
    return planes[:experts] + planes[experts : 2 * experts] + planes[2 * experts : 3 * experts]


def fill_keys(pieces, kvs, kv_t):
    rows = pieces[0].shape[0]
    for r, piece in enumerate(pieces):
        block = piece[...]
        kvs[r * rows : (r + 1) * rows, :] = block
        kv_t[:, r * rows : (r + 1) * rows] = block.astype(F32).T.astype(BF16)


def attend_kernel(micro, peers, capacity, images, tid, dev, *refs):
    emb = refs[0]
    kv_in = refs[1 : 1 + peers]
    picks, gates_in, slots = refs[1 + peers : 4 + peers]
    weights = refs[4 + peers : 4 + 2 * peers]
    norms, router = refs[4 + 2 * peers : 6 + 2 * peers]
    probs_att, counts = refs[6 + 2 * peers : 8 + 2 * peers]
    res_out, sent, mix_out, lse, probs_out = refs[8 + 2 * peers : 13 + 2 * peers]
    table, kvs, kv_t, q_t, mix = refs[13 + 2 * peers :]
    experts, tokens = gates_in.shape
    owned = weights[0].shape[1] // HEAD
    task = tid[micro, pl.program_id(0)]
    width = router.shape[0] // 2
    mine = dev[0]
    embedded = emb[...]
    _, _, normed = norm_forward(embedded, norms[0:1], norms[1:2])
    low = normed.astype(BF16)
    span = owned * HEAD
    for r in range(peers):
        q_t[r * span : (r + 1) * span, :] = mm_nt(weights[r][0], low).astype(BF16).astype(F32)
    fill_keys(kv_in, kvs, kv_t)
    mix[...] = jnp.zeros(mix.shape, F32)
    blocks = [(r, e, (r * owned + e) * HEAD) for r in range(peers) for e in range(owned)]
    rows = expert_rows(experts, tokens)
    blank = jnp.zeros((HEAD, tokens), BF16)

    def one_pick(k, carry):
        pick = picks[0, pl.ds(k, 1), :]
        query = jnp.zeros((HEAD, tokens), F32)
        for r, e, at in blocks:
            here = pick == (mine ^ r) * owned + e
            query = query + jnp.where(here, q_t[at : at + HEAD, :], 0.0)
        gate = jnp.sum(jnp.where(rows == pick, gates_in[...], 0.0), axis=0, keepdims=True)
        scores = mm(kvs[...], jnp.concatenate([(query * HEAD ** (-0.5)).astype(BF16), blank], axis=0))
        top = jnp.max(scores, axis=0, keepdims=True)
        powers = jnp.exp(scores - top)
        total = jnp.sum(powers, axis=0, keepdims=True)
        lse[pl.ds(k, 1), :] = top + jnp.log(total)
        weighted = (powers * (gate / total)).astype(BF16)
        out = mm(kv_t[HEAD:, :], weighted)
        for r, e, at in blocks:
            here = pick == (mine ^ r) * owned + e
            mix[at : at + HEAD, :] = mix[at : at + HEAD, :] + jnp.where(here, out, 0.0)
        return carry

    lax.fori_loop(0, picks.shape[1], one_pick, 0, unroll=True)
    resid = embedded
    for r in range(peers):
        block = mix[r * span : (r + 1) * span, :].astype(BF16)
        mix_out[0, r * span : (r + 1) * span, :] = block
        resid = resid + mm_tn(block, weights[r][1])
    res_out[...] = resid
    _, _, normed_two = norm_forward(resid, norms[2:3], norms[3:4])
    prob = router_forward(router[width:], normed_two, task, experts)
    probs_out[...] = prob
    both = jnp.concatenate([probs_att[...], prob], axis=0)
    lane = lanes_of((2 * experts, LANES))
    per_task = jnp.where(lane == task, jnp.sum(both, axis=1, keepdims=True), 0.0)
    add_to(table, ..., per_task, pl.program_id(0) == 0)
    slot = slots[0]
    gates = gate_forward(prob, (slot < NOWHERE).astype(F32))
    places = jnp.minimum(slot, capacity).astype(F32)
    low_two = normed_two.astype(BF16)
    put_planes(sent, split_planes(gates) + [places], pl.program_id(0), low_two, images)

    @pl.when(pl.program_id(0) == images - 1)
    def _():
        rest = jnp.zeros((2 * experts - 8, LANES), F32)
        block = jnp.concatenate([table[...], counts[...], rest], axis=0)
        put_statistics(sent, images, tokens, block)


def read_planes(block, experts, count):
    chunks = get_planes(block, count, experts, block.shape[1] // LANES)
    gates = jnp.concatenate([three_sum(chunk, experts) for chunk in chunks], axis=1)
    return jnp.concatenate([chunk[3 * experts :] for chunk in chunks], axis=1), gates


def one_row(rows, at):
    index = expert_rows(rows.shape[0], rows.shape[1])
    return jnp.sum(jnp.where(index == at, rows, 0.0), axis=0, keepdims=True)


def loss_scale(counts, task):
    own = jnp.where(lanes_of(counts.shape) == task, counts, 0.0)
    return 1.0 / jnp.sum(own, axis=1, keepdims=True)


def dispatch(blocks, at, experts, count, hot, gate, scale=None):
    capacity = hot.shape[0] // len(blocks)
    places = lax.broadcasted_iota(jnp.int32, (capacity, count), 0).astype(F32)
    for r, block in enumerate(blocks):
        slots, gates = read_planes(block, experts, count)
        here = one_row(slots, at) == places
        rows = slice(r * capacity, (r + 1) * capacity)
        hot[rows, :] = here.astype(F32).astype(BF16)
        own = one_row(gates, at)
        if scale is not None:
            own = own * scale
        gate[rows, :] = jnp.sum(jnp.where(here, own, 0.0), axis=1, keepdims=True)


def moe_forward_kernel(peers, owned, experts, merged, dev, *refs):
    made_outs = 1 + peers // 2 if merged else peers
    arrays = refs[:peers]
    weights = refs[peers]
    outs = refs[peers + 1 : peers + 1 + made_outs]
    kept, made, statistics, hot, gate, back = refs[peers + 1 + made_outs :]
    e = pl.program_id(0)
    count = hot.shape[1]
    capacity = hot.shape[0] // peers
    dispatch([a[count:, :] for a in arrays], dev[0] * owned + e, experts, count, hot, gate)
    for r in range(peers):
        rows = slice(r * capacity, (r + 1) * capacity)
        kept[0, rows, :] = mm(hot[rows, :], arrays[r][:count, :]).astype(BF16)
    before = mm(kept[0], weights[0, 0])
    bent = jnp.tanh(before * (GELU_C + GELU_C * GELU_A * (before * before)))
    halved = 0.5 * before
    out = mm_nt((halved + halved * bent).astype(BF16), weights[0, 1])
    made[0] = out.astype(BF16)
    weighted = (out * gate[...]).astype(BF16)
    for r in range(peers):
        rows = slice(r * capacity, (r + 1) * capacity)
        value = mm_tn(hot[rows, :], weighted[rows, :])
        if owned > 1:
            add_to(back, r, value, e == 0)

    @pl.when(e == owned - 1)
    def _():
        for r in range(peers):
            piece = back[r].astype(BF16) if owned > 1 else value.astype(BF16)
            if not merged:
                outs[r][...] = piece
            elif r % 2:
                outs[0][r // 2] = piece
            else:
                outs[1 + r // 2][...] = piece
        rows = statistics.shape[0]
        block = jnp.zeros(statistics.shape, F32)
        for a in arrays:
            block = block + get_statistics(a[a.shape[0] - rows :, a.shape[1] - LANES :])
        statistics[...] = block


def head_kernel(micro, parts, tasks, tid, *refs):
    res = refs[0]
    moe = refs[1 : 1 + parts]
    targets, masks, norms, head_w = refs[1 + parts : 5 + parts]
    slope_out, slope_low, grad_head, grad_norm, squares = refs[5 + parts :]
    image = pl.program_id(0)
    task = tid[micro, image]
    resid = res[...]
    for part in moe:
        resid = resid + part[...].astype(F32)
    scaled, inverse, normed = norm_forward(resid, norms[4:5], norms[5:6])
    low = normed.astype(BF16)
    head_low = head_w[...].astype(BF16)
    pred = mm(low, head_low)
    mask = masks[0, 0].astype(F32)
    pixels = mask.shape[1]
    depth_on = jnp.where(task == 0, 1.0, 0.0)
    normal_on = jnp.where(task == 0, 0.0, 1.0)
    slopes = []
    total = jnp.zeros((1, pixels), F32)
    for group in range(4):
        on = depth_on if group == 0 else normal_on
        at = group * pixels
        gap = pred[:, at : at + pixels] - targets[0, 0, :, at : at + pixels].astype(F32)
        masked = mask * gap
        total = total + on * jnp.sum(masked * gap, axis=0, keepdims=True)
        slopes.append((masked * (2.0 * on)).astype(BF16))
    slope = jnp.concatenate(slopes, axis=1)
    first = image == 0
    spots = lax.broadcasted_iota(jnp.int32, (8, LANES), 0) * LANES + lanes_of((8, LANES))
    add_to(squares, ..., jnp.where(spots == task, jnp.sum(total, axis=1, keepdims=True), 0.0), first)
    add_to(grad_head, ..., mm_tn(slope, low), first)
    grad, gain, shift = norm_backward(mm_nt(slope, head_low), scaled, inverse, norms[4:5])
    both = jnp.concatenate([gain, shift], axis=0)
    for t in range(tasks):
        add_to(grad_norm, slice(2 * t, 2 * t + 2), jnp.where(task == t, both, 0.0), first)
    slope_out[...] = grad
    slope_low[...] = grad.astype(BF16)


def moe_backward_kernel(shape, more_grads, more_tokens, split, tid, dev, place, *refs):
    peers, micro, images, local_expert, owned, experts = shape
    refs = list(refs)

    def take(count):
        out = refs[:count]
        del refs[:count]
        return out

    slopes, extras = take(peers), take(peers)
    kept, made, weights, tables = take(4)
    if more_grads:
        (prior_grads,) = take(1)
    if more_tokens:
        prior_pieces = take(peers)
    outs = take(peers)
    grads_out = take(2 if split else 1)
    hot, gate, plain = take(3)
    count, model = slopes[0].shape
    capacity = hot.shape[0] // peers
    at = dev[0] * owned + local_expert
    counts = tables[2 * experts : 2 * experts + 1, :]
    per_image = count // images
    scale = jnp.concatenate(
        [
            jnp.broadcast_to(loss_scale(counts, tid[micro, image]), (1, per_image))
            for image in range(images)
        ],
        axis=1,
    )
    dispatch([extra[...] for extra in extras], at, experts, count, hot, gate, scale)
    gate_slopes = []
    for r in range(peers):
        rows = slice(r * capacity, (r + 1) * capacity)
        value = mm(hot[rows, :], slopes[r][...])
        gate_slopes.append(jnp.sum(value * made[0, rows, :].astype(F32), axis=1, keepdims=True))
        plain[rows, :] = (value * gate[rows, :]).astype(BF16)
    before = mm(kept[0], weights[0, 0])
    hidden = mm(plain[...], weights[0, 1])
    cubic = GELU_C * GELU_A * (before * before)
    bent = jnp.tanh(before * (GELU_C + cubic))
    middle = 0.5 + 0.5 * bent
    inner = (before * middle).astype(BF16)
    bend = middle + (middle - middle * bent) * (before * (GELU_C + 3.0 * cubic))
    slope = (hidden * bend).astype(BF16)
    entry = mm_tn(kept[0], slope)
    leave = mm_tn(plain[...], inner)
    if more_grads:
        entry = entry + prior_grads[0].astype(F32)
        leave = leave + prior_grads[1].astype(F32)
    if split:
        flip = place[0] == 0
        grads_out[0][...] = jnp.where(flip, entry, leave).astype(BF16)
        grads_out[1][...] = jnp.where(flip, leave, entry).astype(BF16)
    else:
        grads_out[0][0] = entry.astype(BF16)
        grads_out[0][1] = leave.astype(BF16)
    received = mm_nt(slope, weights[0, 0]).astype(BF16)
    columns, chunks, height = model // LANES, count // LANES, 4 * experts
    rows_of = expert_rows(experts, count)
    lane = lanes_of((capacity, LANES))
    for r in range(peers):
        rows = slice(r * capacity, (r + 1) * capacity)
        tokens_back = mm_tn(hot[rows, :], received[rows, :])
        terms = split_planes(gate_slopes[r])
        terms = jnp.where(lane == 0, terms[0], jnp.where(lane == 1, terms[1], terms[2]))
        terms = jnp.where(lane < 3, terms, 0.0).astype(BF16)
        gate_row = jnp.sum(mm_tn(terms, hot[rows, :])[:8, :], axis=0, keepdims=True) * scale
        planes = split_planes(jnp.where(rows_of == at, gate_row, 0.0))
        block = jnp.concatenate(planes + [jnp.zeros((experts, count), F32)], axis=0)
        lines = []
        for line in range(-(-chunks // columns)):
            cells = [
                block[:, c * LANES : (c + 1) * LANES]
                if c < chunks
                else jnp.zeros((height, LANES), F32)
                for c in range(line * columns, (line + 1) * columns)
            ]
            lines.append(jnp.concatenate(cells, axis=1))
        piece = jnp.concatenate([tokens_back] + lines, axis=0)
        if more_tokens:
            piece = piece + prior_pieces[r][...].astype(F32)
        outs[r][...] = piece.astype(BF16)


def table_slope(table, task, tasks):
    lane = lanes_of(table.shape)
    valid = lane < tasks
    table = jnp.where(valid, table, 0.0)
    total = jnp.sum(jnp.sum(table, axis=1, keepdims=True), axis=0, keepdims=True)
    share = table / total
    by_expert = jnp.sum(share, axis=1, keepdims=True)
    by_task_sum = jnp.sum(share, axis=0, keepdims=True)
    safe = jnp.where(valid, share, 1.0)
    gain = jnp.log(safe) - jnp.log(jnp.where(valid, by_task_sum, 1.0)) - jnp.log(by_expert)
    gain = jnp.where(valid, gain, 0.0)
    mean = jnp.sum(jnp.sum(gain * share, axis=1, keepdims=True), axis=0, keepdims=True)
    slope = -MI_WEIGHT * (gain - mean) / total
    return jnp.sum(jnp.where(lane == task, slope, 0.0), axis=1, keepdims=True), mean


def back_kernel(micro, peers, parts, image_count, tid, dev, *refs):
    slope_in = refs[0]
    sent_parts = refs[1 : 1 + parts]
    gate_parts = refs[1 + parts : 1 + 2 * parts]
    at = 1 + 2 * parts
    res, emb, probs_mlp, slots = refs[at : at + 4]
    at += 4
    tables = refs[at]
    kv_in = refs[at + 1 : at + 1 + peers]
    at += 1 + peers
    picks, gates_in, probs_att, lse = refs[at : at + 4]
    weights = refs[at + 4 : at + 4 + peers]
    at += 4 + peers
    mix_in, norms, router = refs[at : at + 3]
    slope_one, normed_slope = refs[at + 3 : at + 5]
    kv_outs = refs[at + 5 : at + 5 + peers]
    at += 5 + peers
    grad_att, grad_router, grad_norm, mutual = refs[at : at + 4]
    kvs, kv_t, q_t, d_t, dkv, dq_t, dgate = refs[at + 4 :]
    experts, tokens = gates_in.shape
    owned = weights[0].shape[1] // HEAD
    image = pl.program_id(0)
    first = image == 0
    task = tid[micro, image]
    width = router.shape[0] // 2
    tasks = width // experts
    span = owned * HEAD
    mine = dev[0]
    rows = expert_rows(experts, tokens)

    grad_sent = jnp.zeros(slope_in.shape, F32)
    for part in sent_parts:
        grad_sent = grad_sent + part[...].astype(F32)
    planes = gate_parts[0][...].astype(F32)
    for part in gate_parts[1:]:
        planes = planes + part[...].astype(F32)
    columns = planes.shape[1] // LANES
    chunks = get_planes(planes, image_count * tokens, experts, columns)
    per = tokens // LANES
    grad_gates = jnp.zeros((experts, tokens), F32)
    for i in range(image_count):
        cells = [three_sum(c, experts) for c in chunks[i * per : (i + 1) * per]]
        grad_gates = jnp.where(image == i, jnp.concatenate(cells, axis=1), grad_gates)
    scaled_two, inverse_two, normed_two = norm_forward(res[...], norms[2:3], norms[3:4])
    chosen = (slots[0] < NOWHERE).astype(F32)
    table, gain_mlp = table_slope(tables[experts : 2 * experts, :], task, tasks)
    logits = to_tasks(gate_backward(probs_mlp[...], chosen, grad_gates, table), task, tasks)
    grad_two = grad_sent + small_tn(logits, router[width:])
    add_to(grad_router, slice(width, 2 * width), fine(mm, logits, normed_two, 0), first)
    grad, gain, shift = norm_backward(grad_two, scaled_two, inverse_two, norms[2:3])
    add_to(grad_norm, slice(2, 3), gain, first)
    add_to(grad_norm, slice(3, 4), shift, first)
    scale = loss_scale(tables[2 * experts : 2 * experts + 1, :], task)
    resid_slope = slope_in[...] * scale + grad
    slope_one[...] = resid_slope
    branch = resid_slope.astype(BF16)

    _, _, normed = norm_forward(emb[...], norms[0:1], norms[1:2])
    low = normed.astype(BF16)
    for r in range(peers):
        at_r = slice(r * span, (r + 1) * span)
        q_t[at_r, :] = mm_nt(weights[r][0], low).astype(BF16).astype(F32)
        d_t[at_r, :] = mm_nt(weights[r][1], branch).astype(BF16).astype(F32)
        add_to(grad_att, (r, 1), mm(mix_in[0, at_r, :], branch), first)
    fill_keys(kv_in, kvs, kv_t)
    dkv[...] = jnp.zeros(dkv.shape, F32)
    dq_t[...] = jnp.zeros(dq_t.shape, F32)
    dgate[...] = jnp.zeros(dgate.shape, F32)
    blocks = [(r, e, (r * owned + e) * HEAD) for r in range(peers) for e in range(owned)]
    blank = jnp.zeros((HEAD, tokens), BF16)

    def one_pick(k, carry):
        pick = picks[0, pl.ds(k, 1), :]
        query = jnp.zeros((HEAD, tokens), F32)
        down = jnp.zeros((HEAD, tokens), F32)
        for r, e, at in blocks:
            here = pick == (mine ^ r) * owned + e
            query = query + jnp.where(here, q_t[at : at + HEAD, :], 0.0)
            down = down + jnp.where(here, d_t[at : at + HEAD, :], 0.0)
        gate = jnp.sum(jnp.where(rows == pick, gates_in[...], 0.0), axis=0, keepdims=True)
        query_low, down_low = query.astype(BF16), down.astype(BF16)
        scores = mm(kvs[...], jnp.concatenate([(query * HEAD ** (-0.5)).astype(BF16), blank], axis=0))
        probs = jnp.exp(scores - lse[pl.ds(k, 1), :])
        slope = mm(kvs[...], jnp.concatenate([blank, down_low], axis=0))
        delta = jnp.sum(probs * slope, axis=0, keepdims=True)
        gated = probs * gate
        weighted = gated.astype(BF16)
        grad_scores = (gated * (slope - delta) * HEAD ** (-0.5)).astype(BF16)
        joint = jnp.concatenate([grad_scores, weighted], axis=1)
        other = jnp.concatenate(
            [
                jnp.concatenate([query_low, blank], axis=0),
                jnp.concatenate([blank, down_low], axis=0),
            ],
            axis=1,
        )
        dkv[...] = dkv[...] + mm_nt(joint, other)
        dq = mm(kv_t[:HEAD, :], grad_scores)
        for r, e, at in blocks:
            here = pick == (mine ^ r) * owned + e
            dq_t[at : at + HEAD, :] = dq_t[at : at + HEAD, :] + jnp.where(here, dq, 0.0)
        dgate[...] = dgate[...] + jnp.where(rows == pick, delta, 0.0)
        return carry

    lax.fori_loop(0, picks.shape[1], one_pick, 0, unroll=True)
    for r in range(peers):
        block = dkv[r * tokens : (r + 1) * tokens, :].astype(BF16)
        kv_outs[r][...] = block

    table, gain_att = table_slope(tables[:experts, :], task, tasks)
    mutual[...] = jnp.broadcast_to(gain_att + gain_mlp, mutual.shape)
    chosen = picked_hot(picks[0], experts)
    logits = to_tasks(gate_backward(probs_att[...], chosen, dgate[...], table), task, tasks)
    grad_one = small_tn(logits, router[0:width])
    add_to(grad_router, slice(0, width), fine(mm, logits, normed, 0), first)
    for r in range(peers):
        block = dq_t[r * span : (r + 1) * span, :].astype(BF16)
        grad_one = grad_one + mm_tn(block, weights[r][0])
        add_to(grad_att, (r, 0), mm(block, low), first)
    normed_slope[...] = grad_one


def last_kernel(parts, *refs):
    patches, emb, slope_one, normed_slope = refs[:4]
    kv_parts = refs[4 : 4 + parts]
    keyval_w, norms = refs[4 + parts : 6 + parts]
    grad_patch, grad_keyval, grad_norm = refs[6 + parts :]
    first = pl.program_id(0) == 0
    scaled, inverse, normed = norm_forward(emb[...], norms[0:1], norms[1:2])
    grad_kv = jnp.zeros(kv_parts[0].shape, F32)
    for part in kv_parts:
        grad_kv = grad_kv + part[...].astype(F32)
    grad_kv = grad_kv.astype(BF16)
    add_to(grad_keyval, ..., mm_tn(grad_kv, normed.astype(BF16)), first)
    slope = normed_slope[...] + mm_nt(grad_kv, keyval_w[...].astype(BF16))
    grad, gain, shift = norm_backward(slope, scaled, inverse, norms[0:1])
    add_to(grad_norm, slice(0, 1), gain, first)
    add_to(grad_norm, slice(1, 2), shift, first)
    add_to(grad_patch, ..., mm_tn(patches[0, 0], (slope_one[...] + grad).astype(BF16)), first)


def pack_kernel(peers, micros, dense_rows, sizes, dev, *refs):
    names = 8
    values = []
    for n in range(names):
        value = refs[n][...]
        for m in range(1, micros):
            value = value + refs[m * names + n][...]
        values.append(value)
    head, patch, keyval, router, one, two, three, attention = values
    tables, odd = refs[micros * names : micros * names + 2]
    evens = refs[micros * names + 2 : -1]
    dense = refs[-1]
    tasks, pixels, count_row = sizes
    scales = [loss_scale(tables[count_row : count_row + 1, :], t) for t in range(tasks)]
    head = jnp.concatenate([head[:pixels] * scales[0], head[pixels:] * scales[1]], axis=0)
    three = sum(three[2 * t : 2 * t + 2] * scales[t] for t in range(tasks))
    at = 0
    for value in (head, patch, keyval):
        dense[at : at + value.shape[0], :] = value.astype(BF16)
        at += value.shape[0]
    rest = [router, one[0:2], two[2:4], three]
    pad = dense_rows - at - router.shape[0] - 6
    if pad:
        rest.append(jnp.zeros((pad, dense.shape[1]), F32))
    dense[at:, :] = jnp.concatenate(rest, axis=0).astype(BF16)
    share = dense_rows // peers
    model = dense.shape[1]
    for r in range(peers):
        start = pl.multiple_of((dev[0] ^ r) * share, 16)
        rows = dense[pl.ds(start, share), :]
        owned_rows = attention[r].reshape(-1, model).astype(BF16)
        if r % 2:
            odd[r // 2, :share] = rows
            odd[r // 2, share:] = owned_rows
        else:
            evens[r // 2][0, :share] = rows
            evens[r // 2][0, share:] = owned_rows


def halves_kernel(parts, place, *refs):
    keep, send, total = refs[parts:]
    value = refs[0][0].astype(F32)
    for part in refs[1:parts]:
        value = value + part[0].astype(F32)
    total[...] = value.astype(BF16)
    rows = keep.shape[0]
    keep[...] = total[pl.ds(pl.multiple_of(place[0] * rows, 16), rows), :]
    send[...] = total[pl.ds(pl.multiple_of((1 - place[0]) * rows, 16), rows), :]


def share_sum_kernel(dense_rows, place, shares, outs, squares):
    count, rows, width = shares.shape
    value = shares[0].astype(F32)
    for r in range(1, count):
        value = value + shares[r].astype(F32)
    low = value.astype(BF16)
    for r in range(count):
        outs[r] = low
    value = low.astype(F32)
    value = value * value
    both = jnp.sum(value, axis=0, keepdims=True)
    if dense_rows:
        start = (place[0] * count + place[1]) * rows
        row = lax.broadcasted_iota(jnp.int32, (rows, width), 0) + start
        dense = jnp.sum(jnp.where(row < dense_rows, value, 0.0), axis=0, keepdims=True)
    else:
        dense = jnp.zeros((1, width), F32)
    spots = lax.broadcasted_iota(jnp.int32, (8, LANES), 0) * LANES + lanes_of((8, LANES))
    own = jnp.sum(both - dense, axis=1, keepdims=True)
    dense = jnp.sum(dense, axis=1, keepdims=True)
    squares[...] = jnp.where(spots == 2, own, 0.0) + jnp.where(spots == 3, dense, 0.0)


def join_halves_kernel(dense_rows, place, own, other, dense, rest, total):
    rows = own.shape[0]
    total[pl.ds(pl.multiple_of(place[0] * rows, 16), rows), :] = own[...]
    total[pl.ds(pl.multiple_of((1 - place[0]) * rows, 16), rows), :] = other[...]
    dense[...] = total[:dense_rows, :]
    rest[...] = total[dense_rows:, :]


def clip_factor(sums, other_sums, limit):
    total = sums[0:1, :] + other_sums[0:1, :]
    own, dense = total[:, 2:3], total[:, 3:4]
    norm = jnp.sqrt(own + dense)
    return jnp.minimum(1.0, limit / norm), norm, jnp.sqrt(own), total


def adam_step(weight, first, second, gradient, rate, factor, scales):
    gradient = gradient * factor
    moment = BETA_ONE * first + (1.0 - BETA_ONE) * gradient
    square = BETA_TWO * second + ((1.0 - BETA_TWO) * gradient) * gradient
    step = (moment * (rate * scales[0])) / (jnp.sqrt(square * scales[1]) + EPSILON)
    return weight * (1.0 - rate * DECAY) - step, moment, square


def adam_kernel(rate, limit, place, scales, *refs):
    own, other, sums, other_sums, weight, first, second = refs[:7]
    factor = clip_factor(sums, other_sums, limit)[0]
    gradient = jnp.where(pl.program_id(0) == place[0], own[...], other[...]).astype(F32)
    news = adam_step(weight[0, 0], first[0, 0], second[0, 0], gradient, rate, factor, scales)
    for ref, new in zip(refs[-3:], news):
        ref[0, 0] = new


def adam_dense_kernel(peers, rates, limit, tasks, count_row, dev, scales, *refs):
    pieces, attention = refs[:peers], refs[peers]
    sums, other_sums, counts, mutual = refs[peers + 1 : peers + 5]
    states = [refs[peers + 5 + 3 * n : peers + 8 + 3 * n] for n in range(6)]
    outs = [refs[peers + 23 + 3 * n : peers + 26 + 3 * n] for n in range(6)]
    scalars, dense = refs[-4:-1], refs[-1]
    factor, norm, own_norm, total = clip_factor(sums, other_sums, limit)
    lane = lanes_of((1, LANES))
    ratio = total / jnp.where(lane < tasks, counts[count_row : count_row + 1, :], 1.0)
    loss = jnp.sum(jnp.where(lane < tasks, ratio, 0.0), axis=1, keepdims=True)
    loss = loss - MI_WEIGHT * mutual[0:1, 0:1]
    for ref, value in zip(scalars, (loss, norm, own_norm)):
        ref[...] = value
    share = pieces[0].shape[0]
    for r in range(peers):
        dense[pl.ds(pl.multiple_of((dev[0] ^ r) * share, 16), share), :] = pieces[r][...]

    def update(n, index, gradient):
        olds = [ref[index] for ref in states[n]]
        news = adam_step(*olds, gradient, rates[n], factor, scales)
        for ref, new in zip(outs[n], news):
            ref[index] = new

    outputs = states[0][0].shape[1]
    step = 2 * LANES
    for left in range(0, outputs, step):
        block = dense[left : left + step, :].astype(F32).T
        update(0, (slice(None), slice(left, left + step)), block)
    at = outputs
    rows = states[1][0].shape[0]
    update(1, ..., dense[at : at + rows, :].astype(F32))
    at += rows
    width = states[2][0].shape[1]
    update(2, ..., dense[at : at + width, :].astype(F32).T)
    at += width
    rest = dense[at:, :].astype(F32)
    rows = states[3][0].shape[0]
    update(3, ..., rest[:rows])
    update(4, ..., rest[rows : rows + states[4][0].shape[0]])
    width = states[5][0].shape[2]
    for n in range(2):
        update(5, n, attention[n * width : (n + 1) * width, :].astype(F32).T)


def whole(array):
    rank = len(array.shape)
    return pl.BlockSpec(array.shape, lambda *_: (0,) * rank, pipeline_mode=pl.Buffered(1))


def kept_out(shape):
    rank = len(shape)
    return pl.BlockSpec(shape, lambda *_: (0,) * rank)


def shape_of(shape, dtype):
    return jax.ShapeDtypeStruct(shape, dtype)


def call(kernel, grid, scalars, inputs, outputs, scratch, cost, name, room=None):
    spec = pltpu.PrefetchScalarGridSpec(
        num_scalar_prefetch=len(scalars),
        grid=grid,
        in_specs=[s for _, s in inputs],
        out_specs=[s for _, s in outputs],
        scratch_shapes=scratch,
    )
    return pl.pallas_call(
        kernel,
        grid_spec=spec,
        out_shape=[o for o, _ in outputs],
        cost_estimate=pl.CostEstimate(
            flops=int(cost[0]), bytes_accessed=int(cost[1]), transcendentals=0
        ),
        compiler_params=None if room is None else pltpu.CompilerParams(vmem_limit_bytes=room << 20),
        name=name,
    )(*scalars, *[a for a, _ in inputs])


def swap(value, axis, mask):
    size = lax.axis_size(axis)
    return lax.ppermute(value, axis, [(i, i ^ mask) for i in range(size)])


def bits_of(axis):
    return [1 << b for b in range(lax.axis_size(axis).bit_length() - 1)]


def gather_direct(value):
    return [value] + [swap(value, "expert", r) for r in range(1, lax.axis_size("expert"))]


def scatter_direct(pieces):
    return [pieces[0]] + [swap(pieces[r], "expert", r) for r in range(1, len(pieces))]


def across(value):
    rest = [swap(value, "expert", r) for r in range(2, lax.axis_size("expert"), 2)]
    return rest + [swap(value, "expert", 1)]


def beside(value, came):
    rest = came[:-1]
    return [swap(block, "expert", 1) for block in rest]


def ordered(value, came, more):
    out = [value, came[-1]]
    for block, other in zip(came[:-1], more):
        out += [block, other]
    return out


def gather_pieces(value):
    came = across(value)
    return ordered(value, came, beside(value, came))


def after(value, *anchors):
    return lax.optimization_barrier((value,) + anchors)[0]


class Hops:
    def __init__(self, value, axes):
        self.value = value
        self.steps = [(axis, bit) for axis in axes for bit in bits_of(axis)]
        if len(axes) > 1:
            self.steps.sort(key=lambda step: step == (axes[1], 1))
        self.came = []

    def start(self):
        if self.steps:
            self.came = [swap(self.value, *self.steps.pop(0))]

    def land(self, came):
        if self.came:
            self.value = self.value + came[-1]
            self.came = []
        self.start()

    def finish(self):
        while self.came or self.steps:
            self.land(self.came)
        return self.value


def along_z(value):
    size = lax.axis_size("dp")
    groups = [[i for i in range(size) if i % 2 == low] for low in range(2)]
    return lax.all_to_all(
        value, "dp", split_axis=0, concat_axis=0, axis_index_groups=groups, tiled=True
    )


def local(
    patches,
    routes,
    masks,
    targets,
    task_ids,
    step_count,
    patch_weight,
    patch_moment,
    patch_square,
    keyval_weight,
    keyval_moment,
    keyval_square,
    router_weight,
    router_moment,
    router_square,
    norm_weight,
    norm_moment,
    norm_square,
    head_weight,
    head_moment,
    head_square,
    attention_weight,
    attention_moment,
    attention_square,
    expert_weight,
    expert_moment,
    expert_square,
):
    peers = lax.axis_size("expert")
    half_peers = peers // 2
    micros, images, patch_count, patch_in = patches.shape
    _, _, _, _, tasks, top = routes.shape
    owned = expert_weight.shape[0]
    experts = owned * peers
    model, hidden = expert_weight.shape[2:]
    tokens = images * patch_count
    capacity = max(2, tokens * top // experts)
    pixels = masks.shape[3]
    outputs = targets.shape[3]
    pair_width = 2 * HEAD
    span = owned * HEAD
    keys = peers * patch_count
    head_rows = peers * span
    extra = extra_rows(tokens, experts, model)
    long = tokens + extra
    far = lax.axis_size("dp") // 2
    dev = lax.axis_index("expert").astype(jnp.int32).reshape(1)
    spot = lax.axis_index("dp").astype(jnp.int32)
    place = jnp.stack([spot & 1, spot >> 1])
    router_rows = router_weight.T
    router_count = router_rows.shape[0]
    routes_lanes = jnp.transpose(routes, (0, 1, 3, 4, 5, 2))
    attention_own = jnp.transpose(attention_weight, (0, 2, 1)).astype(BF16)
    attention = gather_direct(attention_own)

    order = [task_ids, dev]

    def settle(*values):
        out = lax.optimization_barrier((order[0], order[1]) + values)
        order[:] = out[:2]
        return list(out[2:])

    def settle_groups(*groups):
        out = settle(*[value for group in groups for value in group])
        back = []
        for group in groups:
            back.append(out[: len(group)])
            out = out[len(group) :]
        return back

    token_block = pl.BlockSpec((patch_count, model), lambda i, *_: (i, 0))
    expert_block = pl.BlockSpec((experts, patch_count), lambda i, *_: (0, i))
    kv_block = pl.BlockSpec((patch_count, pair_width), lambda i, *_: (i, 0))
    top_block = pl.BlockSpec((top, patch_count), lambda i, *_: (0, i))

    def micro_block(shape, micro):
        return pl.BlockSpec((1,) + shape, lambda i, *_, m=micro: (m,) + (0,) * (len(shape) - 1) + (i,))

    def image_block(array, micro):
        return pl.BlockSpec((1, 1) + array.shape[2:], lambda i, *_, m=micro: (m, i, 0, 0))

    def pieces_out(rows, width):
        return [(shape_of((rows, width), BF16), kept_out((rows, width)))] * peers


    def one_whole(array, lead):
        return pl.BlockSpec(
            (pl.Squeezed(), patch_count, array.shape[2]), lambda i, *_: (lead, i, 0)
        )

    state = [SimpleNamespace() for _ in range(micros)]

    def run_routing():
        return call(
            route_kernel,
            (micros,),
            (order[0],),
            [
                (
                    routes_lanes,
                    pl.BlockSpec((1,) + routes_lanes.shape[1:], lambda m, *_: (m, 0, 0, 0, 0, 0)),
                ),
                (masks, pl.BlockSpec((1,) + masks.shape[1:], lambda m, *_: (m, 0, 0, 0))),
            ],
            [
                (
                    shape_of((micros, top, tokens), jnp.int32),
                    pl.BlockSpec((1, top, tokens), lambda m, *_: (m, 0, 0)),
                ),
                (
                    shape_of((micros, experts, tokens), jnp.int32),
                    pl.BlockSpec((1, experts, tokens), lambda m, *_: (m, 0, 0)),
                ),
                (
                    shape_of((micros, tasks, pixels), F32),
                    pl.BlockSpec((1, tasks, pixels), lambda m, *_: (m, 0, 0)),
                ),
            ],
            [],
            (micros * tokens * tokens * 32, masks.size * 4),
            "routing",
        )

    def run_embed(micro):
        s = state[micro]
        s.emb, kv, s.gates_att, s.probs_att = call(
            partial(embed_kernel, micro),
            (images,),
            (order[0],),
            [
                (patches, image_block(patches, micro)),
                (patch_weight, whole(patch_weight)),
                (keyval_weight, whole(keyval_weight)),
                (norm_weight, whole(norm_weight)),
                (router_rows, whole(router_rows)),
                (picks, micro_block((top, patch_count), micro)),
            ],
            [
                (shape_of((tokens, model), F32), token_block),
                (shape_of((tokens, pair_width), BF16), kv_block),
                (shape_of((experts, tokens), F32), expert_block),
                (shape_of((experts, tokens), F32), expert_block),
            ],
            [],
            (2 * tokens * model * (patch_in + pair_width), tokens * (2 * patch_in + 4 * model) + patch_weight.size * 4),
            "embedding",
        )
        return kv

    attention_flops = 2 * top * tokens * keys * HEAD * 8

    def run_attend(micro):
        s = state[micro]
        s.res, s.sent, s.mix, s.lse, s.probs_mlp = call(
            partial(attend_kernel, micro, peers, capacity, images),
            (images,),
            (order[0], order[1]),
            [(s.emb, token_block)]
            + [(piece, kv_block) for piece in s.kv]
            + [
                (picks, micro_block((top, patch_count), micro)),
                (s.gates_att, expert_block),
                (slots, micro_block((experts, patch_count), micro)),
            ]
            + [(piece, whole(piece)) for piece in attention]
            + [
                (norm_weight, whole(norm_weight)),
                (router_rows, whole(router_rows)),
                (s.probs_att, expert_block),
                (counts, whole(counts)),
            ],
            [
                (shape_of((tokens, model), F32), token_block),
                (shape_of((long, model), BF16), kept_out((long, model))),
                (
                    shape_of((images, head_rows, patch_count), BF16),
                    pl.BlockSpec((1, head_rows, patch_count), lambda i, *_: (i, 0, 0)),
                ),
                (shape_of((top, tokens), F32), top_block),
                (shape_of((experts, tokens), F32), expert_block),
            ],
            [
                pltpu.VMEM((2 * experts, LANES), F32),
                pltpu.VMEM((keys, pair_width), BF16),
                pltpu.VMEM((pair_width, keys), BF16),
                pltpu.VMEM((head_rows, patch_count), F32),
                pltpu.VMEM((head_rows, patch_count), F32),
            ],
            (attention_flops, tokens * model * 12),
            "attention",
        )

    moe_flops = 2 * owned * peers * capacity * model * (2 * hidden + 2 * tokens)
    expert_bytes = expert_weight.size * 2
    odd_shape = (half_peers, tokens, model)

    slots_total = peers * capacity
    by_slot = shape_of((owned, slots_total, model), BF16)
    slot_block = pl.BlockSpec((1, slots_total, model), lambda e, *_: (e, 0, 0))

    def run_experts(micro, merged):
        s = state[micro]
        results = call(
            partial(moe_forward_kernel, peers, owned, experts, merged),
            (owned,),
            (order[1],),
            [(piece, whole(piece)) for piece in s.tokens]
            + [(expert_low, pl.BlockSpec((1, 2, model, hidden), lambda e, *_: (e, 0, 0, 0)))],
            (
                [(shape_of(odd_shape, BF16), kept_out(odd_shape))]
                + [(shape_of((tokens, model), BF16), kept_out((tokens, model)))] * half_peers
                if merged
                else pieces_out(tokens, model)
            )
            + [
                (by_slot, slot_block),
                (by_slot, slot_block),
                (shape_of((4 * experts, LANES), F32), kept_out((4 * experts, LANES))),
            ],
            [
                pltpu.VMEM((slots_total, tokens), BF16),
                pltpu.VMEM((slots_total, 1), F32),
                pltpu.VMEM((peers, tokens, model), F32),
            ],
            (moe_flops, expert_bytes + 4 * peers * tokens * model),
            "experts",
        )
        s.kept, s.made, s.statistics = results[-3:]
        return list(results[:-3])

    count_row = 2 * experts

    def run_head(micro):
        s = state[micro]
        s.slope, slope_low, s.grad_head, s.norm_three, s.squares = call(
            partial(head_kernel, micro, len(s.moe), tasks),
            (images,),
            (order[0],),
            [(s.res, token_block)]
            + [
                (part, token_block if lead is None else one_whole(part, lead))
                for part, lead in s.moe
            ]
            + [
                (targets, image_block(targets, micro)),
                (masks, image_block(masks, micro)),
                (norm_weight, whole(norm_weight)),
                (head_weight, whole(head_weight)),
            ],
            [
                (shape_of((tokens, model), F32), token_block),
                (shape_of((tokens, model), BF16), token_block),
                (shape_of((outputs, model), F32), kept_out((outputs, model))),
                (shape_of((8, model), F32), kept_out((8, model))),
                (shape_of((8, LANES), F32), kept_out((8, LANES))),
            ],
            [],
            (6 * tokens * model * outputs, tokens * (outputs * 2 + pixels * 4 + 12 * model)),
            "head",
        )
        return slope_low

    extra_block = pl.BlockSpec(
        (extra, model), lambda *_: (tokens // extra, 0), pipeline_mode=pl.Buffered(1)
    )

    def run_experts_back(micro, e, prior):
        s = state[micro]
        more_grads, more_tokens = prior is not None, e > 0
        split = micro == micros - 1
        one_block = pl.BlockSpec(
            (1, slots_total, model), lambda *_: (e, 0, 0), pipeline_mode=pl.Buffered(1)
        )
        weight_block = pl.BlockSpec(
            (1, 2, model, hidden), lambda *_: (e, 0, 0, 0), pipeline_mode=pl.Buffered(1)
        )
        inputs = (
            [(piece, whole(piece)) for piece in s.slopes]
            + [(piece, extra_block) for piece in s.tokens]
            + [(s.kept, one_block), (s.made, one_block), (expert_low, weight_block)]
            + [(tables, whole(tables))]
        )
        if more_grads:
            inputs.append((prior, whole(prior)))
        if more_tokens:
            inputs += [(piece, whole(piece)) for piece in s.pieces]
        grad_shape = (2, model, hidden)
        grads_out = (
            [(shape_of(grad_shape[1:], BF16), kept_out(grad_shape[1:]))] * 2
            if split
            else [(shape_of(grad_shape, BF16), kept_out(grad_shape))]
        )
        results = call(
            partial(
                moe_backward_kernel,
                (peers, micro, images, e, owned, experts),
                more_grads,
                more_tokens,
                split,
            ),
            (1,),
            (order[0], order[1], place),
            inputs,
            pieces_out(long, model) + grads_out,
            [
                pltpu.VMEM((slots_total, tokens), BF16),
                pltpu.VMEM((slots_total, 1), F32),
                pltpu.VMEM((slots_total, model), BF16),
            ],
            (3 * moe_flops // owned, expert_bytes * 5 // owned + 4 * peers * tokens * model),
            "experts_back",
        )
        s.pieces = list(results[:peers])
        return list(results[peers:])

    def run_attend_back(micro):
        s = state[micro]
        parts = s.sent_parts
        results = call(
            partial(back_kernel, micro, peers, peers, images),
            (images,),
            (order[0], order[1]),
            [(s.slope, token_block)]
            + [(part, token_block) for part in parts]
            + [
                (part, pl.BlockSpec((extra, model), lambda *_: (tokens // extra, 0)))
                for part in parts
            ]
            + [
                (s.res, token_block),
                (s.emb, token_block),
                (s.probs_mlp, expert_block),
                (slots, micro_block((experts, patch_count), micro)),
                (tables, whole(tables)),
            ]
            + [(piece, kv_block) for piece in s.kv]
            + [
                (picks, micro_block((top, patch_count), micro)),
                (s.gates_att, expert_block),
                (s.probs_att, expert_block),
                (s.lse, top_block),
            ]
            + [(piece, whole(piece)) for piece in attention]
            + [
                (s.mix, pl.BlockSpec((1, head_rows, patch_count), lambda i, *_: (i, 0, 0))),
                (norm_weight, whole(norm_weight)),
                (router_rows, whole(router_rows)),
            ],
            [
                (shape_of((tokens, model), F32), token_block),
                (shape_of((tokens, model), F32), token_block),
            ]
            + [(shape_of((tokens, pair_width), BF16), kv_block)] * peers
            + [
                (shape_of((peers, 2, span, model), F32), kept_out((peers, 2, span, model))),
                (shape_of((router_count, model), F32), kept_out((router_count, model))),
                (shape_of((8, model), F32), kept_out((8, model))),
                (shape_of((8, LANES), F32), kept_out((8, LANES))),
            ],
            [
                pltpu.VMEM((keys, pair_width), BF16),
                pltpu.VMEM((pair_width, keys), BF16),
                pltpu.VMEM((head_rows, patch_count), F32),
                pltpu.VMEM((head_rows, patch_count), F32),
                pltpu.VMEM((keys, pair_width), F32),
                pltpu.VMEM((head_rows, patch_count), F32),
                pltpu.VMEM((experts, patch_count), F32),
            ],
            (attention_flops * 3, tokens * model * 30),
            "attention_back",
        )
        s.slope_one, s.normed_slope = results[:2]
        s.grad_att, s.grad_router, s.norm_two, s.mutual = results[2 + peers :]
        return list(results[2 : 2 + peers])

    def run_last(micro):
        s = state[micro]
        s.grad_patch, s.grad_keyval, s.norm_one = call(
            partial(last_kernel, peers),
            (images,),
            (),
            [
                (patches, image_block(patches, micro)),
                (s.emb, token_block),
                (s.slope_one, token_block),
                (s.normed_slope, token_block),
            ]
            + [(part, kv_block) for part in s.kv_parts]
            + [(keyval_weight, whole(keyval_weight)), (norm_weight, whole(norm_weight))],
            [
                (shape_of((patch_in, model), F32), kept_out((patch_in, model))),
                (shape_of((pair_width, model), F32), kept_out((pair_width, model))),
                (shape_of((8, model), F32), kept_out((8, model))),
            ],
            [],
            (2 * tokens * model * (patch_in + 2 * pair_width), tokens * model * 20),
            "embedding_back",
            24,
        )

    step_value = step_count[0].astype(F32)
    scales = jnp.stack(
        [1.0 / (1.0 - jnp.power(BETA_ONE, step_value)), 1.0 / (1.0 - jnp.power(BETA_TWO, step_value))]
    )
    first, second = state
    came_w = across(attention_own)
    picks, slots, count_rows = run_routing()
    (picks,) = settle(picks)
    counts = jnp.zeros((8, LANES), F32).at[0, :tasks].set(jnp.sum(count_rows, axis=(0, 2)))
    kv = run_embed(0)
    (first.emb, kv), came_w = settle_groups([first.emb, kv], came_w)
    more_w = beside(attention_own, came_w)
    first.kv = gather_direct(kv)
    kv = run_embed(1)
    (second.emb, kv), more_w, first.kv = settle_groups([second.emb, kv], more_w, first.kv)
    attention = ordered(attention_own, came_w, more_w)
    second.kv = gather_direct(kv)

    run_attend(0)
    (first.res, first.sent), second.kv = settle_groups([first.res, first.sent], second.kv)
    counts = jnp.zeros((8, LANES), F32)
    came_first = across(first.sent)
    run_attend(1)
    (second.res, second.sent), came_first = settle_groups(
        [second.res, second.sent], came_first
    )
    more_first = beside(first.sent, came_first)
    came_second = across(second.sent)
    expert_low = after(expert_weight, order[1]).astype(BF16)
    (expert_low,), more_first = settle_groups([expert_low], more_first)
    first.tokens = ordered(first.sent, came_first, more_first)

    first_pieces = run_experts(0, False)
    (first.kept,), first_pieces, came_second = settle_groups(
        [first.kept], first_pieces, came_second
    )
    more_second = beside(second.sent, came_second)
    first_parts = scatter_direct(first_pieces)
    (more_second,) = settle_groups(more_second)
    second.tokens = ordered(second.sent, came_second, more_second)
    second_odd, *second_evens = run_experts(1, True)
    (second.kept, second_odd), rest = settle_groups([second.kept, second_odd], first_parts[1:])
    first.moe = [(part, None) for part in first_parts[:1] + rest]
    second_crossed = swap(second_odd, "expert", 1)
    hops = Hops(first.statistics + second.statistics, ("dp",))
    hops.start()
    (second_crossed,) = settle(second_crossed)
    second_rest = [
        swap(
            (second_evens[n].astype(F32) + second_crossed[n].astype(F32)).astype(BF16),
            "expert",
            2 * n,
        )
        for n in range(1, half_peers)
    ]

    first_low = run_head(0)
    (first.slope, first_low), came = settle_groups([first.slope, first_low], hops.came)
    came_first = across(first_low)
    hops.land(came)
    (second_rest,) = settle_groups(second_rest)
    second.moe = [(second_evens[0], None), (second_crossed, 0)]
    second.moe += [(part, None) for part in second_rest]
    second_low = run_head(1)
    (second.slope, second_low), came_first, came = settle_groups(
        [second.slope, second_low], came_first, hops.came
    )
    more_first = beside(first_low, came_first)
    second.slopes = gather_direct(second_low)
    hops.land(came)
    more_first, came = settle_groups(more_first, hops.came)
    hops.land(came)
    first.slopes = ordered(first_low, came_first, more_first)
    tables = hops.finish()

    def small_call(kernel, scalars, inputs, shapes, scratch, name, room=24):
        return call(
            kernel,
            (1,),
            scalars,
            [(a, whole(a)) for a in inputs],
            [(s, kept_out(s.shape)) for s in shapes],
            scratch,
            (0, 1000),
            name,
            room,
        )

    exchanged = [dev]

    def exchange(value):
        value = along_z(after(value, exchanged[0], order[1]))
        exchanged[0] = value
        return value

    def cut_shares(keep, came):
        rows, width = keep.shape
        total = (keep.astype(F32) + came.astype(F32)).astype(BF16)
        return exchange(total.reshape(far, rows // far, width))

    def sum_shares(moved, dense_rows):
        return small_call(
            partial(share_sum_kernel, dense_rows),
            (place,),
            [moved],
            [shape_of(moved.shape, BF16), shape_of((8, LANES), F32)],
            [],
            "share_sum",
        )

    prior = run_experts_back(0, 0, None)
    first.pieces, second.slopes, prior = settle_groups(first.pieces, second.slopes, prior)
    keep_first, send_first = run_experts_back(1, 0, prior[0])
    second.pieces, (keep_first, send_first) = settle_groups(
        second.pieces, [keep_first, send_first]
    )
    came_x_first = swap(send_first, "dp", 1)
    prior = run_experts_back(0, 1, None)
    first.pieces, prior = settle_groups(first.pieces, prior)
    first.sent_parts = scatter_direct(first.pieces)
    keep_second, send_second = run_experts_back(1, 1, prior[0])
    came_x_second = swap(send_second, "dp", 1)
    (keep_second,), second.pieces, first.sent_parts, (came_x_first,) = settle_groups(
        [keep_second], second.pieces, first.sent_parts, [came_x_first]
    )
    second.sent_parts = scatter_direct(second.pieces)
    square_parts = [s.squares for s in state]
    shares_first = cut_shares(keep_first, came_x_first)

    kv_parts = run_attend_back(0)
    kv_parts, second.sent_parts, (came_x_second, shares_first) = settle_groups(
        kv_parts, second.sent_parts, [came_x_second, shares_first]
    )
    first.kv_parts = scatter_direct(kv_parts)
    summed_first, squares = sum_shares(shares_first, 0)
    square_parts.append(squares)
    shares_second = cut_shares(keep_second, came_x_second)
    (summed_first,) = settle(summed_first)
    kv_parts = run_attend_back(1)
    kv_parts, first.kv_parts, (shares_second,) = settle_groups(
        kv_parts, first.kv_parts, [shares_second]
    )
    second.kv_parts = scatter_direct(kv_parts)
    own_first = exchange(summed_first).reshape(model, hidden)
    summed_second, squares = sum_shares(shares_second, 0)
    square_parts.append(squares)
    (summed_second,) = settle(summed_second)
    run_last(0)
    (first.norm_one,), second.kv_parts = settle_groups([first.norm_one], second.kv_parts)
    run_last(1)
    (second.norm_one,) = settle(second.norm_one)

    packed_parts = []
    for s in state:
        packed_parts += [s.grad_head, s.grad_patch, s.grad_keyval, s.grad_router]
        packed_parts += [s.norm_one, s.norm_two, s.norm_three, s.grad_att]
    used_rows = outputs + patch_in + pair_width + router_count + 6
    dense_rows = -(-used_rows // 256) * 256
    dense_share = dense_rows // peers
    all_rows = dense_share + 2 * span
    packed = small_call(
        partial(pack_kernel, peers, micros, dense_rows, (tasks, pixels, count_row)),
        (order[1],),
        packed_parts + [tables],
        [shape_of((half_peers, all_rows, model), BF16)]
        + [shape_of((1, all_rows, model), BF16)] * half_peers,
        [pltpu.VMEM((dense_rows, model), BF16)],
        "pack",
    )
    packed = settle(*packed)
    odd, evens = packed[0], packed[1:]
    crossed = swap(odd, "expert", 1)
    (crossed,) = settle(crossed)
    pairs = [
        (evens[n].astype(F32) + crossed[n : n + 1].astype(F32)).astype(BF16)
        for n in range(1, half_peers)
    ]
    pairs = settle(*pairs)
    lead_parts = [evens[0], crossed] + [
        swap(pair, "expert", 2 * n + 2) for n, pair in enumerate(pairs)
    ]
    own_first = after(own_first, order[1])
    own_second = exchange(summed_second).reshape(model, hidden)
    *lead_parts, scales = settle(*lead_parts, scales)
    parts = [(part, 0) for part in lead_parts]
    half_shape = shape_of((all_rows // 2, model), BF16)
    keep, send = call(
        partial(halves_kernel, len(parts)),
        (1,),
        (place,),
        [(part, pl.BlockSpec((1, all_rows, model), lambda *_, lead=lead: (lead, 0, 0))) for part, lead in parts],
        [(half_shape, kept_out(half_shape.shape))] * 2,
        [pltpu.VMEM((all_rows, model), BF16)],
        (0, 8 * all_rows * model),
        "halves",
        24,
    )
    keep, send = settle(keep, send)
    came = swap(send, "dp", 1)
    came, own_first = settle(came, own_first)
    other_first = swap(own_first, "dp", 1)
    (own_second,) = settle(own_second)
    shares, squares = sum_shares(cut_shares(keep, came), dense_share)
    sums = squares
    for part in square_parts:
        sums = sums + part
    sums, shares = settle(sums, shares)
    hops = Hops(sums, ("expert", "dp"))
    hops.start()
    own = exchange(shares).reshape(all_rows // 2, model)
    while len(hops.steps) > 2:
        hops.land(settle(*hops.came))
    (own, other_first), came = settle_groups([own, other_first], hops.came)
    other = swap(own, "dp", 1)
    hops.land(came)
    (other,), came = settle_groups([other], hops.came)
    hops.land(came)
    dense_part, attention_part = small_call(
        partial(join_halves_kernel, dense_share),
        (place,),
        [own, other],
        [shape_of((dense_share, model), BF16), shape_of((2 * span, model), BF16)],
        [pltpu.VMEM((all_rows, model), BF16)],
        "join_halves",
    )
    came_quarters = across(dense_part)
    (last_came,) = settle(*hops.came)
    sums = hops.value
    other_second = swap(after(own_second, order[1]), "dp", 1)
    total_params = (
        patch_weight.size
        + keyval_weight.size
        + router_weight.size
        + norm_weight.size
        + head_weight.size
        + (attention_weight.size + expert_weight.size) * peers
    )
    limit = CLIP_UNIT * math.sqrt(total_params)
    block_rows = model // 2
    def adam_expert(e, own, other, before):
        block = pl.BlockSpec((1, 1, block_rows, hidden), lambda w, b, *_: (e, w, b, 0))
        grad_block = pl.BlockSpec((block_rows, hidden), lambda w, b, *_: (b, 0))
        inputs = [own, other, sums, last_came, expert_weight, expert_moment, expert_square]
        specs = [grad_block, grad_block, whole(sums), whole(last_came), block, block, block]
        aliases = {}
        if before is not None:
            aliases = {2 + len(inputs) + n: n for n in range(3)}
            inputs += list(before)
            specs += [pl.BlockSpec(memory_space=pl.ANY)] * 3
        return pl.pallas_call(
            partial(adam_kernel, RATES[6], limit),
            grid_spec=pltpu.PrefetchScalarGridSpec(
                num_scalar_prefetch=2,
                grid=(2, model // block_rows),
                in_specs=specs,
                out_specs=[block] * 3,
            ),
            out_shape=[shape_of(expert_weight.shape, F32)] * 3,
            input_output_aliases=aliases,
            cost_estimate=pl.CostEstimate(
                flops=expert_weight.size * 20 // owned,
                bytes_accessed=expert_weight.size * 26 // owned,
                transcendentals=0,
            ),
            name="adam",
        )(place, scales, *inputs)

    expert_results = adam_expert(0, own_first, other_first, None)
    (expert_results, came_quarters) = settle_groups(list(expert_results), came_quarters)
    quarters = ordered(dense_part, came_quarters, beside(dense_part, came_quarters))
    expert_results = adam_expert(1, own_second, other_second, expert_results)
    dense_states = [
        head_weight,
        head_moment,
        head_square,
        patch_weight,
        patch_moment,
        patch_square,
        keyval_weight,
        keyval_moment,
        keyval_square,
        router_rows,
        router_moment.T,
        router_square.T,
        norm_weight,
        norm_moment,
        norm_square,
        attention_weight,
        attention_moment,
        attention_square,
    ]
    dense_results = small_call(
        partial(
            adam_dense_kernel,
            peers,
            (RATES[4], RATES[0], RATES[1], RATES[2], RATES[3], RATES[5]),
            limit,
            tasks,
            count_row,
        ),
        (order[1], scales),
        quarters
        + [attention_part, sums, last_came, tables, state[0].mutual]
        + dense_states,
        [shape_of(a.shape, F32) for a in dense_states] + [shape_of((1, 1), F32)] * 3,
        [pltpu.VMEM((dense_rows, model), BF16)],
        "adam_dense",
        None,
    )
    new_head, new_patch, new_keyval, new_router, new_norm, new_attention = [
        list(dense_results[3 * n : 3 * n + 3]) for n in range(6)
    ]
    new_router = [a.T for a in new_router]
    return tuple(
        [dense_results[18 + n].reshape(()) for n in range(3)]
        + new_patch
        + new_keyval
        + new_router
        + new_norm
        + new_head
        + new_attention
        + list(expert_results)
    )


def solution(mesh):
    tokens = P(None, "dp", "expert", None)
    by_columns = P(None, None, "expert")
    by_expert = P("expert", None, None, None)
    same = P()
    placed = (
        (tokens, P(None, "dp", "expert", None, None, None), tokens, tokens, P(None, "dp"), same)
        + (same,) * 15
        + (by_columns,) * 3
        + (by_expert,) * 3
    )
    return jax.shard_map(
        local,
        mesh=mesh,
        in_specs=placed,
        out_specs=(same,) * 18 + (by_columns,) * 3 + (by_expert,) * 3,
        check_vma=False,
    )
```

```python
from functools import partial
import math
from types import SimpleNamespace

import jax
import jax.numpy as jnp
from jax import lax
from jax.experimental import pallas as pl
from jax.experimental.pallas import tpu as pltpu
from jax.sharding import PartitionSpec as P

HEAD = 64
NORM_EPS = 1e-06
MI_WEIGHT = 0.5
CLIP_UNIT = 3e-07
BETA_ONE = 0.9
BETA_TWO = 0.999
EPSILON = 1e-08
RATES = (0.02, 0.02, 0.02, 0.3, 0.02, 1.2, 0.02)
DECAY = 0.05
F32 = jnp.float32
BF16 = jnp.bfloat16
NOWHERE = 1 << 20
LANES = 128
GELU_A = 0.044715
GELU_C = math.sqrt(2.0 / math.pi)


def mm(left, right, precision=None):
    return lax.dot_general(
        left, right, (((1,), (0,)), ((), ())), precision=precision, preferred_element_type=F32
    )


def mm_nt(left, right, precision=None):
    return lax.dot_general(
        left, right, (((1,), (1,)), ((), ())), precision=precision, preferred_element_type=F32
    )


def mm_tn(left, right, precision=None):
    return lax.dot_general(
        left, right, (((0,), (0,)), ((), ())), precision=precision, preferred_element_type=F32
    )


def two_terms(values):
    high = values.astype(BF16)
    return high, (values - high.astype(F32)).astype(BF16)


def fine(product, left, right, axis):
    left_high, left_low = two_terms(left)
    right_high, right_low = two_terms(right)
    both = product(jnp.concatenate([left_high, left_low], axis=axis), right_high)
    rest = product(left_high, right_low)
    rows = rest.shape[0]
    if both.shape[0] == rows:
        return both + rest
    return both[:rows] + both[rows:] + rest


def small_tn(left, right):
    left_high, left_low = two_terms(left)
    right_high, right_low = two_terms(right)
    return mm_tn(
        jnp.concatenate([left_high, left_low, left_high], axis=0),
        jnp.concatenate([right_high, right_high, right_low], axis=0),
    )


def norm_forward(values, gain, shift):
    centred = values - jnp.mean(values, axis=-1, keepdims=True)
    inverse = lax.rsqrt(jnp.mean(centred * centred, axis=-1, keepdims=True) + NORM_EPS)
    scaled = centred * inverse
    return scaled, inverse, scaled * gain + shift


def norm_backward(slope, scaled, inverse, gain):
    inner = slope * gain
    grad = inverse * (
        inner
        - jnp.mean(inner, axis=-1, keepdims=True)
        - scaled * jnp.mean(inner * scaled, axis=-1, keepdims=True)
    )
    return grad, jnp.sum(slope * scaled, axis=0, keepdims=True), jnp.sum(slope, axis=0, keepdims=True)


def expert_rows(experts, tokens):
    return lax.broadcasted_iota(jnp.int32, (experts, tokens), 0)


def by_task(rows, task, experts):
    out = rows[:experts]
    for other in range(1, rows.shape[0] // experts):
        out = jnp.where(task == other, rows[other * experts : (other + 1) * experts], out)
    return out


def to_tasks(rows, task, tasks):
    return jnp.concatenate([jnp.where(task == t, rows, 0.0) for t in range(tasks)], axis=0)


def router_forward(router_rows, normed, task, experts):
    logits = by_task(fine(mm_nt, router_rows, normed, 0), task, experts)
    powers = jnp.exp(logits - jnp.max(logits, axis=0, keepdims=True))
    return powers / jnp.sum(powers, axis=0, keepdims=True)


def gate_forward(probs, chosen):
    picked = probs * chosen
    return picked / jnp.sum(picked, axis=0, keepdims=True)


def gate_backward(probs, chosen, grad_gates, grad_probs):
    total = jnp.sum(probs * chosen, axis=0, keepdims=True)
    gates = probs * chosen / total
    inner = chosen / total * (grad_gates - jnp.sum(grad_gates * gates, axis=0, keepdims=True))
    inner = inner + grad_probs
    return probs * (inner - jnp.sum(probs * inner, axis=0, keepdims=True))


def picked_hot(picks, experts):
    rows = expert_rows(experts, picks.shape[1])
    out = jnp.zeros(rows.shape, F32)
    for k in range(picks.shape[0]):
        out = out + (picks[k : k + 1, :] == rows).astype(F32)
    return out


def add_to(ref, index, value, first):
    @pl.when(first)
    def _():
        ref[index] = value

    @pl.when(jnp.logical_not(first))
    def _():
        ref[index] = ref[index] + value


def route_kernel(tid, routes, masks, picks, slots, counts):
    micro = pl.program_id(0)
    _, images, _, tasks, _, patch_count = routes.shape
    experts = slots.shape[1]
    tokens = images * patch_count
    chosen = []
    pixel_rows = [jnp.zeros((1, masks.shape[3]), F32) for _ in range(tasks)]
    for image in range(images):
        task = tid[micro, image]
        att, mlp = routes[0, image, 0, 0], routes[0, image, 1, 0]
        for t in range(1, tasks):
            att = jnp.where(task == t, routes[0, image, 0, t], att)
            mlp = jnp.where(task == t, routes[0, image, 1, t], mlp)
        picks[0, :, image * patch_count : (image + 1) * patch_count] = att
        chosen.append(picked_hot(mlp, experts))
        column = jnp.sum(masks[0, image].astype(F32), axis=0, keepdims=True)
        for t in range(tasks):
            pixel_rows[t] = pixel_rows[t] + jnp.where(task == t, column, 0.0)
    chosen = jnp.concatenate(chosen, axis=1)
    earlier = lax.broadcasted_iota(jnp.int32, (tokens, tokens), 0) < lax.broadcasted_iota(
        jnp.int32, (tokens, tokens), 1
    )
    before = mm(chosen.astype(BF16), earlier.astype(F32).astype(BF16))
    slots[0] = jnp.where(chosen > 0.0, before.astype(jnp.int32), NOWHERE)
    counts[0] = jnp.concatenate(pixel_rows, axis=0)


def embed_kernel(micro, tid, patches, patch_w, keyval_w, norms, router, picks, emb, kv, gates, probs):
    experts = gates.shape[0]
    task = tid[micro, pl.program_id(0)]
    width = router.shape[0] // 2
    embedded = mm(patches[0, 0], patch_w[...].astype(BF16))
    emb[...] = embedded
    _, _, normed = norm_forward(embedded, norms[0:1], norms[1:2])
    kv[...] = mm(normed.astype(BF16), keyval_w[...].astype(BF16)).astype(BF16)
    prob = router_forward(router[0:width], normed, task, experts)
    probs[...] = prob
    gates[...] = gate_forward(prob, picked_hot(picks[0], experts))


def split_planes(values):
    high = values.astype(BF16).astype(F32)
    middle = (values - high).astype(BF16).astype(F32)
    return [high, middle, (values - high - middle).astype(BF16).astype(F32)]


def put_planes(ref, planes, image, token_rows, images):
    patch_count, model = token_rows.shape
    block = jnp.concatenate(planes, axis=0).astype(BF16)
    height = block.shape[0]
    columns, chunks = model // LANES, patch_count // LANES
    rows, base = ref.shape[0], images * patch_count
    for i in range(images):

        @pl.when(image == i)
        def _(i=i):
            ref[i * patch_count : (i + 1) * patch_count, :] = token_rows
            if i == 0:
                ref[base:, :] = jnp.zeros((rows - base, model), BF16)
            for j in range(chunks):
                c = i * chunks + j
                top, left = base + c // columns * height, c % columns * LANES
                ref[top : top + height, left : left + LANES] = block[:, j * LANES : (j + 1) * LANES]


def lanes_of(shape):
    return lax.broadcasted_iota(jnp.int32, shape, 1)


def put_statistics(ref, images, patch_count, values):
    high, middle, rest = split_planes(values)
    block = high + pltpu.roll(middle, 8, 1) + pltpu.roll(rest, 16, 1)
    ref[ref.shape[0] - values.shape[0] :, ref.shape[1] - LANES :] = block.astype(BF16)


def get_statistics(block):
    block = block.astype(F32)
    total = block + pltpu.roll(block, LANES - 8, 1) + pltpu.roll(block, LANES - 16, 1)
    return jnp.where(lanes_of(block.shape) < 8, total, 0.0)


def extra_rows(count, experts, model):
    return -(-(count // LANES) // (model // LANES)) * 4 * experts


def get_planes(block, count, experts, columns):
    height = 4 * experts
    out = []
    for c in range(count // LANES):
        top, left = c // columns * height, c % columns * LANES
        out.append(block[top : top + height, left : left + LANES].astype(F32))
    return out


def three_sum(planes, experts):
    return planes[:experts] + planes[experts : 2 * experts] + planes[2 * experts : 3 * experts]


def fill_keys(pieces, kvs, kv_t):
    rows = pieces[0].shape[0]
    for r, piece in enumerate(pieces):
        block = piece[...]
        kvs[r * rows : (r + 1) * rows, :] = block
        kv_t[:, r * rows : (r + 1) * rows] = block.astype(F32).T.astype(BF16)


def attend_kernel(micro, peers, capacity, images, tid, dev, *refs):
    emb = refs[0]
    kv_in = refs[1 : 1 + peers]
    picks, gates_in, slots = refs[1 + peers : 4 + peers]
    weights = refs[4 + peers : 4 + 2 * peers]
    norms, router = refs[4 + 2 * peers : 6 + 2 * peers]
    probs_att, counts = refs[6 + 2 * peers : 8 + 2 * peers]
    res_out, sent, mix_out, lse, probs_out = refs[8 + 2 * peers : 13 + 2 * peers]
    table, kvs, kv_t, q_t, mix = refs[13 + 2 * peers :]
    experts, tokens = gates_in.shape
    owned = weights[0].shape[1] // HEAD
    task = tid[micro, pl.program_id(0)]
    width = router.shape[0] // 2
    mine = dev[0]
    embedded = emb[...]
    _, _, normed = norm_forward(embedded, norms[0:1], norms[1:2])
    low = normed.astype(BF16)
    span = owned * HEAD
    for r in range(peers):
        q_t[r * span : (r + 1) * span, :] = mm_nt(weights[r][0], low).astype(BF16).astype(F32)
    fill_keys(kv_in, kvs, kv_t)
    mix[...] = jnp.zeros(mix.shape, F32)
    blocks = [(r, e, (r * owned + e) * HEAD) for r in range(peers) for e in range(owned)]
    rows = expert_rows(experts, tokens)
    blank = jnp.zeros((HEAD, tokens), BF16)

    def one_pick(k, carry):
        pick = picks[0, pl.ds(k, 1), :]
        query = jnp.zeros((HEAD, tokens), F32)
        for r, e, at in blocks:
            here = pick == (mine ^ r) * owned + e
            query = query + jnp.where(here, q_t[at : at + HEAD, :], 0.0)
        gate = jnp.sum(jnp.where(rows == pick, gates_in[...], 0.0), axis=0, keepdims=True)
        scores = mm(kvs[...], jnp.concatenate([(query * HEAD ** (-0.5)).astype(BF16), blank], axis=0))
        top = jnp.max(scores, axis=0, keepdims=True)
        powers = jnp.exp(scores - top)
        total = jnp.sum(powers, axis=0, keepdims=True)
        lse[pl.ds(k, 1), :] = top + jnp.log(total)
        weighted = (powers * (gate / total)).astype(BF16)
        out = mm(kv_t[HEAD:, :], weighted)
        for r, e, at in blocks:
            here = pick == (mine ^ r) * owned + e
            mix[at : at + HEAD, :] = mix[at : at + HEAD, :] + jnp.where(here, out, 0.0)
        return carry

    lax.fori_loop(0, picks.shape[1], one_pick, 0, unroll=True)
    resid = embedded
    for r in range(peers):
        block = mix[r * span : (r + 1) * span, :].astype(BF16)
        mix_out[0, r * span : (r + 1) * span, :] = block
        resid = resid + mm_tn(block, weights[r][1])
    res_out[...] = resid
    _, _, normed_two = norm_forward(resid, norms[2:3], norms[3:4])
    prob = router_forward(router[width:], normed_two, task, experts)
    probs_out[...] = prob
    both = jnp.concatenate([probs_att[...], prob], axis=0)
    lane = lanes_of((2 * experts, LANES))
    per_task = jnp.where(lane == task, jnp.sum(both, axis=1, keepdims=True), 0.0)
    add_to(table, ..., per_task, pl.program_id(0) == 0)
    slot = slots[0]
    gates = gate_forward(prob, (slot < NOWHERE).astype(F32))
    places = jnp.minimum(slot, capacity).astype(F32)
    low_two = normed_two.astype(BF16)
    put_planes(sent, split_planes(gates) + [places], pl.program_id(0), low_two, images)

    @pl.when(pl.program_id(0) == images - 1)
    def _():
        rest = jnp.zeros((2 * experts - 8, LANES), F32)
        block = jnp.concatenate([table[...], counts[...], rest], axis=0)
        put_statistics(sent, images, tokens, block)


def read_planes(block, experts, count):
    chunks = get_planes(block, count, experts, block.shape[1] // LANES)
    gates = jnp.concatenate([three_sum(chunk, experts) for chunk in chunks], axis=1)
    return jnp.concatenate([chunk[3 * experts :] for chunk in chunks], axis=1), gates


def one_row(rows, at):
    index = expert_rows(rows.shape[0], rows.shape[1])
    return jnp.sum(jnp.where(index == at, rows, 0.0), axis=0, keepdims=True)


def loss_scale(counts, task):
    own = jnp.where(lanes_of(counts.shape) == task, counts, 0.0)
    return 1.0 / jnp.sum(own, axis=1, keepdims=True)


def dispatch(blocks, at, experts, count, hot, gate, scale=None):
    capacity = hot.shape[0] // len(blocks)
    places = lax.broadcasted_iota(jnp.int32, (capacity, count), 0).astype(F32)
    for r, block in enumerate(blocks):
        slots, gates = read_planes(block, experts, count)
        here = one_row(slots, at) == places
        rows = slice(r * capacity, (r + 1) * capacity)
        hot[rows, :] = here.astype(F32).astype(BF16)
        own = one_row(gates, at)
        if scale is not None:
            own = own * scale
        gate[rows, :] = jnp.sum(jnp.where(here, own, 0.0), axis=1, keepdims=True)


def moe_forward_kernel(peers, owned, experts, merged, dev, *refs):
    made_outs = 1 + peers // 2 if merged else peers
    arrays = refs[:peers]
    weights = refs[peers]
    outs = refs[peers + 1 : peers + 1 + made_outs]
    kept, made, statistics, *lows, hot, gate, back = refs[peers + 1 + made_outs :]
    if lows:
        lows[0][0] = weights[0].astype(BF16)
        weights = lows[0]
    e = pl.program_id(0)
    count = hot.shape[1]
    capacity = hot.shape[0] // peers
    dispatch([a[count:, :] for a in arrays], dev[0] * owned + e, experts, count, hot, gate)
    for r in range(peers):
        rows = slice(r * capacity, (r + 1) * capacity)
        kept[0, rows, :] = mm(hot[rows, :], arrays[r][:count, :]).astype(BF16)
    before = mm(kept[0], weights[0, 0])
    bent = jnp.tanh(before * (GELU_C + GELU_C * GELU_A * (before * before)))
    halved = 0.5 * before
    out = mm_nt((halved + halved * bent).astype(BF16), weights[0, 1])
    made[0] = out.astype(BF16)
    weighted = (out * gate[...]).astype(BF16)
    for r in range(peers):
        rows = slice(r * capacity, (r + 1) * capacity)
        value = mm_tn(hot[rows, :], weighted[rows, :])
        if owned > 1:
            add_to(back, r, value, e == 0)

    @pl.when(e == owned - 1)
    def _():
        for r in range(peers):
            piece = back[r].astype(BF16) if owned > 1 else value.astype(BF16)
            if not merged:
                outs[r][...] = piece
            elif r % 2:
                outs[0][r // 2] = piece
            else:
                outs[1 + r // 2][...] = piece
        rows = statistics.shape[0]
        block = jnp.zeros(statistics.shape, F32)
        for a in arrays:
            block = block + get_statistics(a[a.shape[0] - rows :, a.shape[1] - LANES :])
        statistics[...] = block


def head_kernel(micro, parts, tasks, tid, *refs):
    res = refs[0]
    moe = refs[1 : 1 + parts]
    targets, masks, norms, head_w = refs[1 + parts : 5 + parts]
    slope_out, slope_low, grad_head, grad_norm, squares = refs[5 + parts :]
    image = pl.program_id(0)
    task = tid[micro, image]
    resid = res[...]
    for part in moe:
        resid = resid + part[...].astype(F32)
    scaled, inverse, normed = norm_forward(resid, norms[4:5], norms[5:6])
    low = normed.astype(BF16)
    head_low = head_w[...].astype(BF16)
    pred = mm(low, head_low)
    mask = masks[0, 0].astype(F32)
    pixels = mask.shape[1]
    depth_on = jnp.where(task == 0, 1.0, 0.0)
    normal_on = jnp.where(task == 0, 0.0, 1.0)
    slopes = []
    total = jnp.zeros((1, pixels), F32)
    for group in range(4):
        on = depth_on if group == 0 else normal_on
        at = group * pixels
        gap = pred[:, at : at + pixels] - targets[0, 0, :, at : at + pixels].astype(F32)
        masked = mask * gap
        total = total + on * jnp.sum(masked * gap, axis=0, keepdims=True)
        slopes.append((masked * (2.0 * on)).astype(BF16))
    slope = jnp.concatenate(slopes, axis=1)
    first = image == 0
    spots = lax.broadcasted_iota(jnp.int32, (8, LANES), 0) * LANES + lanes_of((8, LANES))
    add_to(squares, ..., jnp.where(spots == task, jnp.sum(total, axis=1, keepdims=True), 0.0), first)
    add_to(grad_head, ..., mm_tn(slope, low), first)
    grad, gain, shift = norm_backward(mm_nt(slope, head_low), scaled, inverse, norms[4:5])
    both = jnp.concatenate([gain, shift], axis=0)
    for t in range(tasks):
        add_to(grad_norm, slice(2 * t, 2 * t + 2), jnp.where(task == t, both, 0.0), first)
    slope_out[...] = grad
    slope_low[...] = grad.astype(BF16)


def moe_backward_kernel(shape, more_grads, more_tokens, split, tid, dev, place, *refs):
    peers, micro, images, local_expert, owned, experts = shape
    refs = list(refs)

    def take(count):
        out = refs[:count]
        del refs[:count]
        return out

    slopes, extras = take(peers), take(peers)
    kept, made, weights, tables = take(4)
    if more_grads:
        (prior_grads,) = take(1)
    if more_tokens:
        prior_pieces = take(peers)
    outs = take(peers)
    grads_out = take(2 if split else 1)
    hot, gate, plain = take(3)
    count, model = slopes[0].shape
    capacity = hot.shape[0] // peers
    at = dev[0] * owned + local_expert
    counts = tables[2 * experts : 2 * experts + 1, :]
    per_image = count // images
    scale = jnp.concatenate(
        [
            jnp.broadcast_to(loss_scale(counts, tid[micro, image]), (1, per_image))
            for image in range(images)
        ],
        axis=1,
    )
    dispatch([extra[...] for extra in extras], at, experts, count, hot, gate, scale)
    gate_slopes = []
    for r in range(peers):
        rows = slice(r * capacity, (r + 1) * capacity)
        value = mm(hot[rows, :], slopes[r][...])
        gate_slopes.append(jnp.sum(value * made[0, rows, :].astype(F32), axis=1, keepdims=True))
        plain[rows, :] = (value * gate[rows, :]).astype(BF16)
    before = mm(kept[0], weights[0, 0])
    hidden = mm(plain[...], weights[0, 1])
    cubic = GELU_C * GELU_A * (before * before)
    bent = jnp.tanh(before * (GELU_C + cubic))
    middle = 0.5 + 0.5 * bent
    inner = (before * middle).astype(BF16)
    bend = middle + (middle - middle * bent) * (before * (GELU_C + 3.0 * cubic))
    slope = (hidden * bend).astype(BF16)
    entry = mm_tn(kept[0], slope)
    leave = mm_tn(plain[...], inner)
    if more_grads:
        entry = entry + prior_grads[0].astype(F32)
        leave = leave + prior_grads[1].astype(F32)
    if split:
        flip = place[0] == 0
        grads_out[0][...] = jnp.where(flip, entry, leave).astype(BF16)
        grads_out[1][...] = jnp.where(flip, leave, entry).astype(BF16)
    else:
        grads_out[0][0] = entry.astype(BF16)
        grads_out[0][1] = leave.astype(BF16)
    received = mm_nt(slope, weights[0, 0]).astype(BF16)
    columns, chunks, height = model // LANES, count // LANES, 4 * experts
    rows_of = expert_rows(experts, count)
    lane = lanes_of((capacity, LANES))
    for r in range(peers):
        rows = slice(r * capacity, (r + 1) * capacity)
        tokens_back = mm_tn(hot[rows, :], received[rows, :])
        terms = split_planes(gate_slopes[r])
        terms = jnp.where(lane == 0, terms[0], jnp.where(lane == 1, terms[1], terms[2]))
        terms = jnp.where(lane < 3, terms, 0.0).astype(BF16)
        gate_row = jnp.sum(mm_tn(terms, hot[rows, :])[:8, :], axis=0, keepdims=True) * scale
        planes = split_planes(jnp.where(rows_of == at, gate_row, 0.0))
        block = jnp.concatenate(planes + [jnp.zeros((experts, count), F32)], axis=0)
        lines = []
        for line in range(-(-chunks // columns)):
            cells = [
                block[:, c * LANES : (c + 1) * LANES]
                if c < chunks
                else jnp.zeros((height, LANES), F32)
                for c in range(line * columns, (line + 1) * columns)
            ]
            lines.append(jnp.concatenate(cells, axis=1))
        piece = jnp.concatenate([tokens_back] + lines, axis=0)
        if more_tokens:
            piece = piece + prior_pieces[r][...].astype(F32)
        outs[r][...] = piece.astype(BF16)


def table_slope(table, task, tasks):
    lane = lanes_of(table.shape)
    valid = lane < tasks
    table = jnp.where(valid, table, 0.0)
    total = jnp.sum(jnp.sum(table, axis=1, keepdims=True), axis=0, keepdims=True)
    share = table / total
    by_expert = jnp.sum(share, axis=1, keepdims=True)
    by_task_sum = jnp.sum(share, axis=0, keepdims=True)
    safe = jnp.where(valid, share, 1.0)
    gain = jnp.log(safe) - jnp.log(jnp.where(valid, by_task_sum, 1.0)) - jnp.log(by_expert)
    gain = jnp.where(valid, gain, 0.0)
    mean = jnp.sum(jnp.sum(gain * share, axis=1, keepdims=True), axis=0, keepdims=True)
    slope = -MI_WEIGHT * (gain - mean) / total
    return jnp.sum(jnp.where(lane == task, slope, 0.0), axis=1, keepdims=True), mean


def back_kernel(micro, peers, parts, image_count, tid, dev, *refs):
    slope_in = refs[0]
    sent_parts = refs[1 : 1 + parts]
    gate_parts = refs[1 + parts : 1 + 2 * parts]
    at = 1 + 2 * parts
    res, emb, probs_mlp, slots = refs[at : at + 4]
    at += 4
    tables = refs[at]
    kv_in = refs[at + 1 : at + 1 + peers]
    at += 1 + peers
    picks, gates_in, probs_att, lse = refs[at : at + 4]
    weights = refs[at + 4 : at + 4 + peers]
    at += 4 + peers
    mix_in, norms, router = refs[at : at + 3]
    slope_one, normed_slope = refs[at + 3 : at + 5]
    kv_outs = refs[at + 5 : at + 5 + peers]
    at += 5 + peers
    grad_att, grad_router, grad_norm, mutual = refs[at : at + 4]
    kvs, kv_t, q_t, d_t, dkv, dq_t, dgate = refs[at + 4 :]
    experts, tokens = gates_in.shape
    owned = weights[0].shape[1] // HEAD
    image = pl.program_id(0)
    first = image == 0
    task = tid[micro, image]
    width = router.shape[0] // 2
    tasks = width // experts
    span = owned * HEAD
    mine = dev[0]
    rows = expert_rows(experts, tokens)

    grad_sent = jnp.zeros(slope_in.shape, F32)
    for part in sent_parts:
        grad_sent = grad_sent + part[...].astype(F32)
    planes = gate_parts[0][...].astype(F32)
    for part in gate_parts[1:]:
        planes = planes + part[...].astype(F32)
    columns = planes.shape[1] // LANES
    chunks = get_planes(planes, image_count * tokens, experts, columns)
    per = tokens // LANES
    grad_gates = jnp.zeros((experts, tokens), F32)
    for i in range(image_count):
        cells = [three_sum(c, experts) for c in chunks[i * per : (i + 1) * per]]
        grad_gates = jnp.where(image == i, jnp.concatenate(cells, axis=1), grad_gates)
    scaled_two, inverse_two, normed_two = norm_forward(res[...], norms[2:3], norms[3:4])
    chosen = (slots[0] < NOWHERE).astype(F32)
    table, gain_mlp = table_slope(tables[experts : 2 * experts, :], task, tasks)
    logits = to_tasks(gate_backward(probs_mlp[...], chosen, grad_gates, table), task, tasks)
    grad_two = grad_sent + small_tn(logits, router[width:])
    add_to(grad_router, slice(width, 2 * width), fine(mm, logits, normed_two, 0), first)
    grad, gain, shift = norm_backward(grad_two, scaled_two, inverse_two, norms[2:3])
    add_to(grad_norm, slice(2, 3), gain, first)
    add_to(grad_norm, slice(3, 4), shift, first)
    scale = loss_scale(tables[2 * experts : 2 * experts + 1, :], task)
    resid_slope = slope_in[...] * scale + grad
    slope_one[...] = resid_slope
    branch = resid_slope.astype(BF16)

    _, _, normed = norm_forward(emb[...], norms[0:1], norms[1:2])
    low = normed.astype(BF16)
    for r in range(peers):
        at_r = slice(r * span, (r + 1) * span)
        q_t[at_r, :] = mm_nt(weights[r][0], low).astype(BF16).astype(F32)
        d_t[at_r, :] = mm_nt(weights[r][1], branch).astype(BF16).astype(F32)
        add_to(grad_att, (r, 1), mm(mix_in[0, at_r, :], branch), first)
    fill_keys(kv_in, kvs, kv_t)
    dkv[...] = jnp.zeros(dkv.shape, F32)
    dq_t[...] = jnp.zeros(dq_t.shape, F32)
    dgate[...] = jnp.zeros(dgate.shape, F32)
    blocks = [(r, e, (r * owned + e) * HEAD) for r in range(peers) for e in range(owned)]
    blank = jnp.zeros((HEAD, tokens), BF16)

    def one_pick(k, carry):
        pick = picks[0, pl.ds(k, 1), :]
        query = jnp.zeros((HEAD, tokens), F32)
        down = jnp.zeros((HEAD, tokens), F32)
        for r, e, at in blocks:
            here = pick == (mine ^ r) * owned + e
            query = query + jnp.where(here, q_t[at : at + HEAD, :], 0.0)
            down = down + jnp.where(here, d_t[at : at + HEAD, :], 0.0)
        gate = jnp.sum(jnp.where(rows == pick, gates_in[...], 0.0), axis=0, keepdims=True)
        query_low, down_low = query.astype(BF16), down.astype(BF16)
        scores = mm(kvs[...], jnp.concatenate([(query * HEAD ** (-0.5)).astype(BF16), blank], axis=0))
        probs = jnp.exp(scores - lse[pl.ds(k, 1), :])
        slope = mm(kvs[...], jnp.concatenate([blank, down_low], axis=0))
        delta = jnp.sum(probs * slope, axis=0, keepdims=True)
        gated = probs * gate
        weighted = gated.astype(BF16)
        grad_scores = (gated * (slope - delta) * HEAD ** (-0.5)).astype(BF16)
        joint = jnp.concatenate([grad_scores, weighted], axis=1)
        other = jnp.concatenate(
            [
                jnp.concatenate([query_low, blank], axis=0),
                jnp.concatenate([blank, down_low], axis=0),
            ],
            axis=1,
        )
        dkv[...] = dkv[...] + mm_nt(joint, other)
        dq = mm(kv_t[:HEAD, :], grad_scores)
        for r, e, at in blocks:
            here = pick == (mine ^ r) * owned + e
            dq_t[at : at + HEAD, :] = dq_t[at : at + HEAD, :] + jnp.where(here, dq, 0.0)
        dgate[...] = dgate[...] + jnp.where(rows == pick, delta, 0.0)
        return carry

    lax.fori_loop(0, picks.shape[1], one_pick, 0, unroll=True)
    for r in range(peers):
        block = dkv[r * tokens : (r + 1) * tokens, :].astype(BF16)
        kv_outs[r][...] = block

    table, gain_att = table_slope(tables[:experts, :], task, tasks)
    mutual[...] = jnp.broadcast_to(gain_att + gain_mlp, mutual.shape)
    chosen = picked_hot(picks[0], experts)
    logits = to_tasks(gate_backward(probs_att[...], chosen, dgate[...], table), task, tasks)
    grad_one = small_tn(logits, router[0:width])
    add_to(grad_router, slice(0, width), fine(mm, logits, normed, 0), first)
    for r in range(peers):
        block = dq_t[r * span : (r + 1) * span, :].astype(BF16)
        grad_one = grad_one + mm_tn(block, weights[r][0])
        add_to(grad_att, (r, 0), mm(block, low), first)
    normed_slope[...] = grad_one


def last_kernel(parts, *refs):
    patches, emb, slope_one, normed_slope = refs[:4]
    kv_parts = refs[4 : 4 + parts]
    keyval_w, norms = refs[4 + parts : 6 + parts]
    grad_patch, grad_keyval, grad_norm = refs[6 + parts :]
    first = pl.program_id(0) == 0
    scaled, inverse, normed = norm_forward(emb[...], norms[0:1], norms[1:2])
    grad_kv = jnp.zeros(kv_parts[0].shape, F32)
    for part in kv_parts:
        grad_kv = grad_kv + part[...].astype(F32)
    grad_kv = grad_kv.astype(BF16)
    add_to(grad_keyval, ..., mm_tn(grad_kv, normed.astype(BF16)), first)
    slope = normed_slope[...] + mm_nt(grad_kv, keyval_w[...].astype(BF16))
    grad, gain, shift = norm_backward(slope, scaled, inverse, norms[0:1])
    add_to(grad_norm, slice(0, 1), gain, first)
    add_to(grad_norm, slice(1, 2), shift, first)
    add_to(grad_patch, ..., mm_tn(patches[0, 0], (slope_one[...] + grad).astype(BF16)), first)


def pack_kernel(peers, micros, dense_rows, sizes, dev, *refs):
    names = 8
    values = []
    for n in range(names):
        value = refs[n][...]
        for m in range(1, micros):
            value = value + refs[m * names + n][...]
        values.append(value)
    head, patch, keyval, router, one, two, three, attention = values
    tables, odd = refs[micros * names : micros * names + 2]
    evens = refs[micros * names + 2 : -1]
    dense = refs[-1]
    tasks, pixels, count_row = sizes
    scales = [loss_scale(tables[count_row : count_row + 1, :], t) for t in range(tasks)]
    head = jnp.concatenate([head[:pixels] * scales[0], head[pixels:] * scales[1]], axis=0)
    three = sum(three[2 * t : 2 * t + 2] * scales[t] for t in range(tasks))
    at = 0
    for value in (head, patch, keyval):
        dense[at : at + value.shape[0], :] = value.astype(BF16)
        at += value.shape[0]
    rest = [router, one[0:2], two[2:4], three]
    pad = dense_rows - at - router.shape[0] - 6
    if pad:
        rest.append(jnp.zeros((pad, dense.shape[1]), F32))
    dense[at:, :] = jnp.concatenate(rest, axis=0).astype(BF16)
    share = dense_rows // peers
    model = dense.shape[1]
    for r in range(peers):
        start = pl.multiple_of((dev[0] ^ r) * share, 16)
        rows = dense[pl.ds(start, share), :]
        owned_rows = attention[r].reshape(-1, model).astype(BF16)
        if r % 2:
            odd[r // 2, :share] = rows
            odd[r // 2, share:] = owned_rows
        else:
            evens[r // 2][0, :share] = rows
            evens[r // 2][0, share:] = owned_rows


def halves_kernel(parts, place, *refs):
    keep, send, total = refs[parts:]
    value = refs[0][0].astype(F32)
    for part in refs[1:parts]:
        value = value + part[0].astype(F32)
    total[...] = value.astype(BF16)
    rows = keep.shape[0]
    keep[...] = total[pl.ds(pl.multiple_of(place[0] * rows, 16), rows), :]
    send[...] = total[pl.ds(pl.multiple_of((1 - place[0]) * rows, 16), rows), :]


def share_sum_kernel(dense_rows, place, shares, outs, squares):
    count, rows, width = shares.shape
    value = shares[0].astype(F32)
    for r in range(1, count):
        value = value + shares[r].astype(F32)
    low = value.astype(BF16)
    for r in range(count):
        outs[r] = low
    value = low.astype(F32)
    value = value * value
    both = jnp.sum(value, axis=0, keepdims=True)
    if dense_rows:
        start = (place[0] * count + place[1]) * rows
        row = lax.broadcasted_iota(jnp.int32, (rows, width), 0) + start
        dense = jnp.sum(jnp.where(row < dense_rows, value, 0.0), axis=0, keepdims=True)
    else:
        dense = jnp.zeros((1, width), F32)
    spots = lax.broadcasted_iota(jnp.int32, (8, LANES), 0) * LANES + lanes_of((8, LANES))
    own = jnp.sum(both - dense, axis=1, keepdims=True)
    dense = jnp.sum(dense, axis=1, keepdims=True)
    squares[...] = jnp.where(spots == 2, own, 0.0) + jnp.where(spots == 3, dense, 0.0)


def join_halves_kernel(dense_rows, place, own, other, dense, rest, total):
    rows = own.shape[0]
    total[pl.ds(pl.multiple_of(place[0] * rows, 16), rows), :] = own[...]
    total[pl.ds(pl.multiple_of((1 - place[0]) * rows, 16), rows), :] = other[...]
    dense[...] = total[:dense_rows, :]
    rest[...] = total[dense_rows:, :]


def clip_factor(sums, other_sums, limit):
    total = sums[0:1, :] + other_sums[0:1, :]
    own, dense = total[:, 2:3], total[:, 3:4]
    norm = jnp.sqrt(own + dense)
    return jnp.minimum(1.0, limit / norm), norm, jnp.sqrt(own), total


def adam_step(weight, first, second, gradient, rate, factor, scales):
    gradient = gradient * factor
    moment = BETA_ONE * first + (1.0 - BETA_ONE) * gradient
    square = BETA_TWO * second + ((1.0 - BETA_TWO) * gradient) * gradient
    step = (moment * (rate * scales[0])) / (jnp.sqrt(square * scales[1]) + EPSILON)
    return weight * (1.0 - rate * DECAY) - step, moment, square


def adam_kernel(rate, limit, place, scales, *refs):
    own, other, sums, other_sums, weight, first, second = refs[:7]
    factor = clip_factor(sums, other_sums, limit)[0]
    gradient = jnp.where(pl.program_id(0) == place[0], own[...], other[...]).astype(F32)
    news = adam_step(weight[0, 0], first[0, 0], second[0, 0], gradient, rate, factor, scales)
    for ref, new in zip(refs[-3:], news):
        ref[0, 0] = new


def adam_dense_kernel(peers, rates, limit, tasks, count_row, dev, scales, *refs):
    pieces, attention = refs[:peers], refs[peers]
    sums, other_sums, counts, mutual = refs[peers + 1 : peers + 5]
    states = [refs[peers + 5 + 3 * n : peers + 8 + 3 * n] for n in range(6)]
    outs = [refs[peers + 23 + 3 * n : peers + 26 + 3 * n] for n in range(6)]
    scalars, dense = refs[-4:-1], refs[-1]
    factor, norm, own_norm, total = clip_factor(sums, other_sums, limit)
    lane = lanes_of((1, LANES))
    ratio = total / jnp.where(lane < tasks, counts[count_row : count_row + 1, :], 1.0)
    loss = jnp.sum(jnp.where(lane < tasks, ratio, 0.0), axis=1, keepdims=True)
    loss = loss - MI_WEIGHT * mutual[0:1, 0:1]
    for ref, value in zip(scalars, (loss, norm, own_norm)):
        ref[...] = value
    share = pieces[0].shape[0]
    for r in range(peers):
        dense[pl.ds(pl.multiple_of((dev[0] ^ r) * share, 16), share), :] = pieces[r][...]

    def update(n, index, gradient):
        olds = [ref[index] for ref in states[n]]
        news = adam_step(*olds, gradient, rates[n], factor, scales)
        for ref, new in zip(outs[n], news):
            ref[index] = new

    outputs = states[0][0].shape[1]
    step = 2 * LANES
    for left in range(0, outputs, step):
        block = dense[left : left + step, :].astype(F32).T
        update(0, (slice(None), slice(left, left + step)), block)
    at = outputs
    rows = states[1][0].shape[0]
    update(1, ..., dense[at : at + rows, :].astype(F32))
    at += rows
    width = states[2][0].shape[1]
    update(2, ..., dense[at : at + width, :].astype(F32).T)
    at += width
    rest = dense[at:, :].astype(F32)
    rows = states[3][0].shape[0]
    update(3, ..., rest[:rows])
    update(4, ..., rest[rows : rows + states[4][0].shape[0]])
    width = states[5][0].shape[2]
    for n in range(2):
        update(5, n, attention[n * width : (n + 1) * width, :].astype(F32).T)


def whole(array):
    rank = len(array.shape)
    return pl.BlockSpec(array.shape, lambda *_: (0,) * rank, pipeline_mode=pl.Buffered(1))


def kept_out(shape):
    rank = len(shape)
    return pl.BlockSpec(shape, lambda *_: (0,) * rank)


def shape_of(shape, dtype):
    return jax.ShapeDtypeStruct(shape, dtype)


def call(kernel, grid, scalars, inputs, outputs, scratch, cost, name, room=None):
    spec = pltpu.PrefetchScalarGridSpec(
        num_scalar_prefetch=len(scalars),
        grid=grid,
        in_specs=[s for _, s in inputs],
        out_specs=[s for _, s in outputs],
        scratch_shapes=scratch,
    )
    return pl.pallas_call(
        kernel,
        grid_spec=spec,
        out_shape=[o for o, _ in outputs],
        cost_estimate=pl.CostEstimate(
            flops=int(cost[0]), bytes_accessed=int(cost[1]), transcendentals=0
        ),
        compiler_params=None if room is None else pltpu.CompilerParams(vmem_limit_bytes=room << 20),
        name=name,
    )(*scalars, *[a for a, _ in inputs])


def swap(value, axis, mask):
    size = lax.axis_size(axis)
    return lax.ppermute(value, axis, [(i, i ^ mask) for i in range(size)])


def bits_of(axis):
    return [1 << b for b in range(lax.axis_size(axis).bit_length() - 1)]


def gather_direct(value):
    return [value] + [swap(value, "expert", r) for r in range(1, lax.axis_size("expert"))]


def scatter_direct(pieces):
    return [pieces[0]] + [swap(pieces[r], "expert", r) for r in range(1, len(pieces))]


def across(value):
    rest = [swap(value, "expert", r) for r in range(2, lax.axis_size("expert"), 2)]
    return rest + [swap(value, "expert", 1)]


def beside(value, came):
    rest = came[:-1]
    return [swap(block, "expert", 1) for block in rest]


def ordered(value, came, more):
    out = [value, came[-1]]
    for block, other in zip(came[:-1], more):
        out += [block, other]
    return out


def gather_pieces(value):
    came = across(value)
    return ordered(value, came, beside(value, came))


def after(value, *anchors):
    return lax.optimization_barrier((value,) + anchors)[0]


class Hops:
    def __init__(self, value, axes):
        self.value = value
        self.steps = [(axis, bit) for axis in axes for bit in bits_of(axis)]
        if len(axes) > 1:
            self.steps.sort(key=lambda step: step == (axes[1], 1))
        self.came = []

    def start(self):
        if self.steps:
            self.came = [swap(self.value, *self.steps.pop(0))]

    def land(self, came):
        if self.came:
            self.value = self.value + came[-1]
            self.came = []
        self.start()

    def finish(self):
        while self.came or self.steps:
            self.land(self.came)
        return self.value


def along_z(value):
    size = lax.axis_size("dp")
    groups = [[i for i in range(size) if i % 2 == low] for low in range(2)]
    return lax.all_to_all(
        value, "dp", split_axis=0, concat_axis=0, axis_index_groups=groups, tiled=True
    )


def local(
    patches,
    routes,
    masks,
    targets,
    task_ids,
    step_count,
    patch_weight,
    patch_moment,
    patch_square,
    keyval_weight,
    keyval_moment,
    keyval_square,
    router_weight,
    router_moment,
    router_square,
    norm_weight,
    norm_moment,
    norm_square,
    head_weight,
    head_moment,
    head_square,
    attention_weight,
    attention_moment,
    attention_square,
    expert_weight,
    expert_moment,
    expert_square,
):
    peers = lax.axis_size("expert")
    half_peers = peers // 2
    micros, images, patch_count, patch_in = patches.shape
    _, _, _, _, tasks, top = routes.shape
    owned = expert_weight.shape[0]
    experts = owned * peers
    model, hidden = expert_weight.shape[2:]
    tokens = images * patch_count
    capacity = max(2, tokens * top // experts)
    pixels = masks.shape[3]
    outputs = targets.shape[3]
    pair_width = 2 * HEAD
    span = owned * HEAD
    keys = peers * patch_count
    head_rows = peers * span
    extra = extra_rows(tokens, experts, model)
    long = tokens + extra
    far = lax.axis_size("dp") // 2
    dev = lax.axis_index("expert").astype(jnp.int32).reshape(1)
    spot = lax.axis_index("dp").astype(jnp.int32)
    place = jnp.stack([spot & 1, spot >> 1])
    router_rows = router_weight.T
    router_count = router_rows.shape[0]
    routes_lanes = jnp.transpose(routes, (0, 1, 3, 4, 5, 2))
    attention_own = jnp.transpose(attention_weight, (0, 2, 1)).astype(BF16)
    attention = gather_direct(attention_own)

    order = [task_ids, dev]

    def settle(*values):
        out = lax.optimization_barrier((order[0], order[1]) + values)
        order[:] = out[:2]
        return list(out[2:])

    def settle_groups(*groups):
        out = settle(*[value for group in groups for value in group])
        back = []
        for group in groups:
            back.append(out[: len(group)])
            out = out[len(group) :]
        return back

    token_block = pl.BlockSpec((patch_count, model), lambda i, *_: (i, 0))
    expert_block = pl.BlockSpec((experts, patch_count), lambda i, *_: (0, i))
    kv_block = pl.BlockSpec((patch_count, pair_width), lambda i, *_: (i, 0))
    top_block = pl.BlockSpec((top, patch_count), lambda i, *_: (0, i))

    def micro_block(shape, micro):
        return pl.BlockSpec((1,) + shape, lambda i, *_, m=micro: (m,) + (0,) * (len(shape) - 1) + (i,))

    def image_block(array, micro):
        return pl.BlockSpec((1, 1) + array.shape[2:], lambda i, *_, m=micro: (m, i, 0, 0))

    def pieces_out(rows, width):
        return [(shape_of((rows, width), BF16), kept_out((rows, width)))] * peers


    def one_whole(array, lead):
        return pl.BlockSpec(
            (pl.Squeezed(), patch_count, array.shape[2]), lambda i, *_: (lead, i, 0)
        )

    state = [SimpleNamespace() for _ in range(micros)]

    def run_routing():
        return call(
            route_kernel,
            (micros,),
            (order[0],),
            [
                (
                    routes_lanes,
                    pl.BlockSpec((1,) + routes_lanes.shape[1:], lambda m, *_: (m, 0, 0, 0, 0, 0)),
                ),
                (masks, pl.BlockSpec((1,) + masks.shape[1:], lambda m, *_: (m, 0, 0, 0))),
            ],
            [
                (
                    shape_of((micros, top, tokens), jnp.int32),
                    pl.BlockSpec((1, top, tokens), lambda m, *_: (m, 0, 0)),
                ),
                (
                    shape_of((micros, experts, tokens), jnp.int32),
                    pl.BlockSpec((1, experts, tokens), lambda m, *_: (m, 0, 0)),
                ),
                (
                    shape_of((micros, tasks, pixels), F32),
                    pl.BlockSpec((1, tasks, pixels), lambda m, *_: (m, 0, 0)),
                ),
            ],
            [],
            (micros * tokens * tokens * 32, masks.size * 4),
            "routing",
        )

    def run_embed(micro):
        s = state[micro]
        s.emb, kv, s.gates_att, s.probs_att = call(
            partial(embed_kernel, micro),
            (images,),
            (order[0],),
            [
                (patches, image_block(patches, micro)),
                (patch_weight, whole(patch_weight)),
                (keyval_weight, whole(keyval_weight)),
                (norm_weight, whole(norm_weight)),
                (router_rows, whole(router_rows)),
                (picks, micro_block((top, patch_count), micro)),
            ],
            [
                (shape_of((tokens, model), F32), token_block),
                (shape_of((tokens, pair_width), BF16), kv_block),
                (shape_of((experts, tokens), F32), expert_block),
                (shape_of((experts, tokens), F32), expert_block),
            ],
            [],
            (2 * tokens * model * (patch_in + pair_width), tokens * (2 * patch_in + 4 * model) + patch_weight.size * 4),
            "embedding",
        )
        return kv

    attention_flops = 2 * top * tokens * keys * HEAD * 8

    def run_attend(micro):
        s = state[micro]
        s.res, s.sent, s.mix, s.lse, s.probs_mlp = call(
            partial(attend_kernel, micro, peers, capacity, images),
            (images,),
            (order[0], order[1]),
            [(s.emb, token_block)]
            + [(piece, kv_block) for piece in s.kv]
            + [
                (picks, micro_block((top, patch_count), micro)),
                (s.gates_att, expert_block),
                (slots, micro_block((experts, patch_count), micro)),
            ]
            + [(piece, whole(piece)) for piece in attention]
            + [
                (norm_weight, whole(norm_weight)),
                (router_rows, whole(router_rows)),
                (s.probs_att, expert_block),
                (counts, whole(counts)),
            ],
            [
                (shape_of((tokens, model), F32), token_block),
                (shape_of((long, model), BF16), kept_out((long, model))),
                (
                    shape_of((images, head_rows, patch_count), BF16),
                    pl.BlockSpec((1, head_rows, patch_count), lambda i, *_: (i, 0, 0)),
                ),
                (shape_of((top, tokens), F32), top_block),
                (shape_of((experts, tokens), F32), expert_block),
            ],
            [
                pltpu.VMEM((2 * experts, LANES), F32),
                pltpu.VMEM((keys, pair_width), BF16),
                pltpu.VMEM((pair_width, keys), BF16),
                pltpu.VMEM((head_rows, patch_count), F32),
                pltpu.VMEM((head_rows, patch_count), F32),
            ],
            (attention_flops, tokens * model * 12),
            "attention",
        )

    moe_flops = 2 * owned * peers * capacity * model * (2 * hidden + 2 * tokens)
    expert_bytes = expert_weight.size * 2
    odd_shape = (half_peers, tokens, model)

    slots_total = peers * capacity
    by_slot = shape_of((owned, slots_total, model), BF16)
    slot_block = pl.BlockSpec((1, slots_total, model), lambda e, *_: (e, 0, 0))

    def run_experts(micro, merged):
        s = state[micro]
        first_use = micro == 0
        weight_block = pl.BlockSpec((1, 2, model, hidden), lambda e, *_: (e, 0, 0, 0))
        results = call(
            partial(moe_forward_kernel, peers, owned, experts, merged),
            (owned,),
            (order[1],),
            [(piece, whole(piece)) for piece in s.tokens]
            + [(expert_weight if first_use else state[0].low, weight_block)],
            (
                [(shape_of(odd_shape, BF16), kept_out(odd_shape))]
                + [(shape_of((tokens, model), BF16), kept_out((tokens, model)))] * half_peers
                if merged
                else pieces_out(tokens, model)
            )
            + [
                (by_slot, slot_block),
                (by_slot, slot_block),
                (shape_of((4 * experts, LANES), F32), kept_out((4 * experts, LANES))),
            ]
            + ([(shape_of(expert_weight.shape, BF16), weight_block)] if first_use else []),
            [
                pltpu.VMEM((slots_total, tokens), BF16),
                pltpu.VMEM((slots_total, 1), F32),
                pltpu.VMEM((peers, tokens, model), F32),
            ],
            (moe_flops, expert_bytes + 4 * peers * tokens * model),
            "experts",
        )
        if first_use:
            *results, s.low = results
        s.kept, s.made, s.statistics = results[-3:]
        return list(results[:-3])

    count_row = 2 * experts

    def run_head(micro):
        s = state[micro]
        s.slope, slope_low, s.grad_head, s.norm_three, s.squares = call(
            partial(head_kernel, micro, len(s.moe), tasks),
            (images,),
            (order[0],),
            [(s.res, token_block)]
            + [
                (part, token_block if lead is None else one_whole(part, lead))
                for part, lead in s.moe
            ]
            + [
                (targets, image_block(targets, micro)),
                (masks, image_block(masks, micro)),
                (norm_weight, whole(norm_weight)),
                (head_weight, whole(head_weight)),
            ],
            [
                (shape_of((tokens, model), F32), token_block),
                (shape_of((tokens, model), BF16), token_block),
                (shape_of((outputs, model), F32), kept_out((outputs, model))),
                (shape_of((8, model), F32), kept_out((8, model))),
                (shape_of((8, LANES), F32), kept_out((8, LANES))),
            ],
            [],
            (6 * tokens * model * outputs, tokens * (outputs * 2 + pixels * 4 + 12 * model)),
            "head",
        )
        return slope_low

    extra_block = pl.BlockSpec(
        (extra, model), lambda *_: (tokens // extra, 0), pipeline_mode=pl.Buffered(1)
    )

    def run_experts_back(micro, e, prior):
        s = state[micro]
        more_grads, more_tokens = prior is not None, e > 0
        split = micro == micros - 1
        one_block = pl.BlockSpec(
            (1, slots_total, model), lambda *_: (e, 0, 0), pipeline_mode=pl.Buffered(1)
        )
        weight_block = pl.BlockSpec(
            (1, 2, model, hidden), lambda *_: (e, 0, 0, 0), pipeline_mode=pl.Buffered(1)
        )
        inputs = (
            [(piece, whole(piece)) for piece in s.slopes]
            + [(piece, extra_block) for piece in s.tokens]
            + [(s.kept, one_block), (s.made, one_block), (expert_low, weight_block)]
            + [(tables, whole(tables))]
        )
        if more_grads:
            inputs.append((prior, whole(prior)))
        if more_tokens:
            inputs += [(piece, whole(piece)) for piece in s.pieces]
        grad_shape = (2, model, hidden)
        grads_out = (
            [(shape_of(grad_shape[1:], BF16), kept_out(grad_shape[1:]))] * 2
            if split
            else [(shape_of(grad_shape, BF16), kept_out(grad_shape))]
        )
        results = call(
            partial(
                moe_backward_kernel,
                (peers, micro, images, e, owned, experts),
                more_grads,
                more_tokens,
                split,
            ),
            (1,),
            (order[0], order[1], place),
            inputs,
            pieces_out(long, model) + grads_out,
            [
                pltpu.VMEM((slots_total, tokens), BF16),
                pltpu.VMEM((slots_total, 1), F32),
                pltpu.VMEM((slots_total, model), BF16),
            ],
            (3 * moe_flops // owned, expert_bytes * 5 // owned + 4 * peers * tokens * model),
            "experts_back",
        )
        s.pieces = list(results[:peers])
        return list(results[peers:])

    def run_attend_back(micro):
        s = state[micro]
        parts = s.sent_parts
        results = call(
            partial(back_kernel, micro, peers, peers, images),
            (images,),
            (order[0], order[1]),
            [(s.slope, token_block)]
            + [(part, token_block) for part in parts]
            + [
                (part, pl.BlockSpec((extra, model), lambda *_: (tokens // extra, 0)))
                for part in parts
            ]
            + [
                (s.res, token_block),
                (s.emb, token_block),
                (s.probs_mlp, expert_block),
                (slots, micro_block((experts, patch_count), micro)),
                (tables, whole(tables)),
            ]
            + [(piece, kv_block) for piece in s.kv]
            + [
                (picks, micro_block((top, patch_count), micro)),
                (s.gates_att, expert_block),
                (s.probs_att, expert_block),
                (s.lse, top_block),
            ]
            + [(piece, whole(piece)) for piece in attention]
            + [
                (s.mix, pl.BlockSpec((1, head_rows, patch_count), lambda i, *_: (i, 0, 0))),
                (norm_weight, whole(norm_weight)),
                (router_rows, whole(router_rows)),
            ],
            [
                (shape_of((tokens, model), F32), token_block),
                (shape_of((tokens, model), F32), token_block),
            ]
            + [(shape_of((tokens, pair_width), BF16), kv_block)] * peers
            + [
                (shape_of((peers, 2, span, model), F32), kept_out((peers, 2, span, model))),
                (shape_of((router_count, model), F32), kept_out((router_count, model))),
                (shape_of((8, model), F32), kept_out((8, model))),
                (shape_of((8, LANES), F32), kept_out((8, LANES))),
            ],
            [
                pltpu.VMEM((keys, pair_width), BF16),
                pltpu.VMEM((pair_width, keys), BF16),
                pltpu.VMEM((head_rows, patch_count), F32),
                pltpu.VMEM((head_rows, patch_count), F32),
                pltpu.VMEM((keys, pair_width), F32),
                pltpu.VMEM((head_rows, patch_count), F32),
                pltpu.VMEM((experts, patch_count), F32),
            ],
            (attention_flops * 3, tokens * model * 30),
            "attention_back",
        )
        s.slope_one, s.normed_slope = results[:2]
        s.grad_att, s.grad_router, s.norm_two, s.mutual = results[2 + peers :]
        return list(results[2 : 2 + peers])

    def run_last(micro):
        s = state[micro]
        s.grad_patch, s.grad_keyval, s.norm_one = call(
            partial(last_kernel, peers),
            (images,),
            (),
            [
                (patches, image_block(patches, micro)),
                (s.emb, token_block),
                (s.slope_one, token_block),
                (s.normed_slope, token_block),
            ]
            + [(part, kv_block) for part in s.kv_parts]
            + [(keyval_weight, whole(keyval_weight)), (norm_weight, whole(norm_weight))],
            [
                (shape_of((patch_in, model), F32), kept_out((patch_in, model))),
                (shape_of((pair_width, model), F32), kept_out((pair_width, model))),
                (shape_of((8, model), F32), kept_out((8, model))),
            ],
            [],
            (2 * tokens * model * (patch_in + 2 * pair_width), tokens * model * 20),
            "embedding_back",
            24,
        )

    step_value = step_count[0].astype(F32)
    scales = jnp.stack(
        [1.0 / (1.0 - jnp.power(BETA_ONE, step_value)), 1.0 / (1.0 - jnp.power(BETA_TWO, step_value))]
    )
    first, second = state
    came_w = across(attention_own)
    picks, slots, count_rows = run_routing()
    (picks,) = settle(picks)
    counts = jnp.zeros((8, LANES), F32).at[0, :tasks].set(jnp.sum(count_rows, axis=(0, 2)))
    kv = run_embed(0)
    (first.emb, kv), came_w = settle_groups([first.emb, kv], came_w)
    more_w = beside(attention_own, came_w)
    first.kv = gather_direct(kv)
    kv = run_embed(1)
    (second.emb, kv), more_w, first.kv = settle_groups([second.emb, kv], more_w, first.kv)
    attention = ordered(attention_own, came_w, more_w)
    second.kv = gather_direct(kv)

    run_attend(0)
    (first.res, first.sent), second.kv = settle_groups([first.res, first.sent], second.kv)
    counts = jnp.zeros((8, LANES), F32)
    came_first = across(first.sent)
    run_attend(1)
    (second.res, second.sent), came_first = settle_groups(
        [second.res, second.sent], came_first
    )
    more_first = beside(first.sent, came_first)
    came_second = across(second.sent)
    (more_first,) = settle_groups(more_first)
    first.tokens = ordered(first.sent, came_first, more_first)

    first_pieces = run_experts(0, False)
    (first.kept,), first_pieces, came_second = settle_groups(
        [first.kept], first_pieces, came_second
    )
    expert_low = first.low
    more_second = beside(second.sent, came_second)
    first_parts = scatter_direct(first_pieces)
    (more_second,) = settle_groups(more_second)
    second.tokens = ordered(second.sent, came_second, more_second)
    second_odd, *second_evens = run_experts(1, True)
    (second.kept, second_odd), rest = settle_groups([second.kept, second_odd], first_parts[1:])
    first.moe = [(part, None) for part in first_parts[:1] + rest]
    second_crossed = swap(second_odd, "expert", 1)
    hops = Hops(first.statistics + second.statistics, ("dp",))
    hops.start()
    (second_crossed,) = settle(second_crossed)
    second_rest = [
        swap(
            (second_evens[n].astype(F32) + second_crossed[n].astype(F32)).astype(BF16),
            "expert",
            2 * n,
        )
        for n in range(1, half_peers)
    ]

    first_low = run_head(0)
    (first.slope, first_low), came = settle_groups([first.slope, first_low], hops.came)
    came_first = across(first_low)
    hops.land(came)
    (second_rest,) = settle_groups(second_rest)
    second.moe = [(second_evens[0], None), (second_crossed, 0)]
    second.moe += [(part, None) for part in second_rest]
    second_low = run_head(1)
    (second.slope, second_low), came_first, came = settle_groups(
        [second.slope, second_low], came_first, hops.came
    )
    more_first = beside(first_low, came_first)
    second.slopes = gather_direct(second_low)
    hops.land(came)
    more_first, came = settle_groups(more_first, hops.came)
    hops.land(came)
    first.slopes = ordered(first_low, came_first, more_first)
    tables = hops.finish()

    def small_call(kernel, scalars, inputs, shapes, scratch, name, room=24):
        return call(
            kernel,
            (1,),
            scalars,
            [(a, whole(a)) for a in inputs],
            [(s, kept_out(s.shape)) for s in shapes],
            scratch,
            (0, 1000),
            name,
            room,
        )

    exchanged = [dev]

    def exchange(value):
        value = along_z(after(value, exchanged[0], order[1]))
        exchanged[0] = value
        return value

    def cut_shares(keep, came):
        rows, width = keep.shape
        total = (keep.astype(F32) + came.astype(F32)).astype(BF16)
        return exchange(total.reshape(far, rows // far, width))

    def sum_shares(moved, dense_rows):
        return small_call(
            partial(share_sum_kernel, dense_rows),
            (place,),
            [moved],
            [shape_of(moved.shape, BF16), shape_of((8, LANES), F32)],
            [],
            "share_sum",
        )

    prior = run_experts_back(0, 0, None)
    first.pieces, second.slopes, prior = settle_groups(first.pieces, second.slopes, prior)
    keep_first, send_first = run_experts_back(1, 0, prior[0])
    second.pieces, (keep_first, send_first) = settle_groups(
        second.pieces, [keep_first, send_first]
    )
    came_x_first = swap(send_first, "dp", 1)
    prior = run_experts_back(0, 1, None)
    first.pieces, prior = settle_groups(first.pieces, prior)
    first.sent_parts = scatter_direct(first.pieces)
    keep_second, send_second = run_experts_back(1, 1, prior[0])
    came_x_second = swap(send_second, "dp", 1)
    (keep_second,), second.pieces, first.sent_parts, (came_x_first,) = settle_groups(
        [keep_second], second.pieces, first.sent_parts, [came_x_first]
    )
    second.sent_parts = scatter_direct(second.pieces)
    square_parts = [s.squares for s in state]
    shares_first = cut_shares(keep_first, came_x_first)

    kv_parts = run_attend_back(0)
    kv_parts, second.sent_parts, (came_x_second, shares_first) = settle_groups(
        kv_parts, second.sent_parts, [came_x_second, shares_first]
    )
    first.kv_parts = scatter_direct(kv_parts)
    summed_first, squares = sum_shares(shares_first, 0)
    square_parts.append(squares)
    shares_second = cut_shares(keep_second, came_x_second)
    (summed_first,) = settle(summed_first)
    kv_parts = run_attend_back(1)
    kv_parts, first.kv_parts, (shares_second,) = settle_groups(
        kv_parts, first.kv_parts, [shares_second]
    )
    second.kv_parts = scatter_direct(kv_parts)
    own_first = exchange(summed_first).reshape(model, hidden)
    summed_second, squares = sum_shares(shares_second, 0)
    square_parts.append(squares)
    (summed_second,) = settle(summed_second)
    run_last(0)
    (first.norm_one,), second.kv_parts = settle_groups([first.norm_one], second.kv_parts)
    run_last(1)
    (second.norm_one,) = settle(second.norm_one)

    packed_parts = []
    for s in state:
        packed_parts += [s.grad_head, s.grad_patch, s.grad_keyval, s.grad_router]
        packed_parts += [s.norm_one, s.norm_two, s.norm_three, s.grad_att]
    used_rows = outputs + patch_in + pair_width + router_count + 6
    dense_rows = -(-used_rows // 256) * 256
    dense_share = dense_rows // peers
    all_rows = dense_share + 2 * span
    packed = small_call(
        partial(pack_kernel, peers, micros, dense_rows, (tasks, pixels, count_row)),
        (order[1],),
        packed_parts + [tables],
        [shape_of((half_peers, all_rows, model), BF16)]
        + [shape_of((1, all_rows, model), BF16)] * half_peers,
        [pltpu.VMEM((dense_rows, model), BF16)],
        "pack",
    )
    packed = settle(*packed)
    odd, evens = packed[0], packed[1:]
    crossed = swap(odd, "expert", 1)
    (crossed,) = settle(crossed)
    pairs = [
        (evens[n].astype(F32) + crossed[n : n + 1].astype(F32)).astype(BF16)
        for n in range(1, half_peers)
    ]
    pairs = settle(*pairs)
    lead_parts = [evens[0], crossed] + [
        swap(pair, "expert", 2 * n + 2) for n, pair in enumerate(pairs)
    ]
    own_first = after(own_first, order[1])
    own_second = exchange(summed_second).reshape(model, hidden)
    *lead_parts, scales = settle(*lead_parts, scales)
    parts = [(part, 0) for part in lead_parts]
    half_shape = shape_of((all_rows // 2, model), BF16)
    keep, send = call(
        partial(halves_kernel, len(parts)),
        (1,),
        (place,),
        [(part, pl.BlockSpec((1, all_rows, model), lambda *_, lead=lead: (lead, 0, 0))) for part, lead in parts],
        [(half_shape, kept_out(half_shape.shape))] * 2,
        [pltpu.VMEM((all_rows, model), BF16)],
        (0, 8 * all_rows * model),
        "halves",
        24,
    )
    keep, send = settle(keep, send)
    came = swap(send, "dp", 1)
    came, own_first = settle(came, own_first)
    other_first = swap(own_first, "dp", 1)
    (own_second,) = settle(own_second)
    shares, squares = sum_shares(cut_shares(keep, came), dense_share)
    sums = squares
    for part in square_parts:
        sums = sums + part
    sums, shares = settle(sums, shares)
    hops = Hops(sums, ("expert", "dp"))
    hops.start()
    own = exchange(shares).reshape(all_rows // 2, model)
    while len(hops.steps) > 2:
        hops.land(settle(*hops.came))
    (own, other_first), came = settle_groups([own, other_first], hops.came)
    other = swap(own, "dp", 1)
    hops.land(came)
    (other,), came = settle_groups([other], hops.came)
    hops.land(came)
    dense_part, attention_part = small_call(
        partial(join_halves_kernel, dense_share),
        (place,),
        [own, other],
        [shape_of((dense_share, model), BF16), shape_of((2 * span, model), BF16)],
        [pltpu.VMEM((all_rows, model), BF16)],
        "join_halves",
    )
    came_quarters = across(dense_part)
    (last_came,) = settle(*hops.came)
    sums = hops.value
    other_second = swap(after(own_second, order[1]), "dp", 1)
    total_params = (
        patch_weight.size
        + keyval_weight.size
        + router_weight.size
        + norm_weight.size
        + head_weight.size
        + (attention_weight.size + expert_weight.size) * peers
    )
    limit = CLIP_UNIT * math.sqrt(total_params)
    block_rows = model // 2
    def adam_expert(e, own, other, before):
        block = pl.BlockSpec((1, 1, block_rows, hidden), lambda w, b, *_: (e, w, b, 0))
        grad_block = pl.BlockSpec((block_rows, hidden), lambda w, b, *_: (b, 0))
        inputs = [own, other, sums, last_came, expert_weight, expert_moment, expert_square]
        specs = [grad_block, grad_block, whole(sums), whole(last_came), block, block, block]
        aliases = {}
        if before is not None:
            aliases = {2 + len(inputs) + n: n for n in range(3)}
            inputs += list(before)
            specs += [pl.BlockSpec(memory_space=pl.ANY)] * 3
        return pl.pallas_call(
            partial(adam_kernel, RATES[6], limit),
            grid_spec=pltpu.PrefetchScalarGridSpec(
                num_scalar_prefetch=2,
                grid=(2, model // block_rows),
                in_specs=specs,
                out_specs=[block] * 3,
            ),
            out_shape=[shape_of(expert_weight.shape, F32)] * 3,
            input_output_aliases=aliases,
            cost_estimate=pl.CostEstimate(
                flops=expert_weight.size * 20 // owned,
                bytes_accessed=expert_weight.size * 26 // owned,
                transcendentals=0,
            ),
            name="adam",
        )(place, scales, *inputs)

    expert_results = adam_expert(0, own_first, other_first, None)
    (expert_results, came_quarters) = settle_groups(list(expert_results), came_quarters)
    quarters = ordered(dense_part, came_quarters, beside(dense_part, came_quarters))
    expert_results = adam_expert(1, own_second, other_second, expert_results)
    dense_states = [
        head_weight,
        head_moment,
        head_square,
        patch_weight,
        patch_moment,
        patch_square,
        keyval_weight,
        keyval_moment,
        keyval_square,
        router_rows,
        router_moment.T,
        router_square.T,
        norm_weight,
        norm_moment,
        norm_square,
        attention_weight,
        attention_moment,
        attention_square,
    ]
    dense_results = small_call(
        partial(
            adam_dense_kernel,
            peers,
            (RATES[4], RATES[0], RATES[1], RATES[2], RATES[3], RATES[5]),
            limit,
            tasks,
            count_row,
        ),
        (order[1], scales),
        quarters
        + [attention_part, sums, last_came, tables, state[0].mutual]
        + dense_states,
        [shape_of(a.shape, F32) for a in dense_states] + [shape_of((1, 1), F32)] * 3,
        [pltpu.VMEM((dense_rows, model), BF16)],
        "adam_dense",
        None,
    )
    new_head, new_patch, new_keyval, new_router, new_norm, new_attention = [
        list(dense_results[3 * n : 3 * n + 3]) for n in range(6)
    ]
    new_router = [a.T for a in new_router]
    return tuple(
        [dense_results[18 + n].reshape(()) for n in range(3)]
        + new_patch
        + new_keyval
        + new_router
        + new_norm
        + new_head
        + new_attention
        + list(expert_results)
    )


def solution(mesh):
    tokens = P(None, "dp", "expert", None)
    by_columns = P(None, None, "expert")
    by_expert = P("expert", None, None, None)
    same = P()
    placed = (
        (tokens, P(None, "dp", "expert", None, None, None), tokens, tokens, P(None, "dp"), same)
        + (same,) * 15
        + (by_columns,) * 3
        + (by_expert,) * 3
    )
    return jax.shard_map(
        local,
        mesh=mesh,
        in_specs=placed,
        out_specs=(same,) * 18 + (by_columns,) * 3 + (by_expert,) * 3,
        check_vma=False,
    )
```
